32 devices in a mesh: fsdp: 32 (over z, y, x, core).
Axes of the slice: x: 2, y: 2, z: 4, core: 2. Of those that a mesh axis runs over, the one named last changes fastest.
Arguments:
- tokens: bfloat16 [65536, 768], P('fsdp'), may hold values from -6 to 6
- segments: int32 [65536], P('fsdp'), may hold values from 0 to 4, as said below
- cotangent: bfloat16 [65536, 768], P('fsdp'), may hold values from -6 to 6
- ln1_gain: float32 [768], P('fsdp'), may hold values from 0.25 to 1.75
- ln1_shift: float32 [768], P('fsdp'), may hold values from -3 to 3
- w_qkv: float32 [768, 2304], P('fsdp'), may hold values from -0.21875 to 0.21875
- bias_q: float32 [768], P('fsdp'), may hold values from -3 to 3
- bias_v: float32 [768], P('fsdp'), may hold values from -3 to 3
- w_out: float32 [768, 768], P('fsdp'), may hold values from -1.75 to 1.75
- bias_out: float32 [768], P('fsdp'), may hold values from -3 to 3
- ln2_gain: float32 [768], P('fsdp'), may hold values from 0.25 to 1.75
- ln2_shift: float32 [768], P('fsdp'), may hold values from -3 to 3
- w_up: float32 [768, 3072], P('fsdp'), may hold values from -0.21875 to 0.21875
- bias_up: float32 [3072], P('fsdp'), may hold values from -3 to 3
- w_down: float32 [3072, 768], P('fsdp'), may hold values from -0.109375 to 0.109375
- bias_down: float32 [768], P('fsdp'), may hold values from -3 to 3
Outputs:
- layer_out: bfloat16 [65536, 768], P('fsdp')
- input_grad: bfloat16 [65536, 768], P('fsdp')
- grad_ln1_gain: float32 [768], P('fsdp')
- grad_ln1_shift: float32 [768], P('fsdp')
- grad_w_qkv: float32 [768, 2304], P('fsdp')
- grad_bias_q: float32 [768], P('fsdp')
- grad_bias_v: float32 [768], P('fsdp')
- grad_w_out: float32 [768, 768], P('fsdp')
- grad_bias_out: float32 [768], P('fsdp')
- grad_ln2_gain: float32 [768], P('fsdp')
- grad_ln2_shift: float32 [768], P('fsdp')
- grad_w_up: float32 [768, 3072], P('fsdp')
- grad_bias_up: float32 [3072], P('fsdp')
- grad_w_down: float32 [3072, 768], P('fsdp')
- grad_bias_down: float32 [768], P('fsdp')
The draws below stay inside these ranges and needn't reach their ends.
Inputs may be any that keep to these rules, and one draw needn't show every extreme that they name: `segments`: in each sequence of 1024 positions, documents with ids 1 to 4 follow one another in order, each of 60 tokens or more, then padding with id 0, of one token or more, to the end.
All inputs are finite; a program needn't handle non-finite values.
Results may differ from the reference program's by a relative error of at most 0.012.
The reference program's roundings to bfloat16 on the way count: a program that leaves them out, or rounds other values in their place, can miss the bound.
Values may be sent and summed in bfloat16 or wider, within the bound.
A program may use at most 192 MiB of HBM per device.

```python
import math
import jax
import jax.numpy as jnp
from jax import lax

D = 768
HEADS = 12
HD = 64
FF = 3072
MICRO = 2
DOCS = 4
MINDOC = 60
SEQ = 1024
TOKENS = 65536
N_FSDP = 32


def draw_segments(key, part):
    first, second = jax.random.split(jax.random.fold_in(key, 17))
    count = N_FSDP * MICRO
    shares = jax.random.randint(first, (count, DOCS), 1, 65)
    padding = jax.random.randint(second, (count, 1), 1, SEQ // 8 + 1)
    avail = SEQ - padding - DOCS * MINDOC
    lengths = MINDOC + shares * avail // jnp.sum(shares, axis=1, keepdims=True)
    ends = jnp.cumsum(lengths, axis=1)
    places = jnp.arange(SEQ, dtype=jnp.int32)
    ids = jnp.sum((places[None, :, None] >= ends[:, None, :]).astype(jnp.int32), axis=2) + 1
    ids = jnp.where(ids > DOCS, 0, ids).astype(jnp.int32)
    return ids.reshape(-1)


def levels(key, shape, cuts, least, top_value):
    loudness = 1.0
    for position, shards_of in cuts:
        steps = jax.random.uniform(jax.random.fold_in(jax.random.fold_in(key, 6), position), (shards_of,), jnp.float32, least / len(cuts), top_value / len(cuts))
        loudness = loudness * jnp.repeat(jnp.exp(steps), shape[position] // shards_of).reshape((-1,) + (1,) * (len(shape) - 1 - position))
    return loudness


def normal_values(key, shape, width, bound, cuts=(), kind=jnp.bfloat16):
    level = levels(key, shape, cuts, -0.22, 0.18) if cuts else 1.0
    values = jax.random.normal(key, shape, jnp.float32) * width * level
    return jnp.minimum(jnp.maximum(values, -bound), bound).astype(kind)


def setup_inputs(seed: int = 0) -> dict:
    seeds = jax.random.split(jax.random.key(seed), 17)
    return {
        "tokens": normal_values(seeds[0], (TOKENS, D), 1.0, 6.0, ((0, 32),)),
        "segments": draw_segments(jax.random.fold_in(seeds[16], 71), 0),
        "cotangent": normal_values(seeds[2], (TOKENS, D), 1.0, 6.0, ((0, 32),)),
        "ln1_gain": jnp.clip(1.0 + 0.15 * jax.random.normal(seeds[3], (D,), jnp.float32), 0.25, 1.75),
        "ln1_shift": normal_values(seeds[4], (D,), 0.5, 3.0, ((0, 32),), jnp.float32),
        "w_qkv": normal_values(seeds[5], (D, 3 * D), D ** -0.5, 0.21875, ((0, 32),), jnp.float32),
        "bias_q": normal_values(seeds[6], (D,), 0.5, 3.0, ((0, 32),), jnp.float32),
        "bias_v": normal_values(seeds[7], (D,), 0.5, 3.0, ((0, 32),), jnp.float32),
        "w_out": normal_values(seeds[8], (D, D), (D // 64) ** -0.5, 1.75, ((0, 32),), jnp.float32),
        "bias_out": normal_values(seeds[9], (D,), 0.5, 3.0, ((0, 32),), jnp.float32),
        "ln2_gain": jnp.clip(1.0 + 0.15 * jax.random.normal(seeds[10], (D,), jnp.float32), 0.25, 1.75),
        "ln2_shift": normal_values(seeds[11], (D,), 0.5, 3.0, ((0, 32),), jnp.float32),
        "w_up": normal_values(seeds[12], (D, FF), D ** -0.5, 0.21875, ((0, 32),), jnp.float32),
        "bias_up": normal_values(seeds[13], (FF,), 0.5, 3.0, ((0, 32),), jnp.float32),
        "w_down": normal_values(seeds[14], (FF, D), FF ** -0.5, 0.109375, ((0, 32),), jnp.float32),
        "bias_down": normal_values(seeds[15], (D,), 0.5, 3.0, ((0, 32),), jnp.float32),
    }


@jax.custom_vjp
def low(v):
    return lax.optimization_barrier(v.astype(jnp.bfloat16)).astype(jnp.float32)

@jax.custom_vjp
def low_back(v):
    return v

def low_keep(v):
    return (low(v), None)

def low_pass(kept, grad):
    return (grad,)

def back_keep(v):
    return (v, None)

def back_low(kept, grad):
    return (low(grad),)
low.defvjp(low_keep, low_pass)
low_back.defvjp(back_keep, back_low)
EPSILON = 1e-06
HIGH = lax.Precision.HIGHEST
MASKED = -1000000000.0

def layer_norm(rows, gain, shift):
    mean = lax.optimization_barrier(jnp.mean(rows, axis=-1, keepdims=True))
    centered = rows - mean
    var = lax.optimization_barrier(jnp.mean(centered * centered, axis=-1, keepdims=True))
    return centered * lax.rsqrt(var + EPSILON) * gain + shift

def attend(pieces):
    query, key_rows, value_rows, segment = pieces
    qh = query.reshape(SEQ, HEADS, HD)
    kh = key_rows.reshape(SEQ, HEADS, HD)
    vh = value_rows.reshape(SEQ, HEADS, HD)
    scores = jnp.einsum('qhd,khd->hqk', qh, kh, precision=HIGH) * HD ** (-0.5)
    scores = low_back(scores)
    allowed = segment[:, None] == segment[None, :]
    scores = jnp.where(allowed[None], scores, MASKED)
    probs = low(jax.nn.softmax(scores, axis=-1))
    mixed = jnp.einsum('hqk,khd->qhd', probs, vh, precision=HIGH)
    return mixed.reshape(SEQ, D)

def forward(rows, params, segs):
    g1, c1, wqkv, bq, bv, wo, bo, g2, c2, w1, b1, w2, b2 = params
    count = segs.shape[0]
    n1 = low(layer_norm(rows, low(g1), low(c1)))
    qkv = jnp.dot(n1, low(wqkv), precision=HIGH)
    query = low_back(low(qkv[:, :D] + low(bq)))
    keys = low_back(low(qkv[:, D:2 * D]))
    values = low_back(low(qkv[:, 2 * D:] + low(bv)))
    shaped = (query.reshape(count, SEQ, D), keys.reshape(count, SEQ, D), values.reshape(count, SEQ, D), segs)
    attn = lax.map(jax.checkpoint(attend), shaped).reshape(count * SEQ, D)
    attn = low_back(low(attn))
    branch = low_back(jnp.dot(attn, low(wo), precision=HIGH) + low(bo))
    middle = rows + branch
    n2 = low(layer_norm(middle, low(g2), low(c2)))
    pre = low_back(jnp.dot(n2, low(w1), precision=HIGH) + low(b1))
    act = low(jax.nn.gelu(pre, approximate=True))
    return middle + jnp.dot(act, low(w2), precision=HIGH) + low(b2)

def reference(tokens, segments, cotangent, ln1_gain, ln1_shift, w_qkv, bias_q, bias_v, w_out, bias_out, ln2_gain, ln2_shift, w_up, bias_up, w_down, bias_down):
    params = tuple((p.astype(jnp.float32) for p in (ln1_gain, ln1_shift, w_qkv, bias_q, bias_v, w_out, bias_out, ln2_gain, ln2_shift, w_up, bias_up, w_down, bias_down)))
    nseq = TOKENS // SEQ
    group = math.gcd(max(1, 4096 // SEQ), nseq)
    rows = tokens.astype(jnp.float32).reshape(nseq // group, group, SEQ, D)
    segs = segments.reshape(nseq // group, group, SEQ)
    cots = cotangent.astype(jnp.float32).reshape(nseq // group, group, SEQ, D)

    def step(carry, pieces):
        xg, sg, cg = pieces

        def run(x_rows, *plist):
            return forward(x_rows, plist, sg)
        result, pull = jax.vjp(run, xg.reshape(group * SEQ, D), *params)
        grads = pull(cg.reshape(group * SEQ, D))
        carry = tuple((a + b for a, b in zip(carry, grads[1:])))
        return (carry, (result.reshape(group, SEQ, D), grads[0].reshape(group, SEQ, D)))
    init = tuple((jnp.zeros_like(p) for p in params))
    sums, (results, dxs) = lax.scan(step, init, (rows, segs, cots))
    layer_out = results.reshape(TOKENS, D).astype(jnp.bfloat16)
    input_grad = dxs.reshape(TOKENS, D).astype(jnp.bfloat16)
    return (layer_out, input_grad, sums[0], sums[1], sums[2], sums[3], sums[4], sums[5], sums[6], sums[7], sums[8], sums[9], sums[10], sums[11], sums[12])
```

```python
import functools
import jax
import jax.numpy as jnp
from jax import lax
from jax.experimental import pallas as pl
from jax.experimental.pallas import tpu as pltpu
from jax.sharding import PartitionSpec as P

HD = 64
QB = 128
KB = 128
NEG = -1000000000.0
BF = jnp.bfloat16
F32 = jnp.float32
EPSILON = 1e-06
NT = (((1,), (1,)), ((), ()))


def mm(a, b):
    return jnp.dot(a, b, preferred_element_type=F32)


def mm_nt(a, b):
    return lax.dot_general(a, b, NT, preferred_element_type=F32)


def pair_diag(top, bottom):
    zero = jnp.zeros_like(top)
    return jnp.concatenate(
        [jnp.concatenate([top, zero], axis=1), jnp.concatenate([zero, bottom], axis=1)], axis=0
    )


SPANS = (2, 3, 4, 5, 6, 8)


def by_span(lo, hi, rows, run):
    need = hi - lo
    below = 0
    for span in SPANS:
        if below * KB >= rows:
            break
        size = min(span * KB, rows)
        last = size == rows

        @pl.when((need > below) & (last | (need <= span)))
        def _(size=size):
            run(pl.multiple_of(jnp.minimum(lo * KB, rows - size), KB), size)

        below = span


def chunks(k0, size):
    return [(pl.multiple_of(k0 + c, KB), min(2 * KB, size - c)) for c in range(0, size, 2 * KB)]


def terms(pieces):
    width = pieces[0].shape[1]
    row = lax.broadcasted_iota(jnp.int32, (8, width), 0)
    tail = jnp.zeros((8, width), F32)
    for i, piece in enumerate(pieces):
        tail = jnp.where(row == i, piece, tail)
    return tail


def three_parts(x):
    first = x.astype(BF).astype(F32)
    rest = x - first
    second = rest.astype(BF).astype(F32)
    return first, second, rest - second


def pair_rhs(feat, extra, p, qs):
    a = 128 * p
    block = pair_diag(feat[a : a + 64, qs], feat[a + 64 : a + 128, qs])
    rows = jnp.concatenate([extra[2 * p, :, qs], extra[2 * p + 1, :, qs]], axis=1)
    return block, jnp.concatenate([block, rows, jnp.zeros((112, 2 * QB), BF)], axis=0)


def attn_fwd_kernel(
    earlier, lo, hi, q_ref, k_ref, v_ref, oh_ref, mr_ref, *rest
):
    o_ref, ot_ref, lse_ref, qt, vt, extra, tops = rest[earlier:]
    seq = pl.program_id(0)
    rows = q_ref.shape[0]
    pairs = q_ref.shape[1] // 128
    heads = 2 * pairs
    vt[...] = v_ref[...].T
    qt[...] = (q_ref[...] * 0.125).astype(BF).T
    lane = lax.broadcasted_iota(jnp.int32, (8, heads * HD), 1) // HD
    pick = (lane == lax.broadcasted_iota(jnp.int32, (8, heads * HD), 0)).astype(BF)
    square = k_ref[...].astype(F32)
    norms = mm_nt(pick, (square * square).astype(BF))
    bound = jnp.sqrt(jnp.max(norms, axis=1, keepdims=True)) * 1.01
    for h in range(heads):
        qh = qt[64 * h : 64 * h + 64, :].astype(F32)
        length = jnp.sqrt(jnp.sum(qh * qh, axis=0, keepdims=True)) * 1.01
        m = (length * bound[h : h + 1, :]).astype(BF).astype(F32)
        tops[h : h + 1, :] = m
        extra[h, :, :] = jnp.concatenate([mr_ref[0], terms([-m])], axis=0).astype(BF)

    def keep(qs, p, l, full):
        a = 128 * p
        ot_ref[0, a : a + 64, qs] = full[0:64, 0:QB]
        ot_ref[0, a + 64 : a + 128, qs] = full[64:128, QB:]
        lse_ref[0, 0, 2 * p : 2 * p + 1, qs] = l[:, 0:QB]
        lse_ref[0, 0, 2 * p + 1 : 2 * p + 2, qs] = l[:, QB:]

    def q_step(qb, carry):
        qs = pl.ds(pl.multiple_of(qb * QB, QB), QB)

        def run(k0, size):
            rhs = [pair_rhs(qt, extra, p, qs)[1] for p in range(pairs)]
            l = [jnp.zeros((1, 2 * QB), F32)] * pairs
            acc = [None] * pairs
            for c0, cs in chunks(k0, size):
                ks = pl.ds(c0, cs)
                oh = oh_ref[ks, :]
                for p in range(pairs):
                    cols = slice(128 * p, 128 * p + 128)
                    w = jnp.exp(mm(jnp.concatenate([k_ref[ks, cols], oh], axis=1), rhs[p]))
                    l[p] = l[p] + jnp.sum(w, axis=0, keepdims=True)
                    part = mm(vt[cols, ks], w.astype(BF))
                    acc[p] = part if acc[p] is None else acc[p] + part
            for p in range(pairs):
                keep(qs, p, l[p], acc[p])

        by_span(lo[seq, qb], hi[seq, qb], rows, run)
        return carry

    lax.fori_loop(0, rows // QB, q_step, 0)

    @pl.when(jnp.min(lse_ref[0, 0]) < 1e-20)
    def _():
        for h in range(heads):
            extra[h, :, :] = jnp.concatenate([mr_ref[0], jnp.zeros_like(mr_ref[0])], axis=0).astype(BF)

        def q_again(qb, carry):
            qs = pl.ds(pl.multiple_of(qb * QB, QB), QB)
            for p in range(pairs):
                cols = slice(128 * p, 128 * p + 128)
                rhs = pair_rhs(qt, extra, p, qs)[1]

                def scores(kb):
                    ks = pl.ds(pl.multiple_of(kb * KB, KB), KB)
                    return ks, mm(jnp.concatenate([k_ref[ks, cols], oh_ref[ks, :]], axis=1), rhs)

                def top_step(kb, m):
                    return jnp.maximum(m, jnp.max(scores(kb)[1], axis=0, keepdims=True))

                blocks = rows // KB
                m = lax.fori_loop(0, blocks, top_step, jnp.full((1, 2 * QB), 2 * NEG, F32))

                def sum_step(kb, state):
                    ks, st = scores(kb)
                    w = jnp.exp(st - m)
                    return state[0] + jnp.sum(w, axis=0, keepdims=True), state[1] + mm(vt[cols, ks], w.astype(BF))

                start = (jnp.zeros((1, 2 * QB), F32), jnp.zeros((128, 2 * QB), F32))
                l, full = lax.fori_loop(0, blocks, sum_step, start)
                tops[2 * p : 2 * p + 1, qs] = m[:, 0:QB]
                tops[2 * p + 1 : 2 * p + 2, qs] = m[:, QB:]
                keep(qs, p, l, full)
            return carry

        lax.fori_loop(0, rows // QB, q_again, 0)

    for h in range(heads):
        l = lse_ref[0, 0, h : h + 1, :]
        hs = slice(64 * h, 64 * h + 64)
        ot_ref[0, hs, :] = ot_ref[0, hs, :] * (1.0 / l)
        lse_ref[0, 0, h : h + 1, :] = tops[h : h + 1, :] + jnp.log(l)
    o_ref[...] = ot_ref[0].astype(BF).T


def attn_bwd_kernel(
    lo, hi, part, q_ref, k_ref, v_ref, do_ref, ot_ref, lse_ref, oh_ref, mr_ref, dqkv_ref,
    qt, kt, dot, extra_q, extra_d, dqt, dkt, dvt,
):
    seq = pl.program_id(0)
    rows = q_ref.shape[0]
    pairs = q_ref.shape[1] // 128
    qt[...] = (q_ref[...] * 0.125).astype(BF).T
    kt[...] = k_ref[...].T
    dot[...] = do_ref[...].T
    for h in range(2 * pairs):
        r = slice(64 * h, 64 * h + 64)
        delta = jnp.sum(dot[r, :].astype(F32) * ot_ref[0, r, :], axis=0, keepdims=True)
        lse = lse_ref[0, 0, h : h + 1, :]
        extra_q[h, :, :] = jnp.concatenate([mr_ref[0], terms(three_parts(-lse))], axis=0).astype(BF)
        tail = terms(three_parts(-delta))
        extra_d[h, :, :] = jnp.concatenate([jnp.zeros_like(tail), tail], axis=0).astype(BF)
    dkt[...] = jnp.zeros_like(dkt)
    dvt[...] = jnp.zeros_like(dvt)

    def q_step(qb, carry):
        qs = pl.ds(pl.multiple_of(qb * QB, QB), QB)

        def run(k0, size):
            ks = pl.ds(k0, size)
            oh = oh_ref[ks, :]
            for p in range(pairs):
                a = 128 * p
                cols = slice(a, a + 128)
                qm, qx = pair_rhs(qt, extra_q, p, qs)
                dom, dx = pair_rhs(dot, extra_d, p, qs)
                w = jnp.exp(mm(jnp.concatenate([k_ref[ks, cols], oh], axis=1), qx))
                ds = (w * mm(jnp.concatenate([v_ref[ks, cols], oh], axis=1), dx)).astype(BF)
                dvt[cols, ks] += mm_nt(dom, w.astype(BF))
                dkt[cols, ks] += mm_nt(qm, ds)
                dq = mm(kt[cols, ks], ds)
                dqt[a : a + 64, qs] = dq[0:64, 0:QB]
                dqt[a + 64 : a + 128, qs] = dq[64:128, QB:]

        by_span(lo[seq, qb], hi[seq, qb], rows, run)
        return carry

    lax.fori_loop(0, rows // QB, q_step, 0)
    wide = dqt.shape[0]
    dqkv_ref[:, 0:wide] = (dqt[...] * 0.125).astype(BF).T
    dqkv_ref[:, wide : 2 * wide] = dkt[...].astype(BF).T
    dqkv_ref[:, 2 * wide :] = dvt[...].astype(BF).T


WIDE = 384
TILE = 512
VMEM_LIMIT = 60 * 1024 * 1024


def params(*semantics):
    return pltpu.CompilerParams(dimension_semantics=semantics or None, vmem_limit_bytes=VMEM_LIMIT)


def cost(flops, data):
    return pl.CostEstimate(flops=int(flops), bytes_accessed=int(data), transcendentals=0)


def whole(shape):
    zero = (0,) * len(shape)
    return pl.BlockSpec(shape, lambda *_: zero)


ANYWHERE = pl.BlockSpec(memory_space=pl.ANY)


def attention_tables(segs):
    order = jnp.where(segs == 0, 1 << 20, segs)
    seqs, length = segs.shape
    first = order[:, ::QB]
    last = order[:, QB - 1 :: QB]
    lo = jnp.sum((order[:, None, :] < first[:, :, None]).astype(jnp.int32), axis=2) // KB
    hi = (jnp.sum((order[:, None, :] <= last[:, :, None]).astype(jnp.int32), axis=2) + KB - 1) // KB
    ids = jnp.arange(128, dtype=jnp.int32)[None, :]
    onehot = (segs.reshape(-1)[:, None] == ids) | ((ids >= 8) & (ids < 16))
    differ = segs[:, None, :] != jnp.arange(8, dtype=jnp.int32)[None, :, None]
    return lo, hi, onehot.astype(BF), jnp.where(differ, NEG, 0.0)


def attention_fwd(qkv, lo, hi, onehot, miss, part, earlier=()):
    seqs = lo.shape[0]
    rows = qkv.shape[0] // seqs
    wide = WIDE
    width = qkv.shape[1] // 3
    col = lambda at: pl.BlockSpec((rows, wide), lambda s, *_: (s, at))
    return pl.pallas_call(
        functools.partial(attn_fwd_kernel, len(earlier)),
        grid_spec=pltpu.PrefetchScalarGridSpec(
            num_scalar_prefetch=2,
            grid=(seqs,),
            in_specs=[
                col(3 * part), col(3 * part + 1), col(3 * part + 2),
                pl.BlockSpec((rows, 128), lambda s, *_: (s, 0)),
                pl.BlockSpec((1, 8, rows), lambda s, *_: (s, 0, 0)),
            ]
            + [ANYWHERE] * len(earlier),
            out_specs=[
                col(part),
                pl.BlockSpec((1, wide, rows), lambda s, *_: (s, part, 0)),
                pl.BlockSpec((1, 1, wide // HD, rows), lambda s, *_: (s, part, 0, 0)),
            ],
            scratch_shapes=[
                pltpu.VMEM((wide, rows), BF),
                pltpu.VMEM((wide, rows), BF),
                pltpu.VMEM((wide // HD, 16, rows), BF),
                pltpu.VMEM((8, rows), F32),
            ],
        ),
        out_shape=[
            jax.ShapeDtypeStruct((qkv.shape[0], width), BF),
            jax.ShapeDtypeStruct((seqs, width, rows), F32),
            jax.ShapeDtypeStruct((seqs, width // wide, wide // HD, rows), F32),
        ],
        input_output_aliases={7 + i: i for i in range(len(earlier))},
        compiler_params=params("arbitrary"),
        cost_estimate=cost(12e9, 2e7),
        name="attention_forward",
    )(lo, hi, qkv, qkv, qkv, onehot, miss, *earlier)


def attention_bwd(qkv, d_attn, ot, lse, lo, hi, onehot, miss, part):
    seqs = lo.shape[0]
    rows = qkv.shape[0] // seqs
    wide = WIDE
    col = lambda at: pl.BlockSpec((rows, wide), lambda s, lo, hi, p: (s, 3 * p[0] + at))
    return pl.pallas_call(
        attn_bwd_kernel,
        grid_spec=pltpu.PrefetchScalarGridSpec(
            num_scalar_prefetch=3,
            grid=(seqs,),
            in_specs=[
                col(0), col(1), col(2),
                pl.BlockSpec((rows, wide), lambda s, lo, hi, p: (s, p[0])),
                pl.BlockSpec((1, wide, rows), lambda s, lo, hi, p: (s, p[0], 0)),
                pl.BlockSpec((1, 1, wide // HD, rows), lambda s, lo, hi, p: (s, p[0], 0, 0)),
                pl.BlockSpec((rows, 128), lambda s, *_: (s, 0)),
                pl.BlockSpec((1, 8, rows), lambda s, *_: (s, 0, 0)),
            ],
            out_specs=pl.BlockSpec((rows, 3 * wide), lambda s, *_: (s, 0)),
            scratch_shapes=[
                pltpu.VMEM((wide, rows), BF),
                pltpu.VMEM((wide, rows), BF),
                pltpu.VMEM((wide, rows), BF),
                pltpu.VMEM((wide // HD, 16, rows), BF),
                pltpu.VMEM((wide // HD, 16, rows), BF),
                pltpu.VMEM((wide, rows), F32),
                pltpu.VMEM((wide, rows), F32),
                pltpu.VMEM((wide, rows), F32),
            ],
        ),
        out_shape=jax.ShapeDtypeStruct((qkv.shape[0], 3 * wide), BF),
        compiler_params=params("arbitrary"),
        cost_estimate=cost(22e9, 2e7),
        name="attention_backward",
    )(lo, hi, part, qkv, qkv, qkv, d_attn, ot, lse, onehot, miss)


def normalized(x):
    mean = jnp.mean(x, axis=-1, keepdims=True)
    centered = x - mean
    scale = lax.rsqrt(jnp.mean(centered * centered, axis=-1, keepdims=True) + EPSILON)
    return centered * scale, scale


def norm_back(d, xhat, scale, gain):
    e = d * gain
    return scale * (e - jnp.mean(e, axis=-1, keepdims=True) - xhat * jnp.mean(e * xhat, axis=-1, keepdims=True))


def clear_first(*refs):
    @pl.when(pl.program_id(0) == 0)
    def _():
        for ref in refs:
            ref[...] = jnp.zeros_like(ref)


def add_row(ref, row, values):
    ref[row : row + 1, 0 : values.shape[1]] += jnp.sum(values, axis=0, keepdims=True)


def fetch(place, core, held, other, spots, outs, sems):
    for c in range(2):

        @pl.when(core[0] == c)
        def _(c=c):
            for h in range(2):
                src = held if h == c else other
                for chip in range(place.shape[1]):
                    for row, count, which, target in spots(h, chip):
                        pltpu.make_async_copy(
                            src.at[place[h, chip], pl.ds(row, count), :], outs[which].at[target], sems.at[which]
                        ).start()


def fetched(out, sem):
    pltpu.make_async_copy(out, out, sem).wait()


def qkv_kernel(spots, place, core, tok, vec, bias, held, other, n1, qkv, w, sem):
    if spots is not None:

        @pl.when(pl.program_id(0) == 0)
        def _():
            fetch(place, core, held, other, spots, [w], sem)

    xhat, _ = normalized(tok[...].astype(F32))
    n = (xhat * vec[0:1] + vec[1:2]).astype(BF)
    n1[...] = n
    if spots is not None:

        @pl.when(pl.program_id(0) == 0)
        def _():
            fetched(w, sem.at[0])

    qkv[...] = (mm(n, w[...] if spots is not None else held[...]) + bias[...]).astype(BF)


def project_qkv(tokens, vec, bias, held, other, place, core, spots):
    count, width = tokens.shape
    cols = 3 * width
    tile = lambda w: pl.BlockSpec((TILE, w), lambda i, *_: (i, 0))
    return pl.pallas_call(
        functools.partial(qkv_kernel, spots),
        grid_spec=pltpu.PrefetchScalarGridSpec(
            num_scalar_prefetch=2,
            grid=(count // TILE,),
            in_specs=[tile(width), whole(vec.shape), whole(bias.shape), ANYWHERE, ANYWHERE],
            out_specs=[tile(width), tile(cols), whole((width, cols))],
            scratch_shapes=[pltpu.SemaphoreType.DMA((1,))],
        ),
        out_shape=[
            jax.ShapeDtypeStruct((count, width), BF),
            jax.ShapeDtypeStruct((count, cols), BF),
            jax.ShapeDtypeStruct((width, cols), BF),
        ],
        compiler_params=params("arbitrary"),
        cost_estimate=cost(2 * count * width * cols, 2e7),
        name="norm_and_qkv",
    )(place, core, tokens, vec, bias, held, other)


STRIP = 256
CURVE = 0.7978845608028654
CUBIC = 0.044715


def up_kernel(spots, place, core, attn, tok, vec, b1, held, other, mid, n2, pre, act, wo, w1, sem):
    @pl.when(pl.program_id(0) == 0)
    def _():
        fetch(place, core, held, other, spots, [wo, w1], sem)
        fetched(wo, sem.at[0])

    x = tok[...].astype(F32) + mm(attn[...], wo[...]) + vec[2:3]
    mid[...] = x
    xhat, _ = normalized(x)
    n = (xhat * vec[0:1] + vec[1:2]).astype(BF)
    n2[...] = n

    @pl.when(pl.program_id(0) == 0)
    def _():
        fetched(w1, sem.at[1])

    width = STRIP
    for j in range(w1.shape[1] // width):
        cols = slice(j * width, (j + 1) * width)
        u = mm(n, w1[:, cols]) + b1[:, cols]
        pre[:, cols] = u
        th = jnp.tanh(u * (CURVE + (CURVE * CUBIC) * (u * u)))
        act[:, cols] = (u * (0.5 + 0.5 * th)).astype(BF)


def up_part(attn, tokens, vec, b1, held, other, place, core, spots):
    count, width = tokens.shape
    hidden = b1.shape[1]
    rows = TILE // 2
    tile = lambda w: pl.BlockSpec((rows, w), lambda i, *_: (i, 0))
    return pl.pallas_call(
        functools.partial(up_kernel, spots),
        grid_spec=pltpu.PrefetchScalarGridSpec(
            num_scalar_prefetch=2,
            grid=(count // rows,),
            in_specs=[tile(width), tile(width), whole(vec.shape), whole(b1.shape), ANYWHERE, ANYWHERE],
            out_specs=[
                tile(width), tile(width), tile(hidden), tile(hidden), whole((width, width)), whole((width, hidden)),
            ],
            scratch_shapes=[pltpu.SemaphoreType.DMA((2,))],
        ),
        out_shape=[
            jax.ShapeDtypeStruct((count, width), F32),
            jax.ShapeDtypeStruct((count, width), BF),
            jax.ShapeDtypeStruct((count, hidden), F32),
            jax.ShapeDtypeStruct((count, hidden), BF),
            jax.ShapeDtypeStruct((width, width), BF),
            jax.ShapeDtypeStruct((width, hidden), BF),
        ],
        compiler_params=params("arbitrary"),
        cost_estimate=cost(2 * count * width * (width + hidden), 6e7),
        name="out_and_up",
    )(place, core, attn, tokens, vec, b1, held, other)


def down_kernel(
    spots, place, core, act, mid, pre, cot, vec, w1, wo, held, other,
    out, d_pre, d_mid, d_branch, d_attn, sums, sum_up, w2, sem,
):
    @pl.when(pl.program_id(0) == 0)
    def _():
        fetch(place, core, held, other, spots, [w2], sem)
        fetched(w2, sem.at[0])

    clear_first(sums, sum_up)
    x = mid[...]
    width = x.shape[1]
    d_out = cot[...]
    d_n2 = None
    y = x + vec[3:4]
    for j in range(act.shape[1] // width):
        cols = slice(j * width, (j + 1) * width)
        d_act = mm_nt(d_out, w2[cols, :])
        y = y + mm(act[:, cols], w2[cols, :])
        u = pre[:, cols]
        square = u * u
        th = jnp.tanh(u * (CURVE + (CURVE * CUBIC) * square))
        slope = (0.5 + 0.5 * th) + (0.5 * u) * (1.0 - th * th) * (CURVE + (3.0 * CURVE * CUBIC) * square)
        low = (d_act * slope).astype(BF)
        d_pre[:, cols] = low
        sum_up[:, cols] += jnp.sum(low.astype(F32), axis=0, keepdims=True)
        part = mm_nt(low, w1[:, cols])
        d_n2 = part if d_n2 is None else d_n2 + part
    out[...] = y.astype(BF)
    xhat, scale = normalized(x)
    add_row(sums, 0, d_n2 * xhat)
    add_row(sums, 1, d_n2)
    g = d_out.astype(F32)
    add_row(sums, 3, g)
    d = g + norm_back(d_n2, xhat, scale, vec[0:1])
    d_mid[...] = d
    low = d.astype(BF)
    d_branch[...] = low
    add_row(sums, 2, low.astype(F32))
    d_attn[...] = mm_nt(low, wo[...]).astype(BF)


def down_part(act, mid, pre, cotangent, vec, w1, wo, held, other, place, core, spots):
    count, width = mid.shape
    hidden = act.shape[1]
    rows = TILE // 2
    tile = lambda w: pl.BlockSpec((rows, w), lambda i, *_: (i, 0))
    return pl.pallas_call(
        functools.partial(down_kernel, spots),
        grid_spec=pltpu.PrefetchScalarGridSpec(
            num_scalar_prefetch=2,
            grid=(count // rows,),
            in_specs=[
                tile(hidden), tile(width), tile(hidden), tile(width), whole(vec.shape), whole(w1.shape),
                whole(wo.shape), ANYWHERE, ANYWHERE,
            ],
            out_specs=[
                tile(width), tile(hidden), tile(width), tile(width), tile(width), whole((8, width)), whole((1, hidden)),
            ],
            scratch_shapes=[pltpu.VMEM((hidden, width), BF), pltpu.SemaphoreType.DMA((1,))],
        ),
        out_shape=[
            jax.ShapeDtypeStruct((count, width), BF),
            jax.ShapeDtypeStruct((count, hidden), BF),
            jax.ShapeDtypeStruct((count, width), F32),
            jax.ShapeDtypeStruct((count, width), BF),
            jax.ShapeDtypeStruct((count, width), BF),
            jax.ShapeDtypeStruct((8, width), F32),
            jax.ShapeDtypeStruct((1, hidden), F32),
        ],
        compiler_params=params("arbitrary"),
        cost_estimate=cost(2 * count * width * (width + 3 * hidden), 8e7),
        name="down_and_back",
    )(place, core, act, mid, pre, cotangent, vec, w1, wo, held, other)


def first_norm_kernel(parts, far, near, w_far, w_near, tok, d_mid, vec, out, sums):
    clear_first(sums)
    d = mm_nt(far[...], w_far[...]) + mm_nt(near[...], w_near[...])
    xhat, scale = normalized(tok[...].astype(F32))
    add_row(sums, 0, d * xhat)
    add_row(sums, 1, d)
    add_row(sums, 2, far[...].astype(F32))
    add_row(sums, 3, near[...].astype(F32))
    out[...] = (d_mid[...] + norm_back(d, xhat, scale, vec[0:1])).astype(BF)


def first_norm_back(far, near, w, tokens, d_mid, vec, parts):
    count, width = tokens.shape
    cols = far.shape[1]
    tile = lambda w: pl.BlockSpec((TILE, w), lambda i, p: (i, 0))
    return pl.pallas_call(
        first_norm_kernel,
        grid_spec=pltpu.PrefetchScalarGridSpec(
            num_scalar_prefetch=1,
            grid=(count // TILE,),
            in_specs=[
                tile(cols), tile(cols),
                pl.BlockSpec((width, cols), lambda i, p: (0, p[0])),
                pl.BlockSpec((width, cols), lambda i, p: (0, p[1])),
                tile(width), tile(width), whole(vec.shape),
            ],
            out_specs=[tile(width), whole((8, cols))],
        ),
        out_shape=[jax.ShapeDtypeStruct((count, width), BF), jax.ShapeDtypeStruct((8, cols), F32)],
        compiler_params=params("arbitrary"),
        cost_estimate=cost(4 * count * width * cols, 3e7),
        name="first_norm_back",
    )(parts, far, near, w, w, tokens, d_mid, vec)


def tn(a, b):
    return lax.dot_general(a, b, (((0,), (0,)), ((), ())), preferred_element_type=F32)


def spread_chunks(send_at, keep_at, acc, got, send, keep):
    def body(j, carry):
        for at, out in ((send_at, send), (keep_at, keep)):
            i = at[j]
            out[j] = (acc[i].astype(F32) + got[i].astype(F32)).astype(BF)
        return carry

    lax.fori_loop(0, send.shape[0], body, 0)


def grad_down_kernel(near, part, send_at, keep_at, cot, act, *refs):
    got, outs, (turned, acc) = (refs[0], refs[1:3], refs[3:]) if near else (None, refs[:1], (refs[1], refs[0]))
    step = pl.program_id(0)

    @pl.when(step == 0)
    def _():
        turned[...] = cot[...].T

    sums = mm(turned[...], act[...])
    chips, blocks, rows, _ = acc.shape
    some = chips // pl.num_programs(0)
    sums = (sums if near else sums.astype(BF)).T.reshape(act.shape[1] // (blocks * rows), blocks, rows, WIDE)
    acc[pl.ds(step * sums.shape[0], sums.shape[0])] = sums.astype(acc.dtype)
    if near:

        @pl.when(step == pl.num_programs(0) - 1)
        def _():
            spread_chunks(send_at, keep_at, acc, got, *outs)


def grad_cols_kernel(widths, near, part, send_at, keep_at, *refs):
    count = len(widths)
    ins, refs = refs[: 2 * count], refs[2 * count :]
    got, outs, acc = (refs[0], refs[1:3], refs[3]) if near else (None, refs[:1], refs[0])
    step = pl.program_id(0)
    chips, _, rows, _ = acc.shape
    at = base = 0
    for k, (blocks, steps) in enumerate(widths):
        for i in range(steps):

            @pl.when(step == at + i)
            def _(k=k, blocks=blocks, first=base + i * blocks):
                sums = tn(ins[2 * k][...], ins[2 * k + 1][...]).astype(acc.dtype)
                for b in range(blocks):
                    acc[:, first + b] = sums[:, b * WIDE : (b + 1) * WIDE].reshape(chips, rows, WIDE)

        at += steps
        base += steps * blocks
    if near:

        @pl.when(step == pl.num_programs(0) - 1)
        def _():
            spread_chunks(send_at, keep_at, acc, got, *outs)


def grad_call(kernel, steps, specs, arrays, shape, part, got, order, scratch, flops, name):
    near = got is not None
    chips = shape[0]
    out = jax.ShapeDtypeStruct(((chips // 2,) if near else (chips,)) + shape[1:], BF)
    spec = whole(out.shape)
    if near:
        specs, arrays = specs + [whole(got.shape)], arrays + [got]
        scratch = scratch + [pltpu.VMEM(shape, F32)]
    return pl.pallas_call(
        kernel,
        grid_spec=pltpu.PrefetchScalarGridSpec(
            num_scalar_prefetch=3,
            grid=(steps,),
            in_specs=specs,
            out_specs=[spec, spec] if near else spec,
            scratch_shapes=scratch,
        ),
        out_shape=[out, out] if near else out,
        compiler_params=params("arbitrary"),
        cost_estimate=cost(flops, 2e7),
        name=name,
    )(part, *(order or (part, part)), *arrays)


def grad_down(cot, act, part, chips, name, got=None, order=None):
    tokens, width = cot.shape
    hidden = act.shape[1]
    shape = (chips, 4, hidden // chips // 4, WIDE)
    specs = [
        pl.BlockSpec((tokens, WIDE), lambda i, p, *_: (0, p[0])),
        pl.BlockSpec((tokens, width), lambda i, *_: (0, i)),
    ]
    return grad_call(
        functools.partial(grad_down_kernel, got is not None), hidden // width, specs, [cot, act], shape, part, got,
        order, [pltpu.VMEM((WIDE, tokens), BF)], 2 * tokens * WIDE * hidden, name,
    )


def grad_cols(pairs, part, chips, name, got=None, order=None):
    tokens, width = pairs[0][0].shape
    specs, arrays, widths, at, flops = [], [], [], 0, 0
    for lhs, rhs, blocks, steps, by_part in pairs:
        def column(i, p, *_, at=at, steps=steps, by_part=by_part):
            j = jnp.clip(i - at, 0, steps - 1)
            return (0, p[0] * steps + j if by_part else j)

        specs += [pl.BlockSpec((tokens, width), lambda i, *_: (0, 0)), pl.BlockSpec((tokens, blocks * WIDE), column)]
        arrays += [lhs, rhs]
        widths.append((blocks, steps))
        at += steps
        flops += 2 * tokens * width * WIDE * blocks * steps
    shape = (chips, sum(b * s for b, s in widths), width // chips, WIDE)
    return grad_call(
        functools.partial(grad_cols_kernel, tuple(widths), got is not None), at, specs, arrays, shape, part, got,
        order, [], flops, name,
    )


def here():
    me = lax.axis_index("fsdp")
    return me // 8, (me // 4) % 2, (me // 2) % 2, me % 2


def pairs_of(devices, move):
    depth = devices // 8
    found = []
    for i in range(devices):
        z, y, x, c = move(i // 8, (i // 4) % 2, (i // 2) % 2, i % 2)
        found.append((i, (((z % depth) * 2 + y) * 2 + x) * 2 + c))
    return found


class Moves:
    def __init__(self, devices):
        self.depth = devices // 8
        self.chips = devices // 2
        self.core = pairs_of(devices, lambda z, y, x, c: (z, y, x, 1 - c))
        self.first = pairs_of(devices, lambda z, y, x, c: (z, 1 - y, x, c) if c == 0 else (z, y, 1 - x, c))
        self.second = pairs_of(devices, lambda z, y, x, c: (z, y, 1 - x, c) if c == 0 else (z, 1 - y, x, c))
        self.deep = [pairs_of(devices, lambda z, y, x, c, k=k: (z + k, y, x, c)) for k in range(self.depth)]


def swap(x, moves):
    return lax.ppermute(x, "fsdp", moves)


def of_two(pick_second, a, b):
    return jnp.where(pick_second, b, a)


def pair_kernel(blocks, core, own, got, chunk):
    for c in range(2):

        @pl.when(core[0] == c)
        def _(c=c):
            parts = (own, got) if c == 0 else (got, own)
            at = 0
            for size in blocks:
                for k in range(2):
                    chunk[0, 2 * at + k * size : 2 * at + (k + 1) * size, :] = parts[k][at : at + size, :]
                at += size


def pair_rows(own, got, blocks, core):
    shape = jax.ShapeDtypeStruct((1, 2 * own.shape[0], own.shape[1]), BF)
    return pl.pallas_call(
        functools.partial(pair_kernel, blocks),
        grid_spec=pltpu.PrefetchScalarGridSpec(
            num_scalar_prefetch=1,
            grid=(1,),
            in_specs=[whole(own.shape), whole(own.shape)],
            out_specs=whole(shape.shape),
        ),
        out_shape=shape,
        name="pair_rows",
    )(core, own, got)


def pack_kernel(core, *refs):
    (wqkv, small, wo, w1, w2), outs = refs[:5], refs[5:]
    width = wo.shape[1]
    for c in range(2):

        @pl.when(core[0] == c)
        def _(c=c):
            for h in range(2):
                first, second, third = outs[:3] if h == c else outs[3:]
                rows = wo.shape[0]
                for t in range(3):
                    first[rows * t : rows * (t + 1), :] = wqkv[:, t * width + h * WIDE : t * width + (h + 1) * WIDE].astype(BF)
                first[3 * rows :, :] = small[...].astype(BF)
                second[0:rows, :] = wo[:, h * WIDE : (h + 1) * WIDE].astype(BF)
                for b in range(4):
                    cols = slice((4 * h + b) * WIDE, (4 * h + b + 1) * WIDE)
                    second[rows * (1 + b) : rows * (2 + b), :] = w1[:, cols].astype(BF)
                third[...] = w2[:, h * WIDE : (h + 1) * WIDE].astype(BF)


def pack(wqkv, small, wo, w1, w2, core):
    rows = wo.shape[0]
    ins = (wqkv, small, wo, w1, w2)
    shapes = [(3 * rows + small.shape[0], WIDE), (5 * rows, WIDE), (w2.shape[0], WIDE)] * 2
    return pl.pallas_call(
        pack_kernel,
        grid_spec=pltpu.PrefetchScalarGridSpec(
            num_scalar_prefetch=1,
            grid=(1,),
            in_specs=[whole(x.shape) for x in ins],
            out_specs=[whole(s) for s in shapes],
        ),
        out_shape=[jax.ShapeDtypeStruct(s, BF) for s in shapes],
        name="pack_shards",
    )(core, *ins)


def gate(x, *after):
    return lax.optimization_barrier((x,) + after)[0]


def chunk_places(moves):
    z, y, x, c = here()
    chip = jnp.arange(moves.chips, dtype=jnp.int32)
    deep = (z - chip // 4) % moves.depth
    far_y, far_x = (chip // 2) % 2 ^ y, chip % 2 ^ x
    half0 = (far_x * 2 + far_y) * moves.depth + deep
    half1 = (far_y * 2 + far_x) * moves.depth + deep
    return jnp.stack([half0, half1]).astype(jnp.int32), c.astype(jnp.int32).reshape(1)


def fold_kernel(send_at, keep_at, a_send, b_send, a_keep, b_keep, send, keep):
    send[...] = (a_send[...].astype(F32) + b_send[...].astype(F32)).astype(BF)
    keep[...] = (a_keep[...].astype(F32) + b_keep[...].astype(F32)).astype(BF)


def fold(a, b, send_at, keep_at):
    count = send_at.shape[0]
    block = (1,) + a.shape[1:]
    none = (0,) * (a.ndim - 1)
    sent = pl.BlockSpec(block, lambda j, s, k: (s[j],) + none)
    kept = pl.BlockSpec(block, lambda j, s, k: (k[j],) + none)
    out = pl.BlockSpec(block, lambda j, s, k: (j,) + none)
    shape = jax.ShapeDtypeStruct((count,) + a.shape[1:], BF)
    return pl.pallas_call(
        fold_kernel,
        grid_spec=pltpu.PrefetchScalarGridSpec(
            num_scalar_prefetch=2, grid=(count,), in_specs=[sent, sent, kept, kept], out_specs=[out, out]
        ),
        out_shape=[shape, shape],
        cost_estimate=pl.CostEstimate(flops=0, bytes_accessed=3 * 2 * a.size, transcendentals=0),
        name="fold_sums",
    )(send_at, keep_at, a, b, a, b)


def fold_places(moves):
    z, y, x, c = here()
    plane = jnp.arange(2 * moves.depth, dtype=jnp.int32)
    deep, side = plane // 2, plane % 2
    bit = jnp.where(c == 0, x, y)

    def spread(b):
        return jnp.where(c == 0, deep * 4 + side * 2 + b, deep * 4 + b * 2 + side).astype(jnp.int32)

    level = jnp.arange(moves.depth, dtype=jnp.int32)
    turn = (z + level) % moves.depth
    mine = jnp.where(c == 0, y, x)
    return (
        (spread(1 - bit), spread(bit)),
        ((turn * 2 + 1 - mine).astype(jnp.int32), (turn * 2 + mine).astype(jnp.int32)),
    )


def level_kernel(keep, got, first, *rest):
    first[...] = keep[0].astype(F32) + got[0].astype(F32)
    for k, out in enumerate(rest):
        out[...] = (keep[k + 1].astype(F32) + got[k + 1].astype(F32)).astype(BF)


def level(keep, got):
    shape = keep.shape[1:]
    outs = [jax.ShapeDtypeStruct(shape, F32)] + [jax.ShapeDtypeStruct(shape, BF)] * (keep.shape[0] - 1)
    return pl.pallas_call(
        level_kernel,
        in_specs=[whole(keep.shape)] * 2,
        out_specs=[whole(shape)] * keep.shape[0],
        grid=(1,),
        out_shape=outs,
        compiler_params=params("arbitrary"),
        cost_estimate=cost(0, 4 * keep.size),
        name="level_sums",
    )(keep, got)


def scattered_small(sums, moves, places):
    c = here()[3]
    odd = c == 1
    part = of_two(odd, sums[:, 0], sums[:, 1]) + swap(of_two(odd, sums[:, 1], sums[:, 0]), moves.core)
    for (send_at, keep_at), move in zip(places, (moves.second, moves.first)):
        part = jnp.take(part, keep_at, axis=0) + swap(jnp.take(part, send_at, axis=0), move)
    total = part[0]
    for k in range(1, moves.depth):
        total = total + swap(part[k], moves.deep[k])
    return total


def halves(total, cores_axis, moves):
    odd = here()[3] == 1
    zero = lax.index_in_dim(total, 0, cores_axis, keepdims=False)
    one = lax.index_in_dim(total, 1, cores_axis, keepdims=False)
    mine = of_two(odd, zero, one)
    got = swap(of_two(odd, one, zero), moves.core)
    return jnp.stack([of_two(odd, mine, got), of_two(odd, got, mine)])


def by_neighbours(devices, width, hidden, count):
    rows = width // devices
    fits = rows * devices == width and rows % 8 == 0 and devices % 8 == 0
    return fits and width == 2 * WIDE and hidden == 4 * width and count % TILE == 0


def weight_halves(w):
    rows = w.shape[0]
    return w.reshape(rows, 3, 2, WIDE).transpose(0, 2, 1, 3).reshape(rows, -1)


def local(
    tokens, segments, cotangent, ln1_gain, ln1_shift, w_qkv, bias_q, bias_v, w_out, bias_out,
    ln2_gain, ln2_shift, w_up, bias_up, w_down, bias_down, *, seq,
):
    masters = (
        ln1_gain, ln1_shift, w_qkv, bias_q, bias_v, w_out, bias_out,
        ln2_gain, ln2_shift, w_up, bias_up, w_down, bias_down,
    )
    count, width = tokens.shape
    tables = attention_tables(segments.reshape(-1, seq))
    run = by_chips if by_neighbours(lax.axis_size("fsdp"), width, w_up.shape[1], count) else by_collectives
    return run(tokens, cotangent, tables, masters)


def by_collectives(tokens, cotangent, tables, masters):
    def norm(x, gain, shift):
        return normalized(x)[0] * gain + shift

    width = tokens.shape[1]
    full = [lax.all_gather(m.astype(BF), "fsdp", axis=0, tiled=True) for m in masters]
    g1, c1, wqkv, bq, bv, wo, bo, g2, c2, w1, b1, w2, b2 = [p.astype(F32) if p.ndim == 1 else p for p in full]
    wqkv = weight_halves(wqkv)
    rows = tokens.astype(F32)
    n1 = norm(rows, g1, c1).astype(BF)
    bias = weight_halves(jnp.concatenate([bq, jnp.zeros_like(bq), bv])[None])
    qkv = (mm(n1, wqkv) + bias).astype(BF)
    kept = attention_fwd(qkv, *tables, 0)
    attn, attn_t, lse = attention_fwd(qkv, *tables, 1, tuple(kept))
    middle = rows + mm(attn, wo) + bo
    n2 = norm(middle, g2, c2).astype(BF)
    act_value, gelu_pull = jax.vjp(functools.partial(jax.nn.gelu, approximate=True), mm(n2, w1) + b1)
    act = act_value.astype(BF)
    layer_out = (middle + mm(act, w2) + b2).astype(BF)
    d_out = cotangent.astype(F32)
    d_pre = gelu_pull(mm_nt(cotangent, w2))[0].astype(BF)
    _, pull = jax.vjp(norm, middle, g2, c2)
    d_mid, d_g2, d_c2 = pull(mm_nt(d_pre, w1))
    d_mid = d_out + d_mid
    d_branch = d_mid.astype(BF)
    d_attn = mm_nt(d_branch, wo).astype(BF)
    parts = [
        attention_bwd(qkv, d_attn, attn_t, lse, *tables, jnp.full((1,), h, jnp.int32)) for h in range(2)
    ]
    d_qkv = jnp.concatenate(parts, axis=1)
    _, pull = jax.vjp(norm, rows, g1, c1)
    d_rows, d_g1, d_c1 = pull(mm_nt(d_qkv, wqkv))
    input_grad = (d_mid + d_rows).astype(BF)
    total = lambda x: jnp.sum(x.astype(F32), axis=0)
    by_part = lambda x: x.reshape(-1, 2, 3, WIDE).transpose(0, 2, 1, 3).reshape(x.shape)
    sums = by_part(total(d_qkv)[None])[0]
    grads = (
        d_g1, d_c1, by_part(tn(n1, d_qkv)), sums[:width], sums[2 * width :], tn(attn, d_branch), total(d_branch),
        d_g2, d_c2, tn(n2, d_pre), total(d_pre), tn(act, cotangent), total(d_out),
    )
    return (layer_out, input_grad) + tuple(
        lax.psum_scatter(g, "fsdp", scatter_dimension=0, tiled=True) for g in grads
    )


def by_chips(tokens, cotangent, tables, masters):
    devices = lax.axis_size("fsdp")
    moves = Moves(devices)
    chips = moves.chips
    count, width = tokens.shape
    ln1_gain, ln1_shift, w_qkv, bias_q, bias_v, w_out, bias_out, ln2_gain, ln2_shift, w_up, bias_up, w_down, bias_down = masters
    part = width // devices
    two = 2 * part
    hidden = w_up.shape[1]
    places, core = chunk_places(moves)

    small = jnp.concatenate([ln1_gain, ln1_shift, bias_q, bias_v, bias_out, ln2_gain, ln2_shift, bias_down, bias_up])
    small = jnp.pad(small[None], ((0, 7), (0, WIDE - small.shape[0])))
    own1, own2, own3, oth1, oth2, oth3 = pack(w_qkv, small, w_out, w_up, w_down, core)

    def deep(chunk):
        return jnp.concatenate([chunk] + [swap(chunk, moves.deep[k]) for k in range(1, moves.depth)], axis=0)

    def along(held, move):
        return jnp.concatenate([held, swap(held, move)], axis=0)

    got1, got2, got3 = swap(oth1, moves.core), swap(oth2, moves.core), swap(oth3, moves.core)
    chunk1 = pair_rows(own1, got1, [part] * 3 + [8], core)
    chunk2 = pair_rows(own2, got2, [part] * 5, core)
    chunk3 = pair_rows(own3, got3, [4 * part], core)
    held1 = deep(chunk1)
    held1 = along(held1, moves.first)
    deep2 = [swap(gate(chunk2, held1), moves.deep[k]) for k in range(1, moves.depth)]
    held1 = along(held1, moves.second)
    other1 = swap(held1, moves.core)

    vecs = jnp.take(held1[:, 6 * part :: 8], of_two(core[0] == 1, places[0], places[1]), axis=0)
    vecs = vecs.reshape(devices, WIDE).astype(F32)
    g1, c1, bq, bv, bo, g2, c2, b2 = [vecs[:, i * part : (i + 1) * part].reshape(-1) for i in range(8)]
    b1 = vecs[:, 8 * part : 12 * part].reshape(1, -1)
    bias = weight_halves(jnp.concatenate([bq, jnp.zeros_like(bq), bv])[None])

    def spots_qkv(h, chip):
        return [
            (two * t, two, 0, (pl.ds(two * chip, two), pl.ds((3 * h + t) * WIDE, WIDE))) for t in range(3)
        ]

    def spots_up(h, chip):
        rows = pl.ds(two * chip, two)
        return [(0, two, 0, (rows, pl.ds(h * WIDE, WIDE)))] + [
            (two * (1 + b), two, 1, (rows, pl.ds((4 * h + b) * WIDE, WIDE))) for b in range(4)
        ]

    def spots_down(h, chip):
        return [(0, 4 * two, 0, (pl.ds(4 * two * chip, 4 * two), pl.ds(h * WIDE, WIDE)))]

    n1, qkv, wqkv = project_qkv(tokens, jnp.stack([g1, c1]), bias, held1, other1, places, core, spots_qkv)
    deep2 = lax.optimization_barrier(tuple(deep2) + (qkv,))[:-1]
    held2 = along(jnp.concatenate([chunk2, *deep2], axis=0), moves.first)
    deep3 = [swap(gate(chunk3, held2), moves.deep[k]) for k in range(1, moves.depth)]
    kept = attention_fwd(gate(qkv, held2), *tables, 0)
    more2 = swap(held2, moves.second)
    *deep3, more2 = lax.optimization_barrier(tuple(deep3) + (more2, kept[0]))[:-1]
    held2 = jnp.concatenate([held2, more2], axis=0)
    held3 = jnp.concatenate([chunk3, *deep3], axis=0)
    kept = lax.optimization_barrier(tuple(kept) + (held2, held3))[:3]
    other2 = swap(held2, moves.core)
    more3 = swap(held3, moves.first)
    attn, attn_t, lse = attention_fwd(qkv, *tables, 1, tuple(kept))
    held3 = jnp.concatenate([held3, gate(more3, attn)], axis=0)
    more3 = swap(held3, moves.second)
    mid, n2, pre, act, wo, w1 = up_part(
        gate(attn, held3), tokens, jnp.stack([g2, c2, bo]), b1, held2, gate(other2, attn), places, core, spots_up
    )
    held3 = jnp.concatenate([held3, gate(more3, act)], axis=0)
    other3 = swap(held3, moves.core)

    far, near = 1 - core, core
    orders = fold_places(moves)
    sent_down = grad_down(gate(cotangent, held3), act, far, chips, "grad_down_far")
    got_down = swap(sent_down, moves.core)
    layer_out, d_pre, d_mid, d_branch, d_attn, sums2, sum_up = down_part(
        gate(act, sent_down), mid, pre, cotangent, jnp.stack([g2, g2, g2, b2]), w1, wo, held3, gate(other3, sent_down),
        places, core, spots_down,
    )
    ups = lambda n2: [(n2, d_pre, 2, 2, True), (attn, d_branch, 1, 1, True)]
    sent_up = grad_cols(ups(n2), far, chips, "grad_up_out_far")
    got_up = swap(sent_up, moves.core)
    send_down, keep_down = grad_down(
        gate(cotangent, sent_up), act, near, chips, "grad_down_near", gate(got_down, d_pre), orders[0]
    )
    got_down = swap(send_down, moves.second)
    send_up, keep_up = grad_cols(
        ups(gate(n2, send_down)), near, chips, "grad_up_out_near", gate(got_up, send_down), orders[0]
    )
    got_up = swap(send_up, moves.second)
    d_qkv_far = attention_bwd(qkv, gate(d_attn, send_up), attn_t, lse, *tables, far)
    send_down, keep_down = fold(keep_down, gate(got_down, d_qkv_far), *orders[1])
    got_down = swap(send_down, moves.first)
    send_up, keep_up = fold(keep_up, gate(got_up, d_qkv_far), *orders[1])
    got_up = swap(send_up, moves.first)
    sent_qkv = grad_cols(
        [(gate(n1, send_up, send_down), d_qkv_far, 3, 1, False)], far, chips, "grad_qkv_far"
    )
    got_qkv = swap(sent_qkv, moves.core)
    d_qkv_near = attention_bwd(qkv, gate(d_attn, sent_qkv), attn_t, lse, *tables, near)

    def spread(others):
        return [swap(x, moves.deep[k + 1]) for k, x in enumerate(others)]

    def total_of(first, gots):
        return sum((g.astype(F32) for g in gots), first)

    first_down, *rest_down = level(keep_down, gate(got_down, d_qkv_near))
    first_up, *rest_up = level(keep_up, gate(got_up, d_qkv_near))
    gots_down, gots_up = spread(rest_down), spread(rest_up)
    send_qkv, keep_qkv = grad_cols(
        [(gate(n1, first_down, first_up), d_qkv_near, 3, 1, False)], near, chips, "grad_qkv_near",
        gate(got_qkv, d_qkv_near), orders[0],
    )
    got_qkv = swap(send_qkv, moves.second)
    input_grad, sums1 = first_norm_back(
        d_qkv_far, gate(d_qkv_near, send_qkv), wqkv, tokens, d_mid, g1[None], jnp.concatenate([far, near])
    )
    send_qkv, keep_qkv = fold(keep_qkv, gate(got_qkv, sums1), *orders[1])
    got_qkv = swap(send_qkv, moves.first)

    odd = core[0] == 1
    by_half = [of_two(odd, sums1[3], sums1[2]), of_two(odd, sums1[2], sums1[3])]
    d_bq = jnp.concatenate([s[:WIDE] for s in by_half])
    d_bv = jnp.concatenate([s[2 * WIDE :] for s in by_half])
    vecs = [sums1[0, :width], sums1[1, :width], d_bq, d_bv, sums2[2], sums2[0], sums2[1], sums2[3]]
    small = jnp.concatenate([v.reshape(devices, part) for v in vecs] + [sum_up.reshape(devices, 4 * part)], axis=1)
    small = jnp.pad(small, ((0, 0), (0, WIDE - small.shape[1]))).reshape(chips, 2, WIDE)
    small = scattered_small(small, moves, orders)
    s = [small[i * part : (i + 1) * part] for i in range(8)]
    s_b1 = small[8 * part : 12 * part]

    total_down = total_of(first_down, gots_down)
    both_halves = halves(total_down.reshape(2, 4 * part, WIDE), 0, moves)
    g_down = both_halves.transpose(1, 0, 2).reshape(4 * part, width)
    total_up = total_of(first_up, gots_up)
    both_halves = halves(total_up.reshape(5, 2, part, WIDE), 1, moves)
    g_up = both_halves[:, :4].transpose(2, 0, 1, 3).reshape(part, hidden)
    g_out = both_halves[:, 4].transpose(1, 0, 2).reshape(part, width)
    first_qkv, *rest_qkv = level(keep_qkv, got_qkv)
    total_qkv = total_of(first_qkv, spread(rest_qkv))
    both_halves = halves(total_qkv.reshape(3, 2, part, WIDE), 1, moves)
    g_qkv = both_halves.transpose(2, 1, 0, 3).reshape(part, 3 * width)
    return (
        layer_out, input_grad, s[0], s[1], g_qkv, s[2], s[3], g_out, s[4], s[5], s[6], g_up, s_b1, g_down, s[7],
    )


MICRO = 2


def solution(mesh):
    line, table = P("fsdp"), P("fsdp", None)
    weights = (line, line, table, line, line, table, line, line, line, table, line, table, line)

    def step(tokens, *rest):
        seq = tokens.shape[0] // (mesh.shape["fsdp"] * MICRO)
        return jax.shard_map(
            functools.partial(local, seq=seq),
            mesh=mesh,
            in_specs=(table, line, table) + weights,
            out_specs=(table, table) + weights,
            check_vma=False,
        )(tokens, *rest)

    return step
```

```python
import functools
import jax
import jax.numpy as jnp
from jax import lax
from jax.experimental import pallas as pl
from jax.experimental.pallas import tpu as pltpu
from jax.sharding import PartitionSpec as P

HD = 64
QB = 128
KB = 128
NEG = -1000000000.0
BF = jnp.bfloat16
F32 = jnp.float32
EPSILON = 1e-06
NT = (((1,), (1,)), ((), ()))


def mm(a, b):
    return jnp.dot(a, b, preferred_element_type=F32)


def mm_nt(a, b):
    return lax.dot_general(a, b, NT, preferred_element_type=F32)


def pair_diag(top, bottom):
    zero = jnp.zeros_like(top)
    return jnp.concatenate(
        [jnp.concatenate([top, zero], axis=1), jnp.concatenate([zero, bottom], axis=1)], axis=0
    )


SPANS = (2, 3, 4, 5, 6, 8)


def by_span(lo, hi, rows, run):
    need = hi - lo
    below = 0
    for span in SPANS:
        if below * KB >= rows:
            break
        size = min(span * KB, rows)
        last = size == rows

        @pl.when((need > below) & (last | (need <= span)))
        def _(size=size):
            run(pl.multiple_of(jnp.minimum(lo * KB, rows - size), KB), size)

        below = span


def chunks(k0, size):
    return [(pl.multiple_of(k0 + c, KB), min(2 * KB, size - c)) for c in range(0, size, 2 * KB)]


def terms(pieces):
    width = pieces[0].shape[1]
    row = lax.broadcasted_iota(jnp.int32, (8, width), 0)
    tail = jnp.zeros((8, width), F32)
    for i, piece in enumerate(pieces):
        tail = jnp.where(row == i, piece, tail)
    return tail


def three_parts(x):
    first = x.astype(BF).astype(F32)
    rest = x - first
    second = rest.astype(BF).astype(F32)
    return first, second, rest - second


def pair_rhs(feat, extra, p, qs):
    a = 128 * p
    block = pair_diag(feat[a : a + 64, qs], feat[a + 64 : a + 128, qs])
    rows = jnp.concatenate([extra[2 * p, :, qs], extra[2 * p + 1, :, qs]], axis=1)
    return block, jnp.concatenate([block, rows, jnp.zeros((112, 2 * QB), BF)], axis=0)


def attn_fwd_kernel(
    lo, hi, q_ref, k_ref, v_ref, oh_ref, mr_ref, o_ref, ot_ref, lse_ref, qt, vt, extra, tops
):
    seq = pl.program_id(0)
    rows = q_ref.shape[0]
    pairs = q_ref.shape[1] // 128
    heads = 2 * pairs
    vt[...] = v_ref[...].T
    qt[...] = (q_ref[...] * 0.125).astype(BF).T
    lane = lax.broadcasted_iota(jnp.int32, (8, heads * HD), 1) // HD
    pick = (lane == lax.broadcasted_iota(jnp.int32, (8, heads * HD), 0)).astype(BF)
    square = k_ref[...].astype(F32)
    norms = mm_nt(pick, (square * square).astype(BF))
    bound = jnp.sqrt(jnp.max(norms, axis=1, keepdims=True)) * 1.01
    for h in range(heads):
        qh = qt[64 * h : 64 * h + 64, :].astype(F32)
        length = jnp.sqrt(jnp.sum(qh * qh, axis=0, keepdims=True)) * 1.01
        m = (length * bound[h : h + 1, :]).astype(BF).astype(F32)
        tops[h : h + 1, :] = m
        extra[h, :, :] = jnp.concatenate([mr_ref[0], terms([-m])], axis=0).astype(BF)

    def keep(qs, p, l, full):
        a = 128 * p
        ot_ref[0, a : a + 64, qs] = full[0:64, 0:QB]
        ot_ref[0, a + 64 : a + 128, qs] = full[64:128, QB:]
        lse_ref[0, 0, 2 * p : 2 * p + 1, qs] = l[:, 0:QB]
        lse_ref[0, 0, 2 * p + 1 : 2 * p + 2, qs] = l[:, QB:]

    def q_step(qb, carry):
        qs = pl.ds(pl.multiple_of(qb * QB, QB), QB)

        def run(k0, size):
            rhs = [pair_rhs(qt, extra, p, qs)[1] for p in range(pairs)]
            l = [jnp.zeros((1, 2 * QB), F32)] * pairs
            acc = [None] * pairs
            for c0, cs in chunks(k0, size):
                ks = pl.ds(c0, cs)
                oh = oh_ref[ks, :]
                for p in range(pairs):
                    cols = slice(128 * p, 128 * p + 128)
                    w = jnp.exp(mm(jnp.concatenate([k_ref[ks, cols], oh], axis=1), rhs[p]))
                    l[p] = l[p] + jnp.sum(w, axis=0, keepdims=True)
                    part = mm(vt[cols, ks], w.astype(BF))
                    acc[p] = part if acc[p] is None else acc[p] + part
            for p in range(pairs):
                keep(qs, p, l[p], acc[p])

        by_span(lo[seq, qb], hi[seq, qb], rows, run)
        return carry

    lax.fori_loop(0, rows // QB, q_step, 0)

    @pl.when(jnp.min(lse_ref[0, 0]) < 1e-20)
    def _():
        for h in range(heads):
            extra[h, :, :] = jnp.concatenate([mr_ref[0], jnp.zeros_like(mr_ref[0])], axis=0).astype(BF)

        def q_again(qb, carry):
            qs = pl.ds(pl.multiple_of(qb * QB, QB), QB)
            for p in range(pairs):
                cols = slice(128 * p, 128 * p + 128)
                rhs = pair_rhs(qt, extra, p, qs)[1]

                def scores(kb):
                    ks = pl.ds(pl.multiple_of(kb * KB, KB), KB)
                    return ks, mm(jnp.concatenate([k_ref[ks, cols], oh_ref[ks, :]], axis=1), rhs)

                def top_step(kb, m):
                    return jnp.maximum(m, jnp.max(scores(kb)[1], axis=0, keepdims=True))

                blocks = rows // KB
                m = lax.fori_loop(0, blocks, top_step, jnp.full((1, 2 * QB), 2 * NEG, F32))

                def sum_step(kb, state):
                    ks, st = scores(kb)
                    w = jnp.exp(st - m)
                    return state[0] + jnp.sum(w, axis=0, keepdims=True), state[1] + mm(vt[cols, ks], w.astype(BF))

                start = (jnp.zeros((1, 2 * QB), F32), jnp.zeros((128, 2 * QB), F32))
                l, full = lax.fori_loop(0, blocks, sum_step, start)
                tops[2 * p : 2 * p + 1, qs] = m[:, 0:QB]
                tops[2 * p + 1 : 2 * p + 2, qs] = m[:, QB:]
                keep(qs, p, l, full)
            return carry

        lax.fori_loop(0, rows // QB, q_again, 0)

    for h in range(heads):
        l = lse_ref[0, 0, h : h + 1, :]
        hs = slice(64 * h, 64 * h + 64)
        ot_ref[0, hs, :] = ot_ref[0, hs, :] * (1.0 / l)
        lse_ref[0, 0, h : h + 1, :] = tops[h : h + 1, :] + jnp.log(l)
    o_ref[...] = ot_ref[0].astype(BF).T


def attn_bwd_kernel(
    lo, hi, part, q_ref, k_ref, v_ref, do_ref, ot_ref, lse_ref, oh_ref, mr_ref, dqkv_ref,
    qt, kt, dot, extra_q, extra_d, dqt, dkt, dvt,
):
    seq = pl.program_id(0)
    rows = q_ref.shape[0]
    pairs = q_ref.shape[1] // 128
    qt[...] = (q_ref[...] * 0.125).astype(BF).T
    kt[...] = k_ref[...].T
    dot[...] = do_ref[...].T
    for h in range(2 * pairs):
        r = slice(64 * h, 64 * h + 64)
        delta = jnp.sum(dot[r, :].astype(F32) * ot_ref[0, r, :], axis=0, keepdims=True)
        lse = lse_ref[0, 0, h : h + 1, :]
        extra_q[h, :, :] = jnp.concatenate([mr_ref[0], terms(three_parts(-lse))], axis=0).astype(BF)
        tail = terms(three_parts(-delta))
        extra_d[h, :, :] = jnp.concatenate([jnp.zeros_like(tail), tail], axis=0).astype(BF)
    dkt[...] = jnp.zeros_like(dkt)
    dvt[...] = jnp.zeros_like(dvt)

    def q_step(qb, carry):
        qs = pl.ds(pl.multiple_of(qb * QB, QB), QB)

        def run(k0, size):
            ks = pl.ds(k0, size)
            oh = oh_ref[ks, :]
            for p in range(pairs):
                a = 128 * p
                cols = slice(a, a + 128)
                qm, qx = pair_rhs(qt, extra_q, p, qs)
                dom, dx = pair_rhs(dot, extra_d, p, qs)
                w = jnp.exp(mm(jnp.concatenate([k_ref[ks, cols], oh], axis=1), qx))
                ds = (w * mm(jnp.concatenate([v_ref[ks, cols], oh], axis=1), dx)).astype(BF)
                dvt[cols, ks] += mm_nt(dom, w.astype(BF))
                dkt[cols, ks] += mm_nt(qm, ds)
                dq = mm(kt[cols, ks], ds)
                dqt[a : a + 64, qs] = dq[0:64, 0:QB]
                dqt[a + 64 : a + 128, qs] = dq[64:128, QB:]

        by_span(lo[seq, qb], hi[seq, qb], rows, run)
        return carry

    lax.fori_loop(0, rows // QB, q_step, 0)
    wide = dqt.shape[0]
    dqkv_ref[:, 0:wide] = (dqt[...] * 0.125).astype(BF).T
    dqkv_ref[:, wide : 2 * wide] = dkt[...].astype(BF).T
    dqkv_ref[:, 2 * wide :] = dvt[...].astype(BF).T


WIDE = 384
TILE = 512
VMEM_LIMIT = 60 * 1024 * 1024


def params(*semantics):
    return pltpu.CompilerParams(dimension_semantics=semantics or None, vmem_limit_bytes=VMEM_LIMIT)


def cost(flops, data):
    return pl.CostEstimate(flops=int(flops), bytes_accessed=int(data), transcendentals=0)


def whole(shape):
    zero = (0,) * len(shape)
    return pl.BlockSpec(shape, lambda *_: zero)


ANYWHERE = pl.BlockSpec(memory_space=pl.ANY)


def attention_tables(segs):
    order = jnp.where(segs == 0, 1 << 20, segs)
    seqs, length = segs.shape
    first = order[:, ::QB]
    last = order[:, QB - 1 :: QB]
    lo = jnp.sum((order[:, None, :] < first[:, :, None]).astype(jnp.int32), axis=2) // KB
    hi = (jnp.sum((order[:, None, :] <= last[:, :, None]).astype(jnp.int32), axis=2) + KB - 1) // KB
    ids = jnp.arange(128, dtype=jnp.int32)[None, :]
    onehot = (segs.reshape(-1)[:, None] == ids) | ((ids >= 8) & (ids < 16))
    differ = segs[:, None, :] != jnp.arange(8, dtype=jnp.int32)[None, :, None]
    return lo, hi, onehot.astype(BF), jnp.where(differ, NEG, 0.0)


def attention_fwd(qkv, lo, hi, onehot, miss):
    seqs = lo.shape[0]
    rows = qkv.shape[0] // seqs
    wide = WIDE
    width = qkv.shape[1] // 3
    parts = width // wide
    col = lambda at: pl.BlockSpec((rows, wide), lambda s, j, *_: (s, 3 * j + at))
    return pl.pallas_call(
        attn_fwd_kernel,
        grid_spec=pltpu.PrefetchScalarGridSpec(
            num_scalar_prefetch=2,
            grid=(seqs, parts),
            in_specs=[
                col(0), col(1), col(2),
                pl.BlockSpec((rows, 128), lambda s, *_: (s, 0)),
                pl.BlockSpec((1, 8, rows), lambda s, *_: (s, 0, 0)),
            ],
            out_specs=[
                pl.BlockSpec((rows, wide), lambda s, j, *_: (s, j)),
                pl.BlockSpec((1, wide, rows), lambda s, j, *_: (s, j, 0)),
                pl.BlockSpec((1, 1, wide // HD, rows), lambda s, j, *_: (s, j, 0, 0)),
            ],
            scratch_shapes=[
                pltpu.VMEM((wide, rows), BF),
                pltpu.VMEM((wide, rows), BF),
                pltpu.VMEM((wide // HD, 16, rows), BF),
                pltpu.VMEM((8, rows), F32),
            ],
        ),
        out_shape=[
            jax.ShapeDtypeStruct((qkv.shape[0], width), BF),
            jax.ShapeDtypeStruct((seqs, width, rows), F32),
            jax.ShapeDtypeStruct((seqs, parts, wide // HD, rows), F32),
        ],
        compiler_params=params("arbitrary", "arbitrary"),
        cost_estimate=cost(24e9, 2e7),
        name="attention_forward",
    )(lo, hi, qkv, qkv, qkv, onehot, miss)


def attention_bwd(qkv, d_attn, ot, lse, lo, hi, onehot, miss, part):
    seqs = lo.shape[0]
    rows = qkv.shape[0] // seqs
    wide = WIDE
    col = lambda at: pl.BlockSpec((rows, wide), lambda s, lo, hi, p: (s, 3 * p[0] + at))
    return pl.pallas_call(
        attn_bwd_kernel,
        grid_spec=pltpu.PrefetchScalarGridSpec(
            num_scalar_prefetch=3,
            grid=(seqs,),
            in_specs=[
                col(0), col(1), col(2),
                pl.BlockSpec((rows, wide), lambda s, lo, hi, p: (s, p[0])),
                pl.BlockSpec((1, wide, rows), lambda s, lo, hi, p: (s, p[0], 0)),
                pl.BlockSpec((1, 1, wide // HD, rows), lambda s, lo, hi, p: (s, p[0], 0, 0)),
                pl.BlockSpec((rows, 128), lambda s, *_: (s, 0)),
                pl.BlockSpec((1, 8, rows), lambda s, *_: (s, 0, 0)),
            ],
            out_specs=pl.BlockSpec((rows, 3 * wide), lambda s, *_: (s, 0)),
            scratch_shapes=[
                pltpu.VMEM((wide, rows), BF),
                pltpu.VMEM((wide, rows), BF),
                pltpu.VMEM((wide, rows), BF),
                pltpu.VMEM((wide // HD, 16, rows), BF),
                pltpu.VMEM((wide // HD, 16, rows), BF),
                pltpu.VMEM((wide, rows), F32),
                pltpu.VMEM((wide, rows), F32),
                pltpu.VMEM((wide, rows), F32),
            ],
        ),
        out_shape=jax.ShapeDtypeStruct((qkv.shape[0], 3 * wide), BF),
        compiler_params=params("arbitrary"),
        cost_estimate=cost(22e9, 2e7),
        name="attention_backward",
    )(lo, hi, part, qkv, qkv, qkv, d_attn, ot, lse, onehot, miss)


def normalized(x):
    mean = jnp.mean(x, axis=-1, keepdims=True)
    centered = x - mean
    scale = lax.rsqrt(jnp.mean(centered * centered, axis=-1, keepdims=True) + EPSILON)
    return centered * scale, scale


def norm_back(d, xhat, scale, gain):
    e = d * gain
    return scale * (e - jnp.mean(e, axis=-1, keepdims=True) - xhat * jnp.mean(e * xhat, axis=-1, keepdims=True))


def clear_first(*refs):
    @pl.when(pl.program_id(0) == 0)
    def _():
        for ref in refs:
            ref[...] = jnp.zeros_like(ref)


def add_row(ref, row, values):
    ref[row : row + 1, 0 : values.shape[1]] += jnp.sum(values, axis=0, keepdims=True)


def fetch(chunks, spots, outs, sems):
    for h in range(2):
        for chip in range(chunks.shape[1]):
            for row, count, which, target in spots(h, chip):
                pltpu.make_async_copy(
                    chunks.at[h, chip, pl.ds(row, count), :], outs[which].at[target], sems.at[which]
                ).start()


def fetched(out, sem):
    pltpu.make_async_copy(out, out, sem).wait()


def qkv_kernel(spots, tok, vec, bias, chunks, n1, qkv, w, sem):
    @pl.when(pl.program_id(0) == 0)
    def _():
        fetch(chunks, spots, [w], sem)

    xhat, _ = normalized(tok[...].astype(F32))
    n = (xhat * vec[0:1] + vec[1:2]).astype(BF)
    n1[...] = n

    @pl.when(pl.program_id(0) == 0)
    def _():
        fetched(w, sem.at[0])

    qkv[...] = (mm(n, w[...]) + bias[...]).astype(BF)


def project_qkv(tokens, vec, bias, chunks, spots):
    count, width = tokens.shape
    cols = 3 * width
    tile = lambda w: pl.BlockSpec((TILE, w), lambda i: (i, 0))
    return pl.pallas_call(
        functools.partial(qkv_kernel, spots),
        grid=(count // TILE,),
        in_specs=[tile(width), whole(vec.shape), whole(bias.shape), ANYWHERE],
        out_specs=[tile(width), tile(cols), whole((width, cols))],
        scratch_shapes=[pltpu.SemaphoreType.DMA((1,))],
        out_shape=[
            jax.ShapeDtypeStruct((count, width), BF),
            jax.ShapeDtypeStruct((count, cols), BF),
            jax.ShapeDtypeStruct((width, cols), BF),
        ],
        compiler_params=params("arbitrary"),
        cost_estimate=cost(2 * count * width * cols, 2e7),
        name="norm_and_qkv",
    )(tokens, vec, bias, chunks)


STRIP = 768
CURVE = 0.7978845608028654
CUBIC = 0.044715


def middle_kernel(
    spots, attn, tok, cot, vec, b1, chunks2, chunks3,
    out, n2, act, d_pre, d_mid, d_branch, d_attn, sums, sum_up, wo, w1, w2, sem,
):
    @pl.when(pl.program_id(0) == 0)
    def _():
        fetch(chunks2, spots[0], [wo, w1], sem)
        fetch(chunks3, spots[1], [w2], sem.at[pl.ds(2, 1)])
        for ref in (sums, sum_up):
            ref[...] = jnp.zeros_like(ref)
        for k, ref in enumerate((wo, w1, w2)):
            fetched(ref, sem.at[k])

    x = tok[...].astype(F32) + mm(attn[...], wo[...]) + vec[2:3]
    xhat, scale = normalized(x)
    n = (xhat * vec[0:1] + vec[1:2]).astype(BF)
    n2[...] = n
    d_out = cot[...]
    y = x + vec[3:4]
    d_n2 = None
    for j in range(w1.shape[1] // STRIP):
        cols = slice(j * STRIP, (j + 1) * STRIP)
        u = mm(n, w1[:, cols]) + b1[:, cols]
        d_act = mm_nt(d_out, w2[cols, :])
        square = u * u
        th = jnp.tanh(u * (CURVE + (CURVE * CUBIC) * square))
        half = 0.5 * u
        hidden = (half + half * th).astype(BF)
        act[:, cols] = hidden
        y = y + mm(hidden, w2[cols, :])
        slope = (0.5 + 0.5 * th) + half * (1.0 - th * th) * (CURVE + (3.0 * CURVE * CUBIC) * square)
        low = (d_act * slope).astype(BF)
        d_pre[:, cols] = low
        sum_up[:, cols] += jnp.sum(low.astype(F32), axis=0, keepdims=True)
        part = mm_nt(low, w1[:, cols])
        d_n2 = part if d_n2 is None else d_n2 + part
    out[...] = y.astype(BF)
    add_row(sums, 0, d_n2 * xhat)
    add_row(sums, 1, d_n2)
    g = d_out.astype(F32)
    add_row(sums, 3, g)
    d = g + norm_back(d_n2, xhat, scale, vec[0:1])
    d_mid[...] = d
    low = d.astype(BF)
    d_branch[...] = low
    add_row(sums, 2, low.astype(F32))
    d_attn[...] = mm_nt(low, wo[...]).astype(BF)


def middle_part(attn, tokens, cotangent, vec, b1, gathered, spots):
    count, width = tokens.shape
    hidden = b1.shape[1]
    rows = TILE // 2
    tile = lambda w: pl.BlockSpec((rows, w), lambda i: (i, 0))
    row = lambda w, kind: jax.ShapeDtypeStruct((count, w), kind)
    return pl.pallas_call(
        functools.partial(middle_kernel, spots),
        grid=(count // rows,),
        in_specs=[tile(width), tile(width), tile(width), whole(vec.shape), whole(b1.shape)] + [ANYWHERE] * 2,
        out_specs=[
            tile(width), tile(width), tile(hidden), tile(hidden), tile(width), tile(width), tile(width),
            whole((8, width)), whole((1, hidden)),
        ],
        scratch_shapes=[
            pltpu.VMEM((width, width), BF),
            pltpu.VMEM((width, hidden), BF),
            pltpu.VMEM((hidden, width), BF),
            pltpu.SemaphoreType.DMA((3,)),
        ],
        out_shape=[
            row(width, BF), row(width, BF), row(hidden, BF), row(hidden, BF), row(width, F32), row(width, BF),
            row(width, BF), jax.ShapeDtypeStruct((8, width), F32), jax.ShapeDtypeStruct((1, hidden), F32),
        ],
        compiler_params=params("arbitrary"),
        cost_estimate=cost(4 * count * width * (width + 2 * hidden), 6e7),
        name="middle",
    )(attn, tokens, cotangent, vec, b1, *gathered)


def first_norm_kernel(parts, far, near, w_far, w_near, tok, d_mid, vec, out, sums):
    clear_first(sums)
    d = mm_nt(far[...], w_far[...]) + mm_nt(near[...], w_near[...])
    xhat, scale = normalized(tok[...].astype(F32))
    add_row(sums, 0, d * xhat)
    add_row(sums, 1, d)
    add_row(sums, 2, far[...].astype(F32))
    add_row(sums, 3, near[...].astype(F32))
    out[...] = (d_mid[...] + norm_back(d, xhat, scale, vec[0:1])).astype(BF)


def first_norm_back(far, near, w, tokens, d_mid, vec, parts):
    count, width = tokens.shape
    cols = far.shape[1]
    tile = lambda w: pl.BlockSpec((TILE, w), lambda i, p: (i, 0))
    return pl.pallas_call(
        first_norm_kernel,
        grid_spec=pltpu.PrefetchScalarGridSpec(
            num_scalar_prefetch=1,
            grid=(count // TILE,),
            in_specs=[
                tile(cols), tile(cols),
                pl.BlockSpec((width, cols), lambda i, p: (0, p[0])),
                pl.BlockSpec((width, cols), lambda i, p: (0, p[1])),
                tile(width), tile(width), whole(vec.shape),
            ],
            out_specs=[tile(width), whole((8, cols))],
        ),
        out_shape=[jax.ShapeDtypeStruct((count, width), BF), jax.ShapeDtypeStruct((8, cols), F32)],
        compiler_params=params("arbitrary"),
        cost_estimate=cost(4 * count * width * cols, 3e7),
        name="first_norm_back",
    )(parts, far, near, w, w, tokens, d_mid, vec)


def tn(a, b):
    return lax.dot_general(a, b, (((0,), (0,)), ((), ())), preferred_element_type=F32)


def grad_kernel(layout, near, part, send_at, keep_at, *refs):
    count = len(layout)
    ins, refs = refs[: 2 * count], refs[2 * count :]
    if near:
        got, (send, keep), (sums, total, held, sem) = refs[0], refs[1:3], (refs[3 : 3 + count], *refs[3 + count :])
    else:
        out, sums = refs[0], refs[1 : 1 + count]
    step = pl.program_id(0)
    arrival = pltpu.make_async_copy(got, held, sem.at[0]) if near else None

    @pl.when(step == 0)
    def _():
        if near:
            arrival.start()
        for acc in sums:
            acc[...] = jnp.zeros_like(acc)

    for k in range(count):
        sums[k][...] += tn(ins[2 * k][...], ins[2 * k + 1][...])

    @pl.when(step == pl.num_programs(0) - 1)
    def _():
        target = total if near else out
        chips, _, rows, _ = target.shape
        kind = target.dtype
        base = 0
        for k, blocks in enumerate(layout):
            if blocks == 0:
                target[...] = sums[k][...].astype(kind).T.reshape(target.shape)
            for b in range(blocks):
                cols = slice(b * WIDE, (b + 1) * WIDE)
                target[:, base + b] = sums[k][:, cols].astype(kind).reshape(chips, rows, WIDE)
            base += blocks
        if near:
            arrival.wait()

            def body(j, carry):
                for at, ref in ((send_at, send), (keep_at, keep)):
                    i = at[j]
                    ref[j] = (total[i] + held[i].astype(F32)).astype(BF)
                return carry

            lax.fori_loop(0, chips // 2, body, 0)


def grad_part(pairs, part, chips, name, got=None, order=None):
    tokens = pairs[0][0].shape[0]
    near = got is not None
    specs, arrays, scratch, layout, flops = [], [], [], [], 0
    for lhs, tall, lhs_part, rhs, wide, rhs_part in pairs:
        for x, cols, by_part in ((lhs, tall, lhs_part), (rhs, wide, rhs_part)):
            specs.append(pl.BlockSpec((TILE, cols), lambda i, p, *_, by_part=by_part: (i, p[0] if by_part else 0)))
            arrays.append(x)
        scratch.append(pltpu.VMEM((tall, wide), F32))
        layout.append(0 if tall == WIDE else wide // WIDE)
        flops += 2 * tokens * tall * wide
    if layout[0] == 0:
        shape = (chips, 4, pairs[0][4] // chips // 4, WIDE)
    else:
        shape = (chips, sum(layout), pairs[0][1] // chips, WIDE)
    out = jax.ShapeDtypeStruct((chips // 2 if near else chips,) + shape[1:], BF)
    spec = whole(out.shape)
    if near:
        specs, arrays = specs + [ANYWHERE], arrays + [got]
        scratch += [pltpu.VMEM(shape, F32), pltpu.VMEM(shape, BF), pltpu.SemaphoreType.DMA((1,))]
    return pl.pallas_call(
        functools.partial(grad_kernel, tuple(layout), near),
        grid_spec=pltpu.PrefetchScalarGridSpec(
            num_scalar_prefetch=3,
            grid=(tokens // TILE,),
            in_specs=specs,
            out_specs=[spec, spec] if near else spec,
            scratch_shapes=scratch,
        ),
        out_shape=[out, out] if near else out,
        compiler_params=params("arbitrary"),
        cost_estimate=cost(flops, 2e7),
        name=name,
    )(part, *(order or (part, part)), *arrays)


def here():
    me = lax.axis_index("fsdp")
    return me // 8, (me // 4) % 2, (me // 2) % 2, me % 2


def pairs_of(devices, move):
    depth = devices // 8
    found = []
    for i in range(devices):
        z, y, x, c = move(i // 8, (i // 4) % 2, (i // 2) % 2, i % 2)
        found.append((i, (((z % depth) * 2 + y) * 2 + x) * 2 + c))
    return found


class Moves:
    def __init__(self, devices):
        self.depth = devices // 8
        self.chips = devices // 2
        self.core = pairs_of(devices, lambda z, y, x, c: (z, y, x, 1 - c))
        self.first = pairs_of(devices, lambda z, y, x, c: (z, 1 - y, x, c) if c == 0 else (z, y, 1 - x, c))
        self.second = pairs_of(devices, lambda z, y, x, c: (z, y, 1 - x, c) if c == 0 else (z, 1 - y, x, c))
        self.deep = [pairs_of(devices, lambda z, y, x, c, k=k: (z + k, y, x, c)) for k in range(self.depth)]


def swap(x, moves):
    return lax.ppermute(x, "fsdp", moves)


def of_two(pick_second, a, b):
    return jnp.where(pick_second, b, a)


def neighbours():
    me = lax.axis_index("fsdp")
    core = lax.rem(me, 2)
    x = lax.rem(me // 2, 2)
    y = lax.rem(me // 4, 2)
    along_y = 4 * (1 - 2 * y)
    along_x = 2 * (1 - 2 * x)
    first = (1 - core) * along_y + core * along_x
    second = along_y + along_x - first
    return me, core, me // 8, first, second


def greet(others):
    barrier = pltpu.get_barrier_semaphore()
    for other in others:
        pl.semaphore_signal(barrier, inc=1, device_id=(other,), device_id_type=pl.DeviceIdType.MESH)
    pl.semaphore_wait(barrier, len(others))


def gather_kernel(blocks, depth, *refs):
    flows = len(blocks)
    owns, oths, outs = refs[:flows], refs[flows : 2 * flows], refs[2 * flows : 3 * flows]
    sems = refs[3 * flows :]
    me, core, z, first, second = neighbours()
    twin = me + 1 - 2 * core
    chip = me // 2
    deep = [chip * 2 + core] + [lax.rem(z + k, depth) * 8 + lax.rem(me, 8) for k in range(1, depth)]
    greet([twin, me + first, me + second] + deep[1:])
    mine = [lax.rem(z + depth - k, depth) * 4 + lax.rem(chip, 4) for k in range(depth)]
    theirs = [at + first // 2 for at in mine]
    last = [at + second // 2 for at in mine + theirs]

    def send(f, at, send_sem, recv_sem, device):
        pltpu.make_async_remote_copy(
            src_ref=outs[f].at[core, at],
            dst_ref=outs[f].at[core, at],
            send_sem=send_sem,
            recv_sem=recv_sem,
            device_id=(device,),
            device_id_type=pl.DeviceIdType.MESH,
        ).start()

    def arrived(ref, sem):
        pltpu.make_async_copy(ref, ref, sem).wait()

    def onward(f, k, at, steps):
        far, near, cross, seen, local, out, twin_out, twin_in, pair_out, pair_in = sems[10 * f : 10 * f + 10]
        if steps == 2:
            send(f, at, out.at[0], near.at[k], me + first)
        if steps >= 1:
            send(f, at, out.at[0], cross.at[k if steps == 2 else depth + k], me + second)
        send(f, at, twin_out.at[0], twin_in.at[0], twin)

    for f in range(flows):
        pair_out, pair_in, local = sems[10 * f + 8], sems[10 * f + 9], sems[10 * f + 4]
        row = 0
        for size in blocks[f]:
            here_rows = pl.ds(pl.multiple_of(2 * row + core * size, 8), size)
            pltpu.make_async_copy(
                owns[f].at[pl.ds(row, size), :], outs[f].at[core, chip, here_rows, :], local.at[0]
            ).start()
            pltpu.make_async_remote_copy(
                src_ref=oths[f].at[pl.ds(row, size), :],
                dst_ref=outs[f].at[1 - core, chip, here_rows, :],
                send_sem=pair_out.at[0],
                recv_sem=pair_in.at[0],
                device_id=(twin,),
                device_id_type=pl.DeviceIdType.MESH,
            ).start()
            row += size
    for f in range(flows):
        far, out = sems[10 * f], sems[10 * f + 5]
        arrived(owns[f], sems[10 * f + 4].at[0])
        arrived(owns[f], sems[10 * f + 9].at[0])
        for k in range(1, depth):
            send(f, chip, out.at[0], far.at[k], deep[k])
        onward(f, 0, chip, 2)

    def from_far(f):
        for k in range(1, depth):
            arrived(outs[f].at[core, mine[k]], sems[10 * f].at[k])
            onward(f, k, mine[k], 2)

    def from_near(f):
        for k in range(depth):
            arrived(outs[f].at[core, theirs[k]], sems[10 * f + 1].at[k])
            onward(f, k, theirs[k], 1)

    def from_cross(f):
        for k in range(2 * depth):
            arrived(outs[f].at[core, last[k]], sems[10 * f + 2].at[k])
            onward(f, k, last[k], 0)

    for step in range(flows + 2):
        for stage, run in enumerate((from_far, from_near, from_cross)):
            if 0 <= step - stage < flows:
                run(step - stage)
    for f in range(flows):
        chips = outs[f].shape[1]
        arrived(outs[f].at[1 - core], sems[10 * f + 7].at[0])
        arrived(outs[f].at[0], sems[10 * f + 6].at[0])
        arrived(outs[f].at[0, pl.ds(0, chips - 1)], sems[10 * f + 5].at[0])
        arrived(oths[f], sems[10 * f + 8].at[0])


def gather_shards(owns, oths, blocks, depth):
    chips = 4 * depth
    outs = [jax.ShapeDtypeStruct((2, chips, 2 * o.shape[0], WIDE), BF) for o in owns]
    dma = lambda n: pltpu.SemaphoreType.DMA((n,))
    scratch = []
    for _ in owns:
        scratch += [dma(depth), dma(depth), dma(2 * depth)] + [dma(1)] * 7
    return pl.pallas_call(
        functools.partial(gather_kernel, blocks, depth),
        in_specs=[ANYWHERE] * (2 * len(owns)),
        out_specs=[ANYWHERE] * len(owns),
        out_shape=outs,
        scratch_shapes=scratch,
        compiler_params=pltpu.CompilerParams(collective_id=0, has_side_effects=True),
        cost_estimate=cost(0, 3e7),
        name="gather_shards",
    )(*owns, *oths)


def pack_kernel(core, *refs):
    (wqkv, small, wo, w1, w2), outs = refs[:5], refs[5:]
    width = wo.shape[1]
    for c in range(2):

        @pl.when(core[0] == c)
        def _(c=c):
            for h in range(2):
                first, second, third = outs[:3] if h == c else outs[3:]
                rows = wo.shape[0]
                for t in range(3):
                    first[rows * t : rows * (t + 1), :] = wqkv[:, t * width + h * WIDE : t * width + (h + 1) * WIDE].astype(BF)
                first[3 * rows :, :] = small[...].astype(BF)
                second[0:rows, :] = wo[:, h * WIDE : (h + 1) * WIDE].astype(BF)
                for b in range(4):
                    cols = slice((4 * h + b) * WIDE, (4 * h + b + 1) * WIDE)
                    second[rows * (1 + b) : rows * (2 + b), :] = w1[:, cols].astype(BF)
                third[...] = w2[:, h * WIDE : (h + 1) * WIDE].astype(BF)


def pack(wqkv, small, wo, w1, w2, core):
    rows = wo.shape[0]
    ins = (wqkv, small, wo, w1, w2)
    shapes = [(3 * rows + small.shape[0], WIDE), (5 * rows, WIDE), (w2.shape[0], WIDE)] * 2
    return pl.pallas_call(
        pack_kernel,
        grid_spec=pltpu.PrefetchScalarGridSpec(
            num_scalar_prefetch=1,
            grid=(1,),
            in_specs=[whole(x.shape) for x in ins],
            out_specs=[whole(s) for s in shapes],
        ),
        out_shape=[jax.ShapeDtypeStruct(s, BF) for s in shapes],
        name="pack_shards",
    )(core, *ins)


def gate(x, *after):
    return lax.optimization_barrier((x,) + after)[0]


def fold_kernel(send_at, keep_at, a_send, b_send, a_keep, b_keep, send, keep):
    send[...] = (a_send[...].astype(F32) + b_send[...].astype(F32)).astype(BF)
    keep[...] = (a_keep[...].astype(F32) + b_keep[...].astype(F32)).astype(BF)


def fold(a, b, send_at, keep_at):
    count = send_at.shape[0]
    block = (1,) + a.shape[1:]
    none = (0,) * (a.ndim - 1)
    sent = pl.BlockSpec(block, lambda j, s, k: (s[j],) + none)
    kept = pl.BlockSpec(block, lambda j, s, k: (k[j],) + none)
    out = pl.BlockSpec(block, lambda j, s, k: (j,) + none)
    shape = jax.ShapeDtypeStruct((count,) + a.shape[1:], BF)
    return pl.pallas_call(
        fold_kernel,
        grid_spec=pltpu.PrefetchScalarGridSpec(
            num_scalar_prefetch=2, grid=(count,), in_specs=[sent, sent, kept, kept], out_specs=[out, out]
        ),
        out_shape=[shape, shape],
        cost_estimate=pl.CostEstimate(flops=0, bytes_accessed=3 * 2 * a.size, transcendentals=0),
        name="fold_sums",
    )(send_at, keep_at, a, b, a, b)


def fold_places(moves):
    z, y, x, c = here()
    plane = jnp.arange(2 * moves.depth, dtype=jnp.int32)
    deep, side = plane // 2, plane % 2
    bit = jnp.where(c == 0, x, y)

    def spread(b):
        return jnp.where(c == 0, deep * 4 + side * 2 + b, deep * 4 + b * 2 + side).astype(jnp.int32)

    level = jnp.arange(moves.depth, dtype=jnp.int32)
    turn = (z + level) % moves.depth
    mine = jnp.where(c == 0, y, x)
    return (
        (spread(1 - bit), spread(bit)),
        ((turn * 2 + 1 - mine).astype(jnp.int32), (turn * 2 + mine).astype(jnp.int32)),
    )


def level_kernel(keep, got, first, *rest):
    first[...] = keep[0].astype(F32) + got[0].astype(F32)
    for k, out in enumerate(rest):
        out[...] = (keep[k + 1].astype(F32) + got[k + 1].astype(F32)).astype(BF)


def level(keep, got):
    shape = keep.shape[1:]
    outs = [jax.ShapeDtypeStruct(shape, F32)] + [jax.ShapeDtypeStruct(shape, BF)] * (keep.shape[0] - 1)
    return pl.pallas_call(
        level_kernel,
        in_specs=[whole(keep.shape)] * 2,
        out_specs=[whole(shape)] * keep.shape[0],
        grid=(1,),
        out_shape=outs,
        compiler_params=params("arbitrary"),
        cost_estimate=cost(0, 4 * keep.size),
        name="level_sums",
    )(keep, got)


def scattered_small(sums, moves, places):
    c = here()[3]
    odd = c == 1
    part = of_two(odd, sums[:, 0], sums[:, 1]) + swap(of_two(odd, sums[:, 1], sums[:, 0]), moves.core)
    for (send_at, keep_at), move in zip(places, (moves.second, moves.first)):
        part = jnp.take(part, keep_at, axis=0) + swap(jnp.take(part, send_at, axis=0), move)
    total = part[0]
    for k in range(1, moves.depth):
        total = total + swap(part[k], moves.deep[k])
    return total


def halves(total, cores_axis, moves):
    odd = here()[3] == 1
    zero = lax.index_in_dim(total, 0, cores_axis, keepdims=False)
    one = lax.index_in_dim(total, 1, cores_axis, keepdims=False)
    mine = of_two(odd, zero, one)
    got = swap(of_two(odd, one, zero), moves.core)
    return jnp.stack([of_two(odd, mine, got), of_two(odd, got, mine)])


def by_neighbours(devices, width, hidden, count):
    rows = width // devices
    fits = rows * devices == width and rows % 8 == 0 and devices % 8 == 0
    return fits and width == 2 * WIDE and hidden == 4 * width and count % TILE == 0


def weight_halves(w):
    rows = w.shape[0]
    return w.reshape(rows, 3, 2, WIDE).transpose(0, 2, 1, 3).reshape(rows, -1)


def local(
    tokens, segments, cotangent, ln1_gain, ln1_shift, w_qkv, bias_q, bias_v, w_out, bias_out,
    ln2_gain, ln2_shift, w_up, bias_up, w_down, bias_down, *, seq,
):
    masters = (
        ln1_gain, ln1_shift, w_qkv, bias_q, bias_v, w_out, bias_out,
        ln2_gain, ln2_shift, w_up, bias_up, w_down, bias_down,
    )
    count, width = tokens.shape
    tables = attention_tables(segments.reshape(-1, seq))
    run = by_chips if by_neighbours(lax.axis_size("fsdp"), width, w_up.shape[1], count) else by_collectives
    return run(tokens, cotangent, tables, masters)


def by_collectives(tokens, cotangent, tables, masters):
    def norm(x, gain, shift):
        return normalized(x)[0] * gain + shift

    width = tokens.shape[1]
    full = [lax.all_gather(m.astype(BF), "fsdp", axis=0, tiled=True) for m in masters]
    g1, c1, wqkv, bq, bv, wo, bo, g2, c2, w1, b1, w2, b2 = [p.astype(F32) if p.ndim == 1 else p for p in full]
    wqkv = weight_halves(wqkv)
    rows = tokens.astype(F32)
    n1 = norm(rows, g1, c1).astype(BF)
    bias = weight_halves(jnp.concatenate([bq, jnp.zeros_like(bq), bv])[None])
    qkv = (mm(n1, wqkv) + bias).astype(BF)
    attn, attn_t, lse = attention_fwd(qkv, *tables)
    middle = rows + mm(attn, wo) + bo
    n2 = norm(middle, g2, c2).astype(BF)
    act_value, gelu_pull = jax.vjp(functools.partial(jax.nn.gelu, approximate=True), mm(n2, w1) + b1)
    act = act_value.astype(BF)
    layer_out = (middle + mm(act, w2) + b2).astype(BF)
    d_out = cotangent.astype(F32)
    d_pre = gelu_pull(mm_nt(cotangent, w2))[0].astype(BF)
    _, pull = jax.vjp(norm, middle, g2, c2)
    d_mid, d_g2, d_c2 = pull(mm_nt(d_pre, w1))
    d_mid = d_out + d_mid
    d_branch = d_mid.astype(BF)
    d_attn = mm_nt(d_branch, wo).astype(BF)
    parts = [
        attention_bwd(qkv, d_attn, attn_t, lse, *tables, jnp.full((1,), h, jnp.int32)) for h in range(2)
    ]
    d_qkv = jnp.concatenate(parts, axis=1)
    _, pull = jax.vjp(norm, rows, g1, c1)
    d_rows, d_g1, d_c1 = pull(mm_nt(d_qkv, wqkv))
    input_grad = (d_mid + d_rows).astype(BF)
    total = lambda x: jnp.sum(x.astype(F32), axis=0)
    by_part = lambda x: x.reshape(-1, 2, 3, WIDE).transpose(0, 2, 1, 3).reshape(x.shape)
    sums = by_part(total(d_qkv)[None])[0]
    grads = (
        d_g1, d_c1, by_part(tn(n1, d_qkv)), sums[:width], sums[2 * width :], tn(attn, d_branch), total(d_branch),
        d_g2, d_c2, tn(n2, d_pre), total(d_pre), tn(act, cotangent), total(d_out),
    )
    return (layer_out, input_grad) + tuple(
        lax.psum_scatter(g, "fsdp", scatter_dimension=0, tiled=True) for g in grads
    )


def by_chips(tokens, cotangent, tables, masters):
    devices = lax.axis_size("fsdp")
    moves = Moves(devices)
    chips = moves.chips
    count, width = tokens.shape
    ln1_gain, ln1_shift, w_qkv, bias_q, bias_v, w_out, bias_out, ln2_gain, ln2_shift, w_up, bias_up, w_down, bias_down = masters
    part = width // devices
    two = 2 * part
    hidden = w_up.shape[1]
    core = here()[3].astype(jnp.int32).reshape(1)

    small = jnp.concatenate([ln1_gain, ln1_shift, bias_q, bias_v, bias_out, ln2_gain, ln2_shift, bias_down, bias_up])
    small = jnp.pad(small[None], ((0, 7), (0, WIDE - small.shape[0])))
    own1, own2, own3, oth1, oth2, oth3 = pack(w_qkv, small, w_out, w_up, w_down, core)

    chunks1, chunks2, chunks3 = gather_shards(
        (own1, own2, own3), (oth1, oth2, oth3), ([part] * 3 + [8], [part] * 5, [4 * part]), moves.depth
    )
    vecs = chunks1[0, :, 6 * part :: 8].reshape(devices, WIDE).astype(F32)
    g1, c1, bq, bv, bo, g2, c2, b2 = [vecs[:, i * part : (i + 1) * part].reshape(-1) for i in range(8)]
    b1 = vecs[:, 8 * part : 12 * part].reshape(1, -1)
    bias = weight_halves(jnp.concatenate([bq, jnp.zeros_like(bq), bv])[None])

    def spots_qkv(h, chip):
        return [
            (two * t, two, 0, (pl.ds(two * chip, two), pl.ds((3 * h + t) * WIDE, WIDE))) for t in range(3)
        ]

    def spots_up(h, chip):
        rows = pl.ds(two * chip, two)
        return [(0, two, 0, (rows, pl.ds(h * WIDE, WIDE)))] + [
            (two * (1 + b), two, 1, (rows, pl.ds((4 * h + b) * WIDE, WIDE))) for b in range(4)
        ]

    def spots_down(h, chip):
        return [(0, 4 * two, 0, (pl.ds(4 * two * chip, 4 * two), pl.ds(h * WIDE, WIDE)))]

    n1, qkv, wqkv = project_qkv(tokens, jnp.stack([g1, c1]), bias, chunks1, spots_qkv)
    attn, attn_t, lse = attention_fwd(qkv, *tables)
    layer_out, n2, act, d_pre, d_mid, d_branch, d_attn, sums2, sum_up = middle_part(
        attn, tokens, cotangent, jnp.stack([g2, c2, bo, b2]), b1, (chunks2, chunks3), (spots_up, spots_down)
    )

    far, near = 1 - core, core
    orders = fold_places(moves)
    downs = lambda cot: [(cot, WIDE, True, act, hidden, False)]
    ups = lambda n2: [(n2, width, False, d_pre, hidden // 2, True), (attn, width, False, d_branch, WIDE, True)]
    qkvs = lambda n1, d: [(n1, width, False, d, 3 * WIDE, False)]
    sent_down = grad_part(downs(cotangent), far, chips, "grad_down_far")
    got_down = swap(sent_down, moves.core)
    sent_up = grad_part(ups(gate(n2, sent_down)), far, chips, "grad_up_out_far")
    got_up = swap(sent_up, moves.core)
    send_down, keep_down = grad_part(
        downs(gate(cotangent, sent_up)), near, chips, "grad_down_near", gate(got_down, sent_up), orders[0]
    )
    got_down = swap(send_down, moves.second)
    send_up, keep_up = grad_part(
        ups(gate(n2, send_down)), near, chips, "grad_up_out_near", gate(got_up, send_down), orders[0]
    )
    got_up = swap(send_up, moves.second)
    d_qkv_far = attention_bwd(qkv, gate(d_attn, send_up), attn_t, lse, *tables, far)
    send_down, keep_down = fold(keep_down, gate(got_down, d_qkv_far), *orders[1])
    got_down = swap(send_down, moves.first)
    send_up, keep_up = fold(keep_up, gate(got_up, d_qkv_far), *orders[1])
    got_up = swap(send_up, moves.first)
    sent_qkv = grad_part(qkvs(gate(n1, send_up, send_down), d_qkv_far), far, chips, "grad_qkv_far")
    got_qkv = swap(sent_qkv, moves.core)
    d_qkv_near = attention_bwd(qkv, gate(d_attn, sent_qkv), attn_t, lse, *tables, near)

    def spread(others):
        return [swap(x, moves.deep[k + 1]) for k, x in enumerate(others)]

    def total_of(first, gots):
        return sum((g.astype(F32) for g in gots), first)

    first_down, *rest_down = level(keep_down, gate(got_down, d_qkv_near))
    first_up, *rest_up = level(keep_up, gate(got_up, d_qkv_near))
    gots_down, gots_up = spread(rest_down), spread(rest_up)
    input_grad, sums1 = first_norm_back(
        d_qkv_far, gate(d_qkv_near, first_down, first_up), wqkv, tokens, d_mid, g1[None], jnp.concatenate([far, near])
    )
    send_qkv, keep_qkv = grad_part(
        qkvs(gate(n1, sums1), d_qkv_near), near, chips, "grad_qkv_near", gate(got_qkv, sums1), orders[0]
    )
    got_qkv = swap(send_qkv, moves.second)
    first_down, *gots_down = lax.optimization_barrier((first_down, *gots_down, send_qkv))[:-1]
    first_up, *gots_up = lax.optimization_barrier((first_up, *gots_up, send_qkv))[:-1]
    send_qkv, keep_qkv = fold(keep_qkv, got_qkv, *orders[1])
    got_qkv = swap(send_qkv, moves.first)

    odd = core[0] == 1
    by_half = [of_two(odd, sums1[3], sums1[2]), of_two(odd, sums1[2], sums1[3])]
    d_bq = jnp.concatenate([s[:WIDE] for s in by_half])
    d_bv = jnp.concatenate([s[2 * WIDE :] for s in by_half])
    vecs = [sums1[0, :width], sums1[1, :width], d_bq, d_bv, sums2[2], sums2[0], sums2[1], sums2[3]]
    small = jnp.concatenate([v.reshape(devices, part) for v in vecs] + [sum_up.reshape(devices, 4 * part)], axis=1)
    small = jnp.pad(small, ((0, 0), (0, WIDE - small.shape[1]))).reshape(chips, 2, WIDE)
    small = scattered_small(small, moves, orders)
    s = [small[i * part : (i + 1) * part] for i in range(8)]
    s_b1 = small[8 * part : 12 * part]

    total_down = total_of(first_down, gots_down)
    both_halves = halves(total_down.reshape(2, 4 * part, WIDE), 0, moves)
    g_down = both_halves.transpose(1, 0, 2).reshape(4 * part, width)
    total_up = total_of(first_up, gots_up)
    both_halves = halves(total_up.reshape(5, 2, part, WIDE), 1, moves)
    g_up = both_halves[:, :4].transpose(2, 0, 1, 3).reshape(part, hidden)
    g_out = both_halves[:, 4].transpose(1, 0, 2).reshape(part, width)
    first_qkv, *rest_qkv = level(keep_qkv, got_qkv)
    total_qkv = total_of(first_qkv, spread(rest_qkv))
    both_halves = halves(total_qkv.reshape(3, 2, part, WIDE), 1, moves)
    g_qkv = both_halves.transpose(2, 1, 0, 3).reshape(part, 3 * width)
    return (
        layer_out, input_grad, s[0], s[1], g_qkv, s[2], s[3], g_out, s[4], s[5], s[6], g_up, s_b1, g_down, s[7],
    )


MICRO = 2


def solution(mesh):
    line, table = P("fsdp"), P("fsdp", None)
    weights = (line, line, table, line, line, table, line, line, line, table, line, table, line)

    def step(tokens, *rest):
        seq = tokens.shape[0] // (mesh.shape["fsdp"] * MICRO)
        return jax.shard_map(
            functools.partial(local, seq=seq),
            mesh=mesh,
            in_specs=(table, line, table) + weights,
            out_specs=(table, table) + weights,
            check_vma=False,
        )(tokens, *rest)

    return step
```

```python
import functools
import jax
import jax.numpy as jnp
from jax import lax
from jax.experimental import pallas as pl
from jax.experimental.pallas import tpu as pltpu
from jax.sharding import PartitionSpec as P

HD = 64
QB = 128
KB = 128
NEG = -1000000000.0
BF = jnp.bfloat16
F32 = jnp.float32
EPSILON = 1e-06
NT = (((1,), (1,)), ((), ()))


def mm(a, b):
    return jnp.dot(a, b, preferred_element_type=F32)


def mm_nt(a, b):
    return lax.dot_general(a, b, NT, preferred_element_type=F32)


def pair_diag(top, bottom):
    zero = jnp.zeros_like(top)
    return jnp.concatenate(
        [jnp.concatenate([top, zero], axis=1), jnp.concatenate([zero, bottom], axis=1)], axis=0
    )


SPANS = (2, 3, 4, 5, 6, 8)


def by_span(lo, hi, rows, run):
    need = hi - lo
    below = 0
    for span in SPANS:
        if below * KB >= rows:
            break
        size = min(span * KB, rows)
        last = size == rows

        @pl.when((need > below) & (last | (need <= span)))
        def _(size=size):
            run(pl.multiple_of(jnp.minimum(lo * KB, rows - size), KB), size)

        below = span


def chunks(k0, size):
    return [(pl.multiple_of(k0 + c, KB), min(2 * KB, size - c)) for c in range(0, size, 2 * KB)]


def terms(pieces):
    width = pieces[0].shape[1]
    row = lax.broadcasted_iota(jnp.int32, (8, width), 0)
    tail = jnp.zeros((8, width), F32)
    for i, piece in enumerate(pieces):
        tail = jnp.where(row == i, piece, tail)
    return tail


def three_parts(x):
    first = x.astype(BF).astype(F32)
    rest = x - first
    second = rest.astype(BF).astype(F32)
    return first, second, rest - second


def pair_rhs(feat, extra, p, qs):
    a = 128 * p
    block = pair_diag(feat[a : a + 64, qs], feat[a + 64 : a + 128, qs])
    rows = jnp.concatenate([extra[2 * p, :, qs], extra[2 * p + 1, :, qs]], axis=1)
    return block, jnp.concatenate([block, rows, jnp.zeros((112, 2 * QB), BF)], axis=0)


def attn_fwd_kernel(
    lo, hi, q_ref, k_ref, v_ref, oh_ref, mr_ref, o_ref, ot_ref, lse_ref, qt, vt, extra, tops
):
    seq = pl.program_id(0)
    rows = q_ref.shape[0]
    pairs = q_ref.shape[1] // 128
    heads = 2 * pairs
    vt[...] = v_ref[...].T
    qt[...] = (q_ref[...] * 0.125).astype(BF).T
    lane = lax.broadcasted_iota(jnp.int32, (8, heads * HD), 1) // HD
    pick = (lane == lax.broadcasted_iota(jnp.int32, (8, heads * HD), 0)).astype(BF)
    square = k_ref[...].astype(F32)
    norms = mm_nt(pick, (square * square).astype(BF))
    bound = jnp.sqrt(jnp.max(norms, axis=1, keepdims=True)) * 1.01
    for h in range(heads):
        qh = qt[64 * h : 64 * h + 64, :].astype(F32)
        length = jnp.sqrt(jnp.sum(qh * qh, axis=0, keepdims=True)) * 1.01
        m = (length * bound[h : h + 1, :]).astype(BF).astype(F32)
        tops[h : h + 1, :] = m
        extra[h, :, :] = jnp.concatenate([mr_ref[0], terms([-m])], axis=0).astype(BF)

    def keep(qs, p, l, full):
        a = 128 * p
        ot_ref[0, a : a + 64, qs] = full[0:64, 0:QB]
        ot_ref[0, a + 64 : a + 128, qs] = full[64:128, QB:]
        lse_ref[0, 0, 2 * p : 2 * p + 1, qs] = l[:, 0:QB]
        lse_ref[0, 0, 2 * p + 1 : 2 * p + 2, qs] = l[:, QB:]

    def q_step(qb, carry):
        qs = pl.ds(pl.multiple_of(qb * QB, QB), QB)

        def run(k0, size):
            rhs = [pair_rhs(qt, extra, p, qs)[1] for p in range(pairs)]
            l = [jnp.zeros((1, 2 * QB), F32)] * pairs
            acc = [None] * pairs
            for c0, cs in chunks(k0, size):
                ks = pl.ds(c0, cs)
                oh = oh_ref[ks, :]
                for p in range(pairs):
                    cols = slice(128 * p, 128 * p + 128)
                    w = jnp.exp(mm(jnp.concatenate([k_ref[ks, cols], oh], axis=1), rhs[p]))
                    l[p] = l[p] + jnp.sum(w, axis=0, keepdims=True)
                    part = mm(vt[cols, ks], w.astype(BF))
                    acc[p] = part if acc[p] is None else acc[p] + part
            for p in range(pairs):
                keep(qs, p, l[p], acc[p])

        by_span(lo[seq, qb], hi[seq, qb], rows, run)
        return carry

    lax.fori_loop(0, rows // QB, q_step, 0)

    @pl.when(jnp.min(lse_ref[0, 0]) < 1e-20)
    def _():
        for h in range(heads):
            extra[h, :, :] = jnp.concatenate([mr_ref[0], jnp.zeros_like(mr_ref[0])], axis=0).astype(BF)

        def q_again(qb, carry):
            qs = pl.ds(pl.multiple_of(qb * QB, QB), QB)
            for p in range(pairs):
                cols = slice(128 * p, 128 * p + 128)
                rhs = pair_rhs(qt, extra, p, qs)[1]

                def scores(kb):
                    ks = pl.ds(pl.multiple_of(kb * KB, KB), KB)
                    return ks, mm(jnp.concatenate([k_ref[ks, cols], oh_ref[ks, :]], axis=1), rhs)

                def top_step(kb, m):
                    return jnp.maximum(m, jnp.max(scores(kb)[1], axis=0, keepdims=True))

                blocks = rows // KB
                m = lax.fori_loop(0, blocks, top_step, jnp.full((1, 2 * QB), 2 * NEG, F32))

                def sum_step(kb, state):
                    ks, st = scores(kb)
                    w = jnp.exp(st - m)
                    return state[0] + jnp.sum(w, axis=0, keepdims=True), state[1] + mm(vt[cols, ks], w.astype(BF))

                start = (jnp.zeros((1, 2 * QB), F32), jnp.zeros((128, 2 * QB), F32))
                l, full = lax.fori_loop(0, blocks, sum_step, start)
                tops[2 * p : 2 * p + 1, qs] = m[:, 0:QB]
                tops[2 * p + 1 : 2 * p + 2, qs] = m[:, QB:]
                keep(qs, p, l, full)
            return carry

        lax.fori_loop(0, rows // QB, q_again, 0)

    for h in range(heads):
        l = lse_ref[0, 0, h : h + 1, :]
        hs = slice(64 * h, 64 * h + 64)
        ot_ref[0, hs, :] = ot_ref[0, hs, :] * (1.0 / l)
        lse_ref[0, 0, h : h + 1, :] = tops[h : h + 1, :] + jnp.log(l)
    o_ref[...] = ot_ref[0].astype(BF).T


def attn_bwd_kernel(
    lo, hi, q_ref, k_ref, v_ref, do_ref, ot_ref, lse_ref, oh_ref, mr_ref, dqkv_ref,
    qt, kt, dot, extra_q, extra_d, dqt, dkt, dvt,
):
    seq = pl.program_id(0)
    rows = q_ref.shape[0]
    pairs = q_ref.shape[1] // 128
    qt[...] = (q_ref[...] * 0.125).astype(BF).T
    kt[...] = k_ref[...].T
    dot[...] = do_ref[...].T
    for h in range(2 * pairs):
        r = slice(64 * h, 64 * h + 64)
        delta = jnp.sum(dot[r, :].astype(F32) * ot_ref[0, r, :], axis=0, keepdims=True)
        lse = lse_ref[0, 0, h : h + 1, :]
        extra_q[h, :, :] = jnp.concatenate([mr_ref[0], terms(three_parts(-lse))], axis=0).astype(BF)
        tail = terms(three_parts(-delta))
        extra_d[h, :, :] = jnp.concatenate([jnp.zeros_like(tail), tail], axis=0).astype(BF)
    dkt[...] = jnp.zeros_like(dkt)
    dvt[...] = jnp.zeros_like(dvt)

    def q_step(qb, carry):
        qs = pl.ds(pl.multiple_of(qb * QB, QB), QB)

        def run(k0, size):
            ks = pl.ds(k0, size)
            oh = oh_ref[ks, :]
            for p in range(pairs):
                a = 128 * p
                cols = slice(a, a + 128)
                qm, qx = pair_rhs(qt, extra_q, p, qs)
                dom, dx = pair_rhs(dot, extra_d, p, qs)
                w = jnp.exp(mm(jnp.concatenate([k_ref[ks, cols], oh], axis=1), qx))
                ds = (w * mm(jnp.concatenate([v_ref[ks, cols], oh], axis=1), dx)).astype(BF)
                dvt[cols, ks] += mm_nt(dom, w.astype(BF))
                dkt[cols, ks] += mm_nt(qm, ds)
                dq = mm(kt[cols, ks], ds)
                dqt[a : a + 64, qs] = dq[0:64, 0:QB]
                dqt[a + 64 : a + 128, qs] = dq[64:128, QB:]

        by_span(lo[seq, qb], hi[seq, qb], rows, run)
        return carry

    lax.fori_loop(0, rows // QB, q_step, 0)
    wide = dqt.shape[0]
    dqkv_ref[:, 0:wide] = (dqt[...] * 0.125).astype(BF).T
    dqkv_ref[:, wide : 2 * wide] = dkt[...].astype(BF).T
    dqkv_ref[:, 2 * wide :] = dvt[...].astype(BF).T


WIDE = 384
TILE = 512
VMEM_LIMIT = 60 * 1024 * 1024


def params(*semantics):
    return pltpu.CompilerParams(dimension_semantics=semantics or None, vmem_limit_bytes=VMEM_LIMIT)


def cost(flops, data):
    return pl.CostEstimate(flops=int(flops), bytes_accessed=int(data), transcendentals=0)


def whole(shape):
    zero = (0,) * len(shape)
    return pl.BlockSpec(shape, lambda *_: zero)


ANYWHERE = pl.BlockSpec(memory_space=pl.ANY)


def attention_tables(segs):
    order = jnp.where(segs == 0, 1 << 20, segs)
    seqs, length = segs.shape
    first = order[:, ::QB]
    last = order[:, QB - 1 :: QB]
    lo = jnp.sum((order[:, None, :] < first[:, :, None]).astype(jnp.int32), axis=2) // KB
    hi = (jnp.sum((order[:, None, :] <= last[:, :, None]).astype(jnp.int32), axis=2) + KB - 1) // KB
    ids = jnp.arange(128, dtype=jnp.int32)[None, :]
    onehot = (segs.reshape(-1)[:, None] == ids) | ((ids >= 8) & (ids < 16))
    differ = segs[:, None, :] != jnp.arange(8, dtype=jnp.int32)[None, :, None]
    return lo, hi, onehot.astype(BF), jnp.where(differ, NEG, 0.0)


def attention_fwd(qkv, lo, hi, onehot, miss):
    seqs = lo.shape[0]
    rows = qkv.shape[0] // seqs
    wide = WIDE
    width = qkv.shape[1] // 3
    parts = width // wide
    col = lambda at: pl.BlockSpec((rows, wide), lambda s, j, *_: (s, 3 * j + at))
    return pl.pallas_call(
        attn_fwd_kernel,
        grid_spec=pltpu.PrefetchScalarGridSpec(
            num_scalar_prefetch=2,
            grid=(seqs, parts),
            in_specs=[
                col(0), col(1), col(2),
                pl.BlockSpec((rows, 128), lambda s, *_: (s, 0)),
                pl.BlockSpec((1, 8, rows), lambda s, *_: (s, 0, 0)),
            ],
            out_specs=[
                pl.BlockSpec((rows, wide), lambda s, j, *_: (s, j)),
                pl.BlockSpec((1, wide, rows), lambda s, j, *_: (s, j, 0)),
                pl.BlockSpec((1, 1, wide // HD, rows), lambda s, j, *_: (s, j, 0, 0)),
            ],
            scratch_shapes=[
                pltpu.VMEM((wide, rows), BF),
                pltpu.VMEM((wide, rows), BF),
                pltpu.VMEM((wide // HD, 16, rows), BF),
                pltpu.VMEM((8, rows), F32),
            ],
        ),
        out_shape=[
            jax.ShapeDtypeStruct((qkv.shape[0], width), BF),
            jax.ShapeDtypeStruct((seqs, width, rows), F32),
            jax.ShapeDtypeStruct((seqs, parts, wide // HD, rows), F32),
        ],
        compiler_params=params("arbitrary", "arbitrary"),
        cost_estimate=cost(24e9, 2e7),
        name="attention_forward",
    )(lo, hi, qkv, qkv, qkv, onehot, miss)


def attention_bwd(qkv, d_attn, ot, lse, lo, hi, onehot, miss):
    seqs = lo.shape[0]
    rows = qkv.shape[0] // seqs
    wide = WIDE
    col = lambda at: pl.BlockSpec((rows, wide), lambda s, j, *_: (s, 3 * j + at))
    return pl.pallas_call(
        attn_bwd_kernel,
        grid_spec=pltpu.PrefetchScalarGridSpec(
            num_scalar_prefetch=2,
            grid=(seqs, d_attn.shape[1] // wide),
            in_specs=[
                col(0), col(1), col(2),
                pl.BlockSpec((rows, wide), lambda s, j, *_: (s, j)),
                pl.BlockSpec((1, wide, rows), lambda s, j, *_: (s, j, 0)),
                pl.BlockSpec((1, 1, wide // HD, rows), lambda s, j, *_: (s, j, 0, 0)),
                pl.BlockSpec((rows, 128), lambda s, *_: (s, 0)),
                pl.BlockSpec((1, 8, rows), lambda s, *_: (s, 0, 0)),
            ],
            out_specs=pl.BlockSpec((rows, 3 * wide), lambda s, j, *_: (s, j)),
            scratch_shapes=[
                pltpu.VMEM((wide, rows), BF),
                pltpu.VMEM((wide, rows), BF),
                pltpu.VMEM((wide, rows), BF),
                pltpu.VMEM((wide // HD, 16, rows), BF),
                pltpu.VMEM((wide // HD, 16, rows), BF),
                pltpu.VMEM((wide, rows), F32),
                pltpu.VMEM((wide, rows), F32),
                pltpu.VMEM((wide, rows), F32),
            ],
        ),
        out_shape=jax.ShapeDtypeStruct(qkv.shape, BF),
        compiler_params=params("arbitrary", "arbitrary"),
        cost_estimate=cost(44e9, 4e7),
        name="attention_backward",
    )(lo, hi, qkv, qkv, qkv, d_attn, ot, lse, onehot, miss)


def normalized(x):
    mean = jnp.mean(x, axis=-1, keepdims=True)
    centered = x - mean
    scale = lax.rsqrt(jnp.mean(centered * centered, axis=-1, keepdims=True) + EPSILON)
    return centered * scale, scale


def norm_back(d, xhat, scale, gain):
    e = d * gain
    return scale * (e - jnp.mean(e, axis=-1, keepdims=True) - xhat * jnp.mean(e * xhat, axis=-1, keepdims=True))


def clear_first(*refs):
    @pl.when(pl.program_id(0) == 0)
    def _():
        for ref in refs:
            ref[...] = jnp.zeros_like(ref)


def add_row(ref, row, values):
    ref[row : row + 1, 0 : values.shape[1]] += jnp.sum(values, axis=0, keepdims=True)


def fetch(chunks, spots, outs, sems):
    for h in range(2):
        for chip in range(chunks.shape[1]):
            for row, count, which, target in spots(h, chip):
                pltpu.make_async_copy(
                    chunks.at[h, chip, pl.ds(row, count), :], outs[which].at[target], sems.at[which]
                ).start()


def fetched(out, sem):
    pltpu.make_async_copy(out, out, sem).wait()


def qkv_kernel(spots, tok, vec, bias, chunks, n1, qkv, w, sem):
    @pl.when(pl.program_id(0) == 0)
    def _():
        fetch(chunks, spots, [w], sem)

    xhat, _ = normalized(tok[...].astype(F32))
    n = (xhat * vec[0:1] + vec[1:2]).astype(BF)
    n1[...] = n

    @pl.when(pl.program_id(0) == 0)
    def _():
        fetched(w, sem.at[0])

    qkv[...] = (mm(n, w[...]) + bias[...]).astype(BF)


def project_qkv(tokens, vec, bias, chunks, spots):
    count, width = tokens.shape
    cols = 3 * width
    tile = lambda w: pl.BlockSpec((TILE, w), lambda i: (i, 0))
    return pl.pallas_call(
        functools.partial(qkv_kernel, spots),
        grid=(count // TILE,),
        in_specs=[tile(width), whole(vec.shape), whole(bias.shape), ANYWHERE],
        out_specs=[tile(width), tile(cols), whole((width, cols))],
        scratch_shapes=[pltpu.SemaphoreType.DMA((1,))],
        out_shape=[
            jax.ShapeDtypeStruct((count, width), BF),
            jax.ShapeDtypeStruct((count, cols), BF),
            jax.ShapeDtypeStruct((width, cols), BF),
        ],
        compiler_params=params("arbitrary"),
        cost_estimate=cost(2 * count * width * cols, 2e7),
        name="norm_and_qkv",
    )(tokens, vec, bias, chunks)


STRIP = 768
CURVE = 0.7978845608028654
CUBIC = 0.044715


def middle_kernel(
    spots, attn, tok, cot, vec, b1, chunks2, chunks3,
    out, n2, act, d_pre, d_mid, d_branch, d_attn, sums, sum_up, wo, w1, w2, sem,
):
    @pl.when(pl.program_id(0) == 0)
    def _():
        fetch(chunks2, spots[0], [wo, w1], sem)
        fetch(chunks3, spots[1], [w2], sem.at[pl.ds(2, 1)])
        for ref in (sums, sum_up):
            ref[...] = jnp.zeros_like(ref)
        for k, ref in enumerate((wo, w1, w2)):
            fetched(ref, sem.at[k])

    x = tok[...].astype(F32) + mm(attn[...], wo[...]) + vec[2:3]
    xhat, scale = normalized(x)
    n = (xhat * vec[0:1] + vec[1:2]).astype(BF)
    n2[...] = n
    d_out = cot[...]
    y = x + vec[3:4]
    d_n2 = None
    for j in range(w1.shape[1] // STRIP):
        cols = slice(j * STRIP, (j + 1) * STRIP)
        u = mm(n, w1[:, cols]) + b1[:, cols]
        d_act = mm_nt(d_out, w2[cols, :])
        square = u * u
        th = jnp.tanh(u * (CURVE + (CURVE * CUBIC) * square))
        half = 0.5 * u
        hidden = (half + half * th).astype(BF)
        act[:, cols] = hidden
        y = y + mm(hidden, w2[cols, :])
        slope = (0.5 + 0.5 * th) + half * (1.0 - th * th) * (CURVE + (3.0 * CURVE * CUBIC) * square)
        low = (d_act * slope).astype(BF)
        d_pre[:, cols] = low
        sum_up[:, cols] += jnp.sum(low.astype(F32), axis=0, keepdims=True)
        part = mm_nt(low, w1[:, cols])
        d_n2 = part if d_n2 is None else d_n2 + part
    out[...] = y.astype(BF)
    add_row(sums, 0, d_n2 * xhat)
    add_row(sums, 1, d_n2)
    g = d_out.astype(F32)
    add_row(sums, 3, g)
    d = g + norm_back(d_n2, xhat, scale, vec[0:1])
    d_mid[...] = d
    low = d.astype(BF)
    d_branch[...] = low
    add_row(sums, 2, low.astype(F32))
    d_attn[...] = mm_nt(low, wo[...]).astype(BF)


def middle_part(attn, tokens, cotangent, vec, b1, gathered, spots):
    count, width = tokens.shape
    hidden = b1.shape[1]
    rows = TILE // 2
    tile = lambda w: pl.BlockSpec((rows, w), lambda i: (i, 0))
    row = lambda w, kind: jax.ShapeDtypeStruct((count, w), kind)
    return pl.pallas_call(
        functools.partial(middle_kernel, spots),
        grid=(count // rows,),
        in_specs=[tile(width), tile(width), tile(width), whole(vec.shape), whole(b1.shape)] + [ANYWHERE] * 2,
        out_specs=[
            tile(width), tile(width), tile(hidden), tile(hidden), tile(width), tile(width), tile(width),
            whole((8, width)), whole((1, hidden)),
        ],
        scratch_shapes=[
            pltpu.VMEM((width, width), BF),
            pltpu.VMEM((width, hidden), BF),
            pltpu.VMEM((hidden, width), BF),
            pltpu.SemaphoreType.DMA((3,)),
        ],
        out_shape=[
            row(width, BF), row(width, BF), row(hidden, BF), row(hidden, BF), row(width, F32), row(width, BF),
            row(width, BF), jax.ShapeDtypeStruct((8, width), F32), jax.ShapeDtypeStruct((1, hidden), F32),
        ],
        compiler_params=params("arbitrary"),
        cost_estimate=cost(4 * count * width * (width + 2 * hidden), 6e7),
        name="middle",
    )(attn, tokens, cotangent, vec, b1, *gathered)


def first_norm_kernel(d_qkv, w, tok, d_mid, vec, out, sums):
    clear_first(sums)
    d = mm_nt(d_qkv[...], w[...])
    xhat, scale = normalized(tok[...].astype(F32))
    add_row(sums, 0, d * xhat)
    add_row(sums, 1, d)
    add_row(sums, 2, d_qkv[...].astype(F32))
    out[...] = (d_mid[...] + norm_back(d, xhat, scale, vec[0:1])).astype(BF)


def first_norm_back(d_qkv, w, tokens, d_mid, vec):
    count, width = tokens.shape
    cols = d_qkv.shape[1]
    tile = lambda w: pl.BlockSpec((TILE, w), lambda i: (i, 0))
    return pl.pallas_call(
        first_norm_kernel,
        grid=(count // TILE,),
        in_specs=[tile(cols), whole(w.shape), tile(width), tile(width), whole(vec.shape)],
        out_specs=[tile(width), whole((8, cols))],
        out_shape=[jax.ShapeDtypeStruct((count, width), BF), jax.ShapeDtypeStruct((8, cols), F32)],
        compiler_params=params("arbitrary"),
        cost_estimate=cost(2 * count * width * cols, 3e7),
        name="first_norm_back",
    )(d_qkv, w, tokens, d_mid, vec)


def tn(a, b):
    return lax.dot_general(a, b, (((0,), (0,)), ((), ())), preferred_element_type=F32)


def grad_kernel(layout, *refs):
    count = len(layout)
    ins, out, sums = refs[: 2 * count], refs[2 * count], refs[2 * count + 1 :]
    step = pl.program_id(0)

    @pl.when(step == 0)
    def _():
        for acc in sums:
            acc[...] = jnp.zeros_like(acc)

    for k in range(count):
        sums[k][...] += tn(ins[2 * k][...], ins[2 * k + 1][...])

    @pl.when(step == pl.num_programs(0) - 1)
    def _():
        _, chips, _, rows, _ = out.shape
        base = 0
        for k, blocks in enumerate(layout):
            tall = sums[k].shape[0] // (chips * rows)
            for h in range(2):
                for b in range(blocks):
                    at = (h * blocks + b) * WIDE
                    low = sums[k][:, at : at + WIDE].astype(BF)
                    out[h, :, base + b * tall : base + (b + 1) * tall] = low.reshape(chips, tall, rows, WIDE)
            base += blocks * tall


def grad_part(pairs, chips, rows, name):
    tokens = pairs[0][0].shape[0]
    specs, arrays, scratch, layout, flops, total = [], [], [], [], 0, 0
    for lhs, rhs in pairs:
        for x in (lhs, rhs):
            specs.append(pl.BlockSpec((TILE, x.shape[1]), lambda i: (i, 0)))
            arrays.append(x)
        scratch.append(pltpu.VMEM((lhs.shape[1], rhs.shape[1]), F32))
        layout.append(rhs.shape[1] // (2 * WIDE))
        total += layout[-1] * (lhs.shape[1] // (chips * rows))
        flops += 2 * tokens * lhs.shape[1] * rhs.shape[1]
    shape = (2, chips, total, rows, WIDE)
    return pl.pallas_call(
        functools.partial(grad_kernel, tuple(layout)),
        grid=(tokens // TILE,),
        in_specs=specs,
        out_specs=whole(shape),
        out_shape=jax.ShapeDtypeStruct(shape, BF),
        scratch_shapes=scratch,
        compiler_params=params("arbitrary"),
        cost_estimate=cost(flops, 3e7),
        name=name,
    )(*arrays)


def neighbours():
    me = lax.axis_index("fsdp")
    core = lax.rem(me, 2)
    x = lax.rem(me // 2, 2)
    y = lax.rem(me // 4, 2)
    along_y = 4 * (1 - 2 * y)
    along_x = 2 * (1 - 2 * x)
    first = (1 - core) * along_y + core * along_x
    second = along_y + along_x - first
    return me, core, me // 8, first, second


def greet(others):
    barrier = pltpu.get_barrier_semaphore()
    for other in others:
        pl.semaphore_signal(barrier, inc=1, device_id=(other,), device_id_type=pl.DeviceIdType.MESH)
    pl.semaphore_wait(barrier, len(others))


def gather_kernel(blocks, depth, *refs):
    flows = len(blocks)
    owns, oths, outs = refs[:flows], refs[flows : 2 * flows], refs[2 * flows : 3 * flows]
    sems = refs[3 * flows :]
    me, core, z, first, second = neighbours()
    twin = me + 1 - 2 * core
    chip = me // 2
    deep = [chip * 2 + core] + [lax.rem(z + k, depth) * 8 + lax.rem(me, 8) for k in range(1, depth)]
    greet([twin, me + first, me + second] + deep[1:])
    mine = [lax.rem(z + depth - k, depth) * 4 + lax.rem(chip, 4) for k in range(depth)]
    theirs = [at + first // 2 for at in mine]
    last = [at + second // 2 for at in mine + theirs]

    def send(f, at, send_sem, recv_sem, device):
        pltpu.make_async_remote_copy(
            src_ref=outs[f].at[core, at],
            dst_ref=outs[f].at[core, at],
            send_sem=send_sem,
            recv_sem=recv_sem,
            device_id=(device,),
            device_id_type=pl.DeviceIdType.MESH,
        ).start()

    def arrived(ref, sem):
        pltpu.make_async_copy(ref, ref, sem).wait()

    def onward(f, k, at, steps):
        far, near, cross, seen, local, out, twin_out, twin_in, pair_out, pair_in = sems[10 * f : 10 * f + 10]
        if steps == 2:
            send(f, at, out.at[0], near.at[k], me + first)
        if steps >= 1:
            send(f, at, out.at[0], cross.at[k if steps == 2 else depth + k], me + second)
        send(f, at, twin_out.at[0], twin_in.at[0], twin)

    for f in range(flows):
        pair_out, pair_in, local = sems[10 * f + 8], sems[10 * f + 9], sems[10 * f + 4]
        row = 0
        for size in blocks[f]:
            here_rows = pl.ds(pl.multiple_of(2 * row + core * size, 8), size)
            pltpu.make_async_copy(
                owns[f].at[pl.ds(row, size), :], outs[f].at[core, chip, here_rows, :], local.at[0]
            ).start()
            pltpu.make_async_remote_copy(
                src_ref=oths[f].at[pl.ds(row, size), :],
                dst_ref=outs[f].at[1 - core, chip, here_rows, :],
                send_sem=pair_out.at[0],
                recv_sem=pair_in.at[0],
                device_id=(twin,),
                device_id_type=pl.DeviceIdType.MESH,
            ).start()
            row += size
    for f in range(flows):
        far, out = sems[10 * f], sems[10 * f + 5]
        arrived(owns[f], sems[10 * f + 4].at[0])
        arrived(owns[f], sems[10 * f + 9].at[0])
        for k in range(1, depth):
            send(f, chip, out.at[0], far.at[k], deep[k])
        onward(f, 0, chip, 2)

    def from_far(f):
        for k in range(1, depth):
            arrived(outs[f].at[core, mine[k]], sems[10 * f].at[k])
            onward(f, k, mine[k], 2)

    def from_near(f):
        for k in range(depth):
            arrived(outs[f].at[core, theirs[k]], sems[10 * f + 1].at[k])
            onward(f, k, theirs[k], 1)

    def from_cross(f):
        for k in range(2 * depth):
            arrived(outs[f].at[core, last[k]], sems[10 * f + 2].at[k])
            onward(f, k, last[k], 0)

    for step in range(flows + 2):
        for stage, run in enumerate((from_far, from_near, from_cross)):
            if 0 <= step - stage < flows:
                run(step - stage)
    for f in range(flows):
        chips = outs[f].shape[1]
        arrived(outs[f].at[1 - core], sems[10 * f + 7].at[0])
        arrived(outs[f].at[0], sems[10 * f + 6].at[0])
        arrived(outs[f].at[0, pl.ds(0, chips - 1)], sems[10 * f + 5].at[0])
        arrived(oths[f], sems[10 * f + 8].at[0])


def gather_shards(owns, oths, blocks, depth):
    chips = 4 * depth
    outs = [jax.ShapeDtypeStruct((2, chips, 2 * o.shape[0], WIDE), BF) for o in owns]
    dma = lambda n: pltpu.SemaphoreType.DMA((n,))
    scratch = []
    for _ in owns:
        scratch += [dma(depth), dma(depth), dma(2 * depth)] + [dma(1)] * 7
    return pl.pallas_call(
        functools.partial(gather_kernel, blocks, depth),
        in_specs=[ANYWHERE] * (2 * len(owns)),
        out_specs=[ANYWHERE] * len(owns),
        out_shape=outs,
        scratch_shapes=scratch,
        compiler_params=pltpu.CompilerParams(collective_id=0, has_side_effects=True),
        cost_estimate=cost(0, 3e7),
        name="gather_shards",
    )(*owns, *oths)


def pack_kernel(core, *refs):
    (wqkv, small, wo, w1, w2), outs = refs[:5], refs[5:]
    width = wo.shape[1]
    for c in range(2):

        @pl.when(core[0] == c)
        def _(c=c):
            for h in range(2):
                first, second, third = outs[:3] if h == c else outs[3:]
                rows = wo.shape[0]
                for t in range(3):
                    first[rows * t : rows * (t + 1), :] = wqkv[:, t * width + h * WIDE : t * width + (h + 1) * WIDE].astype(BF)
                first[3 * rows :, :] = small[...].astype(BF)
                second[0:rows, :] = wo[:, h * WIDE : (h + 1) * WIDE].astype(BF)
                for b in range(4):
                    cols = slice((4 * h + b) * WIDE, (4 * h + b + 1) * WIDE)
                    second[rows * (1 + b) : rows * (2 + b), :] = w1[:, cols].astype(BF)
                third[...] = w2[:, h * WIDE : (h + 1) * WIDE].astype(BF)


def pack(wqkv, small, wo, w1, w2, core):
    rows = wo.shape[0]
    ins = (wqkv, small, wo, w1, w2)
    shapes = [(3 * rows + small.shape[0], WIDE), (5 * rows, WIDE), (w2.shape[0], WIDE)] * 2
    return pl.pallas_call(
        pack_kernel,
        grid_spec=pltpu.PrefetchScalarGridSpec(
            num_scalar_prefetch=1,
            grid=(1,),
            in_specs=[whole(x.shape) for x in ins],
            out_specs=[whole(s) for s in shapes],
        ),
        out_shape=[jax.ShapeDtypeStruct(s, BF) for s in shapes],
        name="pack_shards",
    )(core, *ins)


def scatter_kernel(depth, splits, *refs):
    flows = len(splits)
    ins, outs, rest = refs[:flows], refs[flows : 2 * flows], refs[2 * flows :]
    me, core, z, first, second = neighbours()
    chip = me // 2
    x, y = lax.rem(chip, 2), lax.rem(chip // 2, 2)
    twin = me + 1 - 2 * core
    deep = [lax.rem(z + k, depth) * 8 + lax.rem(me, 8) for k in range(1, depth)]
    greet([twin, me + first, me + second] + deep)
    plane = 2 * depth
    chips = 2 * plane

    def chip_of(j, core):
        bit2, bit1 = x + core * (y - x), y + core * (x - y)
        keep, side, k = j // plane, lax.rem(j, plane) // depth, lax.rem(j, depth)
        bit2 = (1 - bit2) + keep * (2 * bit2 - 1)
        bit1 = (1 - bit1) + side * (2 * bit1 - 1)
        return lax.rem(z + 1 + k, depth) * 4 + bit1 * (2 - core) + bit2 * (1 + core)

    def remote(src, dst, send_sem, recv_sem, device):
        return pltpu.make_async_remote_copy(
            src_ref=src,
            dst_ref=dst,
            send_sem=send_sem,
            recv_sem=recv_sem,
            device_id=(device,),
            device_id_type=pl.DeviceIdType.MESH,
        )

    def arrived(ref, sem):
        pltpu.make_async_copy(ref, ref, sem).wait()

    def flow(f):
        return rest[8 * f : 8 * f + 8]

    def sems(f):
        return rest[8 * flows + 11 * f : 8 * flows + 11 * f + 11]

    def loop(count, body):
        def step(j, carry):
            body(j)
            return carry

        lax.fori_loop(0, count, step, 0)

    def begin(f):
        own, in0 = flow(f)[:2]
        load, got0, sent0 = sems(f)[0], sems(f)[1], sems(f)[6]

        def body(j):
            pltpu.make_async_copy(ins[f].at[core, chip_of(j, core)], own.at[j], load.at[j]).start()
            remote(ins[f].at[1 - core, chip_of(j, 1 - core)], in0.at[j], sent0.at[0], got0.at[j], twin).start()

        loop(chips, body)

    def sum_of(f, j):
        own, in0 = flow(f)[:2]
        arrived(own.at[j], sems(f)[0].at[j])
        arrived(in0.at[j], sems(f)[1].at[j])
        return own[j].astype(F32) + in0[j].astype(F32)

    def lagging(count, compute, send):
        def body(j):
            compute(j)

            @pl.when(j > 0)
            def _():
                send(j - 1)

        loop(count, body)
        send(count - 1)

    def across(f):
        own, _, in1 = flow(f)[:3]
        got1, sent1 = sems(f)[2], sems(f)[7]

        def compute(j):
            own[j] = sum_of(f, j).astype(own.dtype)

        lagging(plane, compute, lambda j: remote(own.at[j], in1.at[j], sent1.at[0], got1.at[j], me + second).start())

    def kept(f, j):
        in1 = flow(f)[2]
        arrived(in1.at[j], sems(f)[2].at[j])
        return sum_of(f, plane + j) + in1[j].astype(F32)

    def along(f):
        own, in2 = flow(f)[0], flow(f)[3]
        got2, sent2 = sems(f)[3], sems(f)[8]

        def compute(k):
            own[plane + k] = kept(f, k).astype(own.dtype)

        lagging(
            depth, compute, lambda k: remote(own.at[plane + k], in2.at[k], sent2.at[0], got2.at[k], me + first).start()
        )

    def upward(f):
        own, in2, in3, total = flow(f)[0], flow(f)[3], flow(f)[4], flow(f)[5]
        got2, got3, sent3 = sems(f)[3], sems(f)[4], sems(f)[9]

        def value(k):
            arrived(in2.at[k], got2.at[k])
            return kept(f, depth + k) + in2[k].astype(F32)

        for k in range(depth - 1):
            own[plane + depth + k] = value(k).astype(own.dtype)
            if k > 0:
                remote(own.at[plane + depth + k - 1], in3.at[k - 1], sent3.at[0], got3.at[k - 1], deep[k - 1]).start()
        total[...] = value(depth - 1)
        k = depth - 2
        remote(own.at[plane + depth + k], in3.at[k], sent3.at[0], got3.at[k], deep[k]).start()

    def mine(f, ref, which):
        if splits[f] == "rows":
            half = ref.shape[1] // 2
            return ref.at[:, pl.ds(pl.multiple_of(which * half, 8), half), :]
        half = ref.shape[0] // 2
        return ref.at[pl.ds(which * half, half)]

    def finish(f):
        in3, total, theirs = flow(f)[4], flow(f)[5], flow(f)[6]
        for k in range(depth - 1):
            arrived(in3.at[k], sems(f)[4].at[k])
            total[...] += in3[k].astype(F32)
        if splits[f] is None:
            outs[f][...] = total[...]
        else:
            outs[f][core] = mine(f, total, core)[...]
            remote(mine(f, total, 1 - core), theirs, sems(f)[10].at[0], sems(f)[5].at[0], twin).start()

    for f in range(flows):
        begin(f)
    for f in range(flows):
        across(f)
    for step in range(flows + 2):
        for stage, run in enumerate((along, upward, finish)):
            if 0 <= step - stage < flows:
                run(step - stage)
    for f in range(flows):
        _, in0, in1, in2, in3, total, theirs, _ = flow(f)
        if splits[f] is not None:
            arrived(theirs, sems(f)[5].at[0])
            outs[f][1 - core] = theirs[...]
            arrived(theirs, sems(f)[10].at[0])
        for ref, sem in zip((in0, in1, in2, in3), sems(f)[6:10]):
            arrived(ref, sem.at[0])


def scatter_sums(parts, splits, depth):
    chips = 4 * depth
    outs, buffers, signals = [], [], []
    dma = lambda n: pltpu.SemaphoreType.DMA((n,))
    for p, split in zip(parts, splits):
        chunk = p.shape[2:]
        if split == "rows":
            part = (chunk[0], chunk[1] // 2) + chunk[2:]
        elif split == "blocks":
            part = (chunk[0] // 2,) + chunk[1:]
        else:
            part = chunk
        outs.append(jax.ShapeDtypeStruct(part if split is None else (2,) + part, F32))
        for count in (chips, chips, chips // 2, depth, depth - 1):
            buffers.append(pltpu.VMEM((count,) + chunk, p.dtype))
        buffers += [pltpu.VMEM(chunk, F32), pltpu.VMEM(part, F32), dma(1)]
        signals += [dma(chips), dma(chips), dma(chips // 2), dma(depth), dma(depth - 1)] + [dma(1)] * 6
    return pl.pallas_call(
        functools.partial(scatter_kernel, depth, tuple(splits)),
        in_specs=[ANYWHERE] * len(parts),
        out_specs=[pl.BlockSpec(memory_space=pltpu.VMEM)] * len(parts),
        out_shape=outs,
        scratch_shapes=buffers + signals,
        compiler_params=pltpu.CompilerParams(
            collective_id=1, has_side_effects=True, vmem_limit_bytes=VMEM_LIMIT
        ),
        cost_estimate=cost(0, 3e7),
        name="scatter_sums",
    )(*parts)


def by_neighbours(devices, width, hidden, count):
    rows = width // devices
    fits = rows * devices == width and rows % 8 == 0 and devices % 8 == 0
    return fits and width == 2 * WIDE and hidden == 4 * width and count % TILE == 0


def weight_halves(w):
    rows = w.shape[0]
    return w.reshape(rows, 3, 2, WIDE).transpose(0, 2, 1, 3).reshape(rows, -1)


def local(
    tokens, segments, cotangent, ln1_gain, ln1_shift, w_qkv, bias_q, bias_v, w_out, bias_out,
    ln2_gain, ln2_shift, w_up, bias_up, w_down, bias_down, *, seq,
):
    masters = (
        ln1_gain, ln1_shift, w_qkv, bias_q, bias_v, w_out, bias_out,
        ln2_gain, ln2_shift, w_up, bias_up, w_down, bias_down,
    )
    count, width = tokens.shape
    tables = attention_tables(segments.reshape(-1, seq))
    run = by_chips if by_neighbours(lax.axis_size("fsdp"), width, w_up.shape[1], count) else by_collectives
    return run(tokens, cotangent, tables, masters)


def by_collectives(tokens, cotangent, tables, masters):
    def norm(x, gain, shift):
        return normalized(x)[0] * gain + shift

    width = tokens.shape[1]
    full = [lax.all_gather(m.astype(BF), "fsdp", axis=0, tiled=True) for m in masters]
    g1, c1, wqkv, bq, bv, wo, bo, g2, c2, w1, b1, w2, b2 = [p.astype(F32) if p.ndim == 1 else p for p in full]
    wqkv = weight_halves(wqkv)
    rows = tokens.astype(F32)
    n1 = norm(rows, g1, c1).astype(BF)
    bias = weight_halves(jnp.concatenate([bq, jnp.zeros_like(bq), bv])[None])
    qkv = (mm(n1, wqkv) + bias).astype(BF)
    attn, attn_t, lse = attention_fwd(qkv, *tables)
    middle = rows + mm(attn, wo) + bo
    n2 = norm(middle, g2, c2).astype(BF)
    act_value, gelu_pull = jax.vjp(functools.partial(jax.nn.gelu, approximate=True), mm(n2, w1) + b1)
    act = act_value.astype(BF)
    layer_out = (middle + mm(act, w2) + b2).astype(BF)
    d_out = cotangent.astype(F32)
    d_pre = gelu_pull(mm_nt(cotangent, w2))[0].astype(BF)
    _, pull = jax.vjp(norm, middle, g2, c2)
    d_mid, d_g2, d_c2 = pull(mm_nt(d_pre, w1))
    d_mid = d_out + d_mid
    d_branch = d_mid.astype(BF)
    d_attn = mm_nt(d_branch, wo).astype(BF)
    d_qkv = attention_bwd(qkv, d_attn, attn_t, lse, *tables)
    _, pull = jax.vjp(norm, rows, g1, c1)
    d_rows, d_g1, d_c1 = pull(mm_nt(d_qkv, wqkv))
    input_grad = (d_mid + d_rows).astype(BF)
    total = lambda x: jnp.sum(x.astype(F32), axis=0)
    by_part = lambda x: x.reshape(-1, 2, 3, WIDE).transpose(0, 2, 1, 3).reshape(x.shape)
    sums = by_part(total(d_qkv)[None])[0]
    grads = (
        d_g1, d_c1, by_part(tn(n1, d_qkv)), sums[:width], sums[2 * width :], tn(attn, d_branch), total(d_branch),
        d_g2, d_c2, tn(n2, d_pre), total(d_pre), tn(act, cotangent), total(d_out),
    )
    return (layer_out, input_grad) + tuple(
        lax.psum_scatter(g, "fsdp", scatter_dimension=0, tiled=True) for g in grads
    )


def by_chips(tokens, cotangent, tables, masters):
    devices = lax.axis_size("fsdp")
    chips = devices // 2
    depth = devices // 8
    count, width = tokens.shape
    ln1_gain, ln1_shift, w_qkv, bias_q, bias_v, w_out, bias_out, ln2_gain, ln2_shift, w_up, bias_up, w_down, bias_down = masters
    part = width // devices
    two = 2 * part
    hidden = w_up.shape[1]
    core = lax.rem(lax.axis_index("fsdp"), 2).astype(jnp.int32).reshape(1)

    small = jnp.concatenate([ln1_gain, ln1_shift, bias_q, bias_v, bias_out, ln2_gain, ln2_shift, bias_down, bias_up])
    small = jnp.pad(small[None], ((0, 7), (0, WIDE - small.shape[0])))
    own1, own2, own3, oth1, oth2, oth3 = pack(w_qkv, small, w_out, w_up, w_down, core)

    chunks1, chunks2, chunks3 = gather_shards(
        (own1, own2, own3), (oth1, oth2, oth3), ([part] * 3 + [8], [part] * 5, [4 * part]), depth
    )
    vecs = chunks1[0, :, 6 * part :: 8].reshape(devices, WIDE).astype(F32)
    g1, c1, bq, bv, bo, g2, c2, b2 = [vecs[:, i * part : (i + 1) * part].reshape(-1) for i in range(8)]
    b1 = vecs[:, 8 * part : 12 * part].reshape(1, -1)
    bias = weight_halves(jnp.concatenate([bq, jnp.zeros_like(bq), bv])[None])

    def spots_qkv(h, chip):
        return [
            (two * t, two, 0, (pl.ds(two * chip, two), pl.ds((3 * h + t) * WIDE, WIDE))) for t in range(3)
        ]

    def spots_up(h, chip):
        rows = pl.ds(two * chip, two)
        return [(0, two, 0, (rows, pl.ds(h * WIDE, WIDE)))] + [
            (two * (1 + b), two, 1, (rows, pl.ds((4 * h + b) * WIDE, WIDE))) for b in range(4)
        ]

    def spots_down(h, chip):
        return [(0, 4 * two, 0, (pl.ds(4 * two * chip, 4 * two), pl.ds(h * WIDE, WIDE)))]

    n1, qkv, wqkv = project_qkv(tokens, jnp.stack([g1, c1]), bias, chunks1, spots_qkv)
    attn, attn_t, lse = attention_fwd(qkv, *tables)
    layer_out, n2, act, d_pre, d_mid, d_branch, d_attn, sums2, sum_up = middle_part(
        attn, tokens, cotangent, jnp.stack([g2, c2, bo, b2]), b1, (chunks2, chunks3), (spots_up, spots_down)
    )

    g_parts = [
        grad_part([(n2, d_pre), (attn, d_branch)], chips, two, "grad_up_out"),
        grad_part([(act, cotangent)], chips, two, "grad_down"),
    ]
    d_qkv = attention_bwd(qkv, d_attn, attn_t, lse, *tables)
    input_grad, sums1 = first_norm_back(d_qkv, wqkv, tokens, d_mid, g1[None])
    g_parts.append(grad_part([(n1, d_qkv)], chips, two, "grad_qkv"))
    by_half = sums1[2].reshape(2, 3, WIDE)
    vecs = [
        sums1[0, :width], sums1[1, :width], by_half[:, 0].reshape(-1), by_half[:, 2].reshape(-1),
        sums2[2], sums2[0], sums2[1], sums2[3],
    ]
    small = jnp.concatenate([v.reshape(devices, part) for v in vecs] + [sum_up.reshape(devices, 4 * part)], axis=1)
    small = small.reshape(chips, 2, 1, -1).swapaxes(0, 1)
    small = jnp.pad(small, ((0, 0), (0, 0), (0, 7), (0, WIDE - small.shape[3])))
    small, g_up_out, g_down, g_qkv = scatter_sums([small] + g_parts, (None, "rows", "blocks", "rows"), depth)
    small = small[0]
    s = [small[i * part : (i + 1) * part] for i in range(8)]
    s_b1 = small[8 * part : 12 * part]
    g_up = g_up_out[:, :4].transpose(2, 0, 1, 3).reshape(part, hidden)
    g_out = g_up_out[:, 4].transpose(1, 0, 2).reshape(part, width)
    g_down = g_down.reshape(2, 4 * part, WIDE).transpose(1, 0, 2).reshape(4 * part, width)
    g_qkv = g_qkv.transpose(2, 1, 0, 3).reshape(part, 3 * width)
    return (
        layer_out, input_grad, s[0], s[1], g_qkv, s[2], s[3], g_out, s[4], s[5], s[6], g_up, s_b1, g_down, s[7],
    )


MICRO = 2


def solution(mesh):
    line, table = P("fsdp"), P("fsdp", None)
    weights = (line, line, table, line, line, table, line, line, line, table, line, table, line)

    def step(tokens, *rest):
        seq = tokens.shape[0] // (mesh.shape["fsdp"] * MICRO)
        return jax.shard_map(
            functools.partial(local, seq=seq),
            mesh=mesh,
            in_specs=(table, line, table) + weights,
            out_specs=(table, table) + weights,
            check_vma=False,
        )(tokens, *rest)

    return step
```

```python
import functools
import jax
import jax.numpy as jnp
from jax import lax
from jax.experimental import pallas as pl
from jax.experimental.pallas import tpu as pltpu
from jax.sharding import PartitionSpec as P

HD = 64
QB = 128
KB = 128
NEG = -1000000000.0
BF = jnp.bfloat16
F32 = jnp.float32
EPSILON = 1e-06
NT = (((1,), (1,)), ((), ()))


def mm(a, b):
    return jnp.dot(a, b, preferred_element_type=F32)


def mm_nt(a, b):
    return lax.dot_general(a, b, NT, preferred_element_type=F32)


def pair_diag(top, bottom):
    zero = jnp.zeros_like(top)
    return jnp.concatenate(
        [jnp.concatenate([top, zero], axis=1), jnp.concatenate([zero, bottom], axis=1)], axis=0
    )


SPANS = (2, 3, 4, 5, 6, 8)


def by_span(lo, hi, rows, run):
    need = hi - lo
    below = 0
    for span in SPANS:
        if below * KB >= rows:
            break
        size = min(span * KB, rows)
        last = size == rows

        @pl.when((need > below) & (last | (need <= span)))
        def _(size=size):
            run(pl.multiple_of(jnp.minimum(lo * KB, rows - size), KB), size)

        below = span


def chunks(k0, size):
    return [(pl.multiple_of(k0 + c, KB), min(2 * KB, size - c)) for c in range(0, size, 2 * KB)]


def terms(pieces):
    width = pieces[0].shape[1]
    row = lax.broadcasted_iota(jnp.int32, (8, width), 0)
    tail = jnp.zeros((8, width), F32)
    for i, piece in enumerate(pieces):
        tail = jnp.where(row == i, piece, tail)
    return tail


def three_parts(x):
    first = x.astype(BF).astype(F32)
    rest = x - first
    second = rest.astype(BF).astype(F32)
    return first, second, rest - second


def pair_rhs(feat, extra, p, qs):
    a = 128 * p
    block = pair_diag(feat[a : a + 64, qs], feat[a + 64 : a + 128, qs])
    rows = jnp.concatenate([extra[2 * p, :, qs], extra[2 * p + 1, :, qs]], axis=1)
    return block, jnp.concatenate([block, rows, jnp.zeros((112, 2 * QB), BF)], axis=0)


def attn_fwd_kernel(
    lo, hi, q_ref, k_ref, v_ref, oh_ref, mr_ref, o_ref, ot_ref, lse_ref, qt, vt, extra, tops
):
    seq = pl.program_id(0)
    rows = q_ref.shape[0]
    pairs = q_ref.shape[1] // 128
    heads = 2 * pairs
    vt[...] = v_ref[...].T
    qt[...] = (q_ref[...] * 0.125).astype(BF).T
    lane = lax.broadcasted_iota(jnp.int32, (8, heads * HD), 1) // HD
    pick = (lane == lax.broadcasted_iota(jnp.int32, (8, heads * HD), 0)).astype(BF)
    square = k_ref[...].astype(F32)
    norms = mm_nt(pick, (square * square).astype(BF))
    bound = jnp.sqrt(jnp.max(norms, axis=1, keepdims=True)) * 1.01
    for h in range(heads):
        qh = qt[64 * h : 64 * h + 64, :].astype(F32)
        length = jnp.sqrt(jnp.sum(qh * qh, axis=0, keepdims=True)) * 1.01
        m = (length * bound[h : h + 1, :]).astype(BF).astype(F32)
        tops[h : h + 1, :] = m
        extra[h, :, :] = jnp.concatenate([mr_ref[0], terms([-m])], axis=0).astype(BF)

    def keep(qs, p, l, full):
        a = 128 * p
        ot_ref[0, a : a + 64, qs] = full[0:64, 0:QB]
        ot_ref[0, a + 64 : a + 128, qs] = full[64:128, QB:]
        lse_ref[0, 0, 2 * p : 2 * p + 1, qs] = l[:, 0:QB]
        lse_ref[0, 0, 2 * p + 1 : 2 * p + 2, qs] = l[:, QB:]

    def q_step(qb, carry):
        qs = pl.ds(pl.multiple_of(qb * QB, QB), QB)

        def run(k0, size):
            rhs = [pair_rhs(qt, extra, p, qs)[1] for p in range(pairs)]
            l = [jnp.zeros((1, 2 * QB), F32)] * pairs
            acc = [None] * pairs
            for c0, cs in chunks(k0, size):
                ks = pl.ds(c0, cs)
                oh = oh_ref[ks, :]
                for p in range(pairs):
                    cols = slice(128 * p, 128 * p + 128)
                    w = jnp.exp(mm(jnp.concatenate([k_ref[ks, cols], oh], axis=1), rhs[p]))
                    l[p] = l[p] + jnp.sum(w, axis=0, keepdims=True)
                    part = mm(vt[cols, ks], w.astype(BF))
                    acc[p] = part if acc[p] is None else acc[p] + part
            for p in range(pairs):
                keep(qs, p, l[p], acc[p])

        by_span(lo[seq, qb], hi[seq, qb], rows, run)
        return carry

    lax.fori_loop(0, rows // QB, q_step, 0)

    @pl.when(jnp.min(lse_ref[0, 0]) < 1e-20)
    def _():
        for h in range(heads):
            extra[h, :, :] = jnp.concatenate([mr_ref[0], jnp.zeros_like(mr_ref[0])], axis=0).astype(BF)

        def q_again(qb, carry):
            qs = pl.ds(pl.multiple_of(qb * QB, QB), QB)
            for p in range(pairs):
                cols = slice(128 * p, 128 * p + 128)
                rhs = pair_rhs(qt, extra, p, qs)[1]

                def scores(kb):
                    ks = pl.ds(pl.multiple_of(kb * KB, KB), KB)
                    return ks, mm(jnp.concatenate([k_ref[ks, cols], oh_ref[ks, :]], axis=1), rhs)

                def top_step(kb, m):
                    return jnp.maximum(m, jnp.max(scores(kb)[1], axis=0, keepdims=True))

                blocks = rows // KB
                m = lax.fori_loop(0, blocks, top_step, jnp.full((1, 2 * QB), 2 * NEG, F32))

                def sum_step(kb, state):
                    ks, st = scores(kb)
                    w = jnp.exp(st - m)
                    return state[0] + jnp.sum(w, axis=0, keepdims=True), state[1] + mm(vt[cols, ks], w.astype(BF))

                start = (jnp.zeros((1, 2 * QB), F32), jnp.zeros((128, 2 * QB), F32))
                l, full = lax.fori_loop(0, blocks, sum_step, start)
                tops[2 * p : 2 * p + 1, qs] = m[:, 0:QB]
                tops[2 * p + 1 : 2 * p + 2, qs] = m[:, QB:]
                keep(qs, p, l, full)
            return carry

        lax.fori_loop(0, rows // QB, q_again, 0)

    for h in range(heads):
        l = lse_ref[0, 0, h : h + 1, :]
        hs = slice(64 * h, 64 * h + 64)
        ot_ref[0, hs, :] = ot_ref[0, hs, :] * (1.0 / l)
        lse_ref[0, 0, h : h + 1, :] = tops[h : h + 1, :] + jnp.log(l)
    o_ref[...] = ot_ref[0].astype(BF).T


def attn_bwd_kernel(
    lo, hi, q_ref, k_ref, v_ref, do_ref, ot_ref, lse_ref, oh_ref, mr_ref, dqkv_ref,
    qt, kt, dot, extra_q, extra_d, dqt, dkt, dvt,
):
    seq = pl.program_id(0)
    rows = q_ref.shape[0]
    pairs = q_ref.shape[1] // 128
    qt[...] = (q_ref[...] * 0.125).astype(BF).T
    kt[...] = k_ref[...].T
    dot[...] = do_ref[...].T
    for h in range(2 * pairs):
        r = slice(64 * h, 64 * h + 64)
        delta = jnp.sum(dot[r, :].astype(F32) * ot_ref[0, r, :], axis=0, keepdims=True)
        lse = lse_ref[0, 0, h : h + 1, :]
        extra_q[h, :, :] = jnp.concatenate([mr_ref[0], terms(three_parts(-lse))], axis=0).astype(BF)
        tail = terms(three_parts(-delta))
        extra_d[h, :, :] = jnp.concatenate([jnp.zeros_like(tail), tail], axis=0).astype(BF)
    dkt[...] = jnp.zeros_like(dkt)
    dvt[...] = jnp.zeros_like(dvt)

    def q_step(qb, carry):
        qs = pl.ds(pl.multiple_of(qb * QB, QB), QB)

        def run(k0, size):
            ks = pl.ds(k0, size)
            oh = oh_ref[ks, :]
            for p in range(pairs):
                a = 128 * p
                cols = slice(a, a + 128)
                qm, qx = pair_rhs(qt, extra_q, p, qs)
                dom, dx = pair_rhs(dot, extra_d, p, qs)
                w = jnp.exp(mm(jnp.concatenate([k_ref[ks, cols], oh], axis=1), qx))
                ds = (w * mm(jnp.concatenate([v_ref[ks, cols], oh], axis=1), dx)).astype(BF)
                dvt[cols, ks] += mm_nt(dom, w.astype(BF))
                dkt[cols, ks] += mm_nt(qm, ds)
                dq = mm(kt[cols, ks], ds)
                dqt[a : a + 64, qs] = dq[0:64, 0:QB]
                dqt[a + 64 : a + 128, qs] = dq[64:128, QB:]

        by_span(lo[seq, qb], hi[seq, qb], rows, run)
        return carry

    lax.fori_loop(0, rows // QB, q_step, 0)
    wide = dqt.shape[0]
    dqkv_ref[:, 0:wide] = (dqt[...] * 0.125).astype(BF).T
    dqkv_ref[:, wide : 2 * wide] = dkt[...].astype(BF).T
    dqkv_ref[:, 2 * wide :] = dvt[...].astype(BF).T


WIDE = 384
TILE = 512
VMEM_LIMIT = 60 * 1024 * 1024


def params(*semantics):
    return pltpu.CompilerParams(dimension_semantics=semantics or None, vmem_limit_bytes=VMEM_LIMIT)


def cost(flops, data):
    return pl.CostEstimate(flops=int(flops), bytes_accessed=int(data), transcendentals=0)


def whole(shape):
    zero = (0,) * len(shape)
    return pl.BlockSpec(shape, lambda *_: zero)


ANYWHERE = pl.BlockSpec(memory_space=pl.ANY)


def attention_tables(segs):
    order = jnp.where(segs == 0, 1 << 20, segs)
    seqs, length = segs.shape
    first = order[:, ::QB]
    last = order[:, QB - 1 :: QB]
    lo = jnp.sum((order[:, None, :] < first[:, :, None]).astype(jnp.int32), axis=2) // KB
    hi = (jnp.sum((order[:, None, :] <= last[:, :, None]).astype(jnp.int32), axis=2) + KB - 1) // KB
    ids = jnp.arange(128, dtype=jnp.int32)[None, :]
    onehot = (segs.reshape(-1)[:, None] == ids) | ((ids >= 8) & (ids < 16))
    differ = segs[:, None, :] != jnp.arange(8, dtype=jnp.int32)[None, :, None]
    return lo, hi, onehot.astype(BF), jnp.where(differ, NEG, 0.0)


def attention_fwd(qkv, lo, hi, onehot, miss):
    seqs = lo.shape[0]
    rows = qkv.shape[0] // seqs
    wide = WIDE
    width = qkv.shape[1] // 3
    parts = width // wide
    col = lambda at: pl.BlockSpec((rows, wide), lambda s, j, *_: (s, 3 * j + at))
    return pl.pallas_call(
        attn_fwd_kernel,
        grid_spec=pltpu.PrefetchScalarGridSpec(
            num_scalar_prefetch=2,
            grid=(seqs, parts),
            in_specs=[
                col(0), col(1), col(2),
                pl.BlockSpec((rows, 128), lambda s, *_: (s, 0)),
                pl.BlockSpec((1, 8, rows), lambda s, *_: (s, 0, 0)),
            ],
            out_specs=[
                pl.BlockSpec((rows, wide), lambda s, j, *_: (s, j)),
                pl.BlockSpec((1, wide, rows), lambda s, j, *_: (s, j, 0)),
                pl.BlockSpec((1, 1, wide // HD, rows), lambda s, j, *_: (s, j, 0, 0)),
            ],
            scratch_shapes=[
                pltpu.VMEM((wide, rows), BF),
                pltpu.VMEM((wide, rows), BF),
                pltpu.VMEM((wide // HD, 16, rows), BF),
                pltpu.VMEM((8, rows), F32),
            ],
        ),
        out_shape=[
            jax.ShapeDtypeStruct((qkv.shape[0], width), BF),
            jax.ShapeDtypeStruct((seqs, width, rows), F32),
            jax.ShapeDtypeStruct((seqs, parts, wide // HD, rows), F32),
        ],
        compiler_params=params("arbitrary", "arbitrary"),
        cost_estimate=cost(24e9, 2e7),
        name="attention_forward",
    )(lo, hi, qkv, qkv, qkv, onehot, miss)


def attention_bwd(qkv, d_attn, ot, lse, lo, hi, onehot, miss):
    seqs = lo.shape[0]
    rows = qkv.shape[0] // seqs
    wide = WIDE
    col = lambda at: pl.BlockSpec((rows, wide), lambda s, j, *_: (s, 3 * j + at))
    return pl.pallas_call(
        attn_bwd_kernel,
        grid_spec=pltpu.PrefetchScalarGridSpec(
            num_scalar_prefetch=2,
            grid=(seqs, d_attn.shape[1] // wide),
            in_specs=[
                col(0), col(1), col(2),
                pl.BlockSpec((rows, wide), lambda s, j, *_: (s, j)),
                pl.BlockSpec((1, wide, rows), lambda s, j, *_: (s, j, 0)),
                pl.BlockSpec((1, 1, wide // HD, rows), lambda s, j, *_: (s, j, 0, 0)),
                pl.BlockSpec((rows, 128), lambda s, *_: (s, 0)),
                pl.BlockSpec((1, 8, rows), lambda s, *_: (s, 0, 0)),
            ],
            out_specs=pl.BlockSpec((rows, 3 * wide), lambda s, j, *_: (s, j)),
            scratch_shapes=[
                pltpu.VMEM((wide, rows), BF),
                pltpu.VMEM((wide, rows), BF),
                pltpu.VMEM((wide, rows), BF),
                pltpu.VMEM((wide // HD, 16, rows), BF),
                pltpu.VMEM((wide // HD, 16, rows), BF),
                pltpu.VMEM((wide, rows), F32),
                pltpu.VMEM((wide, rows), F32),
                pltpu.VMEM((wide, rows), F32),
            ],
        ),
        out_shape=jax.ShapeDtypeStruct(qkv.shape, BF),
        compiler_params=params("arbitrary", "arbitrary"),
        cost_estimate=cost(44e9, 4e7),
        name="attention_backward",
    )(lo, hi, qkv, qkv, qkv, d_attn, ot, lse, onehot, miss)


def normalized(x):
    mean = jnp.mean(x, axis=-1, keepdims=True)
    centered = x - mean
    scale = lax.rsqrt(jnp.mean(centered * centered, axis=-1, keepdims=True) + EPSILON)
    return centered * scale, scale


def norm_back(d, xhat, scale, gain):
    e = d * gain
    return scale * (e - jnp.mean(e, axis=-1, keepdims=True) - xhat * jnp.mean(e * xhat, axis=-1, keepdims=True))


def clear_first(*refs):
    @pl.when(pl.program_id(0) == 0)
    def _():
        for ref in refs:
            ref[...] = jnp.zeros_like(ref)


def add_row(ref, row, values):
    ref[row : row + 1, 0 : values.shape[1]] += jnp.sum(values, axis=0, keepdims=True)


def fetch(chunks, spots, outs, sems):
    for h in range(2):
        for chip in range(chunks.shape[1]):
            for row, count, which, target in spots(h, chip):
                pltpu.make_async_copy(
                    chunks.at[h, chip, pl.ds(row, count), :], outs[which].at[target], sems.at[which]
                ).start()


def fetched(out, sem):
    pltpu.make_async_copy(out, out, sem).wait()


def qkv_kernel(spots, tok, vec, bias, chunks, n1, qkv, w, sem):
    @pl.when(pl.program_id(0) == 0)
    def _():
        fetch(chunks, spots, [w], sem)

    xhat, _ = normalized(tok[...].astype(F32))
    n = (xhat * vec[0:1] + vec[1:2]).astype(BF)
    n1[...] = n

    @pl.when(pl.program_id(0) == 0)
    def _():
        fetched(w, sem.at[0])

    qkv[...] = (mm(n, w[...]) + bias[...]).astype(BF)


def project_qkv(tokens, vec, bias, chunks, spots):
    count, width = tokens.shape
    cols = 3 * width
    tile = lambda w: pl.BlockSpec((TILE, w), lambda i: (i, 0))
    return pl.pallas_call(
        functools.partial(qkv_kernel, spots),
        grid=(count // TILE,),
        in_specs=[tile(width), whole(vec.shape), whole(bias.shape), ANYWHERE],
        out_specs=[tile(width), tile(cols), whole((width, cols))],
        scratch_shapes=[pltpu.SemaphoreType.DMA((1,))],
        out_shape=[
            jax.ShapeDtypeStruct((count, width), BF),
            jax.ShapeDtypeStruct((count, cols), BF),
            jax.ShapeDtypeStruct((width, cols), BF),
        ],
        compiler_params=params("arbitrary"),
        cost_estimate=cost(2 * count * width * cols, 2e7),
        name="norm_and_qkv",
    )(tokens, vec, bias, chunks)


STRIP = 768
CURVE = 0.7978845608028654
CUBIC = 0.044715


def middle_kernel(
    spots, attn, tok, cot, vec, b1, chunks2, chunks3,
    out, n2, act, d_pre, d_mid, d_branch, d_attn, sums, sum_up, wo, w1, w2, sem,
):
    @pl.when(pl.program_id(0) == 0)
    def _():
        fetch(chunks2, spots[0], [wo, w1], sem)
        fetch(chunks3, spots[1], [w2], sem.at[pl.ds(2, 1)])
        for ref in (sums, sum_up):
            ref[...] = jnp.zeros_like(ref)
        for k, ref in enumerate((wo, w1, w2)):
            fetched(ref, sem.at[k])

    x = tok[...].astype(F32) + mm(attn[...], wo[...]) + vec[2:3]
    xhat, scale = normalized(x)
    n = (xhat * vec[0:1] + vec[1:2]).astype(BF)
    n2[...] = n
    d_out = cot[...]
    y = x + vec[3:4]
    d_n2 = None
    for j in range(w1.shape[1] // STRIP):
        cols = slice(j * STRIP, (j + 1) * STRIP)
        u = mm(n, w1[:, cols]) + b1[:, cols]
        d_act = mm_nt(d_out, w2[cols, :])
        square = u * u
        th = jnp.tanh(u * (CURVE + (CURVE * CUBIC) * square))
        half = 0.5 * u
        hidden = (half + half * th).astype(BF)
        act[:, cols] = hidden
        y = y + mm(hidden, w2[cols, :])
        slope = (0.5 + 0.5 * th) + half * (1.0 - th * th) * (CURVE + (3.0 * CURVE * CUBIC) * square)
        low = (d_act * slope).astype(BF)
        d_pre[:, cols] = low
        sum_up[:, cols] += jnp.sum(low.astype(F32), axis=0, keepdims=True)
        part = mm_nt(low, w1[:, cols])
        d_n2 = part if d_n2 is None else d_n2 + part
    out[...] = y.astype(BF)
    add_row(sums, 0, d_n2 * xhat)
    add_row(sums, 1, d_n2)
    g = d_out.astype(F32)
    add_row(sums, 3, g)
    d = g + norm_back(d_n2, xhat, scale, vec[0:1])
    d_mid[...] = d
    low = d.astype(BF)
    d_branch[...] = low
    add_row(sums, 2, low.astype(F32))
    d_attn[...] = mm_nt(low, wo[...]).astype(BF)


def middle_part(attn, tokens, cotangent, vec, b1, gathered, spots):
    count, width = tokens.shape
    hidden = b1.shape[1]
    rows = TILE // 2
    tile = lambda w: pl.BlockSpec((rows, w), lambda i: (i, 0))
    row = lambda w, kind: jax.ShapeDtypeStruct((count, w), kind)
    return pl.pallas_call(
        functools.partial(middle_kernel, spots),
        grid=(count // rows,),
        in_specs=[tile(width), tile(width), tile(width), whole(vec.shape), whole(b1.shape)] + [ANYWHERE] * 2,
        out_specs=[
            tile(width), tile(width), tile(hidden), tile(hidden), tile(width), tile(width), tile(width),
            whole((8, width)), whole((1, hidden)),
        ],
        scratch_shapes=[
            pltpu.VMEM((width, width), BF),
            pltpu.VMEM((width, hidden), BF),
            pltpu.VMEM((hidden, width), BF),
            pltpu.SemaphoreType.DMA((3,)),
        ],
        out_shape=[
            row(width, BF), row(width, BF), row(hidden, BF), row(hidden, BF), row(width, F32), row(width, BF),
            row(width, BF), jax.ShapeDtypeStruct((8, width), F32), jax.ShapeDtypeStruct((1, hidden), F32),
        ],
        compiler_params=params("arbitrary"),
        cost_estimate=cost(4 * count * width * (width + 2 * hidden), 6e7),
        name="middle",
    )(attn, tokens, cotangent, vec, b1, *gathered)


def first_norm_kernel(d_qkv, w, tok, d_mid, vec, out, sums):
    clear_first(sums)
    d = mm_nt(d_qkv[...], w[...])
    xhat, scale = normalized(tok[...].astype(F32))
    add_row(sums, 0, d * xhat)
    add_row(sums, 1, d)
    add_row(sums, 2, d_qkv[...].astype(F32))
    out[...] = (d_mid[...] + norm_back(d, xhat, scale, vec[0:1])).astype(BF)


def first_norm_back(d_qkv, w, tokens, d_mid, vec):
    count, width = tokens.shape
    cols = d_qkv.shape[1]
    tile = lambda w: pl.BlockSpec((TILE, w), lambda i: (i, 0))
    return pl.pallas_call(
        first_norm_kernel,
        grid=(count // TILE,),
        in_specs=[tile(cols), whole(w.shape), tile(width), tile(width), whole(vec.shape)],
        out_specs=[tile(width), whole((8, cols))],
        out_shape=[jax.ShapeDtypeStruct((count, width), BF), jax.ShapeDtypeStruct((8, cols), F32)],
        compiler_params=params("arbitrary"),
        cost_estimate=cost(2 * count * width * cols, 3e7),
        name="first_norm_back",
    )(d_qkv, w, tokens, d_mid, vec)


def tn(a, b):
    return lax.dot_general(a, b, (((0,), (0,)), ((), ())), preferred_element_type=F32)


def grad_kernel(layout, *refs):
    count = len(layout)
    ins, out, sums = refs[: 2 * count], refs[2 * count], refs[2 * count + 1 :]
    step = pl.program_id(0)

    @pl.when(step == 0)
    def _():
        for acc in sums:
            acc[...] = jnp.zeros_like(acc)

    for k in range(count):
        sums[k][...] += tn(ins[2 * k][...], ins[2 * k + 1][...])

    @pl.when(step == pl.num_programs(0) - 1)
    def _():
        _, chips, _, rows, _ = out.shape
        base = 0
        for k, blocks in enumerate(layout):
            tall = sums[k].shape[0] // (chips * rows)
            for h in range(2):
                for b in range(blocks):
                    at = (h * blocks + b) * WIDE
                    low = sums[k][:, at : at + WIDE].astype(BF)
                    out[h, :, base + b * tall : base + (b + 1) * tall] = low.reshape(chips, tall, rows, WIDE)
            base += blocks * tall


def grad_part(pairs, chips, rows, name):
    tokens = pairs[0][0].shape[0]
    specs, arrays, scratch, layout, flops, total = [], [], [], [], 0, 0
    for lhs, rhs in pairs:
        for x in (lhs, rhs):
            specs.append(pl.BlockSpec((TILE, x.shape[1]), lambda i: (i, 0)))
            arrays.append(x)
        scratch.append(pltpu.VMEM((lhs.shape[1], rhs.shape[1]), F32))
        layout.append(rhs.shape[1] // (2 * WIDE))
        total += layout[-1] * (lhs.shape[1] // (chips * rows))
        flops += 2 * tokens * lhs.shape[1] * rhs.shape[1]
    shape = (2, chips, total, rows, WIDE)
    return pl.pallas_call(
        functools.partial(grad_kernel, tuple(layout)),
        grid=(tokens // TILE,),
        in_specs=specs,
        out_specs=whole(shape),
        out_shape=jax.ShapeDtypeStruct(shape, BF),
        scratch_shapes=scratch,
        compiler_params=params("arbitrary"),
        cost_estimate=cost(flops, 3e7),
        name=name,
    )(*arrays)


def neighbours():
    me = lax.axis_index("fsdp")
    core = lax.rem(me, 2)
    x = lax.rem(me // 2, 2)
    y = lax.rem(me // 4, 2)
    along_y = 4 * (1 - 2 * y)
    along_x = 2 * (1 - 2 * x)
    first = (1 - core) * along_y + core * along_x
    second = along_y + along_x - first
    return me, core, me // 8, first, second


def greet(others):
    barrier = pltpu.get_barrier_semaphore()
    for other in others:
        pl.semaphore_signal(barrier, inc=1, device_id=(other,), device_id_type=pl.DeviceIdType.MESH)
    pl.semaphore_wait(barrier, len(others))


def gather_kernel(blocks, depth, *refs):
    flows = len(blocks)
    owns, oths, outs = refs[:flows], refs[flows : 2 * flows], refs[2 * flows : 3 * flows]
    sems = refs[3 * flows :]
    me, core, z, first, second = neighbours()
    twin = me + 1 - 2 * core
    chip = me // 2
    deep = [chip * 2 + core] + [lax.rem(z + k, depth) * 8 + lax.rem(me, 8) for k in range(1, depth)]
    greet([twin, me + first, me + second] + deep[1:])
    mine = [lax.rem(z + depth - k, depth) * 4 + lax.rem(chip, 4) for k in range(depth)]
    theirs = [at + first // 2 for at in mine]
    last = [at + second // 2 for at in mine + theirs]

    def send(f, at, send_sem, recv_sem, device):
        pltpu.make_async_remote_copy(
            src_ref=outs[f].at[core, at],
            dst_ref=outs[f].at[core, at],
            send_sem=send_sem,
            recv_sem=recv_sem,
            device_id=(device,),
            device_id_type=pl.DeviceIdType.MESH,
        ).start()

    def arrived(ref, sem):
        pltpu.make_async_copy(ref, ref, sem).wait()

    def onward(f, k, at, steps):
        far, near, cross, seen, local, out, twin_out, twin_in, pair_out, pair_in = sems[10 * f : 10 * f + 10]
        if steps == 2:
            send(f, at, out.at[0], near.at[k], me + first)
        if steps >= 1:
            send(f, at, out.at[0], cross.at[k if steps == 2 else depth + k], me + second)
        send(f, at, twin_out.at[0], twin_in.at[0], twin)

    for f in range(flows):
        pair_out, pair_in, local = sems[10 * f + 8], sems[10 * f + 9], sems[10 * f + 4]
        row = 0
        for size in blocks[f]:
            here_rows = pl.ds(pl.multiple_of(2 * row + core * size, 8), size)
            pltpu.make_async_copy(
                owns[f].at[pl.ds(row, size), :], outs[f].at[core, chip, here_rows, :], local.at[0]
            ).start()
            pltpu.make_async_remote_copy(
                src_ref=oths[f].at[pl.ds(row, size), :],
                dst_ref=outs[f].at[1 - core, chip, here_rows, :],
                send_sem=pair_out.at[0],
                recv_sem=pair_in.at[0],
                device_id=(twin,),
                device_id_type=pl.DeviceIdType.MESH,
            ).start()
            row += size
    for f in range(flows):
        far, out = sems[10 * f], sems[10 * f + 5]
        arrived(owns[f], sems[10 * f + 4].at[0])
        arrived(owns[f], sems[10 * f + 9].at[0])
        for k in range(1, depth):
            send(f, chip, out.at[0], far.at[k], deep[k])
        onward(f, 0, chip, 2)

    def from_far(f):
        for k in range(1, depth):
            arrived(outs[f].at[core, mine[k]], sems[10 * f].at[k])
            onward(f, k, mine[k], 2)

    def from_near(f):
        for k in range(depth):
            arrived(outs[f].at[core, theirs[k]], sems[10 * f + 1].at[k])
            onward(f, k, theirs[k], 1)

    def from_cross(f):
        for k in range(2 * depth):
            arrived(outs[f].at[core, last[k]], sems[10 * f + 2].at[k])
            onward(f, k, last[k], 0)

    for f in range(flows):
        from_far(f)
        from_near(f)
        if f > 0:
            from_cross(f - 1)
    from_cross(flows - 1)
    for f in range(flows):
        chips = outs[f].shape[1]
        arrived(outs[f].at[1 - core], sems[10 * f + 7].at[0])
        arrived(outs[f].at[0], sems[10 * f + 6].at[0])
        arrived(outs[f].at[0, pl.ds(0, chips - 1)], sems[10 * f + 5].at[0])
        arrived(oths[f], sems[10 * f + 8].at[0])


def gather_shards(owns, oths, blocks, depth):
    chips = 4 * depth
    outs = [jax.ShapeDtypeStruct((2, chips, 2 * o.shape[0], WIDE), BF) for o in owns]
    dma = lambda n: pltpu.SemaphoreType.DMA((n,))
    scratch = []
    for _ in owns:
        scratch += [dma(depth), dma(depth), dma(2 * depth)] + [dma(1)] * 7
    return pl.pallas_call(
        functools.partial(gather_kernel, blocks, depth),
        in_specs=[ANYWHERE] * (2 * len(owns)),
        out_specs=[ANYWHERE] * len(owns),
        out_shape=outs,
        scratch_shapes=scratch,
        compiler_params=pltpu.CompilerParams(collective_id=0, has_side_effects=True),
        cost_estimate=cost(0, 3e7),
        name="gather_shards",
    )(*owns, *oths)


def pack_kernel(core, *refs):
    (wqkv, small, wo, w1, w2), outs = refs[:5], refs[5:]
    width = wo.shape[1]
    for c in range(2):

        @pl.when(core[0] == c)
        def _(c=c):
            for h in range(2):
                first, second, third = outs[:3] if h == c else outs[3:]
                rows = wo.shape[0]
                for t in range(3):
                    first[rows * t : rows * (t + 1), :] = wqkv[:, t * width + h * WIDE : t * width + (h + 1) * WIDE].astype(BF)
                first[3 * rows :, :] = small[...].astype(BF)
                second[0:rows, :] = wo[:, h * WIDE : (h + 1) * WIDE].astype(BF)
                for b in range(4):
                    cols = slice((4 * h + b) * WIDE, (4 * h + b + 1) * WIDE)
                    second[rows * (1 + b) : rows * (2 + b), :] = w1[:, cols].astype(BF)
                third[...] = w2[:, h * WIDE : (h + 1) * WIDE].astype(BF)


def pack(wqkv, small, wo, w1, w2, core):
    rows = wo.shape[0]
    ins = (wqkv, small, wo, w1, w2)
    shapes = [(3 * rows + small.shape[0], WIDE), (5 * rows, WIDE), (w2.shape[0], WIDE)] * 2
    return pl.pallas_call(
        pack_kernel,
        grid_spec=pltpu.PrefetchScalarGridSpec(
            num_scalar_prefetch=1,
            grid=(1,),
            in_specs=[whole(x.shape) for x in ins],
            out_specs=[whole(s) for s in shapes],
        ),
        out_shape=[jax.ShapeDtypeStruct(s, BF) for s in shapes],
        name="pack_shards",
    )(core, *ins)


def scatter_kernel(depth, splits, *refs):
    flows = len(splits)
    ready = flows - 2
    ins, (act, cot, n1, d_qkv) = refs[:ready], refs[ready : ready + 4]
    outs, rest = refs[ready + 4 : ready + 4 + flows], refs[ready + 4 + flows :]
    (down, thirds, held, slots, held_sem, slot_sem), rest = rest[:6], rest[6:]
    ins = list(ins) + [down, thirds]
    width = cot.shape[1]
    tall = act.shape[1] // width
    tasks = tall + d_qkv.shape[1] // width

    def held_copy(k):
        return pltpu.make_async_copy((cot, n1)[k], held.at[k], held_sem.at[k])

    def fetch_task(t):
        slot = lax.rem(t, 2)

        @pl.when(t < tall)
        def _():
            cols = pl.ds(pl.multiple_of(t * width, 128), width)
            pltpu.make_async_copy(act.at[:, cols], slots.at[slot], slot_sem.at[slot]).start()

        @pl.when(t >= tall)
        def _():
            cols = pl.ds(pl.multiple_of((t - tall) * width, 128), width)
            pltpu.make_async_copy(d_qkv.at[:, cols], slots.at[slot], slot_sem.at[slot]).start()

    for k in range(2):
        held_copy(k).start()
        fetch_task(jnp.int32(k))
    me, core, z, first, second = neighbours()
    chip = me // 2
    x, y = lax.rem(chip, 2), lax.rem(chip // 2, 2)
    twin = me + 1 - 2 * core
    deep = [lax.rem(z + k, depth) * 8 + lax.rem(me, 8) for k in range(1, depth)]
    greet([twin, me + first, me + second] + deep)
    plane = 2 * depth
    chips = 2 * plane

    def chip_of(j, core):
        bit2, bit1 = x + core * (y - x), y + core * (x - y)
        keep, side, k = j // plane, lax.rem(j, plane) // depth, lax.rem(j, depth)
        bit2 = (1 - bit2) + keep * (2 * bit2 - 1)
        bit1 = (1 - bit1) + side * (2 * bit1 - 1)
        return lax.rem(z + 1 + k, depth) * 4 + bit1 * (2 - core) + bit2 * (1 + core)

    def remote(src, dst, send_sem, recv_sem, device):
        return pltpu.make_async_remote_copy(
            src_ref=src,
            dst_ref=dst,
            send_sem=send_sem,
            recv_sem=recv_sem,
            device_id=(device,),
            device_id_type=pl.DeviceIdType.MESH,
        )

    def arrived(ref, sem):
        pltpu.make_async_copy(ref, ref, sem).wait()

    def flow(f):
        return rest[8 * f : 8 * f + 8]

    def sems(f):
        return rest[8 * flows + 11 * f : 8 * flows + 11 * f + 11]

    def loop(count, body):
        def step(j, carry):
            body(j)
            return carry

        lax.fori_loop(0, count, step, 0)

    def begin(f):
        own, in0 = flow(f)[:2]
        load, got0, sent0 = sems(f)[0], sems(f)[1], sems(f)[6]

        def body(j):
            pltpu.make_async_copy(ins[f].at[core, chip_of(j, core)], own.at[j], load.at[j]).start()
            remote(ins[f].at[1 - core, chip_of(j, 1 - core)], in0.at[j], sent0.at[0], got0.at[j], twin).start()

        loop(chips, body)

    def sum_of(f, j):
        own, in0 = flow(f)[:2]
        arrived(own.at[j], sems(f)[0].at[j])
        arrived(in0.at[j], sems(f)[1].at[j])
        return own[j].astype(F32) + in0[j].astype(F32)

    def lagging(count, compute, send):
        def body(j):
            compute(j)

            @pl.when(j > 0)
            def _():
                send(j - 1)

        loop(count, body)
        send(count - 1)

    def across(f):
        own, _, in1 = flow(f)[:3]
        got1, sent1 = sems(f)[2], sems(f)[7]

        def compute(j):
            own[j] = sum_of(f, j).astype(own.dtype)

        lagging(plane, compute, lambda j: remote(own.at[j], in1.at[j], sent1.at[0], got1.at[j], me + second).start())

    def kept(f, j):
        in1 = flow(f)[2]
        arrived(in1.at[j], sems(f)[2].at[j])
        return sum_of(f, plane + j) + in1[j].astype(F32)

    def along(f):
        own, in2 = flow(f)[0], flow(f)[3]
        got2, sent2 = sems(f)[3], sems(f)[8]

        def compute(k):
            own[plane + k] = kept(f, k).astype(own.dtype)

        lagging(
            depth, compute, lambda k: remote(own.at[plane + k], in2.at[k], sent2.at[0], got2.at[k], me + first).start()
        )

    def upward(f):
        own, in2, in3, total = flow(f)[0], flow(f)[3], flow(f)[4], flow(f)[5]
        got2, got3, sent3 = sems(f)[3], sems(f)[4], sems(f)[9]

        def value(k):
            arrived(in2.at[k], got2.at[k])
            return kept(f, depth + k) + in2[k].astype(F32)

        for k in range(depth - 1):
            own[plane + depth + k] = value(k).astype(own.dtype)
            if k > 0:
                remote(own.at[plane + depth + k - 1], in3.at[k - 1], sent3.at[0], got3.at[k - 1], deep[k - 1]).start()
        total[...] = value(depth - 1)
        k = depth - 2
        remote(own.at[plane + depth + k], in3.at[k], sent3.at[0], got3.at[k], deep[k]).start()

    def mine(f, ref, which):
        if splits[f] == "rows":
            half = ref.shape[1] // 2
            return ref.at[:, pl.ds(pl.multiple_of(which * half, 8), half), :]
        half = ref.shape[0] // 2
        return ref.at[pl.ds(which * half, half)]

    def finish(f):
        in3, total, theirs = flow(f)[4], flow(f)[5], flow(f)[6]
        for k in range(depth - 1):
            arrived(in3.at[k], sems(f)[4].at[k])
            total[...] += in3[k].astype(F32)
        if splits[f] is None:
            outs[f][...] = total[...]
        else:
            outs[f][core] = mine(f, total, core)[...]
            remote(mine(f, total, 1 - core), theirs, sems(f)[10].at[0], sems(f)[5].at[0], twin).start()

    def multiply(t):
        slot = lax.rem(t, 2)
        pltpu.make_async_copy(slots.at[slot], slots.at[slot], slot_sem.at[slot]).wait()

        @pl.when(t < tall)
        def _():
            low = tn(slots[slot], held[0]).astype(BF)
            count = down.shape[1] // tall
            for h in range(2):
                part = low[:, h * WIDE : (h + 1) * WIDE].reshape((count,) + down.shape[2:])
                down[h, pl.ds(t * count, count)] = part

        @pl.when(t >= tall)
        def _():
            low = tn(held[1], slots[slot]).astype(BF)
            for i in range(2):
                block = 2 * (t - tall) + i
                part = low[:, i * WIDE : (i + 1) * WIDE].reshape(thirds.shape[1], thirds.shape[3], WIDE)
                thirds[block // 3, :, lax.rem(block, 3)] = part

        @pl.when(t + 2 < tasks)
        def _():
            fetch_task(t + 2)

    up, out, small, low, last = range(flows)
    for f in range(ready):
        begin(f)
    for k in range(2):
        held_copy(k).wait()

    def task(t):
        multiply(t)

        @pl.when(t == 0)
        def _():
            across(up)

        @pl.when(t == 1)
        def _():
            across(out)
            across(small)

        @pl.when(t == tall)
        def _():
            begin(low)

        @pl.when(t == tall + 1)
        def _():
            across(low)
            along(up)

    loop(tasks, task)
    along(out)
    along(small)
    begin(last)
    upward(up)
    across(last)
    upward(out)
    upward(small)
    along(low)
    upward(low)
    along(last)
    for f in range(ready + 1):
        finish(f)
    upward(last)
    finish(last)
    for f in range(flows):
        _, in0, in1, in2, in3, total, theirs, _ = flow(f)
        if splits[f] is not None:
            arrived(theirs, sems(f)[5].at[0])
            outs[f][1 - core] = theirs[...]
            arrived(theirs, sems(f)[10].at[0])
        for ref, sem in zip((in0, in1, in2, in3), sems(f)[6:10]):
            arrived(ref, sem.at[0])


def scatter_sums(parts, act, cot, n1, d_qkv, splits, depth):
    chips = 4 * depth
    tokens, width = cot.shape
    rows = width // chips
    outs, buffers, signals = [], [], []
    dma = lambda n: pltpu.SemaphoreType.DMA((n,))
    shapes = [(2, chips, 4, rows, WIDE), (2, chips, 3, rows, WIDE)]
    work = [pltpu.VMEM(x, BF) for x in shapes]
    work += [pltpu.VMEM((2, tokens, width), BF), pltpu.VMEM((2, tokens, width), BF), dma(2), dma(2)]
    kinds = [(p.shape[2:], p.dtype) for p in parts] + [(x[2:], BF) for x in shapes]
    for (chunk, kind), split in zip(kinds, splits):
        if split == "rows":
            part = (chunk[0], chunk[1] // 2) + chunk[2:]
        elif split == "blocks":
            part = (chunk[0] // 2,) + chunk[1:]
        else:
            part = chunk
        outs.append(jax.ShapeDtypeStruct(part if split is None else (2,) + part, F32))
        for count in (chips, chips, chips // 2, depth, depth - 1):
            buffers.append(pltpu.VMEM((count,) + chunk, kind))
        buffers += [pltpu.VMEM(chunk, F32), pltpu.VMEM(part, F32), dma(1)]
        signals += [dma(chips), dma(chips), dma(chips // 2), dma(depth), dma(depth - 1)] + [dma(1)] * 6
    return pl.pallas_call(
        functools.partial(scatter_kernel, depth, tuple(splits)),
        in_specs=[ANYWHERE] * (len(parts) + 4),
        out_specs=[pl.BlockSpec(memory_space=pltpu.VMEM)] * len(outs),
        out_shape=outs,
        scratch_shapes=work + buffers + signals,
        compiler_params=pltpu.CompilerParams(
            collective_id=1, has_side_effects=True, vmem_limit_bytes=VMEM_LIMIT
        ),
        cost_estimate=cost(0, 3e7),
        name="scatter_sums",
    )(*parts, act, cot, n1, d_qkv)


def by_neighbours(devices, width, hidden, count):
    rows = width // devices
    fits = rows * devices == width and rows % 8 == 0 and devices % 8 == 0
    return fits and width == 2 * WIDE and hidden == 4 * width and count % TILE == 0


def weight_halves(w):
    rows = w.shape[0]
    return w.reshape(rows, 3, 2, WIDE).transpose(0, 2, 1, 3).reshape(rows, -1)


def local(
    tokens, segments, cotangent, ln1_gain, ln1_shift, w_qkv, bias_q, bias_v, w_out, bias_out,
    ln2_gain, ln2_shift, w_up, bias_up, w_down, bias_down, *, seq,
):
    masters = (
        ln1_gain, ln1_shift, w_qkv, bias_q, bias_v, w_out, bias_out,
        ln2_gain, ln2_shift, w_up, bias_up, w_down, bias_down,
    )
    count, width = tokens.shape
    tables = attention_tables(segments.reshape(-1, seq))
    run = by_chips if by_neighbours(lax.axis_size("fsdp"), width, w_up.shape[1], count) else by_collectives
    return run(tokens, cotangent, tables, masters)


def by_collectives(tokens, cotangent, tables, masters):
    def norm(x, gain, shift):
        return normalized(x)[0] * gain + shift

    width = tokens.shape[1]
    full = [lax.all_gather(m.astype(BF), "fsdp", axis=0, tiled=True) for m in masters]
    g1, c1, wqkv, bq, bv, wo, bo, g2, c2, w1, b1, w2, b2 = [p.astype(F32) if p.ndim == 1 else p for p in full]
    wqkv = weight_halves(wqkv)
    rows = tokens.astype(F32)
    n1 = norm(rows, g1, c1).astype(BF)
    bias = weight_halves(jnp.concatenate([bq, jnp.zeros_like(bq), bv])[None])
    qkv = (mm(n1, wqkv) + bias).astype(BF)
    attn, attn_t, lse = attention_fwd(qkv, *tables)
    middle = rows + mm(attn, wo) + bo
    n2 = norm(middle, g2, c2).astype(BF)
    act_value, gelu_pull = jax.vjp(functools.partial(jax.nn.gelu, approximate=True), mm(n2, w1) + b1)
    act = act_value.astype(BF)
    layer_out = (middle + mm(act, w2) + b2).astype(BF)
    d_out = cotangent.astype(F32)
    d_pre = gelu_pull(mm_nt(cotangent, w2))[0].astype(BF)
    _, pull = jax.vjp(norm, middle, g2, c2)
    d_mid, d_g2, d_c2 = pull(mm_nt(d_pre, w1))
    d_mid = d_out + d_mid
    d_branch = d_mid.astype(BF)
    d_attn = mm_nt(d_branch, wo).astype(BF)
    d_qkv = attention_bwd(qkv, d_attn, attn_t, lse, *tables)
    _, pull = jax.vjp(norm, rows, g1, c1)
    d_rows, d_g1, d_c1 = pull(mm_nt(d_qkv, wqkv))
    input_grad = (d_mid + d_rows).astype(BF)
    total = lambda x: jnp.sum(x.astype(F32), axis=0)
    by_part = lambda x: x.reshape(-1, 2, 3, WIDE).transpose(0, 2, 1, 3).reshape(x.shape)
    sums = by_part(total(d_qkv)[None])[0]
    grads = (
        d_g1, d_c1, by_part(tn(n1, d_qkv)), sums[:width], sums[2 * width :], tn(attn, d_branch), total(d_branch),
        d_g2, d_c2, tn(n2, d_pre), total(d_pre), tn(act, cotangent), total(d_out),
    )
    return (layer_out, input_grad) + tuple(
        lax.psum_scatter(g, "fsdp", scatter_dimension=0, tiled=True) for g in grads
    )


def by_chips(tokens, cotangent, tables, masters):
    devices = lax.axis_size("fsdp")
    chips = devices // 2
    depth = devices // 8
    count, width = tokens.shape
    ln1_gain, ln1_shift, w_qkv, bias_q, bias_v, w_out, bias_out, ln2_gain, ln2_shift, w_up, bias_up, w_down, bias_down = masters
    part = width // devices
    two = 2 * part
    hidden = w_up.shape[1]
    core = lax.rem(lax.axis_index("fsdp"), 2).astype(jnp.int32).reshape(1)

    small = jnp.concatenate([ln1_gain, ln1_shift, bias_q, bias_v, bias_out, ln2_gain, ln2_shift, bias_down, bias_up])
    small = jnp.pad(small[None], ((0, 7), (0, WIDE - small.shape[0])))
    own1, own2, own3, oth1, oth2, oth3 = pack(w_qkv, small, w_out, w_up, w_down, core)

    chunks1, chunks2, chunks3 = gather_shards(
        (own1, own2, own3), (oth1, oth2, oth3), ([part] * 3 + [8], [part] * 5, [4 * part]), depth
    )
    vecs = chunks1[0, :, 6 * part :: 8].reshape(devices, WIDE).astype(F32)
    g1, c1, bq, bv, bo, g2, c2, b2 = [vecs[:, i * part : (i + 1) * part].reshape(-1) for i in range(8)]
    b1 = vecs[:, 8 * part : 12 * part].reshape(1, -1)
    bias = weight_halves(jnp.concatenate([bq, jnp.zeros_like(bq), bv])[None])

    def spots_qkv(h, chip):
        return [
            (two * t, two, 0, (pl.ds(two * chip, two), pl.ds((3 * h + t) * WIDE, WIDE))) for t in range(3)
        ]

    def spots_up(h, chip):
        rows = pl.ds(two * chip, two)
        return [(0, two, 0, (rows, pl.ds(h * WIDE, WIDE)))] + [
            (two * (1 + b), two, 1, (rows, pl.ds((4 * h + b) * WIDE, WIDE))) for b in range(4)
        ]

    def spots_down(h, chip):
        return [(0, 4 * two, 0, (pl.ds(4 * two * chip, 4 * two), pl.ds(h * WIDE, WIDE)))]

    n1, qkv, wqkv = project_qkv(tokens, jnp.stack([g1, c1]), bias, chunks1, spots_qkv)
    attn, attn_t, lse = attention_fwd(qkv, *tables)
    layer_out, n2, act, d_pre, d_mid, d_branch, d_attn, sums2, sum_up = middle_part(
        attn, tokens, cotangent, jnp.stack([g2, c2, bo, b2]), b1, (chunks2, chunks3), (spots_up, spots_down)
    )

    g_up = grad_part([(n2, d_pre)], chips, two, "grad_up")
    g_out = grad_part([(attn, d_branch)], chips, two, "grad_out")
    d_qkv = attention_bwd(qkv, d_attn, attn_t, lse, *tables)
    input_grad, sums1 = first_norm_back(d_qkv, wqkv, tokens, d_mid, g1[None])
    by_half = sums1[2].reshape(2, 3, WIDE)
    vecs = [
        sums1[0, :width], sums1[1, :width], by_half[:, 0].reshape(-1), by_half[:, 2].reshape(-1),
        sums2[2], sums2[0], sums2[1], sums2[3],
    ]
    small = jnp.concatenate([v.reshape(devices, part) for v in vecs] + [sum_up.reshape(devices, 4 * part)], axis=1)
    small = small.reshape(chips, 2, 1, -1).swapaxes(0, 1)
    small = jnp.pad(small, ((0, 0), (0, 0), (0, 7), (0, WIDE - small.shape[3])))
    g_up, g_out, small, g_down, g_qkv = scatter_sums(
        [g_up, g_out, small], act, cotangent, n1, d_qkv, ("rows", "rows", None, "blocks", "rows"), depth
    )
    small = small[0]
    s = [small[i * part : (i + 1) * part] for i in range(8)]
    s_b1 = small[8 * part : 12 * part]
    g_up = g_up.transpose(2, 0, 1, 3).reshape(part, hidden)
    g_out = g_out[:, 0].transpose(1, 0, 2).reshape(part, width)
    g_down = g_down.reshape(2, 4 * part, WIDE).transpose(1, 0, 2).reshape(4 * part, width)
    g_qkv = g_qkv.transpose(2, 1, 0, 3).reshape(part, 3 * width)
    return (
        layer_out, input_grad, s[0], s[1], g_qkv, s[2], s[3], g_out, s[4], s[5], s[6], g_up, s_b1, g_down, s[7],
    )


MICRO = 2


def solution(mesh):
    line, table = P("fsdp"), P("fsdp", None)
    weights = (line, line, table, line, line, table, line, line, line, table, line, table, line)

    def step(tokens, *rest):
        seq = tokens.shape[0] // (mesh.shape["fsdp"] * MICRO)
        return jax.shard_map(
            functools.partial(local, seq=seq),
            mesh=mesh,
            in_specs=(table, line, table) + weights,
            out_specs=(table, table) + weights,
            check_vma=False,
        )(tokens, *rest)

    return step
```

```python
import functools
import jax
import jax.numpy as jnp
from jax import lax
from jax.experimental import pallas as pl
from jax.experimental.pallas import tpu as pltpu
from jax.sharding import PartitionSpec as P

HD = 64
QB = 128
KB = 128
NEG = -1000000000.0
BF = jnp.bfloat16
F32 = jnp.float32
EPSILON = 1e-06
NT = (((1,), (1,)), ((), ()))


def mm(a, b):
    return jnp.dot(a, b, preferred_element_type=F32)


def mm_nt(a, b):
    return lax.dot_general(a, b, NT, preferred_element_type=F32)


def pair_diag(top, bottom):
    zero = jnp.zeros_like(top)
    return jnp.concatenate(
        [jnp.concatenate([top, zero], axis=1), jnp.concatenate([zero, bottom], axis=1)], axis=0
    )


SPANS = (2, 3, 4, 5, 6, 8)


def by_span(lo, hi, rows, run):
    need = hi - lo
    below = 0
    for span in SPANS:
        if below * KB >= rows:
            break
        size = min(span * KB, rows)
        last = size == rows

        @pl.when((need > below) & (last | (need <= span)))
        def _(size=size):
            run(pl.multiple_of(jnp.minimum(lo * KB, rows - size), KB), size)

        below = span


def chunks(k0, size):
    return [(pl.multiple_of(k0 + c, KB), min(2 * KB, size - c)) for c in range(0, size, 2 * KB)]


def terms(pieces):
    width = pieces[0].shape[1]
    row = lax.broadcasted_iota(jnp.int32, (8, width), 0)
    tail = jnp.zeros((8, width), F32)
    for i, piece in enumerate(pieces):
        tail = jnp.where(row == i, piece, tail)
    return tail


def three_parts(x):
    first = x.astype(BF).astype(F32)
    rest = x - first
    second = rest.astype(BF).astype(F32)
    return first, second, rest - second


def pair_rhs(feat, extra, p, qs):
    a = 128 * p
    block = pair_diag(feat[a : a + 64, qs], feat[a + 64 : a + 128, qs])
    rows = jnp.concatenate([extra[2 * p, :, qs], extra[2 * p + 1, :, qs]], axis=1)
    return block, jnp.concatenate([block, rows, jnp.zeros((112, 2 * QB), BF)], axis=0)


def attn_fwd_kernel(
    lo, hi, q_ref, k_ref, v_ref, oh_ref, mr_ref, o_ref, ot_ref, lse_ref, qt, vt, extra, tops
):
    seq = pl.program_id(0)
    rows = q_ref.shape[0]
    pairs = q_ref.shape[1] // 128
    heads = 2 * pairs
    vt[...] = v_ref[...].T
    qt[...] = (q_ref[...] * 0.125).astype(BF).T
    lane = lax.broadcasted_iota(jnp.int32, (8, heads * HD), 1) // HD
    pick = (lane == lax.broadcasted_iota(jnp.int32, (8, heads * HD), 0)).astype(BF)
    square = k_ref[...].astype(F32)
    norms = mm_nt(pick, (square * square).astype(BF))
    bound = jnp.sqrt(jnp.max(norms, axis=1, keepdims=True)) * 1.01
    for h in range(heads):
        qh = qt[64 * h : 64 * h + 64, :].astype(F32)
        length = jnp.sqrt(jnp.sum(qh * qh, axis=0, keepdims=True)) * 1.01
        m = (length * bound[h : h + 1, :]).astype(BF).astype(F32)
        tops[h : h + 1, :] = m
        extra[h, :, :] = jnp.concatenate([mr_ref[0], terms([-m])], axis=0).astype(BF)

    def keep(qs, p, l, full):
        a = 128 * p
        ot_ref[0, a : a + 64, qs] = full[0:64, 0:QB]
        ot_ref[0, a + 64 : a + 128, qs] = full[64:128, QB:]
        lse_ref[0, 0, 2 * p : 2 * p + 1, qs] = l[:, 0:QB]
        lse_ref[0, 0, 2 * p + 1 : 2 * p + 2, qs] = l[:, QB:]

    def q_step(qb, carry):
        qs = pl.ds(pl.multiple_of(qb * QB, QB), QB)

        def run(k0, size):
            rhs = [pair_rhs(qt, extra, p, qs)[1] for p in range(pairs)]
            l = [jnp.zeros((1, 2 * QB), F32)] * pairs
            acc = [None] * pairs
            for c0, cs in chunks(k0, size):
                ks = pl.ds(c0, cs)
                oh = oh_ref[ks, :]
                for p in range(pairs):
                    cols = slice(128 * p, 128 * p + 128)
                    w = jnp.exp(mm(jnp.concatenate([k_ref[ks, cols], oh], axis=1), rhs[p]))
                    l[p] = l[p] + jnp.sum(w, axis=0, keepdims=True)
                    part = mm(vt[cols, ks], w.astype(BF))
                    acc[p] = part if acc[p] is None else acc[p] + part
            for p in range(pairs):
                keep(qs, p, l[p], acc[p])

        by_span(lo[seq, qb], hi[seq, qb], rows, run)
        return carry

    lax.fori_loop(0, rows // QB, q_step, 0)

    @pl.when(jnp.min(lse_ref[0, 0]) < 1e-20)
    def _():
        for h in range(heads):
            extra[h, :, :] = jnp.concatenate([mr_ref[0], jnp.zeros_like(mr_ref[0])], axis=0).astype(BF)

        def q_again(qb, carry):
            qs = pl.ds(pl.multiple_of(qb * QB, QB), QB)
            for p in range(pairs):
                cols = slice(128 * p, 128 * p + 128)
                rhs = pair_rhs(qt, extra, p, qs)[1]

                def scores(kb):
                    ks = pl.ds(pl.multiple_of(kb * KB, KB), KB)
                    return ks, mm(jnp.concatenate([k_ref[ks, cols], oh_ref[ks, :]], axis=1), rhs)

                def top_step(kb, m):
                    return jnp.maximum(m, jnp.max(scores(kb)[1], axis=0, keepdims=True))

                blocks = rows // KB
                m = lax.fori_loop(0, blocks, top_step, jnp.full((1, 2 * QB), 2 * NEG, F32))

                def sum_step(kb, state):
                    ks, st = scores(kb)
                    w = jnp.exp(st - m)
                    return state[0] + jnp.sum(w, axis=0, keepdims=True), state[1] + mm(vt[cols, ks], w.astype(BF))

                start = (jnp.zeros((1, 2 * QB), F32), jnp.zeros((128, 2 * QB), F32))
                l, full = lax.fori_loop(0, blocks, sum_step, start)
                tops[2 * p : 2 * p + 1, qs] = m[:, 0:QB]
                tops[2 * p + 1 : 2 * p + 2, qs] = m[:, QB:]
                keep(qs, p, l, full)
            return carry

        lax.fori_loop(0, rows // QB, q_again, 0)

    for h in range(heads):
        l = lse_ref[0, 0, h : h + 1, :]
        hs = slice(64 * h, 64 * h + 64)
        ot_ref[0, hs, :] = ot_ref[0, hs, :] * (1.0 / l)
        lse_ref[0, 0, h : h + 1, :] = tops[h : h + 1, :] + jnp.log(l)
    o_ref[...] = ot_ref[0].astype(BF).T


def attn_bwd_kernel(
    lo, hi, q_ref, k_ref, v_ref, do_ref, ot_ref, lse_ref, oh_ref, mr_ref, dqkv_ref,
    qt, kt, dot, extra_q, extra_d, dqt, dkt, dvt,
):
    seq = pl.program_id(0)
    rows = q_ref.shape[0]
    pairs = q_ref.shape[1] // 128
    qt[...] = (q_ref[...] * 0.125).astype(BF).T
    kt[...] = k_ref[...].T
    dot[...] = do_ref[...].T
    for h in range(2 * pairs):
        r = slice(64 * h, 64 * h + 64)
        delta = jnp.sum(dot[r, :].astype(F32) * ot_ref[0, r, :], axis=0, keepdims=True)
        lse = lse_ref[0, 0, h : h + 1, :]
        extra_q[h, :, :] = jnp.concatenate([mr_ref[0], terms(three_parts(-lse))], axis=0).astype(BF)
        tail = terms(three_parts(-delta))
        extra_d[h, :, :] = jnp.concatenate([jnp.zeros_like(tail), tail], axis=0).astype(BF)
    dkt[...] = jnp.zeros_like(dkt)
    dvt[...] = jnp.zeros_like(dvt)

    def q_step(qb, carry):
        qs = pl.ds(pl.multiple_of(qb * QB, QB), QB)

        def run(k0, size):
            ks = pl.ds(k0, size)
            oh = oh_ref[ks, :]
            for p in range(pairs):
                a = 128 * p
                cols = slice(a, a + 128)
                qm, qx = pair_rhs(qt, extra_q, p, qs)
                dom, dx = pair_rhs(dot, extra_d, p, qs)
                w = jnp.exp(mm(jnp.concatenate([k_ref[ks, cols], oh], axis=1), qx))
                ds = (w * mm(jnp.concatenate([v_ref[ks, cols], oh], axis=1), dx)).astype(BF)
                dvt[cols, ks] += mm_nt(dom, w.astype(BF))
                dkt[cols, ks] += mm_nt(qm, ds)
                dq = mm(kt[cols, ks], ds)
                dqt[a : a + 64, qs] = dq[0:64, 0:QB]
                dqt[a + 64 : a + 128, qs] = dq[64:128, QB:]

        by_span(lo[seq, qb], hi[seq, qb], rows, run)
        return carry

    lax.fori_loop(0, rows // QB, q_step, 0)
    wide = dqt.shape[0]
    dqkv_ref[:, 0:wide] = (dqt[...] * 0.125).astype(BF).T
    dqkv_ref[:, wide : 2 * wide] = dkt[...].astype(BF).T
    dqkv_ref[:, 2 * wide :] = dvt[...].astype(BF).T


WIDE = 384
TILE = 512
VMEM_LIMIT = 60 * 1024 * 1024


def params(*semantics):
    return pltpu.CompilerParams(dimension_semantics=semantics or None, vmem_limit_bytes=VMEM_LIMIT)


def cost(flops, data):
    return pl.CostEstimate(flops=int(flops), bytes_accessed=int(data), transcendentals=0)


def whole(shape):
    zero = (0,) * len(shape)
    return pl.BlockSpec(shape, lambda *_: zero)


ANYWHERE = pl.BlockSpec(memory_space=pl.ANY)


def attention_tables(segs):
    order = jnp.where(segs == 0, 1 << 20, segs)
    seqs, length = segs.shape
    first = order[:, ::QB]
    last = order[:, QB - 1 :: QB]
    lo = jnp.sum((order[:, None, :] < first[:, :, None]).astype(jnp.int32), axis=2) // KB
    hi = (jnp.sum((order[:, None, :] <= last[:, :, None]).astype(jnp.int32), axis=2) + KB - 1) // KB
    ids = jnp.arange(128, dtype=jnp.int32)[None, :]
    onehot = (segs.reshape(-1)[:, None] == ids) | ((ids >= 8) & (ids < 16))
    differ = segs[:, None, :] != jnp.arange(8, dtype=jnp.int32)[None, :, None]
    return lo, hi, onehot.astype(BF), jnp.where(differ, NEG, 0.0)


def attention_fwd(qkv, lo, hi, onehot, miss):
    seqs = lo.shape[0]
    rows = qkv.shape[0] // seqs
    wide = WIDE
    width = qkv.shape[1] // 3
    parts = width // wide
    col = lambda at: pl.BlockSpec((rows, wide), lambda s, j, *_: (s, 3 * j + at))
    return pl.pallas_call(
        attn_fwd_kernel,
        grid_spec=pltpu.PrefetchScalarGridSpec(
            num_scalar_prefetch=2,
            grid=(seqs, parts),
            in_specs=[
                col(0), col(1), col(2),
                pl.BlockSpec((rows, 128), lambda s, *_: (s, 0)),
                pl.BlockSpec((1, 8, rows), lambda s, *_: (s, 0, 0)),
            ],
            out_specs=[
                pl.BlockSpec((rows, wide), lambda s, j, *_: (s, j)),
                pl.BlockSpec((1, wide, rows), lambda s, j, *_: (s, j, 0)),
                pl.BlockSpec((1, 1, wide // HD, rows), lambda s, j, *_: (s, j, 0, 0)),
            ],
            scratch_shapes=[
                pltpu.VMEM((wide, rows), BF),
                pltpu.VMEM((wide, rows), BF),
                pltpu.VMEM((wide // HD, 16, rows), BF),
                pltpu.VMEM((8, rows), F32),
            ],
        ),
        out_shape=[
            jax.ShapeDtypeStruct((qkv.shape[0], width), BF),
            jax.ShapeDtypeStruct((seqs, width, rows), F32),
            jax.ShapeDtypeStruct((seqs, parts, wide // HD, rows), F32),
        ],
        compiler_params=params("arbitrary", "arbitrary"),
        cost_estimate=cost(24e9, 2e7),
        name="attention_forward",
    )(lo, hi, qkv, qkv, qkv, onehot, miss)


def attention_bwd(qkv, d_attn, ot, lse, lo, hi, onehot, miss):
    seqs = lo.shape[0]
    rows = qkv.shape[0] // seqs
    wide = WIDE
    col = lambda at: pl.BlockSpec((rows, wide), lambda s, j, *_: (s, 3 * j + at))
    return pl.pallas_call(
        attn_bwd_kernel,
        grid_spec=pltpu.PrefetchScalarGridSpec(
            num_scalar_prefetch=2,
            grid=(seqs, d_attn.shape[1] // wide),
            in_specs=[
                col(0), col(1), col(2),
                pl.BlockSpec((rows, wide), lambda s, j, *_: (s, j)),
                pl.BlockSpec((1, wide, rows), lambda s, j, *_: (s, j, 0)),
                pl.BlockSpec((1, 1, wide // HD, rows), lambda s, j, *_: (s, j, 0, 0)),
                pl.BlockSpec((rows, 128), lambda s, *_: (s, 0)),
                pl.BlockSpec((1, 8, rows), lambda s, *_: (s, 0, 0)),
            ],
            out_specs=pl.BlockSpec((rows, 3 * wide), lambda s, j, *_: (s, j)),
            scratch_shapes=[
                pltpu.VMEM((wide, rows), BF),
                pltpu.VMEM((wide, rows), BF),
                pltpu.VMEM((wide, rows), BF),
                pltpu.VMEM((wide // HD, 16, rows), BF),
                pltpu.VMEM((wide // HD, 16, rows), BF),
                pltpu.VMEM((wide, rows), F32),
                pltpu.VMEM((wide, rows), F32),
                pltpu.VMEM((wide, rows), F32),
            ],
        ),
        out_shape=jax.ShapeDtypeStruct(qkv.shape, BF),
        compiler_params=params("arbitrary", "arbitrary"),
        cost_estimate=cost(44e9, 4e7),
        name="attention_backward",
    )(lo, hi, qkv, qkv, qkv, d_attn, ot, lse, onehot, miss)


def normalized(x):
    mean = jnp.mean(x, axis=-1, keepdims=True)
    centered = x - mean
    scale = lax.rsqrt(jnp.mean(centered * centered, axis=-1, keepdims=True) + EPSILON)
    return centered * scale, scale


def norm_back(d, xhat, scale, gain):
    e = d * gain
    return scale * (e - jnp.mean(e, axis=-1, keepdims=True) - xhat * jnp.mean(e * xhat, axis=-1, keepdims=True))


def clear_first(*refs):
    @pl.when(pl.program_id(0) == 0)
    def _():
        for ref in refs:
            ref[...] = jnp.zeros_like(ref)


def add_row(ref, row, values):
    ref[row : row + 1, 0 : values.shape[1]] += jnp.sum(values, axis=0, keepdims=True)


def fetch(chunks, spots, outs, sems):
    for h in range(2):
        for chip in range(chunks.shape[1]):
            for row, count, which, target in spots(h, chip):
                pltpu.make_async_copy(
                    chunks.at[h, chip, pl.ds(row, count), :], outs[which].at[target], sems.at[which]
                ).start()


def fetched(out, sem):
    pltpu.make_async_copy(out, out, sem).wait()


GAIN1, SHIFT1, BIAS_Q, BIAS_V, BIAS_OUT, GAIN2, SHIFT2, BIAS_DOWN = range(8)
STRIP = 768
CURVE = 0.7978845608028654
CUBIC = 0.044715


def middle_kernel(
    spots, attn, tok, cot, vec, b1, chunks2, chunks3,
    out, n2, act, d_pre, d_mid, d_branch, d_attn, sums, sum_up, wo, w1, w2, sem,
):
    @pl.when(pl.program_id(0) == 0)
    def _():
        fetch(chunks2, spots[0], [wo, w1], sem)
        fetch(chunks3, spots[1], [w2], sem.at[pl.ds(2, 1)])
        for ref in (sums, sum_up):
            ref[...] = jnp.zeros_like(ref)
        for k, ref in enumerate((wo, w1, w2)):
            fetched(ref, sem.at[k])

    x = tok[...].astype(F32) + mm(attn[...], wo[...]) + vec[BIAS_OUT : BIAS_OUT + 1]
    xhat, scale = normalized(x)
    n = (xhat * vec[GAIN2 : GAIN2 + 1] + vec[SHIFT2 : SHIFT2 + 1]).astype(BF)
    n2[...] = n
    d_out = cot[...]
    y = x + vec[BIAS_DOWN : BIAS_DOWN + 1]
    d_n2 = None
    for j in range(w1.shape[1] // STRIP):
        cols = slice(j * STRIP, (j + 1) * STRIP)
        u = mm(n, w1[:, cols]) + b1[:, cols]
        d_act = mm_nt(d_out, w2[cols, :])
        square = u * u
        th = jnp.tanh(u * (CURVE + (CURVE * CUBIC) * square))
        half = 0.5 * u
        hidden = (half + half * th).astype(BF)
        act[:, cols] = hidden
        y = y + mm(hidden, w2[cols, :])
        slope = (0.5 + 0.5 * th) + half * (1.0 - th * th) * (CURVE + (3.0 * CURVE * CUBIC) * square)
        low = (d_act * slope).astype(BF)
        d_pre[:, cols] = low
        sum_up[:, cols] += jnp.sum(low.astype(F32), axis=0, keepdims=True)
        part = mm_nt(low, w1[:, cols])
        d_n2 = part if d_n2 is None else d_n2 + part
    out[...] = y.astype(BF)
    add_row(sums, 0, d_n2 * xhat)
    add_row(sums, 1, d_n2)
    g = d_out.astype(F32)
    add_row(sums, 3, g)
    d = g + norm_back(d_n2, xhat, scale, vec[GAIN2 : GAIN2 + 1])
    d_mid[...] = d
    low = d.astype(BF)
    d_branch[...] = low
    add_row(sums, 2, low.astype(F32))
    d_attn[...] = mm_nt(low, wo[...]).astype(BF)


def middle_part(attn, tokens, cotangent, vec, b1, gathered, spots):
    count, width = tokens.shape
    hidden = b1.shape[1]
    rows = TILE // 2
    tile = lambda w: pl.BlockSpec((rows, w), lambda i: (i, 0))
    row = lambda w, kind: jax.ShapeDtypeStruct((count, w), kind)
    return pl.pallas_call(
        functools.partial(middle_kernel, spots),
        grid=(count // rows,),
        in_specs=[tile(width), tile(width), tile(width), whole(vec.shape), whole(b1.shape)] + [ANYWHERE] * 2,
        out_specs=[
            tile(width), tile(width), tile(hidden), tile(hidden), tile(width), tile(width), tile(width),
            whole((8, width)), whole((1, hidden)),
        ],
        scratch_shapes=[
            pltpu.VMEM((width, width), BF),
            pltpu.VMEM((width, hidden), BF),
            pltpu.VMEM((hidden, width), BF),
            pltpu.SemaphoreType.DMA((3,)),
        ],
        out_shape=[
            row(width, BF), row(width, BF), row(hidden, BF), row(hidden, BF), row(width, F32), row(width, BF),
            row(width, BF), jax.ShapeDtypeStruct((8, width), F32), jax.ShapeDtypeStruct((1, hidden), F32),
        ],
        compiler_params=params("arbitrary"),
        cost_estimate=cost(4 * count * width * (width + 2 * hidden), 6e7),
        name="middle",
    )(attn, tokens, cotangent, vec, b1, *gathered)


def first_norm_kernel(d_qkv, w, tok, d_mid, vec, out, sums):
    clear_first(sums)
    d = mm_nt(d_qkv[...], w[...])
    xhat, scale = normalized(tok[...].astype(F32))
    add_row(sums, 0, d * xhat)
    add_row(sums, 1, d)
    add_row(sums, 2, d_qkv[...].astype(F32))
    out[...] = (d_mid[...] + norm_back(d, xhat, scale, vec[0:1])).astype(BF)


def first_norm_back(d_qkv, w, tokens, d_mid, vec):
    count, width = tokens.shape
    cols = d_qkv.shape[1]
    tile = lambda w: pl.BlockSpec((TILE, w), lambda i: (i, 0))
    return pl.pallas_call(
        first_norm_kernel,
        grid=(count // TILE,),
        in_specs=[tile(cols), whole(w.shape), tile(width), tile(width), whole(vec.shape)],
        out_specs=[tile(width), whole((8, cols))],
        out_shape=[jax.ShapeDtypeStruct((count, width), BF), jax.ShapeDtypeStruct((8, cols), F32)],
        compiler_params=params("arbitrary"),
        cost_estimate=cost(2 * count * width * cols, 3e7),
        name="first_norm_back",
    )(d_qkv, w, tokens, d_mid, vec)


def tn(a, b):
    return lax.dot_general(a, b, (((0,), (0,)), ((), ())), preferred_element_type=F32)


def neighbours():
    me = lax.axis_index("fsdp")
    core = lax.rem(me, 2)
    x = lax.rem(me // 2, 2)
    y = lax.rem(me // 4, 2)
    along_y = 4 * (1 - 2 * y)
    along_x = 2 * (1 - 2 * x)
    first = (1 - core) * along_y + core * along_x
    second = along_y + along_x - first
    return me, core, me // 8, first, second


def greet(others):
    barrier = pltpu.get_barrier_semaphore()
    for other in others:
        pl.semaphore_signal(barrier, inc=1, device_id=(other,), device_id_type=pl.DeviceIdType.MESH)
    pl.semaphore_wait(barrier, len(others))


def gathered_vectors(rows, vecs, wide):
    width = vecs.shape[1]
    devices = rows.shape[0] // 8
    part = width // devices
    source = lax.broadcasted_iota(jnp.int32, (WIDE, width), 0)
    owner = lax.broadcasted_iota(jnp.int32, (rows.shape[0], width), 0)

    def spread(first, size, lane):
        lanes = lane * width + lax.broadcasted_iota(jnp.int32, (1, width), 1)
        device = lanes // size
        pick = (source == first + lanes - device * size).astype(F32).astype(BF)
        return jnp.sum(jnp.where(owner == 8 * device, mm(rows, pick), 0.0), axis=0, keepdims=True)

    for v in range(8):
        vecs[v : v + 1, :] = spread(v * part, part, 0)
    for b in range(4):
        wide[:, b * width : (b + 1) * width] = spread(8 * part, 4 * part, b)


def gather_kernel(blocks, depth, spots, *refs):
    flows = len(blocks)
    owns, oths, tok_in, refs = refs[:flows], refs[flows : 2 * flows], refs[2 * flows], refs[2 * flows + 1 :]
    outs, (n1_out, qkv_out, w_out, vecs, wide), refs = refs[:flows], refs[flows : flows + 5], refs[flows + 5 :]
    (tok, w, rows, n1, qkv, load_sem, rows_sem, w_sem, put_sem), sems = refs[:9], refs[9:]
    tok_load = pltpu.make_async_copy(tok_in, tok, load_sem.at[0])
    tok_load.start()
    me, core, z, first, second = neighbours()
    twin = me + 1 - 2 * core
    chip = me // 2
    deep = [chip * 2 + core] + [lax.rem(z + k, depth) * 8 + lax.rem(me, 8) for k in range(1, depth)]
    greet([twin, me + first, me + second] + deep[1:])
    mine = [lax.rem(z + depth - k, depth) * 4 + lax.rem(chip, 4) for k in range(depth)]
    theirs = [at + first // 2 for at in mine]
    last = [at + second // 2 for at in mine + theirs]

    def send(f, at, send_sem, recv_sem, device):
        pltpu.make_async_remote_copy(
            src_ref=outs[f].at[core, at],
            dst_ref=outs[f].at[core, at],
            send_sem=send_sem,
            recv_sem=recv_sem,
            device_id=(device,),
            device_id_type=pl.DeviceIdType.MESH,
        ).start()

    def arrived(ref, sem):
        pltpu.make_async_copy(ref, ref, sem).wait()

    def onward(f, k, at, steps):
        far, near, cross, seen, local, out, twin_out, twin_in, pair_out, pair_in = sems[10 * f : 10 * f + 10]
        if steps == 2:
            send(f, at, out.at[0], near.at[k], me + first)
        if steps >= 1:
            send(f, at, out.at[0], cross.at[k if steps == 2 else depth + k], me + second)
        send(f, at, twin_out.at[0], twin_in.at[0], twin)

    for f in range(flows):
        pair_out, pair_in, local = sems[10 * f + 8], sems[10 * f + 9], sems[10 * f + 4]
        row = 0
        for size in blocks[f]:
            here_rows = pl.ds(pl.multiple_of(2 * row + core * size, 8), size)
            pltpu.make_async_copy(
                owns[f].at[pl.ds(row, size), :], outs[f].at[core, chip, here_rows, :], local.at[0]
            ).start()
            pltpu.make_async_remote_copy(
                src_ref=oths[f].at[pl.ds(row, size), :],
                dst_ref=outs[f].at[1 - core, chip, here_rows, :],
                send_sem=pair_out.at[0],
                recv_sem=pair_in.at[0],
                device_id=(twin,),
                device_id_type=pl.DeviceIdType.MESH,
            ).start()
            row += size
    for f in range(flows):
        far, out = sems[10 * f], sems[10 * f + 5]
        arrived(owns[f], sems[10 * f + 4].at[0])
        arrived(owns[f], sems[10 * f + 9].at[0])
        for k in range(1, depth):
            send(f, chip, out.at[0], far.at[k], deep[k])
        onward(f, 0, chip, 2)

    def from_far(f):
        for k in range(1, depth):
            arrived(outs[f].at[core, mine[k]], sems[10 * f].at[k])
            onward(f, k, mine[k], 2)

    def from_near(f):
        for k in range(depth):
            arrived(outs[f].at[core, theirs[k]], sems[10 * f + 1].at[k])
            onward(f, k, theirs[k], 1)

    def from_cross(f):
        for k in range(2 * depth):
            arrived(outs[f].at[core, last[k]], sems[10 * f + 2].at[k])
            onward(f, k, last[k], 0)

    def from_twin(f):
        arrived(outs[f].at[1 - core], sems[10 * f + 7].at[0])

    tile = n1.shape[1]
    tiles = tok.shape[0] // tile

    def put(i):
        slot, span = lax.rem(i, 2), pl.ds(pl.multiple_of(i * tile, tile), tile)
        return (
            pltpu.make_async_copy(n1.at[slot], n1_out.at[span, :], put_sem.at[slot]),
            pltpu.make_async_copy(qkv.at[slot], qkv_out.at[span, :], put_sem.at[2 + slot]),
        )

    def project(i):
        @pl.when(i >= 2)
        def _():
            for copy in put(i - 2):
                copy.wait()

        slot = lax.rem(i, 2)
        x = tok[pl.ds(pl.multiple_of(i * tile, tile), tile), :].astype(F32)
        n = (normalized(x)[0] * vecs[GAIN1 : GAIN1 + 1, :] + vecs[SHIFT1 : SHIFT1 + 1, :]).astype(BF)
        n1[slot] = n
        bias = []
        for h in range(2):
            cols = slice(h * WIDE, (h + 1) * WIDE)
            q, v = vecs[BIAS_Q : BIAS_Q + 1, cols], vecs[BIAS_V : BIAS_V + 1, cols]
            bias += [q, jnp.zeros_like(q), v]
        qkv[slot] = (mm(n, w[...]) + jnp.concatenate(bias, axis=1)).astype(BF)
        for copy in put(i):
            copy.start()

    def several(first, last):
        def step(i, carry):
            project(i)
            return carry

        lax.fori_loop(first, last, step, 0)

    from_far(0)
    from_near(0)
    from_far(1)
    from_near(1)
    from_cross(0)
    from_twin(0)
    fetch(outs[0], spots, [w], w_sem)
    chips = outs[0].shape[1]
    first_row = outs[0].shape[2] - 16
    for at in range(chips):
        pltpu.make_async_copy(outs[0].at[0, at, pl.ds(first_row, 16), :], rows.at[pl.ds(16 * at, 16), :], rows_sem.at[0]).start()
    from_far(2)
    from_near(2)
    arrived(rows, rows_sem.at[0])
    gathered_vectors(rows[...], vecs, wide)
    tok_load.wait()
    fetched(w, w_sem.at[0])
    w_put = pltpu.make_async_copy(w, w_out, load_sem.at[1])
    w_put.start()
    several(0, tiles // 2)
    from_cross(1)
    several(tiles // 2, tiles)
    from_cross(2)
    for i in (tiles - 2, tiles - 1):
        for copy in put(jnp.int32(i)):
            copy.wait()
    w_put.wait()
    for f in range(flows):
        chips = outs[f].shape[1]
        if f > 0:
            from_twin(f)
        arrived(outs[f].at[0], sems[10 * f + 6].at[0])
        arrived(outs[f].at[0, pl.ds(0, chips - 1)], sems[10 * f + 5].at[0])
        arrived(oths[f], sems[10 * f + 8].at[0])


def gather_shards(owns, oths, blocks, tokens, spots, depth):
    chips = 4 * depth
    count, width = tokens.shape
    tile = TILE // 2
    outs = [jax.ShapeDtypeStruct((2, chips, 2 * o.shape[0], WIDE), BF) for o in owns]
    outs += [
        jax.ShapeDtypeStruct((count, width), BF),
        jax.ShapeDtypeStruct((count, 3 * width), BF),
        jax.ShapeDtypeStruct((width, 3 * width), BF),
        jax.ShapeDtypeStruct((8, width), F32),
        jax.ShapeDtypeStruct((1, 4 * width), F32),
    ]
    dma = lambda n: pltpu.SemaphoreType.DMA((n,))
    scratch = [
        pltpu.VMEM((count, width), BF),
        pltpu.VMEM((width, 3 * width), BF),
        pltpu.VMEM((16 * chips, WIDE), BF),
        pltpu.VMEM((2, tile, width), BF),
        pltpu.VMEM((2, tile, 3 * width), BF),
        dma(2), dma(1), dma(1), dma(4),
    ]
    for _ in owns:
        scratch += [dma(depth), dma(depth), dma(2 * depth)] + [dma(1)] * 7
    return pl.pallas_call(
        functools.partial(gather_kernel, blocks, depth, spots),
        in_specs=[ANYWHERE] * (2 * len(owns) + 1),
        out_specs=[ANYWHERE] * (len(owns) + 3) + [pl.BlockSpec(memory_space=pltpu.VMEM)] * 2,
        out_shape=outs,
        scratch_shapes=scratch,
        compiler_params=pltpu.CompilerParams(
            collective_id=0, has_side_effects=True, vmem_limit_bytes=VMEM_LIMIT
        ),
        cost_estimate=cost(6 * count * width * width, 3e7),
        name="gather_and_qkv",
    )(*owns, *oths, tokens)


def pack_kernel(core, *refs):
    (wqkv, small, wo, w1, w2), outs = refs[:5], refs[5:]
    width = wo.shape[1]
    for c in range(2):

        @pl.when(core[0] == c)
        def _(c=c):
            for h in range(2):
                first, second, third = outs[:3] if h == c else outs[3:]
                rows = wo.shape[0]
                for t in range(3):
                    first[rows * t : rows * (t + 1), :] = wqkv[:, t * width + h * WIDE : t * width + (h + 1) * WIDE].astype(BF)
                first[3 * rows :, :] = small[...].astype(BF)
                second[0:rows, :] = wo[:, h * WIDE : (h + 1) * WIDE].astype(BF)
                for b in range(4):
                    cols = slice((4 * h + b) * WIDE, (4 * h + b + 1) * WIDE)
                    second[rows * (1 + b) : rows * (2 + b), :] = w1[:, cols].astype(BF)
                third[...] = w2[:, h * WIDE : (h + 1) * WIDE].astype(BF)


def pack(wqkv, small, wo, w1, w2, core):
    rows = wo.shape[0]
    ins = (wqkv, small, wo, w1, w2)
    shapes = [(3 * rows + small.shape[0], WIDE), (5 * rows, WIDE), (w2.shape[0], WIDE)] * 2
    return pl.pallas_call(
        pack_kernel,
        grid_spec=pltpu.PrefetchScalarGridSpec(
            num_scalar_prefetch=1,
            grid=(1,),
            in_specs=[whole(x.shape) for x in ins],
            out_specs=[whole(s) for s in shapes],
        ),
        out_shape=[jax.ShapeDtypeStruct(s, BF) for s in shapes],
        name="pack_shards",
    )(core, *ins)


def scatter_kernel(depth, splits, *refs):
    flows = len(splits)
    small_in, act, cot, n2, d_pre, attn, d_branch, n1, d_qkv = refs[:9]
    outs, rest = refs[9 : 9 + flows], refs[9 + flows :]
    (down, up, out, thirds, held, slots, held_sem, slot_sem), rest = rest[:8], rest[8:]
    ins = [small_in, down, up, out, thirds]
    width = cot.shape[1]
    tall = act.shape[1] // width
    ends = (tall, 2 * tall, 2 * tall + 1, 2 * tall + 1 + d_qkv.shape[1] // width)
    me, core, z, first, second = neighbours()

    def held_copy(k):
        return pltpu.make_async_copy((cot, n2, attn, n1)[k], held.at[k % 2], held_sem.at[k % 2])

    def level(t):
        return lax.rem(z + 1 + t, depth)

    def fetch_task(t):
        slot = lax.rem(t, 2)
        start = 0
        for source, end in zip((act, d_pre, d_branch, d_qkv), ends):
            block = level(t) if source is act else t - start

            @pl.when((t >= start) & (t < end))
            def _(source=source, block=block):
                cols = pl.ds(pl.multiple_of(block * width, 128), width)
                pltpu.make_async_copy(source.at[:, cols], slots.at[slot], slot_sem.at[slot]).start()

            start = end

    for k in range(2):
        held_copy(k).start()
        fetch_task(jnp.int32(k))
    chip = me // 2
    x, y = lax.rem(chip, 2), lax.rem(chip // 2, 2)
    twin = me + 1 - 2 * core
    deep = [lax.rem(z + k, depth) * 8 + lax.rem(me, 8) for k in range(1, depth)]
    greet([twin, me + first, me + second] + deep)
    plane = 2 * depth
    chips = 2 * plane

    def chip_of(j, core):
        bit2, bit1 = x + core * (y - x), y + core * (x - y)
        keep, side, k = j // plane, lax.rem(j, plane) // depth, lax.rem(j, depth)
        bit2 = (1 - bit2) + keep * (2 * bit2 - 1)
        bit1 = (1 - bit1) + side * (2 * bit1 - 1)
        return lax.rem(z + 1 + k, depth) * 4 + bit1 * (2 - core) + bit2 * (1 + core)

    def remote(src, dst, send_sem, recv_sem, device):
        return pltpu.make_async_remote_copy(
            src_ref=src,
            dst_ref=dst,
            send_sem=send_sem,
            recv_sem=recv_sem,
            device_id=(device,),
            device_id_type=pl.DeviceIdType.MESH,
        )

    def arrived(ref, sem):
        pltpu.make_async_copy(ref, ref, sem).wait()

    def flow(f):
        return rest[8 * f : 8 * f + 8]

    def sems(f):
        return rest[8 * flows + 11 * f : 8 * flows + 11 * f + 11]

    def loop(count, body):
        def step(j, carry):
            body(j)
            return carry

        lax.fori_loop(0, count, step, 0)

    def begin(f, some=None):
        own, in0 = flow(f)[:2]
        load, got0, sent0 = sems(f)[0], sems(f)[1], sems(f)[6]

        def body(j):
            pltpu.make_async_copy(ins[f].at[core, chip_of(j, core)], own.at[j], load.at[j]).start()
            remote(ins[f].at[1 - core, chip_of(j, 1 - core)], in0.at[j], sent0.at[0], got0.at[j], twin).start()

        loop(chips, body) if some is None else [body(j) for j in some]

    def sum_of(f, j):
        own, in0 = flow(f)[:2]
        arrived(own.at[j], sems(f)[0].at[j])
        arrived(in0.at[j], sems(f)[1].at[j])
        return own[j].astype(F32) + in0[j].astype(F32)

    def lagging(count, compute, send):
        def body(j):
            compute(j)

            @pl.when(j > 0)
            def _():
                send(j - 1)

        loop(count, body)
        send(count - 1)

    def across(f):
        own, _, in1 = flow(f)[:3]
        got1, sent1 = sems(f)[2], sems(f)[7]

        def compute(j):
            own[j] = sum_of(f, j).astype(own.dtype)

        lagging(plane, compute, lambda j: remote(own.at[j], in1.at[j], sent1.at[0], got1.at[j], me + second).start())

    def kept(f, j):
        in1 = flow(f)[2]
        arrived(in1.at[j], sems(f)[2].at[j])
        return sum_of(f, plane + j) + in1[j].astype(F32)

    def along(f):
        own, in2 = flow(f)[0], flow(f)[3]
        got2, sent2 = sems(f)[3], sems(f)[8]

        def compute(k):
            own[plane + k] = kept(f, k).astype(own.dtype)

        lagging(
            depth, compute, lambda k: remote(own.at[plane + k], in2.at[k], sent2.at[0], got2.at[k], me + first).start()
        )

    def upward(f):
        own, in2, in3, total = flow(f)[0], flow(f)[3], flow(f)[4], flow(f)[5]
        got2, got3, sent3 = sems(f)[3], sems(f)[4], sems(f)[9]

        def value(k):
            arrived(in2.at[k], got2.at[k])
            return kept(f, depth + k) + in2[k].astype(F32)

        for k in range(depth - 1):
            own[plane + depth + k] = value(k).astype(own.dtype)
            if k > 0:
                remote(own.at[plane + depth + k - 1], in3.at[k - 1], sent3.at[0], got3.at[k - 1], deep[k - 1]).start()
        total[...] = value(depth - 1)
        k = depth - 2
        remote(own.at[plane + depth + k], in3.at[k], sent3.at[0], got3.at[k], deep[k]).start()

    def mine(f, ref, which):
        if splits[f] == "rows":
            half = ref.shape[1] // 2
            return ref.at[:, pl.ds(pl.multiple_of(which * half, 8), half), :]
        half = ref.shape[0] // 2
        return ref.at[pl.ds(which * half, half)]

    def finish(f):
        in3, total, theirs = flow(f)[4], flow(f)[5], flow(f)[6]
        for k in range(depth - 1):
            arrived(in3.at[k], sems(f)[4].at[k])
            total[...] += in3[k].astype(F32)
        if splits[f] is None:
            outs[f][...] = total[...]
        else:
            outs[f][core] = mine(f, total, core)[...]
            remote(mine(f, total, 1 - core), theirs, sems(f)[10].at[0], sems(f)[5].at[0], twin).start()

    def across_level(f, k):
        own, _, in1 = flow(f)[:3]
        got1, sent1 = sems(f)[2], sems(f)[7]
        for j in (k, depth + k):
            own[j] = sum_of(f, j).astype(own.dtype)
        for j in (k, depth + k):
            remote(own.at[j], in1.at[j], sent1.at[0], got1.at[j], me + second).start()

    def multiply(t):
        slot = lax.rem(t, 2)
        pltpu.make_async_copy(slots.at[slot], slots.at[slot], slot_sem.at[slot]).wait()

        @pl.when(t < tall)
        def _():
            low = tn(slots[slot], held[0]).astype(BF)
            count = chips // tall
            for h in range(2):
                part = low[:, h * WIDE : (h + 1) * WIDE].reshape((count,) + down.shape[2:])
                down[h, pl.ds(level(t) * count, count)] = part

        @pl.when(t >= tall)
        def _():
            k = jnp.where(t == ends[1], 0, 1)
            low = tn(held[k], slots[slot]).astype(BF)
            parts = [low[:, i * WIDE : (i + 1) * WIDE].reshape(chips, width // chips, WIDE) for i in range(2)]

            @pl.when(t < ends[1])
            def _():
                for i in range(2):
                    block = 2 * (t - tall) + i
                    up[block // tall, :, lax.rem(block, tall)] = parts[i]

            @pl.when(t == ends[1])
            def _():
                for i in range(2):
                    out[i, :, 0] = parts[i]

            @pl.when(t > ends[1])
            def _():
                for i in range(2):
                    block = 2 * (t - ends[2]) + i
                    thirds[block // 3, :, lax.rem(block, 3)] = parts[i]

        @pl.when(t + 2 < ends[3])
        def _():
            fetch_task(t + 2)

        for k, at in ((2, ends[0] - 1), (3, ends[1] - 1)):

            @pl.when(t == at)
            def _(k=k):
                held_copy(k).start()

    tiny, low, wide, side, last = range(flows)
    begin(tiny)
    for k in range(2):
        held_copy(k).wait()

    def task(t):
        for k, at in ((2, ends[1]), (3, ends[2])):

            @pl.when(t == at)
            def _(k=k):
                held_copy(k).wait()

        multiply(t)

        @pl.when((t >= 1) & (t <= depth))
        def _():
            begin(low, [t - 1 + q * depth for q in range(4)])

        @pl.when((t >= 2) & (t <= depth + 1))
        def _():
            across_level(low, t - 2)

        @pl.when(t == depth + 2)
        def _():
            across(tiny)

        @pl.when(t == ends[1])
        def _():
            begin(wide)
            along(low)

        @pl.when(t == ends[2])
        def _():
            begin(side)

        @pl.when(t == ends[2] + 1)
        def _():
            across(wide)

        @pl.when(t == ends[2] + 2)
        def _():
            across(side)

    loop(ends[3], task)
    upward(low)
    begin(last)
    along(wide)
    across(last)
    along(side)
    along(tiny)
    upward(wide)
    upward(side)
    upward(tiny)
    along(last)
    for f in range(flows - 1):
        finish(f)
    upward(last)
    finish(last)
    for f in range(flows):
        _, in0, in1, in2, in3, total, theirs, _ = flow(f)
        if splits[f] is not None:
            arrived(theirs, sems(f)[5].at[0])
            outs[f][1 - core] = theirs[...]
            arrived(theirs, sems(f)[10].at[0])
        for ref, sem in zip((in0, in1, in2, in3), sems(f)[6:10]):
            arrived(ref, sem.at[0])


def scatter_sums(small, down, up, out, qkv, depth):
    chips = 4 * depth
    tokens, width = down[1].shape
    rows = width // chips
    outs, buffers, signals = [], [], []
    dma = lambda n: pltpu.SemaphoreType.DMA((n,))
    shapes = [(2, chips, blocks, rows, WIDE) for blocks in (4, 4, 1, 3)]
    work = [pltpu.VMEM(x, BF) for x in shapes]
    work += [pltpu.VMEM((2, tokens, width), BF), pltpu.VMEM((2, tokens, width), BF), dma(2), dma(2)]
    kinds = [(small.shape[2:], small.dtype)] + [(x[2:], BF) for x in shapes]
    splits = (None, "blocks", "rows", "rows", "rows")
    for (chunk, kind), split in zip(kinds, splits):
        if split == "rows":
            part = (chunk[0], chunk[1] // 2) + chunk[2:]
        elif split == "blocks":
            part = (chunk[0] // 2,) + chunk[1:]
        else:
            part = chunk
        outs.append(jax.ShapeDtypeStruct(part if split is None else (2,) + part, F32))
        for count in (chips, chips, chips // 2, depth, depth - 1):
            buffers.append(pltpu.VMEM((count,) + chunk, kind))
        buffers += [pltpu.VMEM(chunk, F32), pltpu.VMEM(part, F32), dma(1)]
        signals += [dma(chips), dma(chips), dma(chips // 2), dma(depth), dma(depth - 1)] + [dma(1)] * 6
    return pl.pallas_call(
        functools.partial(scatter_kernel, depth, splits),
        in_specs=[ANYWHERE] * 9,
        out_specs=[pl.BlockSpec(memory_space=pltpu.VMEM)] * len(outs),
        out_shape=outs,
        scratch_shapes=work + buffers + signals,
        compiler_params=pltpu.CompilerParams(
            collective_id=1, has_side_effects=True, vmem_limit_bytes=63 * 1024 * 1024
        ),
        cost_estimate=cost(0, 3e7),
        name="scatter_sums",
    )(small, *down, *up, *out, *qkv)


def by_neighbours(devices, width, hidden, count):
    rows = width // devices
    fits = rows * devices == width and rows % 8 == 0 and devices % 8 == 0
    return fits and width == 2 * WIDE and hidden == 4 * width and count % TILE == 0


def weight_halves(w):
    rows = w.shape[0]
    return w.reshape(rows, 3, 2, WIDE).transpose(0, 2, 1, 3).reshape(rows, -1)


def local(
    tokens, segments, cotangent, ln1_gain, ln1_shift, w_qkv, bias_q, bias_v, w_out, bias_out,
    ln2_gain, ln2_shift, w_up, bias_up, w_down, bias_down, *, seq,
):
    masters = (
        ln1_gain, ln1_shift, w_qkv, bias_q, bias_v, w_out, bias_out,
        ln2_gain, ln2_shift, w_up, bias_up, w_down, bias_down,
    )
    count, width = tokens.shape
    tables = attention_tables(segments.reshape(-1, seq))
    run = by_chips if by_neighbours(lax.axis_size("fsdp"), width, w_up.shape[1], count) else by_collectives
    return run(tokens, cotangent, tables, masters)


def by_collectives(tokens, cotangent, tables, masters):
    def norm(x, gain, shift):
        return normalized(x)[0] * gain + shift

    width = tokens.shape[1]
    full = [lax.all_gather(m.astype(BF), "fsdp", axis=0, tiled=True) for m in masters]
    g1, c1, wqkv, bq, bv, wo, bo, g2, c2, w1, b1, w2, b2 = [p.astype(F32) if p.ndim == 1 else p for p in full]
    wqkv = weight_halves(wqkv)
    rows = tokens.astype(F32)
    n1 = norm(rows, g1, c1).astype(BF)
    bias = weight_halves(jnp.concatenate([bq, jnp.zeros_like(bq), bv])[None])
    qkv = (mm(n1, wqkv) + bias).astype(BF)
    attn, attn_t, lse = attention_fwd(qkv, *tables)
    middle = rows + mm(attn, wo) + bo
    n2 = norm(middle, g2, c2).astype(BF)
    act_value, gelu_pull = jax.vjp(functools.partial(jax.nn.gelu, approximate=True), mm(n2, w1) + b1)
    act = act_value.astype(BF)
    layer_out = (middle + mm(act, w2) + b2).astype(BF)
    d_out = cotangent.astype(F32)
    d_pre = gelu_pull(mm_nt(cotangent, w2))[0].astype(BF)
    _, pull = jax.vjp(norm, middle, g2, c2)
    d_mid, d_g2, d_c2 = pull(mm_nt(d_pre, w1))
    d_mid = d_out + d_mid
    d_branch = d_mid.astype(BF)
    d_attn = mm_nt(d_branch, wo).astype(BF)
    d_qkv = attention_bwd(qkv, d_attn, attn_t, lse, *tables)
    _, pull = jax.vjp(norm, rows, g1, c1)
    d_rows, d_g1, d_c1 = pull(mm_nt(d_qkv, wqkv))
    input_grad = (d_mid + d_rows).astype(BF)
    total = lambda x: jnp.sum(x.astype(F32), axis=0)
    by_part = lambda x: x.reshape(-1, 2, 3, WIDE).transpose(0, 2, 1, 3).reshape(x.shape)
    sums = by_part(total(d_qkv)[None])[0]
    grads = (
        d_g1, d_c1, by_part(tn(n1, d_qkv)), sums[:width], sums[2 * width :], tn(attn, d_branch), total(d_branch),
        d_g2, d_c2, tn(n2, d_pre), total(d_pre), tn(act, cotangent), total(d_out),
    )
    return (layer_out, input_grad) + tuple(
        lax.psum_scatter(g, "fsdp", scatter_dimension=0, tiled=True) for g in grads
    )


def by_chips(tokens, cotangent, tables, masters):
    devices = lax.axis_size("fsdp")
    chips = devices // 2
    depth = devices // 8
    count, width = tokens.shape
    ln1_gain, ln1_shift, w_qkv, bias_q, bias_v, w_out, bias_out, ln2_gain, ln2_shift, w_up, bias_up, w_down, bias_down = masters
    part = width // devices
    two = 2 * part
    hidden = w_up.shape[1]
    core = lax.rem(lax.axis_index("fsdp"), 2).astype(jnp.int32).reshape(1)

    small = jnp.concatenate([ln1_gain, ln1_shift, bias_q, bias_v, bias_out, ln2_gain, ln2_shift, bias_down, bias_up])
    small = jnp.pad(small[None], ((0, 7), (0, WIDE - small.shape[0])))
    own1, own2, own3, oth1, oth2, oth3 = pack(w_qkv, small, w_out, w_up, w_down, core)

    def spots_qkv(h, chip):
        return [
            (two * t, two, 0, (pl.ds(two * chip, two), pl.ds((3 * h + t) * WIDE, WIDE))) for t in range(3)
        ]

    def spots_up(h, chip):
        rows = pl.ds(two * chip, two)
        return [(0, two, 0, (rows, pl.ds(h * WIDE, WIDE)))] + [
            (two * (1 + b), two, 1, (rows, pl.ds((4 * h + b) * WIDE, WIDE))) for b in range(4)
        ]

    def spots_down(h, chip):
        return [(0, 4 * two, 0, (pl.ds(4 * two * chip, 4 * two), pl.ds(h * WIDE, WIDE)))]

    blocks = ([part] * 3 + [8], [part] * 5, [4 * part])
    _, chunks2, chunks3, n1, qkv, wqkv, vecs, b1 = gather_shards(
        (own1, own2, own3), (oth1, oth2, oth3), blocks, tokens, spots_qkv, depth
    )
    attn, attn_t, lse = attention_fwd(qkv, *tables)
    layer_out, n2, act, d_pre, d_mid, d_branch, d_attn, sums2, sum_up = middle_part(
        attn, tokens, cotangent, vecs, b1, (chunks2, chunks3), (spots_up, spots_down)
    )

    d_qkv = attention_bwd(qkv, d_attn, attn_t, lse, *tables)
    input_grad, sums1 = first_norm_back(d_qkv, wqkv, tokens, d_mid, vecs)
    by_half = sums1[2].reshape(2, 3, WIDE)
    vecs = [
        sums1[0, :width], sums1[1, :width], by_half[:, 0].reshape(-1), by_half[:, 2].reshape(-1),
        sums2[2], sums2[0], sums2[1], sums2[3],
    ]
    small = jnp.concatenate([v.reshape(devices, part) for v in vecs] + [sum_up.reshape(devices, 4 * part)], axis=1)
    small = small.reshape(chips, 2, 1, -1).swapaxes(0, 1)
    small = jnp.pad(small, ((0, 0), (0, 0), (0, 7), (0, WIDE - small.shape[3])))
    small, g_down, g_up, g_out, g_qkv = scatter_sums(
        small, (act, cotangent), (n2, d_pre), (attn, d_branch), (n1, d_qkv), depth
    )
    small = small[0]
    s = [small[i * part : (i + 1) * part] for i in range(8)]
    s_b1 = small[8 * part : 12 * part]
    g_up = g_up.transpose(2, 0, 1, 3).reshape(part, hidden)
    g_out = g_out[:, 0].transpose(1, 0, 2).reshape(part, width)
    g_down = g_down.reshape(2, 4 * part, WIDE).transpose(1, 0, 2).reshape(4 * part, width)
    g_qkv = g_qkv.transpose(2, 1, 0, 3).reshape(part, 3 * width)
    return (
        layer_out, input_grad, s[0], s[1], g_qkv, s[2], s[3], g_out, s[4], s[5], s[6], g_up, s_b1, g_down, s[7],
    )


MICRO = 2


def solution(mesh):
    line, table = P("fsdp"), P("fsdp", None)
    weights = (line, line, table, line, line, table, line, line, line, table, line, table, line)

    def step(tokens, *rest):
        seq = tokens.shape[0] // (mesh.shape["fsdp"] * MICRO)
        return jax.shard_map(
            functools.partial(local, seq=seq),
            mesh=mesh,
            in_specs=(table, line, table) + weights,
            out_specs=(table, table) + weights,
            check_vma=False,
        )(tokens, *rest)

    return step
```

```python
import functools
import jax
import jax.numpy as jnp
from jax import lax
from jax.experimental import pallas as pl
from jax.experimental.pallas import tpu as pltpu
from jax.sharding import PartitionSpec as P

HD = 64
QB = 128
KB = 128
NEG = -1000000000.0
BF = jnp.bfloat16
F32 = jnp.float32
EPSILON = 1e-06
NT = (((1,), (1,)), ((), ()))


def mm(a, b):
    return jnp.dot(a, b, preferred_element_type=F32)


def mm_nt(a, b):
    return lax.dot_general(a, b, NT, preferred_element_type=F32)


def pair_diag(top, bottom):
    zero = jnp.zeros_like(top)
    return jnp.concatenate(
        [jnp.concatenate([top, zero], axis=1), jnp.concatenate([zero, bottom], axis=1)], axis=0
    )


SPANS = (2, 3, 4, 5, 6, 8)


def by_span(lo, hi, rows, run):
    need = hi - lo
    below = 0
    for span in SPANS:
        if below * KB >= rows:
            break
        size = min(span * KB, rows)
        last = size == rows

        @pl.when((need > below) & (last | (need <= span)))
        def _(size=size):
            run(pl.multiple_of(jnp.minimum(lo * KB, rows - size), KB), size)

        below = span


def chunks(k0, size):
    return [(pl.multiple_of(k0 + c, KB), min(2 * KB, size - c)) for c in range(0, size, 2 * KB)]


def terms(pieces):
    width = pieces[0].shape[1]
    row = lax.broadcasted_iota(jnp.int32, (8, width), 0)
    tail = jnp.zeros((8, width), F32)
    for i, piece in enumerate(pieces):
        tail = jnp.where(row == i, piece, tail)
    return tail


def three_parts(x):
    first = x.astype(BF).astype(F32)
    rest = x - first
    second = rest.astype(BF).astype(F32)
    return first, second, rest - second


def pair_rhs(feat, extra, p, qs):
    a = 128 * p
    block = pair_diag(feat[a : a + 64, qs], feat[a + 64 : a + 128, qs])
    rows = jnp.concatenate([extra[2 * p, :, qs], extra[2 * p + 1, :, qs]], axis=1)
    return block, jnp.concatenate([block, rows, jnp.zeros((112, 2 * QB), BF)], axis=0)


def attn_fwd_kernel(
    lo, hi, q_ref, k_ref, v_ref, oh_ref, mr_ref, o_ref, ot_ref, lse_ref, qt, vt, extra, tops
):
    seq = pl.program_id(0)
    rows = q_ref.shape[0]
    pairs = q_ref.shape[1] // 128
    heads = 2 * pairs
    vt[...] = v_ref[...].T
    qt[...] = (q_ref[...] * 0.125).astype(BF).T
    lane = lax.broadcasted_iota(jnp.int32, (8, heads * HD), 1) // HD
    pick = (lane == lax.broadcasted_iota(jnp.int32, (8, heads * HD), 0)).astype(BF)
    square = k_ref[...].astype(F32)
    norms = mm_nt(pick, (square * square).astype(BF))
    bound = jnp.sqrt(jnp.max(norms, axis=1, keepdims=True)) * 1.01
    for h in range(heads):
        qh = qt[64 * h : 64 * h + 64, :].astype(F32)
        length = jnp.sqrt(jnp.sum(qh * qh, axis=0, keepdims=True)) * 1.01
        m = (length * bound[h : h + 1, :]).astype(BF).astype(F32)
        tops[h : h + 1, :] = m
        extra[h, :, :] = jnp.concatenate([mr_ref[0], terms([-m])], axis=0).astype(BF)

    def keep(qs, p, l, full):
        a = 128 * p
        ot_ref[0, a : a + 64, qs] = full[0:64, 0:QB]
        ot_ref[0, a + 64 : a + 128, qs] = full[64:128, QB:]
        lse_ref[0, 0, 2 * p : 2 * p + 1, qs] = l[:, 0:QB]
        lse_ref[0, 0, 2 * p + 1 : 2 * p + 2, qs] = l[:, QB:]

    def q_step(qb, carry):
        qs = pl.ds(pl.multiple_of(qb * QB, QB), QB)

        def run(k0, size):
            rhs = [pair_rhs(qt, extra, p, qs)[1] for p in range(pairs)]
            l = [jnp.zeros((1, 2 * QB), F32)] * pairs
            acc = [None] * pairs
            for c0, cs in chunks(k0, size):
                ks = pl.ds(c0, cs)
                oh = oh_ref[ks, :]
                for p in range(pairs):
                    cols = slice(128 * p, 128 * p + 128)
                    w = jnp.exp(mm(jnp.concatenate([k_ref[ks, cols], oh], axis=1), rhs[p]))
                    l[p] = l[p] + jnp.sum(w, axis=0, keepdims=True)
                    part = mm(vt[cols, ks], w.astype(BF))
                    acc[p] = part if acc[p] is None else acc[p] + part
            for p in range(pairs):
                keep(qs, p, l[p], acc[p])

        by_span(lo[seq, qb], hi[seq, qb], rows, run)
        return carry

    lax.fori_loop(0, rows // QB, q_step, 0)

    @pl.when(jnp.min(lse_ref[0, 0]) < 1e-20)
    def _():
        for h in range(heads):
            extra[h, :, :] = jnp.concatenate([mr_ref[0], jnp.zeros_like(mr_ref[0])], axis=0).astype(BF)

        def q_again(qb, carry):
            qs = pl.ds(pl.multiple_of(qb * QB, QB), QB)
            for p in range(pairs):
                cols = slice(128 * p, 128 * p + 128)
                rhs = pair_rhs(qt, extra, p, qs)[1]

                def scores(kb):
                    ks = pl.ds(pl.multiple_of(kb * KB, KB), KB)
                    return ks, mm(jnp.concatenate([k_ref[ks, cols], oh_ref[ks, :]], axis=1), rhs)

                def top_step(kb, m):
                    return jnp.maximum(m, jnp.max(scores(kb)[1], axis=0, keepdims=True))

                blocks = rows // KB
                m = lax.fori_loop(0, blocks, top_step, jnp.full((1, 2 * QB), 2 * NEG, F32))

                def sum_step(kb, state):
                    ks, st = scores(kb)
                    w = jnp.exp(st - m)
                    return state[0] + jnp.sum(w, axis=0, keepdims=True), state[1] + mm(vt[cols, ks], w.astype(BF))

                start = (jnp.zeros((1, 2 * QB), F32), jnp.zeros((128, 2 * QB), F32))
                l, full = lax.fori_loop(0, blocks, sum_step, start)
                tops[2 * p : 2 * p + 1, qs] = m[:, 0:QB]
                tops[2 * p + 1 : 2 * p + 2, qs] = m[:, QB:]
                keep(qs, p, l, full)
            return carry

        lax.fori_loop(0, rows // QB, q_again, 0)

    for h in range(heads):
        l = lse_ref[0, 0, h : h + 1, :]
        hs = slice(64 * h, 64 * h + 64)
        ot_ref[0, hs, :] = ot_ref[0, hs, :] * (1.0 / l)
        lse_ref[0, 0, h : h + 1, :] = tops[h : h + 1, :] + jnp.log(l)
    o_ref[...] = ot_ref[0].astype(BF).T


def attn_bwd_kernel(
    lo, hi, q_ref, k_ref, v_ref, do_ref, ot_ref, lse_ref, oh_ref, mr_ref, dqkv_ref,
    qt, kt, dot, extra_q, extra_d, dqt, dkt, dvt,
):
    seq = pl.program_id(0)
    rows = q_ref.shape[0]
    pairs = q_ref.shape[1] // 128
    qt[...] = (q_ref[...] * 0.125).astype(BF).T
    kt[...] = k_ref[...].T
    dot[...] = do_ref[...].T
    for h in range(2 * pairs):
        r = slice(64 * h, 64 * h + 64)
        delta = jnp.sum(dot[r, :].astype(F32) * ot_ref[0, r, :], axis=0, keepdims=True)
        lse = lse_ref[0, 0, h : h + 1, :]
        extra_q[h, :, :] = jnp.concatenate([mr_ref[0], terms(three_parts(-lse))], axis=0).astype(BF)
        tail = terms(three_parts(-delta))
        extra_d[h, :, :] = jnp.concatenate([jnp.zeros_like(tail), tail], axis=0).astype(BF)
    dkt[...] = jnp.zeros_like(dkt)
    dvt[...] = jnp.zeros_like(dvt)

    def q_step(qb, carry):
        qs = pl.ds(pl.multiple_of(qb * QB, QB), QB)

        def run(k0, size):
            ks = pl.ds(k0, size)
            oh = oh_ref[ks, :]
            for p in range(pairs):
                a = 128 * p
                cols = slice(a, a + 128)
                qm, qx = pair_rhs(qt, extra_q, p, qs)
                dom, dx = pair_rhs(dot, extra_d, p, qs)
                w = jnp.exp(mm(jnp.concatenate([k_ref[ks, cols], oh], axis=1), qx))
                ds = (w * mm(jnp.concatenate([v_ref[ks, cols], oh], axis=1), dx)).astype(BF)
                dvt[cols, ks] += mm_nt(dom, w.astype(BF))
                dkt[cols, ks] += mm_nt(qm, ds)
                dq = mm(kt[cols, ks], ds)
                dqt[a : a + 64, qs] = dq[0:64, 0:QB]
                dqt[a + 64 : a + 128, qs] = dq[64:128, QB:]

        by_span(lo[seq, qb], hi[seq, qb], rows, run)
        return carry

    lax.fori_loop(0, rows // QB, q_step, 0)
    wide = dqt.shape[0]
    dqkv_ref[:, 0:wide] = (dqt[...] * 0.125).astype(BF).T
    dqkv_ref[:, wide : 2 * wide] = dkt[...].astype(BF).T
    dqkv_ref[:, 2 * wide :] = dvt[...].astype(BF).T


WIDE = 384
TILE = 512
VMEM_LIMIT = 60 * 1024 * 1024


def params(*semantics):
    return pltpu.CompilerParams(dimension_semantics=semantics or None, vmem_limit_bytes=VMEM_LIMIT)


def cost(flops, data):
    return pl.CostEstimate(flops=int(flops), bytes_accessed=int(data), transcendentals=0)


def whole(shape):
    zero = (0,) * len(shape)
    return pl.BlockSpec(shape, lambda *_: zero)


ANYWHERE = pl.BlockSpec(memory_space=pl.ANY)


def attention_tables(segs):
    order = jnp.where(segs == 0, 1 << 20, segs)
    seqs, length = segs.shape
    first = order[:, ::QB]
    last = order[:, QB - 1 :: QB]
    lo = jnp.sum((order[:, None, :] < first[:, :, None]).astype(jnp.int32), axis=2) // KB
    hi = (jnp.sum((order[:, None, :] <= last[:, :, None]).astype(jnp.int32), axis=2) + KB - 1) // KB
    ids = jnp.arange(128, dtype=jnp.int32)[None, :]
    onehot = (segs.reshape(-1)[:, None] == ids) | ((ids >= 8) & (ids < 16))
    differ = segs[:, None, :] != jnp.arange(8, dtype=jnp.int32)[None, :, None]
    return lo, hi, onehot.astype(BF), jnp.where(differ, NEG, 0.0)


def attention_fwd(qkv, lo, hi, onehot, miss):
    seqs = lo.shape[0]
    rows = qkv.shape[0] // seqs
    wide = WIDE
    width = qkv.shape[1] // 3
    parts = width // wide
    col = lambda at: pl.BlockSpec((rows, wide), lambda s, j, *_: (s, 3 * j + at))
    return pl.pallas_call(
        attn_fwd_kernel,
        grid_spec=pltpu.PrefetchScalarGridSpec(
            num_scalar_prefetch=2,
            grid=(seqs, parts),
            in_specs=[
                col(0), col(1), col(2),
                pl.BlockSpec((rows, 128), lambda s, *_: (s, 0)),
                pl.BlockSpec((1, 8, rows), lambda s, *_: (s, 0, 0)),
            ],
            out_specs=[
                pl.BlockSpec((rows, wide), lambda s, j, *_: (s, j)),
                pl.BlockSpec((1, wide, rows), lambda s, j, *_: (s, j, 0)),
                pl.BlockSpec((1, 1, wide // HD, rows), lambda s, j, *_: (s, j, 0, 0)),
            ],
            scratch_shapes=[
                pltpu.VMEM((wide, rows), BF),
                pltpu.VMEM((wide, rows), BF),
                pltpu.VMEM((wide // HD, 16, rows), BF),
                pltpu.VMEM((8, rows), F32),
            ],
        ),
        out_shape=[
            jax.ShapeDtypeStruct((qkv.shape[0], width), BF),
            jax.ShapeDtypeStruct((seqs, width, rows), F32),
            jax.ShapeDtypeStruct((seqs, parts, wide // HD, rows), F32),
        ],
        compiler_params=params("arbitrary", "arbitrary"),
        cost_estimate=cost(24e9, 2e7),
        name="attention_forward",
    )(lo, hi, qkv, qkv, qkv, onehot, miss)


def attention_bwd(qkv, d_attn, ot, lse, lo, hi, onehot, miss):
    seqs = lo.shape[0]
    rows = qkv.shape[0] // seqs
    wide = WIDE
    col = lambda at: pl.BlockSpec((rows, wide), lambda s, j, *_: (s, 3 * j + at))
    return pl.pallas_call(
        attn_bwd_kernel,
        grid_spec=pltpu.PrefetchScalarGridSpec(
            num_scalar_prefetch=2,
            grid=(seqs, d_attn.shape[1] // wide),
            in_specs=[
                col(0), col(1), col(2),
                pl.BlockSpec((rows, wide), lambda s, j, *_: (s, j)),
                pl.BlockSpec((1, wide, rows), lambda s, j, *_: (s, j, 0)),
                pl.BlockSpec((1, 1, wide // HD, rows), lambda s, j, *_: (s, j, 0, 0)),
                pl.BlockSpec((rows, 128), lambda s, *_: (s, 0)),
                pl.BlockSpec((1, 8, rows), lambda s, *_: (s, 0, 0)),
            ],
            out_specs=pl.BlockSpec((rows, 3 * wide), lambda s, j, *_: (s, j)),
            scratch_shapes=[
                pltpu.VMEM((wide, rows), BF),
                pltpu.VMEM((wide, rows), BF),
                pltpu.VMEM((wide, rows), BF),
                pltpu.VMEM((wide // HD, 16, rows), BF),
                pltpu.VMEM((wide // HD, 16, rows), BF),
                pltpu.VMEM((wide, rows), F32),
                pltpu.VMEM((wide, rows), F32),
                pltpu.VMEM((wide, rows), F32),
            ],
        ),
        out_shape=jax.ShapeDtypeStruct(qkv.shape, BF),
        compiler_params=params("arbitrary", "arbitrary"),
        cost_estimate=cost(44e9, 4e7),
        name="attention_backward",
    )(lo, hi, qkv, qkv, qkv, d_attn, ot, lse, onehot, miss)


def normalized(x):
    mean = jnp.mean(x, axis=-1, keepdims=True)
    centered = x - mean
    scale = lax.rsqrt(jnp.mean(centered * centered, axis=-1, keepdims=True) + EPSILON)
    return centered * scale, scale


def norm_back(d, xhat, scale, gain):
    e = d * gain
    return scale * (e - jnp.mean(e, axis=-1, keepdims=True) - xhat * jnp.mean(e * xhat, axis=-1, keepdims=True))


def clear_first(*refs):
    @pl.when(pl.program_id(0) == 0)
    def _():
        for ref in refs:
            ref[...] = jnp.zeros_like(ref)


def add_row(ref, row, values):
    ref[row : row + 1, 0 : values.shape[1]] += jnp.sum(values, axis=0, keepdims=True)


def fetch(chunks, spots, outs, sems):
    for h in range(2):
        for chip in range(chunks.shape[1]):
            for row, count, which, target in spots(h, chip):
                pltpu.make_async_copy(
                    chunks.at[h, chip, pl.ds(row, count), :], outs[which].at[target], sems.at[which]
                ).start()


def fetched(out, sem):
    pltpu.make_async_copy(out, out, sem).wait()


GAIN1, SHIFT1, BIAS_Q, BIAS_V, BIAS_OUT, GAIN2, SHIFT2, BIAS_DOWN = range(8)
STRIP = 768
CURVE = 0.7978845608028654
CUBIC = 0.044715


def middle_kernel(
    spots, attn, tok, cot, vec, b1, chunks2, chunks3,
    out, n2, act, d_pre, d_mid, d_branch, d_attn, sums, sum_up, wo, w1, w2, sem,
):
    @pl.when(pl.program_id(0) == 0)
    def _():
        fetch(chunks2, spots[0], [wo, w1], sem)
        fetch(chunks3, spots[1], [w2], sem.at[pl.ds(2, 1)])
        for ref in (sums, sum_up):
            ref[...] = jnp.zeros_like(ref)
        for k, ref in enumerate((wo, w1, w2)):
            fetched(ref, sem.at[k])

    x = tok[...].astype(F32) + mm(attn[...], wo[...]) + vec[BIAS_OUT : BIAS_OUT + 1]
    xhat, scale = normalized(x)
    n = (xhat * vec[GAIN2 : GAIN2 + 1] + vec[SHIFT2 : SHIFT2 + 1]).astype(BF)
    n2[...] = n
    d_out = cot[...]
    y = x + vec[BIAS_DOWN : BIAS_DOWN + 1]
    d_n2 = None
    for j in range(w1.shape[1] // STRIP):
        cols = slice(j * STRIP, (j + 1) * STRIP)
        u = mm(n, w1[:, cols]) + b1[:, cols]
        d_act = mm_nt(d_out, w2[cols, :])
        square = u * u
        th = jnp.tanh(u * (CURVE + (CURVE * CUBIC) * square))
        half = 0.5 * u
        hidden = (half + half * th).astype(BF)
        act[:, cols] = hidden
        y = y + mm(hidden, w2[cols, :])
        slope = (0.5 + 0.5 * th) + half * (1.0 - th * th) * (CURVE + (3.0 * CURVE * CUBIC) * square)
        low = (d_act * slope).astype(BF)
        d_pre[:, cols] = low
        sum_up[:, cols] += jnp.sum(low.astype(F32), axis=0, keepdims=True)
        part = mm_nt(low, w1[:, cols])
        d_n2 = part if d_n2 is None else d_n2 + part
    out[...] = y.astype(BF)
    add_row(sums, 0, d_n2 * xhat)
    add_row(sums, 1, d_n2)
    g = d_out.astype(F32)
    add_row(sums, 3, g)
    d = g + norm_back(d_n2, xhat, scale, vec[GAIN2 : GAIN2 + 1])
    d_mid[...] = d
    low = d.astype(BF)
    d_branch[...] = low
    add_row(sums, 2, low.astype(F32))
    d_attn[...] = mm_nt(low, wo[...]).astype(BF)


def middle_part(attn, tokens, cotangent, vec, b1, gathered, spots):
    count, width = tokens.shape
    hidden = b1.shape[1]
    rows = TILE // 2
    tile = lambda w: pl.BlockSpec((rows, w), lambda i: (i, 0))
    row = lambda w, kind: jax.ShapeDtypeStruct((count, w), kind)
    return pl.pallas_call(
        functools.partial(middle_kernel, spots),
        grid=(count // rows,),
        in_specs=[tile(width), tile(width), tile(width), whole(vec.shape), whole(b1.shape)] + [ANYWHERE] * 2,
        out_specs=[
            tile(width), tile(width), tile(hidden), tile(hidden), tile(width), tile(width), tile(width),
            whole((8, width)), whole((1, hidden)),
        ],
        scratch_shapes=[
            pltpu.VMEM((width, width), BF),
            pltpu.VMEM((width, hidden), BF),
            pltpu.VMEM((hidden, width), BF),
            pltpu.SemaphoreType.DMA((3,)),
        ],
        out_shape=[
            row(width, BF), row(width, BF), row(hidden, BF), row(hidden, BF), row(width, F32), row(width, BF),
            row(width, BF), jax.ShapeDtypeStruct((8, width), F32), jax.ShapeDtypeStruct((1, hidden), F32),
        ],
        compiler_params=params("arbitrary"),
        cost_estimate=cost(4 * count * width * (width + 2 * hidden), 6e7),
        name="middle",
    )(attn, tokens, cotangent, vec, b1, *gathered)


def first_norm_kernel(d_qkv, w, tok, d_mid, vec, out, sums):
    clear_first(sums)
    d = mm_nt(d_qkv[...], w[...])
    xhat, scale = normalized(tok[...].astype(F32))
    add_row(sums, 0, d * xhat)
    add_row(sums, 1, d)
    add_row(sums, 2, d_qkv[...].astype(F32))
    out[...] = (d_mid[...] + norm_back(d, xhat, scale, vec[0:1])).astype(BF)


def first_norm_back(d_qkv, w, tokens, d_mid, vec):
    count, width = tokens.shape
    cols = d_qkv.shape[1]
    tile = lambda w: pl.BlockSpec((TILE, w), lambda i: (i, 0))
    return pl.pallas_call(
        first_norm_kernel,
        grid=(count // TILE,),
        in_specs=[tile(cols), whole(w.shape), tile(width), tile(width), whole(vec.shape)],
        out_specs=[tile(width), whole((8, cols))],
        out_shape=[jax.ShapeDtypeStruct((count, width), BF), jax.ShapeDtypeStruct((8, cols), F32)],
        compiler_params=params("arbitrary"),
        cost_estimate=cost(2 * count * width * cols, 3e7),
        name="first_norm_back",
    )(d_qkv, w, tokens, d_mid, vec)


def tn(a, b):
    return lax.dot_general(a, b, (((0,), (0,)), ((), ())), preferred_element_type=F32)


def hand_over_kernel(*refs):
    count = len(refs) // 2
    for x, out in zip(refs[:count], refs[count:]):
        out[...] = x[...]


def hand_over(*arrays):
    return pl.pallas_call(
        hand_over_kernel,
        grid=(1,),
        in_specs=[whole(x.shape) for x in arrays],
        out_specs=[whole(x.shape) for x in arrays],
        out_shape=[jax.ShapeDtypeStruct(x.shape, x.dtype) for x in arrays],
        compiler_params=params("arbitrary"),
        name="hand_over",
    )(*arrays)


def neighbours():
    me = lax.axis_index("fsdp")
    core = lax.rem(me, 2)
    x = lax.rem(me // 2, 2)
    y = lax.rem(me // 4, 2)
    along_y = 4 * (1 - 2 * y)
    along_x = 2 * (1 - 2 * x)
    first = (1 - core) * along_y + core * along_x
    second = along_y + along_x - first
    return me, core, me // 8, first, second


def greet(others):
    barrier = pltpu.get_barrier_semaphore()
    for other in others:
        pl.semaphore_signal(barrier, inc=1, device_id=(other,), device_id_type=pl.DeviceIdType.MESH)
    pl.semaphore_wait(barrier, len(others))


def gathered_vectors(rows, vecs, wide):
    width = vecs.shape[1]
    devices = rows.shape[0] // 8
    part = width // devices
    source = lax.broadcasted_iota(jnp.int32, (WIDE, width), 0)
    owner = lax.broadcasted_iota(jnp.int32, (rows.shape[0], width), 0)

    def spread(first, size, lane):
        lanes = lane * width + lax.broadcasted_iota(jnp.int32, (1, width), 1)
        device = lanes // size
        pick = (source == first + lanes - device * size).astype(F32).astype(BF)
        return jnp.sum(jnp.where(owner == 8 * device, mm(rows, pick), 0.0), axis=0, keepdims=True)

    for v in range(8):
        vecs[v : v + 1, :] = spread(v * part, part, 0)
    for b in range(4):
        wide[:, b * width : (b + 1) * width] = spread(8 * part, 4 * part, b)


def gather_kernel(blocks, depth, spots, *refs):
    flows = len(blocks)
    owns, oths, tok_in, refs = refs[:flows], refs[flows : 2 * flows], refs[2 * flows], refs[2 * flows + 1 :]
    outs, (n1_out, qkv_out, w_out, vecs, wide), refs = refs[:flows], refs[flows : flows + 5], refs[flows + 5 :]
    (tok, w, rows, n1, qkv, load_sem, rows_sem, w_sem, put_sem), sems = refs[:9], refs[9:]
    tok_load = pltpu.make_async_copy(tok_in, tok, load_sem.at[0])
    tok_load.start()
    me, core, z, first, second = neighbours()
    twin = me + 1 - 2 * core
    chip = me // 2
    deep = [chip * 2 + core] + [lax.rem(z + k, depth) * 8 + lax.rem(me, 8) for k in range(1, depth)]
    greet([twin, me + first, me + second] + deep[1:])
    mine = [lax.rem(z + depth - k, depth) * 4 + lax.rem(chip, 4) for k in range(depth)]
    theirs = [at + first // 2 for at in mine]
    last = [at + second // 2 for at in mine + theirs]

    def send(f, at, send_sem, recv_sem, device):
        pltpu.make_async_remote_copy(
            src_ref=outs[f].at[core, at],
            dst_ref=outs[f].at[core, at],
            send_sem=send_sem,
            recv_sem=recv_sem,
            device_id=(device,),
            device_id_type=pl.DeviceIdType.MESH,
        ).start()

    def arrived(ref, sem):
        pltpu.make_async_copy(ref, ref, sem).wait()

    def onward(f, k, at, steps):
        far, near, cross, seen, local, out, twin_out, twin_in, pair_out, pair_in = sems[10 * f : 10 * f + 10]
        if steps == 2:
            send(f, at, out.at[0], near.at[k], me + first)
        if steps >= 1:
            send(f, at, out.at[0], cross.at[k if steps == 2 else depth + k], me + second)
        send(f, at, twin_out.at[0], twin_in.at[0], twin)

    for f in range(flows):
        pair_out, pair_in, local = sems[10 * f + 8], sems[10 * f + 9], sems[10 * f + 4]
        row = 0
        for size in blocks[f]:
            here_rows = pl.ds(pl.multiple_of(2 * row + core * size, 8), size)
            pltpu.make_async_copy(
                owns[f].at[pl.ds(row, size), :], outs[f].at[core, chip, here_rows, :], local.at[0]
            ).start()
            pltpu.make_async_remote_copy(
                src_ref=oths[f].at[pl.ds(row, size), :],
                dst_ref=outs[f].at[1 - core, chip, here_rows, :],
                send_sem=pair_out.at[0],
                recv_sem=pair_in.at[0],
                device_id=(twin,),
                device_id_type=pl.DeviceIdType.MESH,
            ).start()
            row += size
    for f in range(flows):
        far, out = sems[10 * f], sems[10 * f + 5]
        arrived(owns[f], sems[10 * f + 4].at[0])
        arrived(owns[f], sems[10 * f + 9].at[0])
        for k in range(1, depth):
            send(f, chip, out.at[0], far.at[k], deep[k])
        onward(f, 0, chip, 2)

    def from_far(f):
        for k in range(1, depth):
            arrived(outs[f].at[core, mine[k]], sems[10 * f].at[k])
            onward(f, k, mine[k], 2)

    def from_near(f):
        for k in range(depth):
            arrived(outs[f].at[core, theirs[k]], sems[10 * f + 1].at[k])
            onward(f, k, theirs[k], 1)

    def from_cross(f):
        for k in range(2 * depth):
            arrived(outs[f].at[core, last[k]], sems[10 * f + 2].at[k])
            onward(f, k, last[k], 0)

    def from_twin(f):
        arrived(outs[f].at[1 - core], sems[10 * f + 7].at[0])

    tile = n1.shape[1]
    tiles = tok.shape[0] // tile

    def put(i):
        slot, span = lax.rem(i, 2), pl.ds(pl.multiple_of(i * tile, tile), tile)
        return (
            pltpu.make_async_copy(n1.at[slot], n1_out.at[span, :], put_sem.at[slot]),
            pltpu.make_async_copy(qkv.at[slot], qkv_out.at[span, :], put_sem.at[2 + slot]),
        )

    def project(i):
        @pl.when(i >= 2)
        def _():
            for copy in put(i - 2):
                copy.wait()

        slot = lax.rem(i, 2)
        x = tok[pl.ds(pl.multiple_of(i * tile, tile), tile), :].astype(F32)
        n = (normalized(x)[0] * vecs[GAIN1 : GAIN1 + 1, :] + vecs[SHIFT1 : SHIFT1 + 1, :]).astype(BF)
        n1[slot] = n
        bias = []
        for h in range(2):
            cols = slice(h * WIDE, (h + 1) * WIDE)
            q, v = vecs[BIAS_Q : BIAS_Q + 1, cols], vecs[BIAS_V : BIAS_V + 1, cols]
            bias += [q, jnp.zeros_like(q), v]
        qkv[slot] = (mm(n, w[...]) + jnp.concatenate(bias, axis=1)).astype(BF)
        for copy in put(i):
            copy.start()

    def several(first, last):
        def step(i, carry):
            project(i)
            return carry

        lax.fori_loop(first, last, step, 0)

    from_far(0)
    from_near(0)
    from_cross(0)
    from_twin(0)
    fetch(outs[0], spots, [w], w_sem)
    chips = outs[0].shape[1]
    first_row = outs[0].shape[2] - 16
    for at in range(chips):
        pltpu.make_async_copy(outs[0].at[0, at, pl.ds(first_row, 16), :], rows.at[pl.ds(16 * at, 16), :], rows_sem.at[0]).start()
    from_far(1)
    from_near(1)
    arrived(rows, rows_sem.at[0])
    gathered_vectors(rows[...], vecs, wide)
    tok_load.wait()
    fetched(w, w_sem.at[0])
    w_put = pltpu.make_async_copy(w, w_out, load_sem.at[1])
    w_put.start()
    several(0, tiles // 4)
    from_far(2)
    several(tiles // 4, tiles // 2)
    from_near(2)
    from_cross(1)
    several(tiles // 2, tiles)
    from_cross(2)
    for i in (tiles - 2, tiles - 1):
        for copy in put(jnp.int32(i)):
            copy.wait()
    w_put.wait()
    for f in range(flows):
        chips = outs[f].shape[1]
        if f > 0:
            from_twin(f)
        arrived(outs[f].at[0], sems[10 * f + 6].at[0])
        arrived(outs[f].at[0, pl.ds(0, chips - 1)], sems[10 * f + 5].at[0])
        arrived(oths[f], sems[10 * f + 8].at[0])


def gather_shards(owns, oths, blocks, tokens, spots, depth):
    chips = 4 * depth
    count, width = tokens.shape
    tile = TILE // 2
    outs = [jax.ShapeDtypeStruct((2, chips, 2 * o.shape[0], WIDE), BF) for o in owns]
    outs += [
        jax.ShapeDtypeStruct((count, width), BF),
        jax.ShapeDtypeStruct((count, 3 * width), BF),
        jax.ShapeDtypeStruct((width, 3 * width), BF),
        jax.ShapeDtypeStruct((8, width), F32),
        jax.ShapeDtypeStruct((1, 4 * width), F32),
    ]
    dma = lambda n: pltpu.SemaphoreType.DMA((n,))
    scratch = [
        pltpu.VMEM((count, width), BF),
        pltpu.VMEM((width, 3 * width), BF),
        pltpu.VMEM((16 * chips, WIDE), BF),
        pltpu.VMEM((2, tile, width), BF),
        pltpu.VMEM((2, tile, 3 * width), BF),
        dma(2), dma(1), dma(1), dma(4),
    ]
    for _ in owns:
        scratch += [dma(depth), dma(depth), dma(2 * depth)] + [dma(1)] * 7
    return pl.pallas_call(
        functools.partial(gather_kernel, blocks, depth, spots),
        in_specs=[ANYWHERE] * (2 * len(owns) + 1),
        out_specs=[ANYWHERE] * (len(owns) + 3) + [pl.BlockSpec(memory_space=pltpu.VMEM)] * 2,
        out_shape=outs,
        scratch_shapes=scratch,
        compiler_params=pltpu.CompilerParams(
            collective_id=0, has_side_effects=True, vmem_limit_bytes=VMEM_LIMIT
        ),
        cost_estimate=cost(6 * count * width * width, 3e7),
        name="gather_and_qkv",
    )(*owns, *oths, tokens)


def pack_kernel(core, *refs):
    (wqkv, small, wo, w1, w2), outs = refs[:5], refs[5:]
    width = wo.shape[1]
    for c in range(2):

        @pl.when(core[0] == c)
        def _(c=c):
            for h in range(2):
                first, second, third = outs[:3] if h == c else outs[3:]
                rows = wo.shape[0]
                for t in range(3):
                    first[rows * t : rows * (t + 1), :] = wqkv[:, t * width + h * WIDE : t * width + (h + 1) * WIDE].astype(BF)
                first[3 * rows :, :] = small[...].astype(BF)
                second[0:rows, :] = wo[:, h * WIDE : (h + 1) * WIDE].astype(BF)
                for b in range(4):
                    cols = slice((4 * h + b) * WIDE, (4 * h + b + 1) * WIDE)
                    second[rows * (1 + b) : rows * (2 + b), :] = w1[:, cols].astype(BF)
                third[...] = w2[:, h * WIDE : (h + 1) * WIDE].astype(BF)


def pack(wqkv, small, wo, w1, w2, core):
    rows = wo.shape[0]
    ins = (wqkv, small, wo, w1, w2)
    shapes = [(3 * rows + small.shape[0], WIDE), (5 * rows, WIDE), (w2.shape[0], WIDE)] * 2
    return pl.pallas_call(
        pack_kernel,
        grid_spec=pltpu.PrefetchScalarGridSpec(
            num_scalar_prefetch=1,
            grid=(1,),
            in_specs=[whole(x.shape) for x in ins],
            out_specs=[whole(s) for s in shapes],
        ),
        out_shape=[jax.ShapeDtypeStruct(s, BF) for s in shapes],
        name="pack_shards",
    )(core, *ins)


def scatter_kernel(depth, splits, *refs):
    flows = len(splits)
    small_in, act, cot, n2, d_pre, attn, d_branch, n1, d_qkv = refs[:9]
    outs, rest = refs[9 : 9 + flows], refs[9 + flows :]
    (down, up, out, thirds, held, slots, held_sem, slot_sem), rest = rest[:8], rest[8:]
    ins = [small_in, down, up, out, thirds]
    width = cot.shape[1]
    tall = act.shape[1] // width
    ends = (tall, 2 * tall, 2 * tall + 1, 2 * tall + 1 + d_qkv.shape[1] // width)
    me, core, z, first, second = neighbours()

    def held_copy(k):
        return pltpu.make_async_copy((cot, n2, attn, n1)[k], held.at[k % 2], held_sem.at[k % 2])

    def level(t):
        return lax.rem(z + 1 + t, depth)

    def fetch_task(t):
        slot = lax.rem(t, 2)
        start = 0
        for source, end in zip((act, d_pre, d_branch, d_qkv), ends):
            block = level(t) if source is act else t - start

            @pl.when((t >= start) & (t < end))
            def _(source=source, block=block):
                cols = pl.ds(pl.multiple_of(block * width, 128), width)
                pltpu.make_async_copy(source.at[:, cols], slots.at[slot], slot_sem.at[slot]).start()

            start = end

    for k in range(2):
        held_copy(k).start()
        fetch_task(jnp.int32(k))
    chip = me // 2
    x, y = lax.rem(chip, 2), lax.rem(chip // 2, 2)
    twin = me + 1 - 2 * core
    deep = [lax.rem(z + k, depth) * 8 + lax.rem(me, 8) for k in range(1, depth)]
    greet([twin, me + first, me + second] + deep)
    plane = 2 * depth
    chips = 2 * plane

    def chip_of(j, core):
        bit2, bit1 = x + core * (y - x), y + core * (x - y)
        keep, side, k = j // plane, lax.rem(j, plane) // depth, lax.rem(j, depth)
        bit2 = (1 - bit2) + keep * (2 * bit2 - 1)
        bit1 = (1 - bit1) + side * (2 * bit1 - 1)
        return lax.rem(z + 1 + k, depth) * 4 + bit1 * (2 - core) + bit2 * (1 + core)

    def remote(src, dst, send_sem, recv_sem, device):
        return pltpu.make_async_remote_copy(
            src_ref=src,
            dst_ref=dst,
            send_sem=send_sem,
            recv_sem=recv_sem,
            device_id=(device,),
            device_id_type=pl.DeviceIdType.MESH,
        )

    def arrived(ref, sem):
        pltpu.make_async_copy(ref, ref, sem).wait()

    def flow(f):
        return rest[8 * f : 8 * f + 8]

    def sems(f):
        return rest[8 * flows + 11 * f : 8 * flows + 11 * f + 11]

    def loop(count, body):
        def step(j, carry):
            body(j)
            return carry

        lax.fori_loop(0, count, step, 0)

    def begin(f, some=None):
        own, in0 = flow(f)[:2]
        load, got0, sent0 = sems(f)[0], sems(f)[1], sems(f)[6]

        def body(j):
            pltpu.make_async_copy(ins[f].at[core, chip_of(j, core)], own.at[j], load.at[j]).start()
            remote(ins[f].at[1 - core, chip_of(j, 1 - core)], in0.at[j], sent0.at[0], got0.at[j], twin).start()

        loop(chips, body) if some is None else [body(j) for j in some]

    def sum_of(f, j):
        own, in0 = flow(f)[:2]
        arrived(own.at[j], sems(f)[0].at[j])
        arrived(in0.at[j], sems(f)[1].at[j])
        return own[j].astype(F32) + in0[j].astype(F32)

    def lagging(count, compute, send):
        def body(j):
            compute(j)

            @pl.when(j > 0)
            def _():
                send(j - 1)

        loop(count, body)
        send(count - 1)

    def across(f):
        own, _, in1 = flow(f)[:3]
        got1, sent1 = sems(f)[2], sems(f)[7]

        def compute(j):
            own[j] = sum_of(f, j).astype(own.dtype)

        lagging(plane, compute, lambda j: remote(own.at[j], in1.at[j], sent1.at[0], got1.at[j], me + second).start())

    def kept(f, j):
        in1 = flow(f)[2]
        arrived(in1.at[j], sems(f)[2].at[j])
        return sum_of(f, plane + j) + in1[j].astype(F32)

    def along(f):
        own, in2 = flow(f)[0], flow(f)[3]
        got2, sent2 = sems(f)[3], sems(f)[8]

        def compute(k):
            own[plane + k] = kept(f, k).astype(own.dtype)

        lagging(
            depth, compute, lambda k: remote(own.at[plane + k], in2.at[k], sent2.at[0], got2.at[k], me + first).start()
        )

    def upward(f):
        own, in2, in3, total = flow(f)[0], flow(f)[3], flow(f)[4], flow(f)[5]
        got2, got3, sent3 = sems(f)[3], sems(f)[4], sems(f)[9]

        def value(k):
            arrived(in2.at[k], got2.at[k])
            return kept(f, depth + k) + in2[k].astype(F32)

        for k in range(depth - 1):
            own[plane + depth + k] = value(k).astype(own.dtype)
            if k > 0:
                remote(own.at[plane + depth + k - 1], in3.at[k - 1], sent3.at[0], got3.at[k - 1], deep[k - 1]).start()
        total[...] = value(depth - 1)
        k = depth - 2
        remote(own.at[plane + depth + k], in3.at[k], sent3.at[0], got3.at[k], deep[k]).start()

    def mine(f, ref, which):
        if splits[f] == "rows":
            half = ref.shape[1] // 2
            return ref.at[:, pl.ds(pl.multiple_of(which * half, 8), half), :]
        half = ref.shape[0] // 2
        return ref.at[pl.ds(which * half, half)]

    def place(f, half, part):
        if splits[f] == "blocks":
            part = part.reshape((1,) + outs[f].shape[:1] + part.shape[2:])
        half_step, block_step = {4: (4, 1), 1: (1, 1), 3: (1, 2)}[part.shape[0]]
        for b in range(part.shape[0]):
            at = (half * half_step + b * block_step) * WIDE
            outs[f][:, pl.ds(pl.multiple_of(at, 128), WIDE)] = part[b]

    def finish(f):
        in3, total, theirs = flow(f)[4], flow(f)[5], flow(f)[6]
        for k in range(depth - 1):
            arrived(in3.at[k], sems(f)[4].at[k])
            total[...] += in3[k].astype(F32)
        if splits[f] is None:
            outs[f][...] = total[...]
        else:
            place(f, core, mine(f, total, core)[...])
            remote(mine(f, total, 1 - core), theirs, sems(f)[10].at[0], sems(f)[5].at[0], twin).start()

    def across_level(f, k):
        own, _, in1 = flow(f)[:3]
        got1, sent1 = sems(f)[2], sems(f)[7]
        for j in (k, depth + k):
            own[j] = sum_of(f, j).astype(own.dtype)
        for j in (k, depth + k):
            remote(own.at[j], in1.at[j], sent1.at[0], got1.at[j], me + second).start()

    def multiply(t):
        slot = lax.rem(t, 2)
        pltpu.make_async_copy(slots.at[slot], slots.at[slot], slot_sem.at[slot]).wait()

        @pl.when(t < tall)
        def _():
            low = tn(slots[slot], held[0]).astype(BF)
            count = chips // tall
            for h in range(2):
                part = low[:, h * WIDE : (h + 1) * WIDE].reshape((count,) + down.shape[2:])
                down[h, pl.ds(level(t) * count, count)] = part

        @pl.when(t >= tall)
        def _():
            k = jnp.where(t == ends[1], 0, 1)
            low = tn(held[k], slots[slot]).astype(BF)
            parts = [low[:, i * WIDE : (i + 1) * WIDE].reshape(chips, width // chips, WIDE) for i in range(2)]

            @pl.when(t < ends[1])
            def _():
                for i in range(2):
                    block = 2 * (t - tall) + i
                    up[block // tall, :, lax.rem(block, tall)] = parts[i]

            @pl.when(t == ends[1])
            def _():
                for i in range(2):
                    out[i, :, 0] = parts[i]

            @pl.when(t > ends[1])
            def _():
                for i in range(2):
                    block = 2 * (t - ends[2]) + i
                    thirds[block // 3, :, lax.rem(block, 3)] = parts[i]

        @pl.when(t + 2 < ends[3])
        def _():
            fetch_task(t + 2)

        for k, at in ((2, ends[0] - 1), (3, ends[1] - 1)):

            @pl.when(t == at)
            def _(k=k):
                held_copy(k).start()

    tiny, low, wide, side, last = range(flows)
    begin(tiny)
    for k in range(2):
        held_copy(k).wait()

    def task(t):
        for k, at in ((2, ends[1]), (3, ends[2])):

            @pl.when(t == at)
            def _(k=k):
                held_copy(k).wait()

        multiply(t)

        @pl.when((t >= 1) & (t <= depth))
        def _():
            begin(low, [t - 1 + q * depth for q in range(4)])

        @pl.when((t >= 2) & (t <= depth + 1))
        def _():
            across_level(low, t - 2)

        @pl.when(t == depth + 2)
        def _():
            across(tiny)

        @pl.when(t == ends[1])
        def _():
            begin(wide)
            along(low)

        @pl.when(t == ends[2])
        def _():
            begin(side)

        @pl.when(t == ends[2] + 1)
        def _():
            across(wide)

        @pl.when(t == ends[2] + 2)
        def _():
            across(side)

    loop(ends[3], task)
    upward(low)
    begin(last)
    along(wide)
    across(last)
    along(side)
    along(tiny)
    upward(wide)
    upward(side)
    upward(tiny)
    along(last)
    for f in range(flows - 1):
        finish(f)
    upward(last)
    finish(last)
    for f in range(flows):
        _, in0, in1, in2, in3, total, theirs, _ = flow(f)
        if splits[f] is not None:
            arrived(theirs, sems(f)[5].at[0])
            place(f, 1 - core, theirs[...])
            arrived(theirs, sems(f)[10].at[0])
        for ref, sem in zip((in0, in1, in2, in3), sems(f)[6:10]):
            arrived(ref, sem.at[0])


def scatter_sums(small, down, up, out, qkv, depth):
    chips = 4 * depth
    tokens, width = down[1].shape
    rows = width // chips
    outs, buffers, signals = [], [], []
    dma = lambda n: pltpu.SemaphoreType.DMA((n,))
    shapes = [(2, chips, blocks, rows, WIDE) for blocks in (4, 4, 1, 3)]
    work = [pltpu.VMEM(x, BF) for x in shapes]
    work += [pltpu.VMEM((2, tokens, width), BF), pltpu.VMEM((2, tokens, width), BF), dma(2), dma(2)]
    kinds = [(small.shape[2:], small.dtype)] + [(x[2:], BF) for x in shapes]
    splits = (None, "blocks", "rows", "rows", "rows")
    for (chunk, kind), split in zip(kinds, splits):
        if split == "rows":
            part = (chunk[0], chunk[1] // 2) + chunk[2:]
        elif split == "blocks":
            part = (chunk[0] // 2,) + chunk[1:]
        else:
            part = chunk
        tall = part[-2] if split == "rows" else part[0] * part[1]
        cols = 2 * WIDE * (chunk[0] if split == "rows" else 1)
        outs.append(jax.ShapeDtypeStruct(part if split is None else (tall, cols), F32))
        for count in (chips, chips, chips // 2, depth, depth - 1):
            buffers.append(pltpu.VMEM((count,) + chunk, kind))
        buffers += [pltpu.VMEM(chunk, F32), pltpu.VMEM(part, F32), dma(1)]
        signals += [dma(chips), dma(chips), dma(chips // 2), dma(depth), dma(depth - 1)] + [dma(1)] * 6
    return pl.pallas_call(
        functools.partial(scatter_kernel, depth, splits),
        in_specs=[ANYWHERE] * 9,
        out_specs=[pl.BlockSpec(memory_space=pltpu.VMEM)] * len(outs),
        out_shape=outs,
        scratch_shapes=work + buffers + signals,
        compiler_params=pltpu.CompilerParams(
            collective_id=1, has_side_effects=True, vmem_limit_bytes=63 * 1024 * 1024
        ),
        cost_estimate=cost(0, 3e7),
        name="scatter_sums",
    )(small, *down, *up, *out, *qkv)


def by_neighbours(devices, width, hidden, count):
    rows = width // devices
    fits = rows * devices == width and rows % 8 == 0 and devices % 8 == 0
    return fits and width == 2 * WIDE and hidden == 4 * width and count % TILE == 0


def weight_halves(w):
    rows = w.shape[0]
    return w.reshape(rows, 3, 2, WIDE).transpose(0, 2, 1, 3).reshape(rows, -1)


def local(
    tokens, segments, cotangent, ln1_gain, ln1_shift, w_qkv, bias_q, bias_v, w_out, bias_out,
    ln2_gain, ln2_shift, w_up, bias_up, w_down, bias_down, *, seq,
):
    masters = (
        ln1_gain, ln1_shift, w_qkv, bias_q, bias_v, w_out, bias_out,
        ln2_gain, ln2_shift, w_up, bias_up, w_down, bias_down,
    )
    count, width = tokens.shape
    tables = attention_tables(segments.reshape(-1, seq))
    run = by_chips if by_neighbours(lax.axis_size("fsdp"), width, w_up.shape[1], count) else by_collectives
    return run(tokens, cotangent, tables, masters)


def by_collectives(tokens, cotangent, tables, masters):
    def norm(x, gain, shift):
        return normalized(x)[0] * gain + shift

    width = tokens.shape[1]
    full = [lax.all_gather(m.astype(BF), "fsdp", axis=0, tiled=True) for m in masters]
    g1, c1, wqkv, bq, bv, wo, bo, g2, c2, w1, b1, w2, b2 = [p.astype(F32) if p.ndim == 1 else p for p in full]
    wqkv = weight_halves(wqkv)
    rows = tokens.astype(F32)
    n1 = norm(rows, g1, c1).astype(BF)
    bias = weight_halves(jnp.concatenate([bq, jnp.zeros_like(bq), bv])[None])
    qkv = (mm(n1, wqkv) + bias).astype(BF)
    attn, attn_t, lse = attention_fwd(qkv, *tables)
    middle = rows + mm(attn, wo) + bo
    n2 = norm(middle, g2, c2).astype(BF)
    act_value, gelu_pull = jax.vjp(functools.partial(jax.nn.gelu, approximate=True), mm(n2, w1) + b1)
    act = act_value.astype(BF)
    layer_out = (middle + mm(act, w2) + b2).astype(BF)
    d_out = cotangent.astype(F32)
    d_pre = gelu_pull(mm_nt(cotangent, w2))[0].astype(BF)
    _, pull = jax.vjp(norm, middle, g2, c2)
    d_mid, d_g2, d_c2 = pull(mm_nt(d_pre, w1))
    d_mid = d_out + d_mid
    d_branch = d_mid.astype(BF)
    d_attn = mm_nt(d_branch, wo).astype(BF)
    d_qkv = attention_bwd(qkv, d_attn, attn_t, lse, *tables)
    _, pull = jax.vjp(norm, rows, g1, c1)
    d_rows, d_g1, d_c1 = pull(mm_nt(d_qkv, wqkv))
    input_grad = (d_mid + d_rows).astype(BF)
    total = lambda x: jnp.sum(x.astype(F32), axis=0)
    by_part = lambda x: x.reshape(-1, 2, 3, WIDE).transpose(0, 2, 1, 3).reshape(x.shape)
    sums = by_part(total(d_qkv)[None])[0]
    grads = (
        d_g1, d_c1, by_part(tn(n1, d_qkv)), sums[:width], sums[2 * width :], tn(attn, d_branch), total(d_branch),
        d_g2, d_c2, tn(n2, d_pre), total(d_pre), tn(act, cotangent), total(d_out),
    )
    return (layer_out, input_grad) + tuple(
        lax.psum_scatter(g, "fsdp", scatter_dimension=0, tiled=True) for g in grads
    )


def by_chips(tokens, cotangent, tables, masters):
    devices = lax.axis_size("fsdp")
    chips = devices // 2
    depth = devices // 8
    count, width = tokens.shape
    ln1_gain, ln1_shift, w_qkv, bias_q, bias_v, w_out, bias_out, ln2_gain, ln2_shift, w_up, bias_up, w_down, bias_down = masters
    part = width // devices
    two = 2 * part
    hidden = w_up.shape[1]
    core = lax.rem(lax.axis_index("fsdp"), 2).astype(jnp.int32).reshape(1)

    small = jnp.concatenate([ln1_gain, ln1_shift, bias_q, bias_v, bias_out, ln2_gain, ln2_shift, bias_down, bias_up])
    small = jnp.pad(small[None], ((0, 7), (0, WIDE - small.shape[0])))
    own1, own2, own3, oth1, oth2, oth3 = pack(w_qkv, small, w_out, w_up, w_down, core)

    def spots_qkv(h, chip):
        return [
            (two * t, two, 0, (pl.ds(two * chip, two), pl.ds((3 * h + t) * WIDE, WIDE))) for t in range(3)
        ]

    def spots_up(h, chip):
        rows = pl.ds(two * chip, two)
        return [(0, two, 0, (rows, pl.ds(h * WIDE, WIDE)))] + [
            (two * (1 + b), two, 1, (rows, pl.ds((4 * h + b) * WIDE, WIDE))) for b in range(4)
        ]

    def spots_down(h, chip):
        return [(0, 4 * two, 0, (pl.ds(4 * two * chip, 4 * two), pl.ds(h * WIDE, WIDE)))]

    blocks = ([part] * 3 + [8], [part] * 5, [4 * part])
    _, chunks2, chunks3, n1, qkv, wqkv, vecs, b1 = gather_shards(
        (own1, own2, own3), (oth1, oth2, oth3), blocks, tokens, spots_qkv, depth
    )
    attn, attn_t, lse = attention_fwd(qkv, *tables)
    layer_out, n2, act, d_pre, d_mid, d_branch, d_attn, sums2, sum_up = middle_part(
        attn, tokens, cotangent, vecs, b1, (chunks2, chunks3), (spots_up, spots_down)
    )

    d_qkv = attention_bwd(qkv, d_attn, attn_t, lse, *tables)
    input_grad, sums1 = first_norm_back(d_qkv, wqkv, tokens, d_mid, vecs)
    by_half = sums1[2].reshape(2, 3, WIDE).swapaxes(0, 1).reshape(3, width)
    vecs = jnp.concatenate([sums1[:2, :width], by_half[0:1], by_half[2:3], sums2[2:3], sums2[0:2], sums2[3:4]])
    vecs = vecs.reshape(8, devices, part).swapaxes(0, 1).reshape(devices, width // devices * 8)
    small = jnp.concatenate([vecs, sum_up.reshape(devices, 4 * part)], axis=1)
    small = small.reshape(chips, 2, 1, -1).swapaxes(0, 1)
    small = jnp.pad(small, ((0, 0), (0, 0), (0, 7), (0, WIDE - small.shape[3])))
    small, g_down, g_up, g_out, g_qkv = scatter_sums(
        small, (act, cotangent), (n2, d_pre), (attn, d_branch), (n1, d_qkv), depth
    )
    small, g_down, g_up, g_out, g_qkv = hand_over(small[:1], g_down, g_up, g_out, g_qkv)
    small = small[0]
    s = [small[i * part : (i + 1) * part] for i in range(8)]
    s_b1 = small[8 * part : 12 * part]
    return (
        layer_out, input_grad, s[0], s[1], g_qkv, s[2], s[3], g_out, s[4], s[5], s[6], g_up, s_b1, g_down, s[7],
    )


MICRO = 2


def solution(mesh):
    line, table = P("fsdp"), P("fsdp", None)
    weights = (line, line, table, line, line, table, line, line, line, table, line, table, line)

    def step(tokens, *rest):
        seq = tokens.shape[0] // (mesh.shape["fsdp"] * MICRO)
        return jax.shard_map(
            functools.partial(local, seq=seq),
            mesh=mesh,
            in_specs=(table, line, table) + weights,
            out_specs=(table, table) + weights,
            check_vma=False,
        )(tokens, *rest)

    return step
```

```python
import functools
import jax
import jax.numpy as jnp
from jax import lax
from jax.experimental import pallas as pl
from jax.experimental.pallas import tpu as pltpu
from jax.sharding import PartitionSpec as P

HD = 64
QB = 128
KB = 128
NEG = -1000000000.0
BF = jnp.bfloat16
F32 = jnp.float32
EPSILON = 1e-06
NT = (((1,), (1,)), ((), ()))


def mm(a, b):
    return jnp.dot(a, b, preferred_element_type=F32)


def mm_nt(a, b):
    return lax.dot_general(a, b, NT, preferred_element_type=F32)


def pair_diag(top, bottom):
    zero = jnp.zeros_like(top)
    return jnp.concatenate(
        [jnp.concatenate([top, zero], axis=1), jnp.concatenate([zero, bottom], axis=1)], axis=0
    )


SPANS = (2, 3, 4, 5, 6, 8)


def by_span(lo, hi, rows, run):
    need = hi - lo
    below = 0
    for span in SPANS:
        if below * KB >= rows:
            break
        size = min(span * KB, rows)
        last = size == rows

        @pl.when((need > below) & (last | (need <= span)))
        def _(size=size):
            run(pl.multiple_of(jnp.minimum(lo * KB, rows - size), KB), size)

        below = span


def chunks(k0, size):
    return [(pl.multiple_of(k0 + c, KB), min(2 * KB, size - c)) for c in range(0, size, 2 * KB)]


def terms(pieces):
    width = pieces[0].shape[1]
    row = lax.broadcasted_iota(jnp.int32, (8, width), 0)
    tail = jnp.zeros((8, width), F32)
    for i, piece in enumerate(pieces):
        tail = jnp.where(row == i, piece, tail)
    return tail


def three_parts(x):
    first = x.astype(BF).astype(F32)
    rest = x - first
    second = rest.astype(BF).astype(F32)
    return first, second, rest - second


def pair_rhs(feat, extra, p, qs):
    a = 128 * p
    block = pair_diag(feat[a : a + 64, qs], feat[a + 64 : a + 128, qs])
    rows = jnp.concatenate([extra[2 * p, :, qs], extra[2 * p + 1, :, qs]], axis=1)
    return block, jnp.concatenate([block, rows, jnp.zeros((112, 2 * QB), BF)], axis=0)


def attn_fwd_kernel(
    lo, hi, q_ref, k_ref, v_ref, oh_ref, mr_ref, o_ref, ot_ref, lse_ref, qt, vt, extra, tops
):
    seq = pl.program_id(0)
    rows = q_ref.shape[0]
    pairs = q_ref.shape[1] // 128
    heads = 2 * pairs
    vt[...] = v_ref[...].T
    qt[...] = (q_ref[...] * 0.125).astype(BF).T
    lane = lax.broadcasted_iota(jnp.int32, (8, heads * HD), 1) // HD
    pick = (lane == lax.broadcasted_iota(jnp.int32, (8, heads * HD), 0)).astype(BF)
    square = k_ref[...].astype(F32)
    norms = mm_nt(pick, (square * square).astype(BF))
    bound = jnp.sqrt(jnp.max(norms, axis=1, keepdims=True)) * 1.01
    for h in range(heads):
        qh = qt[64 * h : 64 * h + 64, :].astype(F32)
        length = jnp.sqrt(jnp.sum(qh * qh, axis=0, keepdims=True)) * 1.01
        m = (length * bound[h : h + 1, :]).astype(BF).astype(F32)
        tops[h : h + 1, :] = m
        extra[h, :, :] = jnp.concatenate([mr_ref[0], terms([-m])], axis=0).astype(BF)

    def keep(qs, p, l, full):
        a = 128 * p
        ot_ref[0, a : a + 64, qs] = full[0:64, 0:QB]
        ot_ref[0, a + 64 : a + 128, qs] = full[64:128, QB:]
        lse_ref[0, 0, 2 * p : 2 * p + 1, qs] = l[:, 0:QB]
        lse_ref[0, 0, 2 * p + 1 : 2 * p + 2, qs] = l[:, QB:]

    def q_step(qb, carry):
        qs = pl.ds(pl.multiple_of(qb * QB, QB), QB)

        def run(k0, size):
            rhs = [pair_rhs(qt, extra, p, qs)[1] for p in range(pairs)]
            l = [jnp.zeros((1, 2 * QB), F32)] * pairs
            acc = [None] * pairs
            for c0, cs in chunks(k0, size):
                ks = pl.ds(c0, cs)
                oh = oh_ref[ks, :]
                for p in range(pairs):
                    cols = slice(128 * p, 128 * p + 128)
                    w = jnp.exp(mm(jnp.concatenate([k_ref[ks, cols], oh], axis=1), rhs[p]))
                    l[p] = l[p] + jnp.sum(w, axis=0, keepdims=True)
                    part = mm(vt[cols, ks], w.astype(BF))
                    acc[p] = part if acc[p] is None else acc[p] + part
            for p in range(pairs):
                keep(qs, p, l[p], acc[p])

        by_span(lo[seq, qb], hi[seq, qb], rows, run)
        return carry

    lax.fori_loop(0, rows // QB, q_step, 0)

    @pl.when(jnp.min(lse_ref[0, 0]) < 1e-20)
    def _():
        for h in range(heads):
            extra[h, :, :] = jnp.concatenate([mr_ref[0], jnp.zeros_like(mr_ref[0])], axis=0).astype(BF)

        def q_again(qb, carry):
            qs = pl.ds(pl.multiple_of(qb * QB, QB), QB)
            for p in range(pairs):
                cols = slice(128 * p, 128 * p + 128)
                rhs = pair_rhs(qt, extra, p, qs)[1]

                def scores(kb):
                    ks = pl.ds(pl.multiple_of(kb * KB, KB), KB)
                    return ks, mm(jnp.concatenate([k_ref[ks, cols], oh_ref[ks, :]], axis=1), rhs)

                def top_step(kb, m):
                    return jnp.maximum(m, jnp.max(scores(kb)[1], axis=0, keepdims=True))

                blocks = rows // KB
                m = lax.fori_loop(0, blocks, top_step, jnp.full((1, 2 * QB), 2 * NEG, F32))

                def sum_step(kb, state):
                    ks, st = scores(kb)
                    w = jnp.exp(st - m)
                    return state[0] + jnp.sum(w, axis=0, keepdims=True), state[1] + mm(vt[cols, ks], w.astype(BF))

                start = (jnp.zeros((1, 2 * QB), F32), jnp.zeros((128, 2 * QB), F32))
                l, full = lax.fori_loop(0, blocks, sum_step, start)
                tops[2 * p : 2 * p + 1, qs] = m[:, 0:QB]
                tops[2 * p + 1 : 2 * p + 2, qs] = m[:, QB:]
                keep(qs, p, l, full)
            return carry

        lax.fori_loop(0, rows // QB, q_again, 0)

    for h in range(heads):
        l = lse_ref[0, 0, h : h + 1, :]
        hs = slice(64 * h, 64 * h + 64)
        ot_ref[0, hs, :] = ot_ref[0, hs, :] * (1.0 / l)
        lse_ref[0, 0, h : h + 1, :] = tops[h : h + 1, :] + jnp.log(l)
    o_ref[...] = ot_ref[0].astype(BF).T


def attn_bwd_kernel(
    lo, hi, q_ref, k_ref, v_ref, do_ref, ot_ref, lse_ref, oh_ref, mr_ref, dqkv_ref,
    qt, kt, dot, extra_q, extra_d, dqt, dkt, dvt,
):
    seq = pl.program_id(0)
    rows = q_ref.shape[0]
    pairs = q_ref.shape[1] // 128
    qt[...] = (q_ref[...] * 0.125).astype(BF).T
    kt[...] = k_ref[...].T
    dot[...] = do_ref[...].T
    for h in range(2 * pairs):
        r = slice(64 * h, 64 * h + 64)
        delta = jnp.sum(dot[r, :].astype(F32) * ot_ref[0, r, :], axis=0, keepdims=True)
        lse = lse_ref[0, 0, h : h + 1, :]
        extra_q[h, :, :] = jnp.concatenate([mr_ref[0], terms(three_parts(-lse))], axis=0).astype(BF)
        tail = terms(three_parts(-delta))
        extra_d[h, :, :] = jnp.concatenate([jnp.zeros_like(tail), tail], axis=0).astype(BF)
    dkt[...] = jnp.zeros_like(dkt)
    dvt[...] = jnp.zeros_like(dvt)

    def q_step(qb, carry):
        qs = pl.ds(pl.multiple_of(qb * QB, QB), QB)

        def run(k0, size):
            ks = pl.ds(k0, size)
            oh = oh_ref[ks, :]
            for p in range(pairs):
                a = 128 * p
                cols = slice(a, a + 128)
                qm, qx = pair_rhs(qt, extra_q, p, qs)
                dom, dx = pair_rhs(dot, extra_d, p, qs)
                w = jnp.exp(mm(jnp.concatenate([k_ref[ks, cols], oh], axis=1), qx))
                ds = (w * mm(jnp.concatenate([v_ref[ks, cols], oh], axis=1), dx)).astype(BF)
                dvt[cols, ks] += mm_nt(dom, w.astype(BF))
                dkt[cols, ks] += mm_nt(qm, ds)
                dq = mm(kt[cols, ks], ds)
                dqt[a : a + 64, qs] = dq[0:64, 0:QB]
                dqt[a + 64 : a + 128, qs] = dq[64:128, QB:]

        by_span(lo[seq, qb], hi[seq, qb], rows, run)
        return carry

    lax.fori_loop(0, rows // QB, q_step, 0)
    wide = dqt.shape[0]
    dqkv_ref[:, 0:wide] = (dqt[...] * 0.125).astype(BF).T
    dqkv_ref[:, wide : 2 * wide] = dkt[...].astype(BF).T
    dqkv_ref[:, 2 * wide :] = dvt[...].astype(BF).T


WIDE = 384
TILE = 512
VMEM_LIMIT = 60 * 1024 * 1024


def params(*semantics):
    return pltpu.CompilerParams(dimension_semantics=semantics or None, vmem_limit_bytes=VMEM_LIMIT)


def cost(flops, data):
    return pl.CostEstimate(flops=int(flops), bytes_accessed=int(data), transcendentals=0)


def whole(shape):
    zero = (0,) * len(shape)
    return pl.BlockSpec(shape, lambda *_: zero)


ANYWHERE = pl.BlockSpec(memory_space=pl.ANY)


def attention_tables(segs):
    order = jnp.where(segs == 0, 1 << 20, segs)
    seqs, length = segs.shape
    first = order[:, ::QB]
    last = order[:, QB - 1 :: QB]
    lo = jnp.sum((order[:, None, :] < first[:, :, None]).astype(jnp.int32), axis=2) // KB
    hi = (jnp.sum((order[:, None, :] <= last[:, :, None]).astype(jnp.int32), axis=2) + KB - 1) // KB
    ids = jnp.arange(128, dtype=jnp.int32)[None, :]
    onehot = (segs.reshape(-1)[:, None] == ids) | ((ids >= 8) & (ids < 16))
    differ = segs[:, None, :] != jnp.arange(8, dtype=jnp.int32)[None, :, None]
    return lo, hi, onehot.astype(BF), jnp.where(differ, NEG, 0.0)


def attention_fwd(qkv, lo, hi, onehot, miss):
    seqs = lo.shape[0]
    rows = qkv.shape[0] // seqs
    wide = WIDE
    width = qkv.shape[1] // 3
    parts = width // wide
    col = lambda at: pl.BlockSpec((rows, wide), lambda s, j, *_: (s, 3 * j + at))
    return pl.pallas_call(
        attn_fwd_kernel,
        grid_spec=pltpu.PrefetchScalarGridSpec(
            num_scalar_prefetch=2,
            grid=(seqs, parts),
            in_specs=[
                col(0), col(1), col(2),
                pl.BlockSpec((rows, 128), lambda s, *_: (s, 0)),
                pl.BlockSpec((1, 8, rows), lambda s, *_: (s, 0, 0)),
            ],
            out_specs=[
                pl.BlockSpec((rows, wide), lambda s, j, *_: (s, j)),
                pl.BlockSpec((1, wide, rows), lambda s, j, *_: (s, j, 0)),
                pl.BlockSpec((1, 1, wide // HD, rows), lambda s, j, *_: (s, j, 0, 0)),
            ],
            scratch_shapes=[
                pltpu.VMEM((wide, rows), BF),
                pltpu.VMEM((wide, rows), BF),
                pltpu.VMEM((wide // HD, 16, rows), BF),
                pltpu.VMEM((8, rows), F32),
            ],
        ),
        out_shape=[
            jax.ShapeDtypeStruct((qkv.shape[0], width), BF),
            jax.ShapeDtypeStruct((seqs, width, rows), F32),
            jax.ShapeDtypeStruct((seqs, parts, wide // HD, rows), F32),
        ],
        compiler_params=params("arbitrary", "arbitrary"),
        cost_estimate=cost(24e9, 2e7),
        name="attention_forward",
    )(lo, hi, qkv, qkv, qkv, onehot, miss)


def attention_bwd(qkv, d_attn, ot, lse, lo, hi, onehot, miss):
    seqs = lo.shape[0]
    rows = qkv.shape[0] // seqs
    wide = WIDE
    col = lambda at: pl.BlockSpec((rows, wide), lambda s, j, *_: (s, 3 * j + at))
    return pl.pallas_call(
        attn_bwd_kernel,
        grid_spec=pltpu.PrefetchScalarGridSpec(
            num_scalar_prefetch=2,
            grid=(seqs, d_attn.shape[1] // wide),
            in_specs=[
                col(0), col(1), col(2),
                pl.BlockSpec((rows, wide), lambda s, j, *_: (s, j)),
                pl.BlockSpec((1, wide, rows), lambda s, j, *_: (s, j, 0)),
                pl.BlockSpec((1, 1, wide // HD, rows), lambda s, j, *_: (s, j, 0, 0)),
                pl.BlockSpec((rows, 128), lambda s, *_: (s, 0)),
                pl.BlockSpec((1, 8, rows), lambda s, *_: (s, 0, 0)),
            ],
            out_specs=pl.BlockSpec((rows, 3 * wide), lambda s, j, *_: (s, j)),
            scratch_shapes=[
                pltpu.VMEM((wide, rows), BF),
                pltpu.VMEM((wide, rows), BF),
                pltpu.VMEM((wide, rows), BF),
                pltpu.VMEM((wide // HD, 16, rows), BF),
                pltpu.VMEM((wide // HD, 16, rows), BF),
                pltpu.VMEM((wide, rows), F32),
                pltpu.VMEM((wide, rows), F32),
                pltpu.VMEM((wide, rows), F32),
            ],
        ),
        out_shape=jax.ShapeDtypeStruct(qkv.shape, BF),
        compiler_params=params("arbitrary", "arbitrary"),
        cost_estimate=cost(44e9, 4e7),
        name="attention_backward",
    )(lo, hi, qkv, qkv, qkv, d_attn, ot, lse, onehot, miss)


def normalized(x):
    mean = jnp.mean(x, axis=-1, keepdims=True)
    centered = x - mean
    scale = lax.rsqrt(jnp.mean(centered * centered, axis=-1, keepdims=True) + EPSILON)
    return centered * scale, scale


def norm_back(d, xhat, scale, gain):
    e = d * gain
    return scale * (e - jnp.mean(e, axis=-1, keepdims=True) - xhat * jnp.mean(e * xhat, axis=-1, keepdims=True))


def clear_first(*refs):
    @pl.when(pl.program_id(0) == 0)
    def _():
        for ref in refs:
            ref[...] = jnp.zeros_like(ref)


def add_row(ref, row, values):
    ref[row : row + 1, 0 : values.shape[1]] += jnp.sum(values, axis=0, keepdims=True)


def fetch(chunks, spots, outs, sems):
    for h in range(2):
        for chip in range(chunks.shape[1]):
            for row, count, which, target in spots(h, chip):
                pltpu.make_async_copy(
                    chunks.at[h, chip, pl.ds(row, count), :], outs[which].at[target], sems.at[which]
                ).start()


def fetched(out, sem):
    pltpu.make_async_copy(out, out, sem).wait()


GAIN1, SHIFT1, BIAS_Q, BIAS_V, BIAS_OUT, GAIN2, SHIFT2, BIAS_DOWN = range(8)
STRIP = 768
CURVE = 0.7978845608028654
CUBIC = 0.044715


def middle_kernel(
    spots, attn, tok, cot, vec, b1, chunks2, chunks3,
    out, n2, act, d_pre, d_mid, d_branch, d_attn, sums, sum_up, wo, w1, w2, sem,
):
    @pl.when(pl.program_id(0) == 0)
    def _():
        fetch(chunks2, spots[0], [wo, w1], sem)
        fetch(chunks3, spots[1], [w2], sem.at[pl.ds(2, 1)])
        for ref in (sums, sum_up):
            ref[...] = jnp.zeros_like(ref)
        for k, ref in enumerate((wo, w1, w2)):
            fetched(ref, sem.at[k])

    x = tok[...].astype(F32) + mm(attn[...], wo[...]) + vec[BIAS_OUT : BIAS_OUT + 1]
    xhat, scale = normalized(x)
    n = (xhat * vec[GAIN2 : GAIN2 + 1] + vec[SHIFT2 : SHIFT2 + 1]).astype(BF)
    n2[...] = n
    d_out = cot[...]
    y = x + vec[BIAS_DOWN : BIAS_DOWN + 1]
    d_n2 = None
    for j in range(w1.shape[1] // STRIP):
        cols = slice(j * STRIP, (j + 1) * STRIP)
        u = mm(n, w1[:, cols]) + b1[:, cols]
        d_act = mm_nt(d_out, w2[cols, :])
        square = u * u
        th = jnp.tanh(u * (CURVE + (CURVE * CUBIC) * square))
        half = 0.5 * u
        hidden = (half + half * th).astype(BF)
        act[:, cols] = hidden
        y = y + mm(hidden, w2[cols, :])
        slope = (0.5 + 0.5 * th) + half * (1.0 - th * th) * (CURVE + (3.0 * CURVE * CUBIC) * square)
        low = (d_act * slope).astype(BF)
        d_pre[:, cols] = low
        sum_up[:, cols] += jnp.sum(low.astype(F32), axis=0, keepdims=True)
        part = mm_nt(low, w1[:, cols])
        d_n2 = part if d_n2 is None else d_n2 + part
    out[...] = y.astype(BF)
    add_row(sums, 0, d_n2 * xhat)
    add_row(sums, 1, d_n2)
    g = d_out.astype(F32)
    add_row(sums, 3, g)
    d = g + norm_back(d_n2, xhat, scale, vec[GAIN2 : GAIN2 + 1])
    d_mid[...] = d
    low = d.astype(BF)
    d_branch[...] = low
    add_row(sums, 2, low.astype(F32))
    d_attn[...] = mm_nt(low, wo[...]).astype(BF)


def middle_part(attn, tokens, cotangent, vec, b1, gathered, spots):
    count, width = tokens.shape
    hidden = b1.shape[1]
    rows = TILE // 2
    tile = lambda w: pl.BlockSpec((rows, w), lambda i: (i, 0))
    row = lambda w, kind: jax.ShapeDtypeStruct((count, w), kind)
    return pl.pallas_call(
        functools.partial(middle_kernel, spots),
        grid=(count // rows,),
        in_specs=[tile(width), tile(width), tile(width), whole(vec.shape), whole(b1.shape)] + [ANYWHERE] * 2,
        out_specs=[
            tile(width), tile(width), tile(hidden), tile(hidden), tile(width), tile(width), tile(width),
            whole((8, width)), whole((1, hidden)),
        ],
        scratch_shapes=[
            pltpu.VMEM((width, width), BF),
            pltpu.VMEM((width, hidden), BF),
            pltpu.VMEM((hidden, width), BF),
            pltpu.SemaphoreType.DMA((3,)),
        ],
        out_shape=[
            row(width, BF), row(width, BF), row(hidden, BF), row(hidden, BF), row(width, F32), row(width, BF),
            row(width, BF), jax.ShapeDtypeStruct((8, width), F32), jax.ShapeDtypeStruct((1, hidden), F32),
        ],
        compiler_params=params("arbitrary"),
        cost_estimate=cost(4 * count * width * (width + 2 * hidden), 6e7),
        name="middle",
    )(attn, tokens, cotangent, vec, b1, *gathered)


def first_norm_kernel(d_qkv, w, tok, d_mid, vec, out, sums):
    clear_first(sums)
    d = mm_nt(d_qkv[...], w[...])
    xhat, scale = normalized(tok[...].astype(F32))
    add_row(sums, 0, d * xhat)
    add_row(sums, 1, d)
    add_row(sums, 2, d_qkv[...].astype(F32))
    out[...] = (d_mid[...] + norm_back(d, xhat, scale, vec[0:1])).astype(BF)


def first_norm_back(d_qkv, w, tokens, d_mid, vec):
    count, width = tokens.shape
    cols = d_qkv.shape[1]
    tile = lambda w: pl.BlockSpec((TILE, w), lambda i: (i, 0))
    return pl.pallas_call(
        first_norm_kernel,
        grid=(count // TILE,),
        in_specs=[tile(cols), whole(w.shape), tile(width), tile(width), whole(vec.shape)],
        out_specs=[tile(width), whole((8, cols))],
        out_shape=[jax.ShapeDtypeStruct((count, width), BF), jax.ShapeDtypeStruct((8, cols), F32)],
        compiler_params=params("arbitrary"),
        cost_estimate=cost(2 * count * width * cols, 3e7),
        name="first_norm_back",
    )(d_qkv, w, tokens, d_mid, vec)


def tn(a, b):
    return lax.dot_general(a, b, (((0,), (0,)), ((), ())), preferred_element_type=F32)


def hand_over_kernel(*refs):
    count = len(refs) // 2
    for x, out in zip(refs[:count], refs[count:]):
        out[...] = x[...]


def hand_over(*arrays):
    return pl.pallas_call(
        hand_over_kernel,
        grid=(1,),
        in_specs=[whole(x.shape) for x in arrays],
        out_specs=[whole(x.shape) for x in arrays],
        out_shape=[jax.ShapeDtypeStruct(x.shape, x.dtype) for x in arrays],
        compiler_params=params("arbitrary"),
        name="hand_over",
    )(*arrays)


def neighbours():
    me = lax.axis_index("fsdp")
    core = lax.rem(me, 2)
    x = lax.rem(me // 2, 2)
    y = lax.rem(me // 4, 2)
    along_y = 4 * (1 - 2 * y)
    along_x = 2 * (1 - 2 * x)
    first = (1 - core) * along_y + core * along_x
    second = along_y + along_x - first
    return me, core, me // 8, first, second


def greet(others):
    barrier = pltpu.get_barrier_semaphore()
    for other in others:
        pl.semaphore_signal(barrier, inc=1, device_id=(other,), device_id_type=pl.DeviceIdType.MESH)
    pl.semaphore_wait(barrier, len(others))


def gathered_vectors(rows, vecs, wide):
    width = vecs.shape[1]
    devices = rows.shape[0] // 8
    part = width // devices
    source = lax.broadcasted_iota(jnp.int32, (WIDE, width), 0)
    owner = lax.broadcasted_iota(jnp.int32, (rows.shape[0], width), 0)

    def spread(first, size, lane):
        lanes = lane * width + lax.broadcasted_iota(jnp.int32, (1, width), 1)
        device = lanes // size
        pick = (source == first + lanes - device * size).astype(F32).astype(BF)
        return jnp.sum(jnp.where(owner == 8 * device, mm(rows, pick), 0.0), axis=0, keepdims=True)

    for v in range(8):
        vecs[v : v + 1, :] = spread(v * part, part, 0)
    for b in range(4):
        wide[:, b * width : (b + 1) * width] = spread(8 * part, 4 * part, b)


def gather_kernel(blocks, depth, spots, *refs):
    flows = len(blocks)
    owns, oths, tok_in, refs = refs[:flows], refs[flows : 2 * flows], refs[2 * flows], refs[2 * flows + 1 :]
    outs, (n1_out, qkv_out, w_out, vecs, wide), refs = refs[:flows], refs[flows : flows + 5], refs[flows + 5 :]
    (tok, w, rows, n1, qkv, load_sem, rows_sem, w_sem, put_sem), sems = refs[:9], refs[9:]
    tok_load = pltpu.make_async_copy(tok_in, tok, load_sem.at[0])
    tok_load.start()
    me, core, z, first, second = neighbours()
    twin = me + 1 - 2 * core
    chip = me // 2
    deep = [chip * 2 + core] + [lax.rem(z + k, depth) * 8 + lax.rem(me, 8) for k in range(1, depth)]
    greet([twin, me + first, me + second] + deep[1:])
    mine = [lax.rem(z + depth - k, depth) * 4 + lax.rem(chip, 4) for k in range(depth)]
    theirs = [at + first // 2 for at in mine]
    last = [at + second // 2 for at in mine + theirs]

    def send(f, at, send_sem, recv_sem, device):
        pltpu.make_async_remote_copy(
            src_ref=outs[f].at[core, at],
            dst_ref=outs[f].at[core, at],
            send_sem=send_sem,
            recv_sem=recv_sem,
            device_id=(device,),
            device_id_type=pl.DeviceIdType.MESH,
        ).start()

    def arrived(ref, sem):
        pltpu.make_async_copy(ref, ref, sem).wait()

    def onward(f, k, at, steps):
        far, near, cross, seen, local, out, twin_out, twin_in, pair_out, pair_in = sems[10 * f : 10 * f + 10]
        if steps == 2:
            send(f, at, out.at[0], near.at[k], me + first)
        if steps >= 1:
            send(f, at, out.at[0], cross.at[k if steps == 2 else depth + k], me + second)
        send(f, at, twin_out.at[0], twin_in.at[0], twin)

    for f in range(flows):
        pair_out, pair_in, local = sems[10 * f + 8], sems[10 * f + 9], sems[10 * f + 4]
        row = 0
        for size in blocks[f]:
            here_rows = pl.ds(pl.multiple_of(2 * row + core * size, 8), size)
            pltpu.make_async_copy(
                owns[f].at[pl.ds(row, size), :], outs[f].at[core, chip, here_rows, :], local.at[0]
            ).start()
            pltpu.make_async_remote_copy(
                src_ref=oths[f].at[pl.ds(row, size), :],
                dst_ref=outs[f].at[1 - core, chip, here_rows, :],
                send_sem=pair_out.at[0],
                recv_sem=pair_in.at[0],
                device_id=(twin,),
                device_id_type=pl.DeviceIdType.MESH,
            ).start()
            row += size
    for f in range(flows):
        far, out = sems[10 * f], sems[10 * f + 5]
        arrived(owns[f], sems[10 * f + 4].at[0])
        arrived(owns[f], sems[10 * f + 9].at[0])
        for k in range(1, depth):
            send(f, chip, out.at[0], far.at[k], deep[k])
        onward(f, 0, chip, 2)

    def from_far(f):
        for k in range(1, depth):
            arrived(outs[f].at[core, mine[k]], sems[10 * f].at[k])
            onward(f, k, mine[k], 2)

    def from_near(f):
        for k in range(depth):
            arrived(outs[f].at[core, theirs[k]], sems[10 * f + 1].at[k])
            onward(f, k, theirs[k], 1)

    def from_cross(f):
        for k in range(2 * depth):
            arrived(outs[f].at[core, last[k]], sems[10 * f + 2].at[k])
            onward(f, k, last[k], 0)

    def from_twin(f):
        arrived(outs[f].at[1 - core], sems[10 * f + 7].at[0])

    tile = n1.shape[1]
    tiles = tok.shape[0] // tile

    def put(i):
        slot, span = lax.rem(i, 2), pl.ds(pl.multiple_of(i * tile, tile), tile)
        return (
            pltpu.make_async_copy(n1.at[slot], n1_out.at[span, :], put_sem.at[slot]),
            pltpu.make_async_copy(qkv.at[slot], qkv_out.at[span, :], put_sem.at[2 + slot]),
        )

    def project(i):
        @pl.when(i >= 2)
        def _():
            for copy in put(i - 2):
                copy.wait()

        slot = lax.rem(i, 2)
        x = tok[pl.ds(pl.multiple_of(i * tile, tile), tile), :].astype(F32)
        n = (normalized(x)[0] * vecs[GAIN1 : GAIN1 + 1, :] + vecs[SHIFT1 : SHIFT1 + 1, :]).astype(BF)
        n1[slot] = n
        bias = []
        for h in range(2):
            cols = slice(h * WIDE, (h + 1) * WIDE)
            q, v = vecs[BIAS_Q : BIAS_Q + 1, cols], vecs[BIAS_V : BIAS_V + 1, cols]
            bias += [q, jnp.zeros_like(q), v]
        qkv[slot] = (mm(n, w[...]) + jnp.concatenate(bias, axis=1)).astype(BF)
        for copy in put(i):
            copy.start()

    def several(first, last):
        def step(i, carry):
            project(i)
            return carry

        lax.fori_loop(first, last, step, 0)

    from_far(0)
    from_near(0)
    from_cross(0)
    from_twin(0)
    fetch(outs[0], spots, [w], w_sem)
    chips = outs[0].shape[1]
    first_row = outs[0].shape[2] - 16
    for at in range(chips):
        pltpu.make_async_copy(outs[0].at[0, at, pl.ds(first_row, 16), :], rows.at[pl.ds(16 * at, 16), :], rows_sem.at[0]).start()
    from_far(1)
    from_near(1)
    arrived(rows, rows_sem.at[0])
    gathered_vectors(rows[...], vecs, wide)
    tok_load.wait()
    fetched(w, w_sem.at[0])
    w_put = pltpu.make_async_copy(w, w_out, load_sem.at[1])
    w_put.start()
    several(0, tiles // 4)
    from_far(2)
    several(tiles // 4, tiles // 2)
    from_near(2)
    from_cross(1)
    several(tiles // 2, tiles)
    from_cross(2)
    for i in (tiles - 2, tiles - 1):
        for copy in put(jnp.int32(i)):
            copy.wait()
    w_put.wait()
    for f in range(flows):
        chips = outs[f].shape[1]
        if f > 0:
            from_twin(f)
        arrived(outs[f].at[0], sems[10 * f + 6].at[0])
        arrived(outs[f].at[0, pl.ds(0, chips - 1)], sems[10 * f + 5].at[0])
        arrived(oths[f], sems[10 * f + 8].at[0])


def gather_shards(owns, oths, blocks, tokens, spots, depth):
    chips = 4 * depth
    count, width = tokens.shape
    tile = TILE // 2
    outs = [jax.ShapeDtypeStruct((2, chips, 2 * o.shape[0], WIDE), BF) for o in owns]
    outs += [
        jax.ShapeDtypeStruct((count, width), BF),
        jax.ShapeDtypeStruct((count, 3 * width), BF),
        jax.ShapeDtypeStruct((width, 3 * width), BF),
        jax.ShapeDtypeStruct((8, width), F32),
        jax.ShapeDtypeStruct((1, 4 * width), F32),
    ]
    dma = lambda n: pltpu.SemaphoreType.DMA((n,))
    scratch = [
        pltpu.VMEM((count, width), BF),
        pltpu.VMEM((width, 3 * width), BF),
        pltpu.VMEM((16 * chips, WIDE), BF),
        pltpu.VMEM((2, tile, width), BF),
        pltpu.VMEM((2, tile, 3 * width), BF),
        dma(2), dma(1), dma(1), dma(4),
    ]
    for _ in owns:
        scratch += [dma(depth), dma(depth), dma(2 * depth)] + [dma(1)] * 7
    return pl.pallas_call(
        functools.partial(gather_kernel, blocks, depth, spots),
        in_specs=[ANYWHERE] * (2 * len(owns) + 1),
        out_specs=[ANYWHERE] * (len(owns) + 3) + [pl.BlockSpec(memory_space=pltpu.VMEM)] * 2,
        out_shape=outs,
        scratch_shapes=scratch,
        compiler_params=pltpu.CompilerParams(
            collective_id=0, has_side_effects=True, vmem_limit_bytes=VMEM_LIMIT
        ),
        cost_estimate=cost(6 * count * width * width, 3e7),
        name="gather_and_qkv",
    )(*owns, *oths, tokens)


def pack_kernel(core, *refs):
    (wqkv, small, wo, w1, w2), outs = refs[:5], refs[5:]
    width = wo.shape[1]
    for c in range(2):

        @pl.when(core[0] == c)
        def _(c=c):
            for h in range(2):
                first, second, third = outs[:3] if h == c else outs[3:]
                rows = wo.shape[0]
                for t in range(3):
                    first[rows * t : rows * (t + 1), :] = wqkv[:, t * width + h * WIDE : t * width + (h + 1) * WIDE].astype(BF)
                first[3 * rows :, :] = small[...].astype(BF)
                second[0:rows, :] = wo[:, h * WIDE : (h + 1) * WIDE].astype(BF)
                for b in range(4):
                    cols = slice((4 * h + b) * WIDE, (4 * h + b + 1) * WIDE)
                    second[rows * (1 + b) : rows * (2 + b), :] = w1[:, cols].astype(BF)
                third[...] = w2[:, h * WIDE : (h + 1) * WIDE].astype(BF)


def pack(wqkv, small, wo, w1, w2, core):
    rows = wo.shape[0]
    ins = (wqkv, small, wo, w1, w2)
    shapes = [(3 * rows + small.shape[0], WIDE), (5 * rows, WIDE), (w2.shape[0], WIDE)] * 2
    return pl.pallas_call(
        pack_kernel,
        grid_spec=pltpu.PrefetchScalarGridSpec(
            num_scalar_prefetch=1,
            grid=(1,),
            in_specs=[whole(x.shape) for x in ins],
            out_specs=[whole(s) for s in shapes],
        ),
        out_shape=[jax.ShapeDtypeStruct(s, BF) for s in shapes],
        name="pack_shards",
    )(core, *ins)


def scatter_kernel(depth, splits, *refs):
    flows = len(splits)
    small_in, act, cot, n2, d_pre, attn, d_branch, n1, d_qkv = refs[:9]
    outs, rest = refs[9 : 9 + flows], refs[9 + flows :]
    (down, up, out, thirds, held, slots, held_sem, slot_sem), rest = rest[:8], rest[8:]
    ins = [small_in, down, up, out, thirds]
    width = cot.shape[1]
    tall = act.shape[1] // width
    ends = (tall, 2 * tall, 2 * tall + 1, 2 * tall + 1 + d_qkv.shape[1] // width)
    me, core, z, first, second = neighbours()

    def held_copy(k):
        return pltpu.make_async_copy((cot, n2, attn, n1)[k], held.at[k % 2], held_sem.at[k % 2])

    def level(t):
        return lax.rem(z + 1 + t, depth)

    def fetch_task(t):
        slot = lax.rem(t, 2)
        start = 0
        for source, end in zip((act, d_pre, d_branch, d_qkv), ends):
            block = level(t) if source is act else t - start

            @pl.when((t >= start) & (t < end))
            def _(source=source, block=block):
                cols = pl.ds(pl.multiple_of(block * width, 128), width)
                pltpu.make_async_copy(source.at[:, cols], slots.at[slot], slot_sem.at[slot]).start()

            start = end

    for k in range(2):
        held_copy(k).start()
        fetch_task(jnp.int32(k))
    chip = me // 2
    x, y = lax.rem(chip, 2), lax.rem(chip // 2, 2)
    twin = me + 1 - 2 * core
    deep = [lax.rem(z + k, depth) * 8 + lax.rem(me, 8) for k in range(1, depth)]
    greet([twin, me + first, me + second] + deep)
    plane = 2 * depth
    chips = 2 * plane

    def chip_of(j, core):
        bit2, bit1 = x + core * (y - x), y + core * (x - y)
        keep, side, k = j // plane, lax.rem(j, plane) // depth, lax.rem(j, depth)
        bit2 = (1 - bit2) + keep * (2 * bit2 - 1)
        bit1 = (1 - bit1) + side * (2 * bit1 - 1)
        return lax.rem(z + 1 + k, depth) * 4 + bit1 * (2 - core) + bit2 * (1 + core)

    def remote(src, dst, send_sem, recv_sem, device):
        return pltpu.make_async_remote_copy(
            src_ref=src,
            dst_ref=dst,
            send_sem=send_sem,
            recv_sem=recv_sem,
            device_id=(device,),
            device_id_type=pl.DeviceIdType.MESH,
        )

    def arrived(ref, sem):
        pltpu.make_async_copy(ref, ref, sem).wait()

    def flow(f):
        return rest[8 * f : 8 * f + 8]

    def sems(f):
        return rest[8 * flows + 11 * f : 8 * flows + 11 * f + 11]

    def loop(count, body):
        def step(j, carry):
            body(j)
            return carry

        lax.fori_loop(0, count, step, 0)

    def begin(f, some=None):
        own, in0 = flow(f)[:2]
        load, got0, sent0 = sems(f)[0], sems(f)[1], sems(f)[6]

        def body(j):
            pltpu.make_async_copy(ins[f].at[core, chip_of(j, core)], own.at[j], load.at[j]).start()
            remote(ins[f].at[1 - core, chip_of(j, 1 - core)], in0.at[j], sent0.at[0], got0.at[j], twin).start()

        loop(chips, body) if some is None else [body(j) for j in some]

    def sum_of(f, j):
        own, in0 = flow(f)[:2]
        arrived(own.at[j], sems(f)[0].at[j])
        arrived(in0.at[j], sems(f)[1].at[j])
        return own[j].astype(F32) + in0[j].astype(F32)

    def lagging(count, compute, send):
        def body(j):
            compute(j)

            @pl.when(j > 0)
            def _():
                send(j - 1)

        loop(count, body)
        send(count - 1)

    def across(f):
        own, _, in1 = flow(f)[:3]
        got1, sent1 = sems(f)[2], sems(f)[7]

        def compute(j):
            own[j] = sum_of(f, j).astype(own.dtype)

        lagging(plane, compute, lambda j: remote(own.at[j], in1.at[j], sent1.at[0], got1.at[j], me + second).start())

    def kept(f, j):
        in1 = flow(f)[2]
        arrived(in1.at[j], sems(f)[2].at[j])
        return sum_of(f, plane + j) + in1[j].astype(F32)

    def along(f):
        own, in2 = flow(f)[0], flow(f)[3]
        got2, sent2 = sems(f)[3], sems(f)[8]

        def compute(k):
            own[plane + k] = kept(f, k).astype(own.dtype)

        lagging(
            depth, compute, lambda k: remote(own.at[plane + k], in2.at[k], sent2.at[0], got2.at[k], me + first).start()
        )

    def upward(f):
        own, in2, in3, total = flow(f)[0], flow(f)[3], flow(f)[4], flow(f)[5]
        got2, got3, sent3 = sems(f)[3], sems(f)[4], sems(f)[9]

        def value(k):
            arrived(in2.at[k], got2.at[k])
            return kept(f, depth + k) + in2[k].astype(F32)

        for k in range(depth - 1):
            own[plane + depth + k] = value(k).astype(own.dtype)
            if k > 0:
                remote(own.at[plane + depth + k - 1], in3.at[k - 1], sent3.at[0], got3.at[k - 1], deep[k - 1]).start()
        total[...] = value(depth - 1)
        k = depth - 2
        remote(own.at[plane + depth + k], in3.at[k], sent3.at[0], got3.at[k], deep[k]).start()

    def mine(f, ref, which):
        if splits[f] == "rows":
            half = ref.shape[1] // 2
            return ref.at[:, pl.ds(pl.multiple_of(which * half, 8), half), :]
        half = ref.shape[0] // 2
        return ref.at[pl.ds(which * half, half)]

    def place(f, half, part):
        if splits[f] == "blocks":
            part = part.reshape((1,) + outs[f].shape[:1] + part.shape[2:])
        half_step, block_step = {4: (4, 1), 1: (1, 1), 3: (1, 2)}[part.shape[0]]
        for b in range(part.shape[0]):
            at = (half * half_step + b * block_step) * WIDE
            outs[f][:, pl.ds(pl.multiple_of(at, 128), WIDE)] = part[b]

    def finish(f):
        in3, total, theirs = flow(f)[4], flow(f)[5], flow(f)[6]
        for k in range(depth - 1):
            arrived(in3.at[k], sems(f)[4].at[k])
            total[...] += in3[k].astype(F32)
        if splits[f] is None:
            outs[f][...] = total[...]
        else:
            place(f, core, mine(f, total, core)[...])
            remote(mine(f, total, 1 - core), theirs, sems(f)[10].at[0], sems(f)[5].at[0], twin).start()

    def across_level(f, k):
        own, _, in1 = flow(f)[:3]
        got1, sent1 = sems(f)[2], sems(f)[7]
        for j in (k, depth + k):
            own[j] = sum_of(f, j).astype(own.dtype)
        for j in (k, depth + k):
            remote(own.at[j], in1.at[j], sent1.at[0], got1.at[j], me + second).start()

    def multiply(t):
        slot = lax.rem(t, 2)
        pltpu.make_async_copy(slots.at[slot], slots.at[slot], slot_sem.at[slot]).wait()

        @pl.when(t < tall)
        def _():
            low = tn(slots[slot], held[0]).astype(BF)
            count = chips // tall
            for h in range(2):
                part = low[:, h * WIDE : (h + 1) * WIDE].reshape((count,) + down.shape[2:])
                down[h, pl.ds(level(t) * count, count)] = part

        @pl.when(t >= tall)
        def _():
            k = jnp.where(t == ends[1], 0, 1)
            low = tn(held[k], slots[slot]).astype(BF)
            parts = [low[:, i * WIDE : (i + 1) * WIDE].reshape(chips, width // chips, WIDE) for i in range(2)]

            @pl.when(t < ends[1])
            def _():
                for i in range(2):
                    block = 2 * (t - tall) + i
                    up[block // tall, :, lax.rem(block, tall)] = parts[i]

            @pl.when(t == ends[1])
            def _():
                for i in range(2):
                    out[i, :, 0] = parts[i]

            @pl.when(t > ends[1])
            def _():
                for i in range(2):
                    block = 2 * (t - ends[2]) + i
                    thirds[block // 3, :, lax.rem(block, 3)] = parts[i]

        @pl.when(t + 2 < ends[3])
        def _():
            fetch_task(t + 2)

        for k, at in ((2, ends[0] - 1), (3, ends[1] - 1)):

            @pl.when(t == at)
            def _(k=k):
                held_copy(k).start()

    tiny, low, wide, side, last = range(flows)
    begin(tiny)
    for k in range(2):
        held_copy(k).wait()

    def task(t):
        for k, at in ((2, ends[1]), (3, ends[2])):

            @pl.when(t == at)
            def _(k=k):
                held_copy(k).wait()

        multiply(t)

        @pl.when((t >= 1) & (t <= depth))
        def _():
            begin(low, [t - 1 + q * depth for q in range(4)])

        @pl.when((t >= 2) & (t <= depth + 1))
        def _():
            across_level(low, t - 2)

        @pl.when(t == depth + 2)
        def _():
            across(tiny)

        @pl.when(t == ends[1])
        def _():
            begin(wide)
            along(low)

        @pl.when(t == ends[2])
        def _():
            begin(side)

        @pl.when(t == ends[2] + 1)
        def _():
            across(wide)

        @pl.when(t == ends[2] + 2)
        def _():
            across(side)

    loop(ends[3], task)
    upward(low)
    begin(last)
    across(last)
    along(wide)
    along(side)
    along(tiny)
    upward(wide)
    along(last)
    upward(side)
    upward(tiny)
    upward(last)
    for f in (low, wide, side, tiny, last):
        finish(f)
    for f in range(flows):
        _, in0, in1, in2, in3, total, theirs, _ = flow(f)
        if splits[f] is not None:
            arrived(theirs, sems(f)[5].at[0])
            place(f, 1 - core, theirs[...])
            arrived(theirs, sems(f)[10].at[0])
        for ref, sem in zip((in0, in1, in2, in3), sems(f)[6:10]):
            arrived(ref, sem.at[0])


def scatter_sums(small, down, up, out, qkv, depth):
    chips = 4 * depth
    tokens, width = down[1].shape
    rows = width // chips
    outs, buffers, signals = [], [], []
    dma = lambda n: pltpu.SemaphoreType.DMA((n,))
    shapes = [(2, chips, blocks, rows, WIDE) for blocks in (4, 4, 1, 3)]
    work = [pltpu.VMEM(x, BF) for x in shapes]
    work += [pltpu.VMEM((2, tokens, width), BF), pltpu.VMEM((2, tokens, width), BF), dma(2), dma(2)]
    kinds = [(small.shape[2:], small.dtype)] + [(x[2:], BF) for x in shapes]
    splits = (None, "blocks", "rows", "rows", "rows")
    for (chunk, kind), split in zip(kinds, splits):
        if split == "rows":
            part = (chunk[0], chunk[1] // 2) + chunk[2:]
        elif split == "blocks":
            part = (chunk[0] // 2,) + chunk[1:]
        else:
            part = chunk
        tall = part[-2] if split == "rows" else part[0] * part[1]
        cols = 2 * WIDE * (chunk[0] if split == "rows" else 1)
        outs.append(jax.ShapeDtypeStruct(part if split is None else (tall, cols), F32))
        for count in (chips, chips, chips // 2, depth, depth - 1):
            buffers.append(pltpu.VMEM((count,) + chunk, kind))
        buffers += [pltpu.VMEM(chunk, F32), pltpu.VMEM(part, F32), dma(1)]
        signals += [dma(chips), dma(chips), dma(chips // 2), dma(depth), dma(depth - 1)] + [dma(1)] * 6
    return pl.pallas_call(
        functools.partial(scatter_kernel, depth, splits),
        in_specs=[ANYWHERE] * 9,
        out_specs=[pl.BlockSpec(memory_space=pltpu.VMEM)] * len(outs),
        out_shape=outs,
        scratch_shapes=work + buffers + signals,
        compiler_params=pltpu.CompilerParams(
            collective_id=1, has_side_effects=True, vmem_limit_bytes=63 * 1024 * 1024
        ),
        cost_estimate=cost(0, 3e7),
        name="scatter_sums",
    )(small, *down, *up, *out, *qkv)


def by_neighbours(devices, width, hidden, count):
    rows = width // devices
    fits = rows * devices == width and rows % 8 == 0 and devices % 8 == 0
    return fits and width == 2 * WIDE and hidden == 4 * width and count % TILE == 0


def weight_halves(w):
    rows = w.shape[0]
    return w.reshape(rows, 3, 2, WIDE).transpose(0, 2, 1, 3).reshape(rows, -1)


def local(
    tokens, segments, cotangent, ln1_gain, ln1_shift, w_qkv, bias_q, bias_v, w_out, bias_out,
    ln2_gain, ln2_shift, w_up, bias_up, w_down, bias_down, *, seq,
):
    masters = (
        ln1_gain, ln1_shift, w_qkv, bias_q, bias_v, w_out, bias_out,
        ln2_gain, ln2_shift, w_up, bias_up, w_down, bias_down,
    )
    count, width = tokens.shape
    tables = attention_tables(segments.reshape(-1, seq))
    run = by_chips if by_neighbours(lax.axis_size("fsdp"), width, w_up.shape[1], count) else by_collectives
    return run(tokens, cotangent, tables, masters)


def by_collectives(tokens, cotangent, tables, masters):
    def norm(x, gain, shift):
        return normalized(x)[0] * gain + shift

    width = tokens.shape[1]
    full = [lax.all_gather(m.astype(BF), "fsdp", axis=0, tiled=True) for m in masters]
    g1, c1, wqkv, bq, bv, wo, bo, g2, c2, w1, b1, w2, b2 = [p.astype(F32) if p.ndim == 1 else p for p in full]
    wqkv = weight_halves(wqkv)
    rows = tokens.astype(F32)
    n1 = norm(rows, g1, c1).astype(BF)
    bias = weight_halves(jnp.concatenate([bq, jnp.zeros_like(bq), bv])[None])
    qkv = (mm(n1, wqkv) + bias).astype(BF)
    attn, attn_t, lse = attention_fwd(qkv, *tables)
    middle = rows + mm(attn, wo) + bo
    n2 = norm(middle, g2, c2).astype(BF)
    act_value, gelu_pull = jax.vjp(functools.partial(jax.nn.gelu, approximate=True), mm(n2, w1) + b1)
    act = act_value.astype(BF)
    layer_out = (middle + mm(act, w2) + b2).astype(BF)
    d_out = cotangent.astype(F32)
    d_pre = gelu_pull(mm_nt(cotangent, w2))[0].astype(BF)
    _, pull = jax.vjp(norm, middle, g2, c2)
    d_mid, d_g2, d_c2 = pull(mm_nt(d_pre, w1))
    d_mid = d_out + d_mid
    d_branch = d_mid.astype(BF)
    d_attn = mm_nt(d_branch, wo).astype(BF)
    d_qkv = attention_bwd(qkv, d_attn, attn_t, lse, *tables)
    _, pull = jax.vjp(norm, rows, g1, c1)
    d_rows, d_g1, d_c1 = pull(mm_nt(d_qkv, wqkv))
    input_grad = (d_mid + d_rows).astype(BF)
    total = lambda x: jnp.sum(x.astype(F32), axis=0)
    by_part = lambda x: x.reshape(-1, 2, 3, WIDE).transpose(0, 2, 1, 3).reshape(x.shape)
    sums = by_part(total(d_qkv)[None])[0]
    grads = (
        d_g1, d_c1, by_part(tn(n1, d_qkv)), sums[:width], sums[2 * width :], tn(attn, d_branch), total(d_branch),
        d_g2, d_c2, tn(n2, d_pre), total(d_pre), tn(act, cotangent), total(d_out),
    )
    return (layer_out, input_grad) + tuple(
        lax.psum_scatter(g, "fsdp", scatter_dimension=0, tiled=True) for g in grads
    )


def by_chips(tokens, cotangent, tables, masters):
    devices = lax.axis_size("fsdp")
    chips = devices // 2
    depth = devices // 8
    count, width = tokens.shape
    ln1_gain, ln1_shift, w_qkv, bias_q, bias_v, w_out, bias_out, ln2_gain, ln2_shift, w_up, bias_up, w_down, bias_down = masters
    part = width // devices
    two = 2 * part
    hidden = w_up.shape[1]
    core = lax.rem(lax.axis_index("fsdp"), 2).astype(jnp.int32).reshape(1)

    small = jnp.concatenate([ln1_gain, ln1_shift, bias_q, bias_v, bias_out, ln2_gain, ln2_shift, bias_down, bias_up])
    small = jnp.pad(small[None], ((0, 7), (0, WIDE - small.shape[0])))
    own1, own2, own3, oth1, oth2, oth3 = pack(w_qkv, small, w_out, w_up, w_down, core)

    def spots_qkv(h, chip):
        return [
            (two * t, two, 0, (pl.ds(two * chip, two), pl.ds((3 * h + t) * WIDE, WIDE))) for t in range(3)
        ]

    def spots_up(h, chip):
        rows = pl.ds(two * chip, two)
        return [(0, two, 0, (rows, pl.ds(h * WIDE, WIDE)))] + [
            (two * (1 + b), two, 1, (rows, pl.ds((4 * h + b) * WIDE, WIDE))) for b in range(4)
        ]

    def spots_down(h, chip):
        return [(0, 4 * two, 0, (pl.ds(4 * two * chip, 4 * two), pl.ds(h * WIDE, WIDE)))]

    blocks = ([part] * 3 + [8], [part] * 5, [4 * part])
    _, chunks2, chunks3, n1, qkv, wqkv, vecs, b1 = gather_shards(
        (own1, own2, own3), (oth1, oth2, oth3), blocks, tokens, spots_qkv, depth
    )
    attn, attn_t, lse = attention_fwd(qkv, *tables)
    layer_out, n2, act, d_pre, d_mid, d_branch, d_attn, sums2, sum_up = middle_part(
        attn, tokens, cotangent, vecs, b1, (chunks2, chunks3), (spots_up, spots_down)
    )

    d_qkv = attention_bwd(qkv, d_attn, attn_t, lse, *tables)
    input_grad, sums1 = first_norm_back(d_qkv, wqkv, tokens, d_mid, vecs)
    by_half = sums1[2].reshape(2, 3, WIDE).swapaxes(0, 1).reshape(3, width)
    vecs = jnp.concatenate([sums1[:2, :width], by_half[0:1], by_half[2:3], sums2[2:3], sums2[0:2], sums2[3:4]])
    vecs = vecs.reshape(8, devices, part).swapaxes(0, 1).reshape(devices, width // devices * 8)
    small = jnp.concatenate([vecs, sum_up.reshape(devices, 4 * part)], axis=1)
    small = small.reshape(chips, 2, 1, -1).swapaxes(0, 1)
    small = jnp.pad(small, ((0, 0), (0, 0), (0, 7), (0, WIDE - small.shape[3])))
    small, g_down, g_up, g_out, g_qkv = scatter_sums(
        small, (act, cotangent), (n2, d_pre), (attn, d_branch), (n1, d_qkv), depth
    )
    small, g_down, g_up, g_out, g_qkv = hand_over(small[:1], g_down, g_up, g_out, g_qkv)
    small = small[0]
    s = [small[i * part : (i + 1) * part] for i in range(8)]
    s_b1 = small[8 * part : 12 * part]
    return (
        layer_out, input_grad, s[0], s[1], g_qkv, s[2], s[3], g_out, s[4], s[5], s[6], g_up, s_b1, g_down, s[7],
    )


MICRO = 2


def solution(mesh):
    line, table = P("fsdp"), P("fsdp", None)
    weights = (line, line, table, line, line, table, line, line, line, table, line, table, line)

    def step(tokens, *rest):
        seq = tokens.shape[0] // (mesh.shape["fsdp"] * MICRO)
        return jax.shard_map(
            functools.partial(local, seq=seq),
            mesh=mesh,
            in_specs=(table, line, table) + weights,
            out_specs=(table, table) + weights,
            check_vma=False,
        )(tokens, *rest)

    return step
```

```python
import functools
import jax
import jax.numpy as jnp
from jax import lax
from jax.experimental import pallas as pl
from jax.experimental.pallas import tpu as pltpu
from jax.sharding import PartitionSpec as P

HD = 64
QB = 128
KB = 128
NEG = -1000000000.0
BF = jnp.bfloat16
F32 = jnp.float32
EPSILON = 1e-06
NT = (((1,), (1,)), ((), ()))


def mm(a, b):
    return jnp.dot(a, b, preferred_element_type=F32)


def mm_nt(a, b):
    return lax.dot_general(a, b, NT, preferred_element_type=F32)


def pair_diag(top, bottom):
    zero = jnp.zeros_like(top)
    return jnp.concatenate(
        [jnp.concatenate([top, zero], axis=1), jnp.concatenate([zero, bottom], axis=1)], axis=0
    )


SPANS = (2, 3, 4, 5, 6, 8)


def by_span(lo, hi, rows, run):
    need = hi - lo
    below = 0
    for span in SPANS:
        if below * KB >= rows:
            break
        size = min(span * KB, rows)
        last = size == rows

        @pl.when((need > below) & (last | (need <= span)))
        def _(size=size):
            run(pl.multiple_of(jnp.minimum(lo * KB, rows - size), KB), size)

        below = span


def chunks(k0, size):
    return [(pl.multiple_of(k0 + c, KB), min(2 * KB, size - c)) for c in range(0, size, 2 * KB)]


def terms(pieces):
    width = pieces[0].shape[1]
    row = lax.broadcasted_iota(jnp.int32, (8, width), 0)
    tail = jnp.zeros((8, width), F32)
    for i, piece in enumerate(pieces):
        tail = jnp.where(row == i, piece, tail)
    return tail


def three_parts(x):
    first = x.astype(BF).astype(F32)
    rest = x - first
    second = rest.astype(BF).astype(F32)
    return first, second, rest - second


def pair_rhs(feat, extra, p, qs):
    a = 128 * p
    block = pair_diag(feat[a : a + 64, qs], feat[a + 64 : a + 128, qs])
    rows = jnp.concatenate([extra[2 * p, :, qs], extra[2 * p + 1, :, qs]], axis=1)
    return block, jnp.concatenate([block, rows, jnp.zeros((112, 2 * QB), BF)], axis=0)


def attn_fwd_kernel(
    lo, hi, q_ref, k_ref, v_ref, oh_ref, mr_ref, o_ref, ot_ref, lse_ref, qt, vt, extra, tops
):
    seq = pl.program_id(0)
    rows = q_ref.shape[0]
    pairs = q_ref.shape[1] // 128
    heads = 2 * pairs
    vt[...] = v_ref[...].T
    qt[...] = (q_ref[...] * 0.125).astype(BF).T
    lane = lax.broadcasted_iota(jnp.int32, (8, heads * HD), 1) // HD
    pick = (lane == lax.broadcasted_iota(jnp.int32, (8, heads * HD), 0)).astype(BF)
    square = k_ref[...].astype(F32)
    norms = mm_nt(pick, (square * square).astype(BF))
    bound = jnp.sqrt(jnp.max(norms, axis=1, keepdims=True)) * 1.01
    for h in range(heads):
        qh = qt[64 * h : 64 * h + 64, :].astype(F32)
        length = jnp.sqrt(jnp.sum(qh * qh, axis=0, keepdims=True)) * 1.01
        m = (length * bound[h : h + 1, :]).astype(BF).astype(F32)
        tops[h : h + 1, :] = m
        extra[h, :, :] = jnp.concatenate([mr_ref[0], terms([-m])], axis=0).astype(BF)

    def keep(qs, p, l, full):
        a = 128 * p
        ot_ref[0, a : a + 64, qs] = full[0:64, 0:QB]
        ot_ref[0, a + 64 : a + 128, qs] = full[64:128, QB:]
        lse_ref[0, 0, 2 * p : 2 * p + 1, qs] = l[:, 0:QB]
        lse_ref[0, 0, 2 * p + 1 : 2 * p + 2, qs] = l[:, QB:]

    def q_step(qb, carry):
        qs = pl.ds(pl.multiple_of(qb * QB, QB), QB)

        def run(k0, size):
            rhs = [pair_rhs(qt, extra, p, qs)[1] for p in range(pairs)]
            l = [jnp.zeros((1, 2 * QB), F32)] * pairs
            acc = [None] * pairs
            for c0, cs in chunks(k0, size):
                ks = pl.ds(c0, cs)
                oh = oh_ref[ks, :]
                for p in range(pairs):
                    cols = slice(128 * p, 128 * p + 128)
                    w = jnp.exp(mm(jnp.concatenate([k_ref[ks, cols], oh], axis=1), rhs[p]))
                    l[p] = l[p] + jnp.sum(w, axis=0, keepdims=True)
                    part = mm(vt[cols, ks], w.astype(BF))
                    acc[p] = part if acc[p] is None else acc[p] + part
            for p in range(pairs):
                keep(qs, p, l[p], acc[p])

        by_span(lo[seq, qb], hi[seq, qb], rows, run)
        return carry

    lax.fori_loop(0, rows // QB, q_step, 0)

    @pl.when(jnp.min(lse_ref[0, 0]) < 1e-20)
    def _():
        for h in range(heads):
            extra[h, :, :] = jnp.concatenate([mr_ref[0], jnp.zeros_like(mr_ref[0])], axis=0).astype(BF)

        def q_again(qb, carry):
            qs = pl.ds(pl.multiple_of(qb * QB, QB), QB)
            for p in range(pairs):
                cols = slice(128 * p, 128 * p + 128)
                rhs = pair_rhs(qt, extra, p, qs)[1]

                def scores(kb):
                    ks = pl.ds(pl.multiple_of(kb * KB, KB), KB)
                    return ks, mm(jnp.concatenate([k_ref[ks, cols], oh_ref[ks, :]], axis=1), rhs)

                def top_step(kb, m):
                    return jnp.maximum(m, jnp.max(scores(kb)[1], axis=0, keepdims=True))

                blocks = rows // KB
                m = lax.fori_loop(0, blocks, top_step, jnp.full((1, 2 * QB), 2 * NEG, F32))

                def sum_step(kb, state):
                    ks, st = scores(kb)
                    w = jnp.exp(st - m)
                    return state[0] + jnp.sum(w, axis=0, keepdims=True), state[1] + mm(vt[cols, ks], w.astype(BF))

                start = (jnp.zeros((1, 2 * QB), F32), jnp.zeros((128, 2 * QB), F32))
                l, full = lax.fori_loop(0, blocks, sum_step, start)
                tops[2 * p : 2 * p + 1, qs] = m[:, 0:QB]
                tops[2 * p + 1 : 2 * p + 2, qs] = m[:, QB:]
                keep(qs, p, l, full)
            return carry

        lax.fori_loop(0, rows // QB, q_again, 0)

    for h in range(heads):
        l = lse_ref[0, 0, h : h + 1, :]
        hs = slice(64 * h, 64 * h + 64)
        ot_ref[0, hs, :] = ot_ref[0, hs, :] * (1.0 / l)
        lse_ref[0, 0, h : h + 1, :] = tops[h : h + 1, :] + jnp.log(l)
    o_ref[...] = ot_ref[0].astype(BF).T


def attn_bwd_kernel(
    lo, hi, q_ref, k_ref, v_ref, do_ref, ot_ref, lse_ref, oh_ref, mr_ref, dqkv_ref,
    qt, kt, dot, extra_q, extra_d, dqt, dkt, dvt,
):
    seq = pl.program_id(0)
    rows = q_ref.shape[0]
    pairs = q_ref.shape[1] // 128
    qt[...] = (q_ref[...] * 0.125).astype(BF).T
    kt[...] = k_ref[...].T
    dot[...] = do_ref[...].T
    for h in range(2 * pairs):
        r = slice(64 * h, 64 * h + 64)
        delta = jnp.sum(dot[r, :].astype(F32) * ot_ref[0, r, :], axis=0, keepdims=True)
        lse = lse_ref[0, 0, h : h + 1, :]
        extra_q[h, :, :] = jnp.concatenate([mr_ref[0], terms(three_parts(-lse))], axis=0).astype(BF)
        tail = terms(three_parts(-delta))
        extra_d[h, :, :] = jnp.concatenate([jnp.zeros_like(tail), tail], axis=0).astype(BF)
    dkt[...] = jnp.zeros_like(dkt)
    dvt[...] = jnp.zeros_like(dvt)

    def q_step(qb, carry):
        qs = pl.ds(pl.multiple_of(qb * QB, QB), QB)

        def run(k0, size):
            ks = pl.ds(k0, size)
            oh = oh_ref[ks, :]
            for p in range(pairs):
                a = 128 * p
                cols = slice(a, a + 128)
                qm, qx = pair_rhs(qt, extra_q, p, qs)
                dom, dx = pair_rhs(dot, extra_d, p, qs)
                w = jnp.exp(mm(jnp.concatenate([k_ref[ks, cols], oh], axis=1), qx))
                ds = (w * mm(jnp.concatenate([v_ref[ks, cols], oh], axis=1), dx)).astype(BF)
                dvt[cols, ks] += mm_nt(dom, w.astype(BF))
                dkt[cols, ks] += mm_nt(qm, ds)
                dq = mm(kt[cols, ks], ds)
                dqt[a : a + 64, qs] = dq[0:64, 0:QB]
                dqt[a + 64 : a + 128, qs] = dq[64:128, QB:]

        by_span(lo[seq, qb], hi[seq, qb], rows, run)
        return carry

    lax.fori_loop(0, rows // QB, q_step, 0)
    wide = dqt.shape[0]
    dqkv_ref[:, 0:wide] = (dqt[...] * 0.125).astype(BF).T
    dqkv_ref[:, wide : 2 * wide] = dkt[...].astype(BF).T
    dqkv_ref[:, 2 * wide :] = dvt[...].astype(BF).T


WIDE = 384
TILE = 512
VMEM_LIMIT = 60 * 1024 * 1024


def params(*semantics):
    return pltpu.CompilerParams(dimension_semantics=semantics or None, vmem_limit_bytes=VMEM_LIMIT)


def cost(flops, data):
    return pl.CostEstimate(flops=int(flops), bytes_accessed=int(data), transcendentals=0)


def whole(shape):
    zero = (0,) * len(shape)
    return pl.BlockSpec(shape, lambda *_: zero)


ANYWHERE = pl.BlockSpec(memory_space=pl.ANY)


def attention_tables(segs):
    order = jnp.where(segs == 0, 1 << 20, segs)
    seqs, length = segs.shape
    first = order[:, ::QB]
    last = order[:, QB - 1 :: QB]
    lo = jnp.sum((order[:, None, :] < first[:, :, None]).astype(jnp.int32), axis=2) // KB
    hi = (jnp.sum((order[:, None, :] <= last[:, :, None]).astype(jnp.int32), axis=2) + KB - 1) // KB
    ids = jnp.arange(128, dtype=jnp.int32)[None, :]
    onehot = (segs.reshape(-1)[:, None] == ids) | ((ids >= 8) & (ids < 16))
    differ = segs[:, None, :] != jnp.arange(8, dtype=jnp.int32)[None, :, None]
    return lo, hi, onehot.astype(BF), jnp.where(differ, NEG, 0.0)


def attention_fwd(qkv, lo, hi, onehot, miss):
    seqs = lo.shape[0]
    rows = qkv.shape[0] // seqs
    wide = WIDE
    width = qkv.shape[1] // 3
    parts = width // wide
    col = lambda at: pl.BlockSpec((rows, wide), lambda s, j, *_: (s, 3 * j + at))
    return pl.pallas_call(
        attn_fwd_kernel,
        grid_spec=pltpu.PrefetchScalarGridSpec(
            num_scalar_prefetch=2,
            grid=(seqs, parts),
            in_specs=[
                col(0), col(1), col(2),
                pl.BlockSpec((rows, 128), lambda s, *_: (s, 0)),
                pl.BlockSpec((1, 8, rows), lambda s, *_: (s, 0, 0)),
            ],
            out_specs=[
                pl.BlockSpec((rows, wide), lambda s, j, *_: (s, j)),
                pl.BlockSpec((1, wide, rows), lambda s, j, *_: (s, j, 0)),
                pl.BlockSpec((1, 1, wide // HD, rows), lambda s, j, *_: (s, j, 0, 0)),
            ],
            scratch_shapes=[
                pltpu.VMEM((wide, rows), BF),
                pltpu.VMEM((wide, rows), BF),
                pltpu.VMEM((wide // HD, 16, rows), BF),
                pltpu.VMEM((8, rows), F32),
            ],
        ),
        out_shape=[
            jax.ShapeDtypeStruct((qkv.shape[0], width), BF),
            jax.ShapeDtypeStruct((seqs, width, rows), F32),
            jax.ShapeDtypeStruct((seqs, parts, wide // HD, rows), F32),
        ],
        compiler_params=params("arbitrary", "arbitrary"),
        cost_estimate=cost(24e9, 2e7),
        name="attention_forward",
    )(lo, hi, qkv, qkv, qkv, onehot, miss)


def attention_bwd(qkv, d_attn, ot, lse, lo, hi, onehot, miss):
    seqs = lo.shape[0]
    rows = qkv.shape[0] // seqs
    wide = WIDE
    col = lambda at: pl.BlockSpec((rows, wide), lambda s, j, *_: (s, 3 * j + at))
    return pl.pallas_call(
        attn_bwd_kernel,
        grid_spec=pltpu.PrefetchScalarGridSpec(
            num_scalar_prefetch=2,
            grid=(seqs, d_attn.shape[1] // wide),
            in_specs=[
                col(0), col(1), col(2),
                pl.BlockSpec((rows, wide), lambda s, j, *_: (s, j)),
                pl.BlockSpec((1, wide, rows), lambda s, j, *_: (s, j, 0)),
                pl.BlockSpec((1, 1, wide // HD, rows), lambda s, j, *_: (s, j, 0, 0)),
                pl.BlockSpec((rows, 128), lambda s, *_: (s, 0)),
                pl.BlockSpec((1, 8, rows), lambda s, *_: (s, 0, 0)),
            ],
            out_specs=pl.BlockSpec((rows, 3 * wide), lambda s, j, *_: (s, j)),
            scratch_shapes=[
                pltpu.VMEM((wide, rows), BF),
                pltpu.VMEM((wide, rows), BF),
                pltpu.VMEM((wide, rows), BF),
                pltpu.VMEM((wide // HD, 16, rows), BF),
                pltpu.VMEM((wide // HD, 16, rows), BF),
                pltpu.VMEM((wide, rows), F32),
                pltpu.VMEM((wide, rows), F32),
                pltpu.VMEM((wide, rows), F32),
            ],
        ),
        out_shape=jax.ShapeDtypeStruct(qkv.shape, BF),
        compiler_params=params("arbitrary", "arbitrary"),
        cost_estimate=cost(44e9, 4e7),
        name="attention_backward",
    )(lo, hi, qkv, qkv, qkv, d_attn, ot, lse, onehot, miss)


def normalized(x):
    mean = jnp.mean(x, axis=-1, keepdims=True)
    centered = x - mean
    scale = lax.rsqrt(jnp.mean(centered * centered, axis=-1, keepdims=True) + EPSILON)
    return centered * scale, scale


def norm_back(d, xhat, scale, gain):
    e = d * gain
    return scale * (e - jnp.mean(e, axis=-1, keepdims=True) - xhat * jnp.mean(e * xhat, axis=-1, keepdims=True))


def clear_first(*refs):
    @pl.when(pl.program_id(0) == 0)
    def _():
        for ref in refs:
            ref[...] = jnp.zeros_like(ref)


def add_row(ref, row, values):
    ref[row : row + 1, 0 : values.shape[1]] += jnp.sum(values, axis=0, keepdims=True)


def fetch(chunks, spots, outs, sems):
    for h in range(2):
        for chip in range(chunks.shape[1]):
            for row, count, which, target in spots(h, chip):
                pltpu.make_async_copy(
                    chunks.at[h, chip, pl.ds(row, count), :], outs[which].at[target], sems.at[which]
                ).start()


def fetched(out, sem):
    pltpu.make_async_copy(out, out, sem).wait()


GAIN1, SHIFT1, BIAS_Q, BIAS_V, BIAS_OUT, GAIN2, SHIFT2, BIAS_DOWN = range(8)
STRIP = 256
CURVE = 0.7978845608028654
CUBIC = 0.044715


def middle_kernel(
    spots, attn, tok, cot, vec, b1, chunks2, chunks3,
    out, n2, act, d_pre, d_mid, d_branch, d_attn, sums, sum_up, wo, w1, w2, sem,
):
    @pl.when(pl.program_id(0) == 0)
    def _():
        fetch(chunks2, spots[0], [wo, w1], sem)
        fetch(chunks3, spots[1], [w2], sem.at[pl.ds(2, 1)])
        for ref in (sums, sum_up):
            ref[...] = jnp.zeros_like(ref)
        for k, ref in enumerate((wo, w1, w2)):
            fetched(ref, sem.at[k])

    x = tok[...].astype(F32) + mm(attn[...], wo[...]) + vec[BIAS_OUT : BIAS_OUT + 1]
    xhat, scale = normalized(x)
    n = (xhat * vec[GAIN2 : GAIN2 + 1] + vec[SHIFT2 : SHIFT2 + 1]).astype(BF)
    n2[...] = n
    d_out = cot[...]
    y = x + vec[BIAS_DOWN : BIAS_DOWN + 1]
    d_n2 = None
    for j in range(w1.shape[1] // STRIP):
        cols = slice(j * STRIP, (j + 1) * STRIP)
        u = mm(n, w1[:, cols]) + b1[:, cols]
        d_act = mm_nt(d_out, w2[cols, :])
        square = u * u
        th = jnp.tanh(u * (CURVE + (CURVE * CUBIC) * square))
        half = 0.5 * u
        hidden = (half + half * th).astype(BF)
        act[:, cols] = hidden
        y = y + mm(hidden, w2[cols, :])
        slope = (0.5 + 0.5 * th) + half * (1.0 - th * th) * (CURVE + (3.0 * CURVE * CUBIC) * square)
        low = (d_act * slope).astype(BF)
        d_pre[:, cols] = low
        sum_up[:, cols] += jnp.sum(low.astype(F32), axis=0, keepdims=True)
        part = mm_nt(low, w1[:, cols])
        d_n2 = part if d_n2 is None else d_n2 + part
    out[...] = y.astype(BF)
    add_row(sums, 0, d_n2 * xhat)
    add_row(sums, 1, d_n2)
    g = d_out.astype(F32)
    add_row(sums, 3, g)
    d = g + norm_back(d_n2, xhat, scale, vec[GAIN2 : GAIN2 + 1])
    d_mid[...] = d
    low = d.astype(BF)
    d_branch[...] = low
    add_row(sums, 2, low.astype(F32))
    d_attn[...] = mm_nt(low, wo[...]).astype(BF)


def middle_part(attn, tokens, cotangent, vec, b1, gathered, spots):
    count, width = tokens.shape
    hidden = b1.shape[1]
    rows = TILE
    tile = lambda w: pl.BlockSpec((rows, w), lambda i: (i, 0))
    row = lambda w, kind: jax.ShapeDtypeStruct((count, w), kind)
    return pl.pallas_call(
        functools.partial(middle_kernel, spots),
        grid=(count // rows,),
        in_specs=[tile(width), tile(width), tile(width), whole(vec.shape), whole(b1.shape)] + [ANYWHERE] * 2,
        out_specs=[
            tile(width), tile(width), tile(hidden), tile(hidden), tile(width), tile(width), tile(width),
            whole((8, width)), whole((1, hidden)),
        ],
        scratch_shapes=[
            pltpu.VMEM((width, width), BF),
            pltpu.VMEM((width, hidden), BF),
            pltpu.VMEM((hidden, width), BF),
            pltpu.SemaphoreType.DMA((3,)),
        ],
        out_shape=[
            row(width, BF), row(width, BF), row(hidden, BF), row(hidden, BF), row(width, F32), row(width, BF),
            row(width, BF), jax.ShapeDtypeStruct((8, width), F32), jax.ShapeDtypeStruct((1, hidden), F32),
        ],
        compiler_params=params("arbitrary"),
        cost_estimate=cost(4 * count * width * (width + 2 * hidden), 6e7),
        name="middle",
    )(attn, tokens, cotangent, vec, b1, *gathered)


def first_norm_kernel(d_qkv, w, tok, d_mid, vec, out, sums):
    clear_first(sums)
    d = mm_nt(d_qkv[...], w[...])
    xhat, scale = normalized(tok[...].astype(F32))
    add_row(sums, 0, d * xhat)
    add_row(sums, 1, d)
    add_row(sums, 2, d_qkv[...].astype(F32))
    out[...] = (d_mid[...] + norm_back(d, xhat, scale, vec[0:1])).astype(BF)


def first_norm_back(d_qkv, w, tokens, d_mid, vec):
    count, width = tokens.shape
    cols = d_qkv.shape[1]
    tile = lambda w: pl.BlockSpec((TILE, w), lambda i: (i, 0))
    return pl.pallas_call(
        first_norm_kernel,
        grid=(count // TILE,),
        in_specs=[tile(cols), whole(w.shape), tile(width), tile(width), whole(vec.shape)],
        out_specs=[tile(width), whole((8, cols))],
        out_shape=[jax.ShapeDtypeStruct((count, width), BF), jax.ShapeDtypeStruct((8, cols), F32)],
        compiler_params=params("arbitrary"),
        cost_estimate=cost(2 * count * width * cols, 3e7),
        name="first_norm_back",
    )(d_qkv, w, tokens, d_mid, vec)


def tn(a, b):
    return lax.dot_general(a, b, (((0,), (0,)), ((), ())), preferred_element_type=F32)


def hand_over_kernel(*refs):
    count = len(refs) // 2
    for x, out in zip(refs[:count], refs[count:]):
        out[...] = x[...]


def hand_over(*arrays):
    return pl.pallas_call(
        hand_over_kernel,
        grid=(1,),
        in_specs=[whole(x.shape) for x in arrays],
        out_specs=[whole(x.shape) for x in arrays],
        out_shape=[jax.ShapeDtypeStruct(x.shape, x.dtype) for x in arrays],
        compiler_params=params("arbitrary"),
        name="hand_over",
    )(*arrays)


def neighbours():
    me = lax.axis_index("fsdp")
    core = lax.rem(me, 2)
    x = lax.rem(me // 2, 2)
    y = lax.rem(me // 4, 2)
    along_y = 4 * (1 - 2 * y)
    along_x = 2 * (1 - 2 * x)
    first = (1 - core) * along_y + core * along_x
    second = along_y + along_x - first
    return me, core, me // 8, first, second


def greet(others):
    barrier = pltpu.get_barrier_semaphore()
    for other in others:
        pl.semaphore_signal(barrier, inc=1, device_id=(other,), device_id_type=pl.DeviceIdType.MESH)
    pl.semaphore_wait(barrier, len(others))


def gathered_vectors(rows, vecs, wide):
    width = vecs.shape[1]
    devices = rows.shape[0] // 8
    part = width // devices
    source = lax.broadcasted_iota(jnp.int32, (WIDE, width), 0)
    owner = lax.broadcasted_iota(jnp.int32, (rows.shape[0], width), 0)

    def spread(first, size, lane):
        lanes = lane * width + lax.broadcasted_iota(jnp.int32, (1, width), 1)
        device = lanes // size
        pick = (source == first + lanes - device * size).astype(F32).astype(BF)
        return jnp.sum(jnp.where(owner == 8 * device, mm(rows, pick), 0.0), axis=0, keepdims=True)

    for v in range(8):
        vecs[v : v + 1, :] = spread(v * part, part, 0)
    for b in range(4):
        wide[:, b * width : (b + 1) * width] = spread(8 * part, 4 * part, b)


def gather_kernel(blocks, depth, spots, *refs):
    flows = len(blocks)
    owns, oths, tok_in, refs = refs[:flows], refs[flows : 2 * flows], refs[2 * flows], refs[2 * flows + 1 :]
    outs, (n1_out, qkv_out, w_out, vecs, wide), refs = refs[:flows], refs[flows : flows + 5], refs[flows + 5 :]
    (tok, w, rows, n1, qkv, load_sem, rows_sem, w_sem, put_sem), sems = refs[:9], refs[9:]
    tok_load = pltpu.make_async_copy(tok_in, tok, load_sem.at[0])
    tok_load.start()
    me, core, z, first, second = neighbours()
    twin = me + 1 - 2 * core
    chip = me // 2
    deep = [chip * 2 + core] + [lax.rem(z + k, depth) * 8 + lax.rem(me, 8) for k in range(1, depth)]
    greet([twin, me + first, me + second] + deep[1:])
    mine = [lax.rem(z + depth - k, depth) * 4 + lax.rem(chip, 4) for k in range(depth)]
    theirs = [at + first // 2 for at in mine]
    last = [at + second // 2 for at in mine + theirs]

    def send(f, at, send_sem, recv_sem, device):
        pltpu.make_async_remote_copy(
            src_ref=outs[f].at[core, at],
            dst_ref=outs[f].at[core, at],
            send_sem=send_sem,
            recv_sem=recv_sem,
            device_id=(device,),
            device_id_type=pl.DeviceIdType.MESH,
        ).start()

    def arrived(ref, sem):
        pltpu.make_async_copy(ref, ref, sem).wait()

    def onward(f, k, at, steps):
        far, near, cross, seen, local, out, twin_out, twin_in, pair_out, pair_in = sems[10 * f : 10 * f + 10]
        if steps == 2:
            send(f, at, out.at[0], near.at[k], me + first)
        if steps >= 1:
            send(f, at, out.at[0], cross.at[k if steps == 2 else depth + k], me + second)
        send(f, at, twin_out.at[0], twin_in.at[0], twin)

    for f in range(flows):
        pair_out, pair_in, local = sems[10 * f + 8], sems[10 * f + 9], sems[10 * f + 4]
        row = 0
        for size in blocks[f]:
            here_rows = pl.ds(pl.multiple_of(2 * row + core * size, 8), size)
            pltpu.make_async_copy(
                owns[f].at[pl.ds(row, size), :], outs[f].at[core, chip, here_rows, :], local.at[0]
            ).start()
            pltpu.make_async_remote_copy(
                src_ref=oths[f].at[pl.ds(row, size), :],
                dst_ref=outs[f].at[1 - core, chip, here_rows, :],
                send_sem=pair_out.at[0],
                recv_sem=pair_in.at[0],
                device_id=(twin,),
                device_id_type=pl.DeviceIdType.MESH,
            ).start()
            row += size
    for f in range(flows):
        far, out = sems[10 * f], sems[10 * f + 5]
        arrived(owns[f], sems[10 * f + 4].at[0])
        arrived(owns[f], sems[10 * f + 9].at[0])
        for k in range(1, depth):
            send(f, chip, out.at[0], far.at[k], deep[k])
        onward(f, 0, chip, 2)

    def from_far(f):
        for k in range(1, depth):
            arrived(outs[f].at[core, mine[k]], sems[10 * f].at[k])
            onward(f, k, mine[k], 2)

    def from_near(f):
        for k in range(depth):
            arrived(outs[f].at[core, theirs[k]], sems[10 * f + 1].at[k])
            onward(f, k, theirs[k], 1)

    def from_cross(f):
        for k in range(2 * depth):
            arrived(outs[f].at[core, last[k]], sems[10 * f + 2].at[k])
            onward(f, k, last[k], 0)

    def from_twin(f):
        arrived(outs[f].at[1 - core], sems[10 * f + 7].at[0])

    tile = n1.shape[1]
    tiles = tok.shape[0] // tile

    def put(i):
        slot, span = lax.rem(i, 2), pl.ds(pl.multiple_of(i * tile, tile), tile)
        return (
            pltpu.make_async_copy(n1.at[slot], n1_out.at[span, :], put_sem.at[slot]),
            pltpu.make_async_copy(qkv.at[slot], qkv_out.at[span, :], put_sem.at[2 + slot]),
        )

    def project(i):
        @pl.when(i >= 2)
        def _():
            for copy in put(i - 2):
                copy.wait()

        slot = lax.rem(i, 2)
        x = tok[pl.ds(pl.multiple_of(i * tile, tile), tile), :].astype(F32)
        n = (normalized(x)[0] * vecs[GAIN1 : GAIN1 + 1, :] + vecs[SHIFT1 : SHIFT1 + 1, :]).astype(BF)
        n1[slot] = n
        bias = []
        for h in range(2):
            cols = slice(h * WIDE, (h + 1) * WIDE)
            q, v = vecs[BIAS_Q : BIAS_Q + 1, cols], vecs[BIAS_V : BIAS_V + 1, cols]
            bias += [q, jnp.zeros_like(q), v]
        qkv[slot] = (mm(n, w[...]) + jnp.concatenate(bias, axis=1)).astype(BF)
        for copy in put(i):
            copy.start()

    def several(first, last):
        def step(i, carry):
            project(i)
            return carry

        lax.fori_loop(first, last, step, 0)

    from_far(0)
    from_near(0)
    from_cross(0)
    from_twin(0)
    fetch(outs[0], spots, [w], w_sem)
    chips = outs[0].shape[1]
    first_row = outs[0].shape[2] - 16
    for at in range(chips):
        pltpu.make_async_copy(outs[0].at[0, at, pl.ds(first_row, 16), :], rows.at[pl.ds(16 * at, 16), :], rows_sem.at[0]).start()
    from_far(1)
    from_near(1)
    arrived(rows, rows_sem.at[0])
    gathered_vectors(rows[...], vecs, wide)
    tok_load.wait()
    fetched(w, w_sem.at[0])
    w_put = pltpu.make_async_copy(w, w_out, load_sem.at[1])
    w_put.start()
    several(0, tiles // 4)
    from_far(2)
    several(tiles // 4, tiles // 2)
    from_near(2)
    from_cross(1)
    several(tiles // 2, tiles)
    from_cross(2)
    for i in (tiles - 2, tiles - 1):
        for copy in put(jnp.int32(i)):
            copy.wait()
    w_put.wait()
    for f in range(flows):
        chips = outs[f].shape[1]
        if f > 0:
            from_twin(f)
        arrived(outs[f].at[0], sems[10 * f + 6].at[0])
        arrived(outs[f].at[0, pl.ds(0, chips - 1)], sems[10 * f + 5].at[0])
        arrived(oths[f], sems[10 * f + 8].at[0])


def gather_shards(owns, oths, blocks, tokens, spots, depth):
    chips = 4 * depth
    count, width = tokens.shape
    tile = TILE // 2
    outs = [jax.ShapeDtypeStruct((2, chips, 2 * o.shape[0], WIDE), BF) for o in owns]
    outs += [
        jax.ShapeDtypeStruct((count, width), BF),
        jax.ShapeDtypeStruct((count, 3 * width), BF),
        jax.ShapeDtypeStruct((width, 3 * width), BF),
        jax.ShapeDtypeStruct((8, width), F32),
        jax.ShapeDtypeStruct((1, 4 * width), F32),
    ]
    dma = lambda n: pltpu.SemaphoreType.DMA((n,))
    scratch = [
        pltpu.VMEM((count, width), BF),
        pltpu.VMEM((width, 3 * width), BF),
        pltpu.VMEM((16 * chips, WIDE), BF),
        pltpu.VMEM((2, tile, width), BF),
        pltpu.VMEM((2, tile, 3 * width), BF),
        dma(2), dma(1), dma(1), dma(4),
    ]
    for _ in owns:
        scratch += [dma(depth), dma(depth), dma(2 * depth)] + [dma(1)] * 7
    return pl.pallas_call(
        functools.partial(gather_kernel, blocks, depth, spots),
        in_specs=[ANYWHERE] * (2 * len(owns) + 1),
        out_specs=[ANYWHERE] * (len(owns) + 3) + [pl.BlockSpec(memory_space=pltpu.VMEM)] * 2,
        out_shape=outs,
        scratch_shapes=scratch,
        compiler_params=pltpu.CompilerParams(
            collective_id=0, has_side_effects=True, vmem_limit_bytes=VMEM_LIMIT
        ),
        cost_estimate=cost(6 * count * width * width, 3e7),
        name="gather_and_qkv",
    )(*owns, *oths, tokens)


def pack_kernel(core, *refs):
    (wqkv, small, wo, w1, w2), outs = refs[:5], refs[5:]
    width = wo.shape[1]
    for c in range(2):

        @pl.when(core[0] == c)
        def _(c=c):
            for h in range(2):
                first, second, third = outs[:3] if h == c else outs[3:]
                rows = wo.shape[0]
                for t in range(3):
                    first[rows * t : rows * (t + 1), :] = wqkv[:, t * width + h * WIDE : t * width + (h + 1) * WIDE].astype(BF)
                first[3 * rows :, :] = small[...].astype(BF)
                second[0:rows, :] = wo[:, h * WIDE : (h + 1) * WIDE].astype(BF)
                for b in range(4):
                    cols = slice((4 * h + b) * WIDE, (4 * h + b + 1) * WIDE)
                    second[rows * (1 + b) : rows * (2 + b), :] = w1[:, cols].astype(BF)
                third[...] = w2[:, h * WIDE : (h + 1) * WIDE].astype(BF)


def pack(wqkv, small, wo, w1, w2, core):
    rows = wo.shape[0]
    ins = (wqkv, small, wo, w1, w2)
    shapes = [(3 * rows + small.shape[0], WIDE), (5 * rows, WIDE), (w2.shape[0], WIDE)] * 2
    return pl.pallas_call(
        pack_kernel,
        grid_spec=pltpu.PrefetchScalarGridSpec(
            num_scalar_prefetch=1,
            grid=(1,),
            in_specs=[whole(x.shape) for x in ins],
            out_specs=[whole(s) for s in shapes],
        ),
        out_shape=[jax.ShapeDtypeStruct(s, BF) for s in shapes],
        name="pack_shards",
    )(core, *ins)


def scatter_kernel(depth, splits, *refs):
    flows = len(splits)
    small_in, act, cot, n2, d_pre, attn, d_branch, n1, d_qkv = refs[:9]
    outs, rest = refs[9 : 9 + flows], refs[9 + flows :]
    (down, up, out, thirds, held, slots, held_sem, slot_sem), rest = rest[:8], rest[8:]
    ins = [small_in, down, up, out, thirds]
    width = cot.shape[1]
    tall = act.shape[1] // width
    ends = (tall, 2 * tall, 2 * tall + 1, 2 * tall + 1 + d_qkv.shape[1] // width)
    me, core, z, first, second = neighbours()

    def held_copy(k):
        return pltpu.make_async_copy((cot, n2, attn, n1)[k], held.at[k % 2], held_sem.at[k % 2])

    def level(t):
        return lax.rem(z + 1 + t, depth)

    def fetch_task(t):
        slot = lax.rem(t, 2)
        start = 0
        for source, end in zip((act, d_pre, d_branch, d_qkv), ends):
            block = level(t) if source is act else t - start

            @pl.when((t >= start) & (t < end))
            def _(source=source, block=block):
                cols = pl.ds(pl.multiple_of(block * width, 128), width)
                pltpu.make_async_copy(source.at[:, cols], slots.at[slot], slot_sem.at[slot]).start()

            start = end

    for k in range(2):
        held_copy(k).start()
        fetch_task(jnp.int32(k))
    chip = me // 2
    x, y = lax.rem(chip, 2), lax.rem(chip // 2, 2)
    twin = me + 1 - 2 * core
    deep = [lax.rem(z + k, depth) * 8 + lax.rem(me, 8) for k in range(1, depth)]
    greet([twin, me + first, me + second] + deep)
    plane = 2 * depth
    chips = 2 * plane

    def chip_of(j, core):
        bit2, bit1 = x + core * (y - x), y + core * (x - y)
        keep, side, k = j // plane, lax.rem(j, plane) // depth, lax.rem(j, depth)
        bit2 = (1 - bit2) + keep * (2 * bit2 - 1)
        bit1 = (1 - bit1) + side * (2 * bit1 - 1)
        return lax.rem(z + 1 + k, depth) * 4 + bit1 * (2 - core) + bit2 * (1 + core)

    def remote(src, dst, send_sem, recv_sem, device):
        return pltpu.make_async_remote_copy(
            src_ref=src,
            dst_ref=dst,
            send_sem=send_sem,
            recv_sem=recv_sem,
            device_id=(device,),
            device_id_type=pl.DeviceIdType.MESH,
        )

    def arrived(ref, sem):
        pltpu.make_async_copy(ref, ref, sem).wait()

    def flow(f):
        return rest[8 * f : 8 * f + 8]

    def sems(f):
        return rest[8 * flows + 11 * f : 8 * flows + 11 * f + 11]

    def loop(count, body):
        def step(j, carry):
            body(j)
            return carry

        lax.fori_loop(0, count, step, 0)

    def begin(f, some=None):
        own, in0 = flow(f)[:2]
        load, got0, sent0 = sems(f)[0], sems(f)[1], sems(f)[6]

        def body(j):
            pltpu.make_async_copy(ins[f].at[core, chip_of(j, core)], own.at[j], load.at[j]).start()
            remote(ins[f].at[1 - core, chip_of(j, 1 - core)], in0.at[j], sent0.at[0], got0.at[j], twin).start()

        loop(chips, body) if some is None else [body(j) for j in some]

    def sum_of(f, j):
        own, in0 = flow(f)[:2]
        arrived(own.at[j], sems(f)[0].at[j])
        arrived(in0.at[j], sems(f)[1].at[j])
        return own[j].astype(F32) + in0[j].astype(F32)

    def lagging(count, compute, send):
        def body(j):
            compute(j)

            @pl.when(j > 0)
            def _():
                send(j - 1)

        loop(count, body)
        send(count - 1)

    def across(f):
        own, _, in1 = flow(f)[:3]
        got1, sent1 = sems(f)[2], sems(f)[7]

        def compute(j):
            own[j] = sum_of(f, j).astype(own.dtype)

        lagging(plane, compute, lambda j: remote(own.at[j], in1.at[j], sent1.at[0], got1.at[j], me + second).start())

    def kept(f, j):
        in1 = flow(f)[2]
        arrived(in1.at[j], sems(f)[2].at[j])
        return sum_of(f, plane + j) + in1[j].astype(F32)

    def along(f):
        own, in2 = flow(f)[0], flow(f)[3]
        got2, sent2 = sems(f)[3], sems(f)[8]

        def compute(k):
            own[plane + k] = kept(f, k).astype(own.dtype)

        lagging(
            depth, compute, lambda k: remote(own.at[plane + k], in2.at[k], sent2.at[0], got2.at[k], me + first).start()
        )

    def upward(f):
        own, in2, in3, total = flow(f)[0], flow(f)[3], flow(f)[4], flow(f)[5]
        got2, got3, sent3 = sems(f)[3], sems(f)[4], sems(f)[9]

        def value(k):
            arrived(in2.at[k], got2.at[k])
            return kept(f, depth + k) + in2[k].astype(F32)

        for k in range(depth - 1):
            own[plane + depth + k] = value(k).astype(own.dtype)
            if k > 0:
                remote(own.at[plane + depth + k - 1], in3.at[k - 1], sent3.at[0], got3.at[k - 1], deep[k - 1]).start()
        total[...] = value(depth - 1)
        k = depth - 2
        remote(own.at[plane + depth + k], in3.at[k], sent3.at[0], got3.at[k], deep[k]).start()

    def mine(f, ref, which):
        if splits[f] == "rows":
            half = ref.shape[1] // 2
            return ref.at[:, pl.ds(pl.multiple_of(which * half, 8), half), :]
        half = ref.shape[0] // 2
        return ref.at[pl.ds(which * half, half)]

    def place(f, half, part):
        if splits[f] == "blocks":
            part = part.reshape((1,) + outs[f].shape[:1] + part.shape[2:])
        half_step, block_step = {4: (4, 1), 1: (1, 1), 3: (1, 2)}[part.shape[0]]
        for b in range(part.shape[0]):
            at = (half * half_step + b * block_step) * WIDE
            outs[f][:, pl.ds(pl.multiple_of(at, 128), WIDE)] = part[b]

    def finish(f):
        in3, total, theirs = flow(f)[4], flow(f)[5], flow(f)[6]
        for k in range(depth - 1):
            arrived(in3.at[k], sems(f)[4].at[k])
            total[...] += in3[k].astype(F32)
        if splits[f] is None:
            outs[f][...] = total[...]
        else:
            place(f, core, mine(f, total, core)[...])
            remote(mine(f, total, 1 - core), theirs, sems(f)[10].at[0], sems(f)[5].at[0], twin).start()

    def across_level(f, k):
        own, _, in1 = flow(f)[:3]
        got1, sent1 = sems(f)[2], sems(f)[7]
        for j in (k, depth + k):
            own[j] = sum_of(f, j).astype(own.dtype)
        for j in (k, depth + k):
            remote(own.at[j], in1.at[j], sent1.at[0], got1.at[j], me + second).start()

    def multiply(t):
        slot = lax.rem(t, 2)
        pltpu.make_async_copy(slots.at[slot], slots.at[slot], slot_sem.at[slot]).wait()

        @pl.when(t < tall)
        def _():
            low = tn(slots[slot], held[0]).astype(BF)
            count = chips // tall
            for h in range(2):
                part = low[:, h * WIDE : (h + 1) * WIDE].reshape((count,) + down.shape[2:])
                down[h, pl.ds(level(t) * count, count)] = part

        @pl.when(t >= tall)
        def _():
            k = jnp.where(t == ends[1], 0, 1)
            low = tn(held[k], slots[slot]).astype(BF)
            parts = [low[:, i * WIDE : (i + 1) * WIDE].reshape(chips, width // chips, WIDE) for i in range(2)]

            @pl.when(t < ends[1])
            def _():
                for i in range(2):
                    block = 2 * (t - tall) + i
                    up[block // tall, :, lax.rem(block, tall)] = parts[i]

            @pl.when(t == ends[1])
            def _():
                for i in range(2):
                    out[i, :, 0] = parts[i]

            @pl.when(t > ends[1])
            def _():
                for i in range(2):
                    block = 2 * (t - ends[2]) + i
                    thirds[block // 3, :, lax.rem(block, 3)] = parts[i]

        @pl.when(t + 2 < ends[3])
        def _():
            fetch_task(t + 2)

        for k, at in ((2, ends[0] - 1), (3, ends[1] - 1)):

            @pl.when(t == at)
            def _(k=k):
                held_copy(k).start()

    tiny, low, wide, side, last = range(flows)
    begin(tiny)
    for k in range(2):
        held_copy(k).wait()

    def task(t):
        for k, at in ((2, ends[1]), (3, ends[2])):

            @pl.when(t == at)
            def _(k=k):
                held_copy(k).wait()

        multiply(t)

        @pl.when((t >= 1) & (t <= depth))
        def _():
            begin(low, [t - 1 + q * depth for q in range(4)])

        @pl.when((t >= 2) & (t <= depth + 1))
        def _():
            across_level(low, t - 2)

        @pl.when(t == depth + 2)
        def _():
            across(tiny)

        @pl.when(t == ends[1])
        def _():
            begin(wide)
            along(low)

        @pl.when(t == ends[2])
        def _():
            begin(side)

        @pl.when(t == ends[2] + 1)
        def _():
            across(wide)

        @pl.when(t == ends[2] + 2)
        def _():
            across(side)

    loop(ends[3], task)
    upward(low)
    begin(last)
    across(last)
    along(wide)
    along(side)
    along(tiny)
    upward(wide)
    along(last)
    upward(side)
    upward(tiny)
    upward(last)
    for f in (low, wide, side, tiny, last):
        finish(f)
    for f in range(flows):
        _, in0, in1, in2, in3, total, theirs, _ = flow(f)
        if splits[f] is not None:
            arrived(theirs, sems(f)[5].at[0])
            place(f, 1 - core, theirs[...])
            arrived(theirs, sems(f)[10].at[0])
        for ref, sem in zip((in0, in1, in2, in3), sems(f)[6:10]):
            arrived(ref, sem.at[0])


def scatter_sums(small, down, up, out, qkv, depth):
    chips = 4 * depth
    tokens, width = down[1].shape
    rows = width // chips
    outs, buffers, signals = [], [], []
    dma = lambda n: pltpu.SemaphoreType.DMA((n,))
    shapes = [(2, chips, blocks, rows, WIDE) for blocks in (4, 4, 1, 3)]
    work = [pltpu.VMEM(x, BF) for x in shapes]
    work += [pltpu.VMEM((2, tokens, width), BF), pltpu.VMEM((2, tokens, width), BF), dma(2), dma(2)]
    kinds = [(small.shape[2:], small.dtype)] + [(x[2:], BF) for x in shapes]
    splits = (None, "blocks", "rows", "rows", "rows")
    for (chunk, kind), split in zip(kinds, splits):
        if split == "rows":
            part = (chunk[0], chunk[1] // 2) + chunk[2:]
        elif split == "blocks":
            part = (chunk[0] // 2,) + chunk[1:]
        else:
            part = chunk
        tall = part[-2] if split == "rows" else part[0] * part[1]
        cols = 2 * WIDE * (chunk[0] if split == "rows" else 1)
        outs.append(jax.ShapeDtypeStruct(part if split is None else (tall, cols), F32))
        for count in (chips, chips, chips // 2, depth, depth - 1):
            buffers.append(pltpu.VMEM((count,) + chunk, kind))
        buffers += [pltpu.VMEM(chunk, F32), pltpu.VMEM(part, F32), dma(1)]
        signals += [dma(chips), dma(chips), dma(chips // 2), dma(depth), dma(depth - 1)] + [dma(1)] * 6
    return pl.pallas_call(
        functools.partial(scatter_kernel, depth, splits),
        in_specs=[ANYWHERE] * 9,
        out_specs=[pl.BlockSpec(memory_space=pltpu.VMEM)] * len(outs),
        out_shape=outs,
        scratch_shapes=work + buffers + signals,
        compiler_params=pltpu.CompilerParams(
            collective_id=1, has_side_effects=True, vmem_limit_bytes=63 * 1024 * 1024
        ),
        cost_estimate=cost(0, 3e7),
        name="scatter_sums",
    )(small, *down, *up, *out, *qkv)


def by_neighbours(devices, width, hidden, count):
    rows = width // devices
    fits = rows * devices == width and rows % 8 == 0 and devices % 8 == 0
    return fits and width == 2 * WIDE and hidden == 4 * width and count % TILE == 0


def weight_halves(w):
    rows = w.shape[0]
    return w.reshape(rows, 3, 2, WIDE).transpose(0, 2, 1, 3).reshape(rows, -1)


def local(
    tokens, segments, cotangent, ln1_gain, ln1_shift, w_qkv, bias_q, bias_v, w_out, bias_out,
    ln2_gain, ln2_shift, w_up, bias_up, w_down, bias_down, *, seq,
):
    masters = (
        ln1_gain, ln1_shift, w_qkv, bias_q, bias_v, w_out, bias_out,
        ln2_gain, ln2_shift, w_up, bias_up, w_down, bias_down,
    )
    count, width = tokens.shape
    tables = attention_tables(segments.reshape(-1, seq))
    run = by_chips if by_neighbours(lax.axis_size("fsdp"), width, w_up.shape[1], count) else by_collectives
    return run(tokens, cotangent, tables, masters)


def by_collectives(tokens, cotangent, tables, masters):
    def norm(x, gain, shift):
        return normalized(x)[0] * gain + shift

    width = tokens.shape[1]
    full = [lax.all_gather(m.astype(BF), "fsdp", axis=0, tiled=True) for m in masters]
    g1, c1, wqkv, bq, bv, wo, bo, g2, c2, w1, b1, w2, b2 = [p.astype(F32) if p.ndim == 1 else p for p in full]
    wqkv = weight_halves(wqkv)
    rows = tokens.astype(F32)
    n1 = norm(rows, g1, c1).astype(BF)
    bias = weight_halves(jnp.concatenate([bq, jnp.zeros_like(bq), bv])[None])
    qkv = (mm(n1, wqkv) + bias).astype(BF)
    attn, attn_t, lse = attention_fwd(qkv, *tables)
    middle = rows + mm(attn, wo) + bo
    n2 = norm(middle, g2, c2).astype(BF)
    act_value, gelu_pull = jax.vjp(functools.partial(jax.nn.gelu, approximate=True), mm(n2, w1) + b1)
    act = act_value.astype(BF)
    layer_out = (middle + mm(act, w2) + b2).astype(BF)
    d_out = cotangent.astype(F32)
    d_pre = gelu_pull(mm_nt(cotangent, w2))[0].astype(BF)
    _, pull = jax.vjp(norm, middle, g2, c2)
    d_mid, d_g2, d_c2 = pull(mm_nt(d_pre, w1))
    d_mid = d_out + d_mid
    d_branch = d_mid.astype(BF)
    d_attn = mm_nt(d_branch, wo).astype(BF)
    d_qkv = attention_bwd(qkv, d_attn, attn_t, lse, *tables)
    _, pull = jax.vjp(norm, rows, g1, c1)
    d_rows, d_g1, d_c1 = pull(mm_nt(d_qkv, wqkv))
    input_grad = (d_mid + d_rows).astype(BF)
    total = lambda x: jnp.sum(x.astype(F32), axis=0)
    by_part = lambda x: x.reshape(-1, 2, 3, WIDE).transpose(0, 2, 1, 3).reshape(x.shape)
    sums = by_part(total(d_qkv)[None])[0]
    grads = (
        d_g1, d_c1, by_part(tn(n1, d_qkv)), sums[:width], sums[2 * width :], tn(attn, d_branch), total(d_branch),
        d_g2, d_c2, tn(n2, d_pre), total(d_pre), tn(act, cotangent), total(d_out),
    )
    return (layer_out, input_grad) + tuple(
        lax.psum_scatter(g, "fsdp", scatter_dimension=0, tiled=True) for g in grads
    )


def by_chips(tokens, cotangent, tables, masters):
    devices = lax.axis_size("fsdp")
    chips = devices // 2
    depth = devices // 8
    count, width = tokens.shape
    ln1_gain, ln1_shift, w_qkv, bias_q, bias_v, w_out, bias_out, ln2_gain, ln2_shift, w_up, bias_up, w_down, bias_down = masters
    part = width // devices
    two = 2 * part
    hidden = w_up.shape[1]
    core = lax.rem(lax.axis_index("fsdp"), 2).astype(jnp.int32).reshape(1)

    small = jnp.concatenate([ln1_gain, ln1_shift, bias_q, bias_v, bias_out, ln2_gain, ln2_shift, bias_down, bias_up])
    small = jnp.pad(small[None], ((0, 7), (0, WIDE - small.shape[0])))
    own1, own2, own3, oth1, oth2, oth3 = pack(w_qkv, small, w_out, w_up, w_down, core)

    def spots_qkv(h, chip):
        return [
            (two * t, two, 0, (pl.ds(two * chip, two), pl.ds((3 * h + t) * WIDE, WIDE))) for t in range(3)
        ]

    def spots_up(h, chip):
        rows = pl.ds(two * chip, two)
        return [(0, two, 0, (rows, pl.ds(h * WIDE, WIDE)))] + [
            (two * (1 + b), two, 1, (rows, pl.ds((4 * h + b) * WIDE, WIDE))) for b in range(4)
        ]

    def spots_down(h, chip):
        return [(0, 4 * two, 0, (pl.ds(4 * two * chip, 4 * two), pl.ds(h * WIDE, WIDE)))]

    blocks = ([part] * 3 + [8], [part] * 5, [4 * part])
    _, chunks2, chunks3, n1, qkv, wqkv, vecs, b1 = gather_shards(
        (own1, own2, own3), (oth1, oth2, oth3), blocks, tokens, spots_qkv, depth
    )
    attn, attn_t, lse = attention_fwd(qkv, *tables)
    layer_out, n2, act, d_pre, d_mid, d_branch, d_attn, sums2, sum_up = middle_part(
        attn, tokens, cotangent, vecs, b1, (chunks2, chunks3), (spots_up, spots_down)
    )

    d_qkv = attention_bwd(qkv, d_attn, attn_t, lse, *tables)
    input_grad, sums1 = first_norm_back(d_qkv, wqkv, tokens, d_mid, vecs)
    by_half = sums1[2].reshape(2, 3, WIDE).swapaxes(0, 1).reshape(3, width)
    vecs = jnp.concatenate([sums1[:2, :width], by_half[0:1], by_half[2:3], sums2[2:3], sums2[0:2], sums2[3:4]])
    vecs = vecs.reshape(8, devices, part).swapaxes(0, 1).reshape(devices, width // devices * 8)
    small = jnp.concatenate([vecs, sum_up.reshape(devices, 4 * part)], axis=1)
    small = small.reshape(chips, 2, 1, -1).swapaxes(0, 1)
    small = jnp.pad(small, ((0, 0), (0, 0), (0, 7), (0, WIDE - small.shape[3])))
    small, g_down, g_up, g_out, g_qkv = scatter_sums(
        small, (act, cotangent), (n2, d_pre), (attn, d_branch), (n1, d_qkv), depth
    )
    small, g_down, g_up, g_out, g_qkv = hand_over(small[:1], g_down, g_up, g_out, g_qkv)
    small = small[0]
    s = [small[i * part : (i + 1) * part] for i in range(8)]
    s_b1 = small[8 * part : 12 * part]
    return (
        layer_out, input_grad, s[0], s[1], g_qkv, s[2], s[3], g_out, s[4], s[5], s[6], g_up, s_b1, g_down, s[7],
    )


MICRO = 2


def solution(mesh):
    line, table = P("fsdp"), P("fsdp", None)
    weights = (line, line, table, line, line, table, line, line, line, table, line, table, line)

    def step(tokens, *rest):
        seq = tokens.shape[0] // (mesh.shape["fsdp"] * MICRO)
        return jax.shard_map(
            functools.partial(local, seq=seq),
            mesh=mesh,
            in_specs=(table, line, table) + weights,
            out_specs=(table, table) + weights,
            check_vma=False,
        )(tokens, *rest)

    return step
```
